32 devices in a mesh: dp: 16 (over z, y, x), tensor: 2 (over core).
Axes of the slice: x: 2, y: 2, z: 4, core: 2. Of those that a mesh axis runs over, the one named last changes fastest.
Arguments:
- images: bfloat16 [64, 256, 768], P(('dp', 'tensor')), may hold values from -6 to 6
- valid_count: int32 [64], P('dp'), may hold values from 16 to 256, as said below
- ln_gain: float32 [2, 2, 768], replicated, may hold values from 0.25 to 1.75
- ln_bias: float32 [2, 2, 768], replicated, may hold values from -1.5 to 1.5
- w_qkv: bfloat16 [2, 768, 3, 768], P(None, None, None, 'tensor'), may hold values from -0.21875 to 0.21875
- qv_bias: float32 [2, 2, 768], P(None, None, 'tensor'), may hold values from -2.5 to 2.5
- w_out: bfloat16 [2, 768, 768], P(None, 'tensor'), may hold values from -0.875 to 0.875
- out_bias: float32 [2, 2, 768], replicated, may hold values from -1.5 to 1.5
- w_up: bfloat16 [2, 768, 3072], P(None, None, 'tensor'), may hold values from -0.21875 to 0.21875
- up_bias: float32 [2, 3072], P(None, 'tensor'), may hold values from -1.5 to 1.5
- w_down: bfloat16 [2, 3072, 768], P(None, 'tensor'), may hold values from -0.109375 to 0.109375
- cotangent: bfloat16 [64, 256, 768], P(('dp', 'tensor')), may hold values from -6 to 6
Outputs:
- layer_out: float32 [64, 256, 768], P(('dp', 'tensor'))
- pooled: float32 [64, 768], P(('dp', 'tensor'))
- input_grad: float32 [64, 256, 768], P(('dp', 'tensor'))
- ln_gain_grad: float32 [2, 2, 768], replicated
- ln_bias_grad: float32 [2, 2, 768], replicated
- qkv_grad: float32 [2, 768, 3, 768], P(None, 'dp', None, 'tensor')
- qv_bias_grad: float32 [2, 2, 768], P(None, None, 'tensor')
- out_grad: float32 [2, 768, 768], P(None, 'tensor', 'dp')
- out_bias_grad: float32 [2, 2, 768], replicated
- up_grad: float32 [2, 768, 3072], P(None, 'dp', 'tensor')
- up_bias_grad: float32 [2, 3072], P(None, 'tensor')
- down_grad: float32 [2, 3072, 768], P(None, 'tensor', 'dp')
The draws below stay inside these ranges and needn't reach their ends.
Inputs may be any that keep to these rules, and one draw needn't show every extreme that they name: `valid_count`: some image has exactly 256 valid patches and some other exactly 16; an image's valid patches are its first slots.
All inputs are finite; a program needn't handle non-finite values.
Results may differ from the reference program's by a relative error of at most 0.024.
Values may be sent and summed in bfloat16 or wider, within the bound.
No kernel may reach another device: no remote copies, remote signals or barrier semaphores. Data moves between devices by JAX's collectives and lax.ppermute only.
A program may use at most 192 MiB of HBM per device.

```python
import math
import jax
import jax.numpy as jnp
from jax import lax

D = 768
HEADS = 12
HEAD_DIM = 64
FF = 3072
LAYERS = 2
SLOTS = 256
MIN_LEN = 16
IMAGES = 64


def draw_valid_count(key, part):
    first_key, second_key, third_key = jax.random.split(key, 3)
    counts = jax.random.randint(first_key, (IMAGES,), MIN_LEN, SLOTS + 1)
    highest = jax.random.randint(second_key, (), 0, IMAGES)
    lowest_at = (highest + 1 + jax.random.randint(third_key, (), 0, IMAGES - 1)) % IMAGES
    counts = counts.at[highest].set(SLOTS).at[lowest_at].set(MIN_LEN)
    return counts.astype(jnp.int32)


def spiked(array, own_key, source, target, shards_of, factor):
    owner, partner = [(jnp.arange(array.shape[axis_at]) // (array.shape[axis_at] // shards_of)).reshape([-1 if axis == axis_at else 1 for axis in range(array.ndim)]) for axis_at in (source, target)]
    chosen = jax.random.permutation(own_key, shards_of)[partner]
    strong = (owner == chosen) | (owner == (partner + shards_of // 2) % shards_of)
    return jnp.where(strong, factor * array, array)


def levels(rng, dims, cuts, least, high):
    def one(position, shards_of):
        draws = jax.random.uniform(jax.random.fold_in(jax.random.fold_in(rng, 6), position), (shards_of,), jnp.float32, least / len(cuts), high / len(cuts))
        return jnp.repeat(jnp.exp(draws), dims[position] // shards_of).reshape((-1,) + (1,) * (len(dims) - position - 1))

    level = one(*cuts[0])
    for cut in cuts[1:]:
        level = level * one(*cut)
    return level


def normal_values(stream_key, dims, scale, reach, shards=(), kind=jnp.bfloat16):
    entries = jax.random.normal(stream_key, dims, jnp.float32) * scale
    if len(shards) > 0:
        entries = levels(stream_key, dims, shards, -0.22, 0.18) * entries
    return jnp.clip(entries, min=-reach, max=reach).astype(kind)


def noise_with(key, dims, spread, limit, cuts, heavy, kind=jnp.bfloat16):
    result = spread * jax.random.normal(key, dims, jnp.float32)
    if cuts:
        result = result * levels(key, dims, cuts, -0.22, 0.18)
    return jnp.clip(spiked(result, jax.random.fold_in(key, 3), *heavy), -limit, limit).astype(kind)


def setup_inputs(seed: int = 0) -> dict:
    key_of = jax.random.split(jax.random.key(seed), 13)
    images = noise_with(key_of[0], (IMAGES, SLOTS, D), 1.0, 6.0, ((0, 32),), (0, 2, 32, 2.75))
    valid_count = draw_valid_count(jax.random.fold_in(key_of[12], 71), 0)
    ln_gain = jnp.clip(1.0 + 0.15 * jax.random.normal(key_of[2], (LAYERS, 2, D), jnp.float32), 0.25, 1.75)
    ln_bias = normal_values(key_of[3], (LAYERS, 2, D), 0.3, 1.5, (), jnp.float32)
    w_qkv = normal_values(key_of[4], (LAYERS, D, 3, D), D ** -0.5, 0.21875, ((3, 2),))
    qv_bias = normal_values(key_of[5], (LAYERS, 2, D), 0.5, 2.5, ((2, 2),), jnp.float32)
    w_out = normal_values(key_of[6], (LAYERS, D, D), (D // 16) ** -0.5, 0.875, ((1, 2),))
    out_bias = normal_values(key_of[7], (LAYERS, 2, D), 0.3, 1.5, (), jnp.float32)
    w_up = normal_values(key_of[8], (LAYERS, D, FF), D ** -0.5, 0.21875, ((2, 2),))
    up_bias = normal_values(key_of[9], (LAYERS, FF), 0.3, 1.5, ((1, 2),), jnp.float32)
    w_down = normal_values(key_of[10], (LAYERS, FF, D), FF ** -0.5, 0.109375, ((1, 2),))
    cotangent = noise_with(key_of[11], (IMAGES, SLOTS, D), 1.0, 6.0, ((0, 32),), (0, 2, 32, 2.75))
    return {"images": images, "valid_count": valid_count, "ln_gain": ln_gain, "ln_bias": ln_bias, "w_qkv": w_qkv, "qv_bias": qv_bias, "w_out": w_out, "out_bias": out_bias, "w_up": w_up, "up_bias": up_bias, "w_down": w_down, "cotangent": cotangent}


HIGHEST = lax.Precision.HIGHEST
EPSILON = 1e-06
NEGATIVE = -1e+30

@jax.custom_vjp
def low(v):
    return lax.optimization_barrier(v.astype(jnp.bfloat16)).astype(jnp.float32)

@jax.custom_vjp
def low_back(v):
    return v

def low_keep(v):
    return (low(v), None)

def low_pass(kept, grad):
    return (grad,)

def back_keep(v):
    return (v, None)

def back_low(kept, grad):
    return (low(grad),)
low.defvjp(low_keep, low_pass)
low_back.defvjp(back_keep, back_low)

def normalize(values, norm_gain, norm_bias):
    average = lax.optimization_barrier(jnp.mean(values, axis=-1, keepdims=True))
    centred = values - average
    variance = lax.optimization_barrier(jnp.mean(centred * centred, axis=-1, keepdims=True))
    return centred * lax.rsqrt(variance + EPSILON) * norm_gain + norm_bias

def project(left, right):
    return jnp.einsum('...k,kn->...n', left, right, precision=HIGHEST)

def attend_group(operands):
    queries, keys_in, values_in, key_mask = operands
    scores = jnp.einsum('bqhe,bkhe->bhqk', queries, keys_in, precision=HIGHEST) * HEAD_DIM ** (-0.5)
    scores = low_back(scores)
    scores = jnp.where(key_mask[:, None, None, :], scores, NEGATIVE)
    weights = low(jax.nn.softmax(scores, axis=-1))
    return jnp.einsum('bhqk,bkhe->bqhe', weights, values_in, precision=HIGHEST)

def reference(images, valid_count, ln_gain, ln_bias, w_qkv, qv_bias, w_out, out_bias, w_up, up_bias, w_down, cotangent):
    count_img = images.shape[0]
    group = math.gcd(count_img, max(1, 4096 // SLOTS))
    key_mask = jnp.arange(SLOTS, dtype=jnp.int32)[None, :] < valid_count[:, None]
    grouped_mask = key_mask.reshape(count_img // group, group, SLOTS)

    def split_heads(values):
        return values.reshape(count_img // group, group, SLOTS, HEADS, HEAD_DIM)

    def forward(stream, gains, biases, qkv_all, qv_all, out_all, outb_all, up_all, upb_all, down_all):
        for layer_index in range(LAYERS):
            normed = low(normalize(stream, gains[layer_index, 0], biases[layer_index, 0]))
            joint = project(normed, qkv_all[layer_index].reshape(D, 3 * D)).reshape(count_img, SLOTS, 3, D)
            queries = low(low_back(joint[:, :, 0]) + qv_all[layer_index, 0])
            keys_in = low(low_back(joint[:, :, 1]))
            values_in = low(low_back(joint[:, :, 2]) + qv_all[layer_index, 1])
            attended = lax.map(jax.checkpoint(attend_group), (split_heads(queries), split_heads(keys_in), split_heads(values_in), grouped_mask))
            attended = low(low_back(attended.reshape(count_img, SLOTS, D)))
            stream = stream + (low_back(project(attended, out_all[layer_index])) + outb_all[layer_index, 0])
            normed = low(normalize(stream, gains[layer_index, 1], biases[layer_index, 1]))
            hidden = low_back(project(normed, up_all[layer_index])) + upb_all[layer_index]
            hidden = low(jax.nn.gelu(hidden, approximate=False))
            stream = stream + (low_back(project(hidden, down_all[layer_index])) + outb_all[layer_index, 1])
        return stream
    float_args = (images.astype(jnp.float32), ln_gain.astype(jnp.float32), ln_bias.astype(jnp.float32), w_qkv.astype(jnp.float32), qv_bias.astype(jnp.float32), w_out.astype(jnp.float32), out_bias.astype(jnp.float32), w_up.astype(jnp.float32), up_bias.astype(jnp.float32), w_down.astype(jnp.float32))
    layer_out, pullback = jax.vjp(forward, *float_args)
    gradients = pullback(cotangent.astype(jnp.float32))
    pooled = lax.optimization_barrier(jnp.sum(jnp.where(key_mask[:, :, None], layer_out, 0.0), axis=1)) / valid_count.astype(jnp.float32)[:, None]
    return (layer_out, pooled, gradients[0], gradients[1], gradients[2], gradients[3], gradients[4], gradients[5], gradients[6], gradients[7], gradients[8], gradients[9])
```

```python
import functools
import math

import jax
import jax.numpy as jnp
from jax import lax
from jax.experimental import pallas as pl
from jax.experimental.pallas import tpu as pltpu
from jax.sharding import PartitionSpec as P

HEAD_DIM = 64
LAYERS = 2
EPSILON = 1e-06
NEGATIVE = -1e30
BF16 = jnp.bfloat16
F32 = jnp.float32
CHUNK = 16


def dot(left, right):
    return lax.dot_general(left, right, (((1,), (0,)), ((), ())), preferred_element_type=F32)


def dot_nt(left, right):
    return lax.dot_general(left, right, (((1,), (1,)), ((), ())), preferred_element_type=F32)


def fixed(shape, *lead):
    where = tuple(lead) + (0,) * (len(shape) - len(lead))
    return pl.BlockSpec(shape, lambda *_: where)


def out(shape, dtype):
    return jax.ShapeDtypeStruct(shape, dtype)


def cost(flops, *arrays):
    total = sum(math.prod(a.shape) * a.dtype.itemsize for a in arrays)
    return pl.CostEstimate(flops=int(flops), bytes_accessed=int(total), transcendentals=0)


def call(body, name, grid, ins, in_specs, outs, out_specs, scratch=(), flops=0):
    return pl.pallas_call(
        body,
        name=name,
        grid=grid,
        in_specs=in_specs,
        out_specs=out_specs,
        out_shape=outs,
        scratch_shapes=list(scratch),
        cost_estimate=cost(flops, *ins, *outs),
    )(*ins)


def by_rows(rows, body, unroll=2):
    def step(index, carry):
        body(pl.multiple_of(index * CHUNK, CHUNK))
        return carry

    lax.fori_loop(0, rows // CHUNK, step, 0, unroll=unroll)


def moments(values):
    average = jnp.mean(values, axis=-1, keepdims=True)
    centred = values - average
    variance = jnp.mean(centred * centred, axis=-1, keepdims=True)
    return centred, lax.rsqrt(variance + EPSILON)


def normalized(values, gain, bias):
    centred, scale = moments(values)
    return centred * scale * gain + bias


def norm_backward(values, grad_normed, gain):
    centred, scale = moments(values)
    unit = centred * scale
    grad_unit = grad_normed * gain
    first = jnp.mean(grad_unit, axis=-1, keepdims=True)
    second = jnp.mean(grad_unit * unit, axis=-1, keepdims=True)
    return scale * (grad_unit - first - unit * second), grad_normed * unit


def fold_rows(values):
    total = values[0:8]
    for start in range(8, values.shape[0], 8):
        total = total + values[start : start + 8]
    return total


def prep_kernel(images, cotangent, gain, bias, order, normed, normed_t, cotangent_t):
    def rows(start):
        here = pl.ds(start, CHUNK)
        values = images[here, :].astype(F32)
        normed[here, :] = normalized(values, gain[0, 0:1, :], bias[0, 0:1, :]).astype(BF16)

    by_rows(images.shape[0], rows)
    normed_t[...] = dot_nt(order[...], normed[...]).astype(BF16)
    cotangent_t[...] = dot_nt(order[...], cotangent[...]).astype(BF16)


def head_masks(slots):
    lane = lax.broadcasted_iota(jnp.int32, (slots, 2 * HEAD_DIM), 1)
    return lane < HEAD_DIM, lane >= HEAD_DIM


def attend_kernel(layer, slots, counts, normed, weight, bias, joint, attended, lse):
    width = attended.shape[1]
    pairs = width // (2 * HEAD_DIM)
    scale = HEAD_DIM ** (-0.5)
    for member in range(3):
        product = dot(normed[...], weight[0, member])
        if member == 0:
            product = product + bias[layer, 0:1, :]
        if member == 2:
            product = product + bias[layer, 1:2, :]
        joint[member] = product.astype(BF16)
    masks = head_masks(slots)
    key_index = lax.broadcasted_iota(jnp.int32, (slots, slots), 0)

    def step(index, carry):
        image = index // pairs
        pair = index % pairs
        rows = pl.ds(pl.multiple_of(image * slots, slots), slots)
        lanes = pl.ds(pl.multiple_of(pair * 2 * HEAD_DIM, 2 * HEAD_DIM), 2 * HEAD_DIM)
        queries = joint[0, rows, lanes]
        keys_in = joint[1, rows, lanes] * jnp.asarray(scale, BF16)
        values_t = joint[2, rows, lanes].T
        valid = key_index < counts[image]
        parts = []
        for side in range(2):
            keys_side = jnp.where(masks[side], keys_in, jnp.zeros_like(keys_in))
            scores = jnp.where(valid, dot_nt(keys_side, queries), NEGATIVE)
            largest = jnp.max(scores, axis=0, keepdims=True)
            exponent = jnp.exp(scores - largest)
            total = jnp.sum(exponent, axis=0, keepdims=True)
            probs = (exponent * (1.0 / total)).astype(BF16)
            parts.append(dot(values_t[side * HEAD_DIM : (side + 1) * HEAD_DIM], probs))
            lse[2 * index + side] = largest + jnp.log(total)
        attended[rows, lanes] = jnp.concatenate(parts, axis=0).T.astype(BF16)
        return carry

    lax.fori_loop(0, (normed.shape[0] // slots) * pairs, step, 0)


def feed_kernel(
    layer,
    slots,
    last_layer,
    counts,
    stream,
    att_own,
    att_far,
    out_own,
    out_far,
    out_bias,
    gain,
    bias,
    order,
    up_own,
    up_far,
    up_bias,
    down_own,
    down_far,
    mid,
    normed_t,
    hid_own,
    hid_far,
    slope_own,
    slope_far,
    stream_out,
    *rest,
):
    if last_layer:
        pooled, normed, total, pre = rest
    else:
        next_normed, next_t, normed, total, pre = rest
    step = pl.program_id(0)
    tokens = stream.shape[0]

    @pl.when(step == 0)
    def _():
        total[...] = dot(att_own[...], out_own[0]) + dot(att_far[...], out_far[0])

        def rows(start):
            here = pl.ds(start, CHUNK)
            value = stream[here, :].astype(F32) + (total[here, :] + out_bias[layer, 0:1, :])
            mid[here, :] = value
            normed[here, :] = normalized(
                value, gain[layer, 1:2, :], bias[layer, 1:2, :]
            ).astype(BF16)

        by_rows(tokens, rows)
        normed_t[...] = dot_nt(order[...], normed[...]).astype(BF16)
        total[...] = jnp.zeros_like(total)

    tile = hid_own.shape[1]
    for side, (weight_up, weight_down, hid, slope) in enumerate(
        ((up_own, down_own, hid_own, slope_own), (up_far, down_far, hid_far, slope_far))
    ):
        pre[...] = dot(normed[...], weight_up[0])
        shift = up_bias[side, layer, pl.ds(step, 1), :]

        def rows(start):
            here = pl.ds(start, CHUNK)
            value = pre[here, :] + shift
            cdf = 0.5 * (1.0 + lax.erf(value * (0.5**0.5)))
            hid[here, :] = (value * cdf).astype(BF16)
            density = jnp.exp(-0.5 * value * value) * ((2.0 * math.pi) ** -0.5)
            slope[here, :] = (cdf + value * density).astype(BF16)

        by_rows(tokens, rows)
        total[...] += dot(hid[...], weight_down[0])

    @pl.when(step == pl.num_programs(0) - 1)
    def _():
        def rows(start):
            here = pl.ds(start, CHUNK)
            value = mid[here, :] + (total[here, :] + out_bias[layer, 1:2, :])
            stream_out[here, :] = value
            if not last_layer:
                next_normed[here, :] = normalized(
                    value, gain[layer + 1, 0:1, :], bias[layer + 1, 0:1, :]
                ).astype(BF16)

        by_rows(tokens, rows)
        if last_layer:
            index = lax.broadcasted_iota(jnp.int32, (slots, 1), 0)
            for image in range(tokens // slots):
                block = stream_out[image * slots : (image + 1) * slots, :]
                count = counts[image]
                summed = jnp.sum(jnp.where(index < count, block, 0.0), axis=0, keepdims=True)
                pooled[image : image + 1, :] = summed / count.astype(F32)
        else:
            next_t[...] = dot_nt(order[...], next_normed[...]).astype(BF16)


def feed_back_kernel(
    layer,
    grad_in,
    mid,
    gain,
    order,
    down_own,
    down_far,
    up_own,
    up_far,
    slope_own,
    slope_far,
    out_own,
    out_far,
    pre_own,
    pre_far,
    bias_own,
    bias_far,
    grad_mid,
    mid_t,
    att_own,
    att_far,
    sums,
    low,
    total,
    hidden,
    partial,
):
    step = pl.program_id(0)
    tokens = grad_in.shape[0]

    @pl.when(step == 0)
    def _():
        partial[...] = jnp.zeros_like(partial)

        def rows(start):
            here = pl.ds(start, CHUNK)
            value = grad_in[here, :].astype(F32)
            low[here, :] = value.astype(BF16)
            partial[0] += fold_rows(value)

        by_rows(tokens, rows)
        total[...] = jnp.zeros_like(total)

    for weight_down, weight_up, slope, pre, bias in (
        (down_far, up_far, slope_far, pre_far, bias_far),
        (down_own, up_own, slope_own, pre_own, bias_own),
    ):
        hidden[...] = dot_nt(low[...], weight_down[0])

        def rows(index, carry):
            here = pl.ds(pl.multiple_of(index * CHUNK, CHUNK), CHUNK)
            value = hidden[here, :] * slope[here, :].astype(F32)
            pre[here, :] = value.astype(BF16)
            return carry + fold_rows(value)

        summed = lax.fori_loop(
            0, tokens // CHUNK, rows, jnp.zeros((8, hidden.shape[1]), F32), unroll=2
        )
        bias[pl.ds(step, 1), :] = jnp.sum(summed, axis=0, keepdims=True)
        total[...] += dot_nt(pre[...], weight_up[0])

    @pl.when(step == pl.num_programs(0) - 1)
    def _():
        def rows(start):
            here = pl.ds(start, CHUNK)
            normed_grad = total[here, :]
            through, gain_term = norm_backward(mid[here, :], normed_grad, gain[layer, 1:2, :])
            value = grad_in[here, :].astype(F32) + through
            grad_mid[here, :] = value
            low[here, :] = value.astype(BF16)
            partial[1] += fold_rows(value)
            partial[2] += fold_rows(gain_term)
            partial[3] += fold_rows(normed_grad)

        by_rows(tokens, rows)
        sums[...] = jnp.sum(partial[...], axis=1)
        mid_t[...] = dot_nt(order[...], low[...]).astype(BF16)
        att_far[...] = dot_nt(low[...], out_far[0]).astype(BF16)
        att_own[...] = dot_nt(low[...], out_own[0]).astype(BF16)


def attend_back_kernel(slots, counts, joint, lse, grad_att, grad_joint, bias_sums):
    width = grad_att.shape[1]
    pairs = width // (2 * HEAD_DIM)
    scale = HEAD_DIM ** (-0.5)
    masks = head_masks(slots)
    key_index = lax.broadcasted_iota(jnp.int32, (slots, slots), 0)
    bias_sums[...] = jnp.zeros_like(bias_sums)

    def step(index, carry):
        image = index // pairs
        pair = index % pairs
        rows = pl.ds(pl.multiple_of(image * slots, slots), slots)
        lanes = pl.ds(pl.multiple_of(pair * 2 * HEAD_DIM, 2 * HEAD_DIM), 2 * HEAD_DIM)
        queries = joint[0, rows, lanes]
        keys_in = joint[1, rows, lanes]
        values_in = joint[2, rows, lanes]
        grads = grad_att[rows, lanes]
        keys_t = keys_in.T
        keys_scaled = keys_in * jnp.asarray(scale, BF16)
        valid = key_index < counts[image]
        zeros = jnp.zeros_like(keys_in)
        query_parts, key_parts, value_parts = [], [], []
        for side in range(2):
            keys_side = jnp.where(masks[side], keys_scaled, zeros)
            values_side = jnp.where(masks[side], values_in, zeros)
            scores = jnp.where(valid, dot_nt(keys_side, queries), NEGATIVE)
            probs = jnp.exp(scores - lse[2 * index + side])
            grad_probs = dot_nt(values_side, grads)
            inner = jnp.sum(grad_probs * probs, axis=0, keepdims=True)
            grad_scores = (probs * (grad_probs - inner)).astype(BF16)
            value_parts.append(dot(probs.astype(BF16), grads))
            key_parts.append(dot(grad_scores, queries))
            query_parts.append(dot(keys_t[side * HEAD_DIM : (side + 1) * HEAD_DIM], grad_scores))
        grad_queries = jnp.concatenate(query_parts, axis=0).T * scale
        grad_keys = jnp.where(masks[0], key_parts[0], key_parts[1]) * scale
        grad_values = jnp.where(masks[0], value_parts[0], value_parts[1])
        bias_sums[0:1, lanes] += jnp.sum(grad_queries, axis=0, keepdims=True)
        bias_sums[1:2, lanes] += jnp.sum(grad_values, axis=0, keepdims=True)
        grad_joint[0, rows, lanes] = grad_queries.astype(BF16)
        grad_joint[1, rows, lanes] = grad_keys.astype(BF16)
        grad_joint[2, rows, lanes] = grad_values.astype(BF16)
        return carry

    lax.fori_loop(0, (grad_att.shape[0] // slots) * pairs, step, 0)


def entry_back_kernel(
    layer, with_low, joint_own, joint_far, weight_own, weight_far, stream, gain, grad_mid, order, *rest
):
    if with_low:
        grad_out, sums, low_t, total, partial, low = rest
    else:
        grad_out, sums, total, partial = rest
    acc = None
    for joint, weight in ((joint_own, weight_own), (joint_far, weight_far)):
        for member in range(3):
            term = dot_nt(joint[member], weight[0, member])
            acc = term if acc is None else acc + term
    total[...] = acc
    partial[...] = jnp.zeros_like(partial)

    def rows(start):
        here = pl.ds(start, CHUNK)
        normed_grad = total[here, :]
        through, gain_term = norm_backward(
            stream[here, :].astype(F32), normed_grad, gain[layer, 0:1, :]
        )
        value = grad_mid[here, :] + through
        grad_out[here, :] = value
        if with_low:
            low[here, :] = value.astype(BF16)
        partial[0] += fold_rows(gain_term)
        partial[1] += fold_rows(normed_grad)

    by_rows(stream.shape[0], rows)
    sums[...] = jnp.sum(partial[...], axis=1)
    if with_low:
        low_t[...] = dot_nt(order[...], low[...]).astype(BF16)


def chunk_sources(order):
    first = list(order[:4])
    sources = []
    for target in range(16):
        source = 0
        for place, bit in enumerate(first):
            if (target >> (3 - place)) & 1:
                source |= 1 << (3 - bit)
        sources.append(source)
    return sources


def weight_kernel(sources, tiles, has_extra, *refs):
    if has_extra:
        left_own, left_far, right_own, right_far, lx_own, lx_far, rx_own, rx_far, keep, send, acc = refs
    else:
        left_own, left_far, right_own, right_far, keep, send, acc = refs

    def product(a_own, a_far, b_own, b_far):
        acc[...] = dot(a_own[...], b_own) + dot(a_far[...], b_far)

    if has_extra:

        @pl.when(pl.program_id(0) < tiles)
        def _():
            product(left_own, left_far, right_own[0], right_far[0])

        @pl.when(pl.program_id(0) == tiles)
        def _():
            product(lx_own, lx_far, rx_own[...], rx_far[...])

    elif len(right_own.shape) == 3:
        product(left_own, left_far, right_own[0], right_far[0])
    else:
        product(left_own, left_far, right_own[...], right_far[...])
    size = acc.shape[0] // 16
    for target, source in enumerate(sources):
        ref = keep if target < 8 else send
        ref[(target % 8) * size : (target % 8 + 1) * size, :] = acc[
            source * size : (source + 1) * size, :
        ].astype(BF16)


def weight_grad(name, order, left, right, extra=None, tiles=None, first=0):
    left_own, left_far = left
    right_own, right_far = right
    width, tokens = left_own.shape
    if right_own.ndim == 3:
        tile = right_own.shape[2]
        right_spec = pl.BlockSpec(
            (1, tokens, tile), lambda j: (jnp.minimum(j, tiles - 1) + first, 0, 0)
        )
    else:
        tile = min(512, right_own.shape[1])
        tiles = right_own.shape[1] // tile
        right_spec = pl.BlockSpec((tokens, tile), lambda j: (0, j))
    steps = tiles + (1 if extra is not None else 0)
    ins = [left_own, left_far, right_own, right_far]
    specs = [fixed((width, tokens))] * 2 + [right_spec] * 2
    if extra is not None:
        ins += list(extra)
        specs += [fixed((width, tokens))] * 2 + [fixed((tokens, tile))] * 2
    half = out((width // 2, steps * tile), BF16)
    half_spec = pl.BlockSpec((width // 2, tile), lambda j: (0, j))
    return call(
        functools.partial(weight_kernel, chunk_sources(order), tiles, extra is not None),
        name,
        (steps,),
        ins,
        specs,
        [half, half],
        [half_spec, half_spec],
        [pltpu.VMEM((width, tile), F32)],
        flops=4 * width * tokens * steps * tile,
    )


def flip(bit):
    size = lax.axis_size("dp")
    return [(index, index ^ (1 << bit)) for index in range(size)]


def sum_over_dp(halves, order):
    keep, send = halves
    parts = [keep]
    rows = keep.shape[0]
    for place, bit in enumerate(order):
        parts.append(lax.ppermute(send, "dp", flip(bit)))
        if place == len(order) - 1:
            break
        rows //= 2
        send = sum(part[rows:].astype(F32) for part in parts).astype(BF16)
        parts = [part[:rows] for part in parts]
    return sum(part.astype(F32) for part in parts)


def swap(values):
    return lax.ppermute(values, "tensor", [(0, 1), (1, 0)])


def shards(
    images,
    valid_count,
    ln_gain,
    ln_bias,
    w_qkv,
    qv_bias,
    w_out,
    out_bias,
    w_up,
    up_bias,
    w_down,
    cotangent,
):
    local_rows, slots, width = images.shape
    tokens = local_rows * slots
    half = w_qkv.shape[3]
    ff_half = w_up.shape[2]
    tile = 512
    steps = ff_half // tile
    heads = half // HEAD_DIM
    dp = lax.axis_size("dp")
    bits = dp.bit_length() - 1
    assert dp == 1 << bits and bits >= 4 and lax.axis_size("tensor") == 2
    tail = tuple(range(4, bits))
    order_a = (0, 1, 2, 3) + tail
    order_b = (1, 0, 2, 3) + tail
    order_c = (2, 3, 0, 1) + tail

    me = lax.axis_index("dp")
    counts = lax.dynamic_slice_in_dim(
        valid_count, lax.axis_index("tensor") * local_rows, local_rows
    )

    block = width // dp
    row = jnp.arange(width, dtype=jnp.int32)
    index = row // block
    mirrored = jnp.zeros_like(index)
    for bit in range(bits):
        mirrored = mirrored | (((index >> (bits - 1 - bit)) & 1) << bit)
    source = (mirrored ^ me) * block + row % block
    order = (source[:, None] == row[None, :]).astype(BF16)

    w_qkv = jnp.transpose(w_qkv, (0, 2, 1, 3))
    biases = jnp.concatenate([qv_bias.reshape(LAYERS, -1), up_bias], axis=1)
    far_biases = swap(biases)
    qkv = (w_qkv, swap(w_qkv))
    wout = (w_out, swap(w_out))
    wup = (w_up, swap(w_up))
    wdown = (w_down, swap(w_down))
    qv = (qv_bias, far_biases[:, : 2 * half].reshape(LAYERS, 2, half))
    upb = jnp.stack([up_bias, far_biases[:, 2 * half :]]).reshape(2, LAYERS, steps, tile)

    images_2d = images.reshape(tokens, width)
    cotangent_2d = cotangent.reshape(tokens, width)
    smem = pl.BlockSpec(memory_space=pltpu.SMEM)
    wide = (tokens, width)
    flops_wide = 2 * width * width * tokens

    normed, normed_t, cotangent_t = call(
        prep_kernel,
        "prep",
        (1,),
        [images_2d, cotangent_2d, ln_gain, ln_bias, order],
        [fixed(wide), fixed(wide), fixed(ln_gain.shape), fixed(ln_bias.shape), fixed(order.shape)],
        [out(wide, BF16), out((width, tokens), BF16), out((width, tokens), BF16)],
        [fixed(wide), fixed((width, tokens)), fixed((width, tokens))],
        flops=2 * flops_wide,
    )

    def attend(layer, side, normed):
        lse_shape = (local_rows * heads, 1, slots)
        return call(
            functools.partial(attend_kernel, layer, slots),
            "attend",
            (1,),
            [counts, normed, qkv[side], qv[side]],
            [
                smem,
                fixed(wide),
                fixed((1, 3, width, half), layer),
                fixed(qv_bias.shape),
            ],
            [out((3, tokens, half), BF16), out((tokens, half), BF16), out(lse_shape, F32)],
            [fixed((3, tokens, half)), fixed((tokens, half)), fixed(lse_shape)],
            flops=6 * tokens * width * half + 4 * tokens * slots * half,
        )

    stream = images_2d
    saved = []
    pooled = None
    for layer in range(LAYERS):
        last = layer == LAYERS - 1
        own = attend(layer, 0, normed)
        far = attend(layer, 1, normed)
        up_spec = pl.BlockSpec((1, width, tile), lambda j, layer=layer: (layer, 0, j))
        down_spec = pl.BlockSpec((1, tile, width), lambda j, layer=layer: (layer, j, 0))
        out_spec = fixed((1, half, width), layer)
        tile_spec = pl.BlockSpec((tokens, tile), lambda j: (0, j))
        ff = out((tokens, ff_half), BF16)
        extra = (
            [out((local_rows, width), F32)]
            if last
            else [out(wide, BF16), out((width, tokens), BF16)]
        )
        extra_specs = [fixed(e.shape) for e in extra]
        results = call(
            functools.partial(feed_kernel, layer, slots, last),
            "feed",
            (steps,),
            [
                counts,
                stream,
                own[1],
                far[1],
                wout[0],
                wout[1],
                out_bias,
                ln_gain,
                ln_bias,
                order,
                wup[0],
                wup[1],
                upb,
                wdown[0],
                wdown[1],
            ],
            [
                smem,
                fixed(wide),
                fixed((tokens, half)),
                fixed((tokens, half)),
                out_spec,
                out_spec,
                fixed(out_bias.shape),
                fixed(ln_gain.shape),
                fixed(ln_bias.shape),
                fixed(order.shape),
                up_spec,
                up_spec,
                fixed(upb.shape),
                down_spec,
                down_spec,
            ],
            [out(wide, F32), out((width, tokens), BF16), ff, ff, ff, ff, out(wide, F32)] + extra,
            [fixed(wide), fixed((width, tokens))] + [tile_spec] * 4 + [fixed(wide)] + extra_specs,
            [pltpu.VMEM(wide, BF16), pltpu.VMEM(wide, F32), pltpu.VMEM((tokens, tile), F32)],
            flops=8 * tokens * width * ff_half + 2 * flops_wide,
        )
        mid, mid_normed_t, hid_own, hid_far, slope_own, slope_far, stream_next = results[:7]
        saved.append(
            dict(
                stream=stream,
                own=own,
                far=far,
                mid=mid,
                slope=(slope_own, slope_far),
                hid=hid_own,
                attended=own[1],
                normed_t=normed_t,
                mid_normed_t=mid_normed_t,
                got_hid=swap(hid_far),
                got_att=swap(far[1]),
                got_normed_t=swap(normed_t),
                got_mid_normed_t=swap(mid_normed_t),
            )
        )
        stream = stream_next
        if last:
            pooled = results[7]
        else:
            normed, normed_t = results[7:9]

    grad = cotangent_2d
    grad_t = cotangent_t
    summed = [None] * LAYERS
    small = [None] * LAYERS
    for layer in reversed(range(LAYERS)):
        kept = saved[layer]
        got_grad_t = swap(grad_t)
        down = sum_over_dp(
            weight_grad(
                "down_grad", order_a, (grad_t, got_grad_t), (kept["hid"], kept["got_hid"])
            ),
            order_a,
        )
        up_spec = pl.BlockSpec((1, width, tile), lambda j, layer=layer: (layer, 0, j))
        down_spec = pl.BlockSpec((1, tile, width), lambda j, layer=layer: (layer, j, 0))
        out_spec = fixed((1, half, width), layer)
        tile_spec = pl.BlockSpec((tokens, tile), lambda j: (0, j))
        ff = out((tokens, ff_half), BF16)
        bias_shape = out((steps, tile), F32)
        att_shape = out((tokens, half), BF16)
        (
            pre_own,
            pre_far,
            upb_own,
            upb_far,
            grad_mid,
            mid_t,
            att_own,
            att_far,
            sums_mid,
        ) = call(
            functools.partial(feed_back_kernel, layer),
            "feed_back",
            (steps,),
            [
                grad,
                kept["mid"],
                ln_gain,
                order,
                wdown[0],
                wdown[1],
                wup[0],
                wup[1],
                kept["slope"][0],
                kept["slope"][1],
                wout[0],
                wout[1],
            ],
            [
                fixed(wide),
                fixed(wide),
                fixed(ln_gain.shape),
                fixed(order.shape),
                down_spec,
                down_spec,
                up_spec,
                up_spec,
                tile_spec,
                tile_spec,
                out_spec,
                out_spec,
            ],
            [
                ff,
                ff,
                bias_shape,
                bias_shape,
                out(wide, F32),
                out((width, tokens), BF16),
                att_shape,
                att_shape,
                out((4, width), F32),
            ],
            [
                tile_spec,
                tile_spec,
                fixed((steps, tile)),
                fixed((steps, tile)),
                fixed(wide),
                fixed((width, tokens)),
                fixed((tokens, half)),
                fixed((tokens, half)),
                fixed((4, width)),
            ],
            [
                pltpu.VMEM(wide, BF16),
                pltpu.VMEM(wide, F32),
                pltpu.VMEM((tokens, tile), F32),
                pltpu.VMEM((4, 8, width), F32),
            ],
            flops=8 * tokens * width * ff_half + 2 * flops_wide,
        )
        got_pre = swap(pre_far)
        got_mid_t = swap(mid_t)
        up = sum_over_dp(
            weight_grad(
                "up_grad",
                order_b,
                (kept["mid_normed_t"], kept["got_mid_normed_t"]),
                (pre_own, got_pre),
            ),
            order_b,
        )

        def attend_back(forward, grad_att):
            joint, _, lse = forward
            return call(
                functools.partial(attend_back_kernel, slots),
                "attend_back",
                (1,),
                [counts, joint, lse, grad_att],
                [smem, fixed(joint.shape), fixed(lse.shape), fixed((tokens, half))],
                [out(joint.shape, BF16), out((2, half), F32)],
                [fixed(joint.shape), fixed((2, half))],
                flops=10 * tokens * slots * half,
            )

        joint_far, qv_far = attend_back(kept["far"], att_far)
        got_joint = swap(joint_far)
        joint_own, qv_own = attend_back(kept["own"], att_own)
        lefts = (kept["normed_t"], kept["got_normed_t"])
        extra = (mid_t, got_mid_t, kept["attended"], kept["got_att"])
        if layer > 0:
            both = sum_over_dp(
                weight_grad(
                    "qkv_out_grad", order_c, lefts, (joint_own, got_joint), extra, tiles=3
                ),
                order_c,
            )
            qkv_grad, out_grad = both[:, : 3 * half], both[:, 3 * half :]
        else:
            one = sum_over_dp(
                weight_grad("qk_grad", order_a, lefts, (joint_own, got_joint), tiles=2), order_a
            )
            two = sum_over_dp(
                weight_grad(
                    "v_out_grad", order_b, lefts, (joint_own, got_joint), extra, tiles=1, first=2
                ),
                order_b,
            )
            qkv_grad = jnp.concatenate([one, two[:, :half]], axis=1)
            out_grad = two[:, half:]
        with_low = layer > 0
        results = call(
            functools.partial(entry_back_kernel, layer, with_low),
            "entry_back",
            (1,),
            [
                joint_own,
                joint_far,
                qkv[0],
                qkv[1],
                kept["stream"],
                ln_gain,
                grad_mid,
                order,
            ],
            [
                fixed(joint_own.shape),
                fixed(joint_far.shape),
                fixed((1, 3, width, half), layer),
                fixed((1, 3, width, half), layer),
                fixed(wide),
                fixed(ln_gain.shape),
                fixed(wide),
                fixed(order.shape),
            ],
            [out(wide, F32), out((2, width), F32)]
            + ([out((width, tokens), BF16)] if with_low else []),
            [fixed(wide), fixed((2, width))] + ([fixed((width, tokens))] if with_low else []),
            [pltpu.VMEM(wide, F32), pltpu.VMEM((2, 8, width), F32)]
            + ([pltpu.VMEM(wide, BF16)] if with_low else []),
            flops=12 * tokens * width * half,
        )
        grad, sums_in = results[:2]
        if with_low:
            grad_t = results[2]
        summed[layer] = (
            qkv_grad.reshape(block, 3, half),
            out_grad.T,
            up,
            down.T,
        )
        small[layer] = (sums_mid, sums_in, qv_own, qv_far, upb_own, upb_far)

    shared = jnp.concatenate([jnp.concatenate([s[0], s[1]]) for s in small]).reshape(-1)
    own_part = jnp.concatenate([jnp.concatenate([s[2].reshape(-1), s[4].reshape(-1)]) for s in small])
    far_part = jnp.concatenate([jnp.concatenate([s[3].reshape(-1), s[5].reshape(-1)]) for s in small])
    vector = jnp.concatenate([shared, own_part]).reshape(-1, 128) + swap(
        jnp.concatenate([shared, far_part]).reshape(-1, 128)
    )
    for bit in range(bits):
        vector = vector + lax.ppermute(vector, "dp", flip(bit))
    vector = vector.reshape(-1)
    shared = vector[: shared.shape[0]].reshape(LAYERS, 6, width)
    own_part = vector[LAYERS * 6 * width :].reshape(LAYERS, 2 * half + ff_half)
    gain_grads = jnp.stack([shared[:, 4], shared[:, 2]], axis=1)
    shift_grads = jnp.stack([shared[:, 5], shared[:, 3]], axis=1)
    outb_grads = jnp.stack([shared[:, 1], shared[:, 0]], axis=1)
    qv_grads = own_part[:, : 2 * half].reshape(LAYERS, 2, half)
    upb_grads = own_part[:, 2 * half :]
    stacked = [jnp.stack([summed[layer][member] for layer in range(LAYERS)]) for member in range(4)]
    return (
        stream.reshape(images.shape),
        pooled,
        grad.reshape(images.shape),
        gain_grads,
        shift_grads,
        stacked[0],
        qv_grads,
        stacked[1],
        outb_grads,
        stacked[2],
        upb_grads,
        stacked[3],
    )


def solution(mesh):
    placed = (
        P(("dp", "tensor"), None, None),
        P("dp"),
        P(),
        P(),
        P(None, None, None, "tensor"),
        P(None, None, "tensor"),
        P(None, "tensor", None),
        P(),
        P(None, None, "tensor"),
        P(None, "tensor"),
        P(None, "tensor", None),
        P(("dp", "tensor"), None, None),
    )
    return jax.shard_map(
        shards,
        mesh=mesh,
        in_specs=placed,
        out_specs=(
            P(("dp", "tensor"), None, None),
            P(("dp", "tensor"), None),
            P(("dp", "tensor"), None, None),
            P(),
            P(),
            P(None, "dp", None, "tensor"),
            P(None, None, "tensor"),
            P(None, "tensor", "dp"),
            P(),
            P(None, "dp", "tensor"),
            P(None, "tensor"),
            P(None, "tensor", "dp"),
        ),
        check_vma=False,
    )
```

```python
import functools
import math

import jax
import jax.numpy as jnp
from jax import lax
from jax.experimental import pallas as pl
from jax.experimental.pallas import tpu as pltpu
from jax.sharding import PartitionSpec as P

HEAD_DIM = 64
LAYERS = 2
EPSILON = 1e-06
NEGATIVE = -1e30
BF16 = jnp.bfloat16
F32 = jnp.float32
CHUNK = 16


def dot(left, right):
    return lax.dot_general(left, right, (((1,), (0,)), ((), ())), preferred_element_type=F32)


def dot_nt(left, right):
    return lax.dot_general(left, right, (((1,), (1,)), ((), ())), preferred_element_type=F32)


def fixed(shape, *lead):
    where = tuple(lead) + (0,) * (len(shape) - len(lead))
    return pl.BlockSpec(shape, lambda *_: where)


def out(shape, dtype):
    return jax.ShapeDtypeStruct(shape, dtype)


def cost(flops, *arrays):
    total = sum(math.prod(a.shape) * a.dtype.itemsize for a in arrays)
    return pl.CostEstimate(flops=int(flops) // 64, bytes_accessed=int(total) // 64, transcendentals=0)


MIB = 1 << 20


def call(body, name, grid, ins, in_specs, outs, out_specs, scratch=(), flops=0, limit=24):
    return pl.pallas_call(
        body,
        name=name,
        grid=grid,
        in_specs=in_specs,
        out_specs=out_specs,
        out_shape=outs,
        scratch_shapes=list(scratch),
        compiler_params=pltpu.CompilerParams(vmem_limit_bytes=limit * MIB),
        cost_estimate=cost(flops, *ins, *outs),
    )(*ins)


def whole():
    return pl.BlockSpec(memory_space=pltpu.VMEM)


def by_rows(rows, body, unroll=1):
    def step(index, carry):
        for part in range(unroll):
            body(pl.multiple_of((index * unroll + part) * CHUNK, CHUNK))
        return carry

    lax.fori_loop(0, rows // (CHUNK * unroll), step, 0)


def moments(values):
    average = jnp.mean(values, axis=-1, keepdims=True)
    centred = values - average
    variance = jnp.mean(centred * centred, axis=-1, keepdims=True)
    return centred, lax.rsqrt(variance + EPSILON)


def normalized(values, gain, bias):
    centred, scale = moments(values)
    return centred * scale * gain + bias


def norm_backward(values, grad_normed, gain):
    centred, scale = moments(values)
    unit = centred * scale
    grad_unit = grad_normed * gain
    first = jnp.mean(grad_unit, axis=-1, keepdims=True)
    second = jnp.mean(grad_unit * unit, axis=-1, keepdims=True)
    return scale * (grad_unit - first - unit * second), grad_normed * unit


def fold_rows(values):
    total = values[0:8]
    for start in range(8, values.shape[0], 8):
        total = total + values[start : start + 8]
    return total


def prep_kernel(images, cotangent, gain, bias, order, normed, normed_t, cotangent_t):
    def rows(start):
        here = pl.ds(start, CHUNK)
        values = images[here, :].astype(F32)
        normed[here, :] = normalized(values, gain[0, 0:1, :], bias[0, 0:1, :]).astype(BF16)

    by_rows(images.shape[0], rows, 4)
    normed_t[...] = dot_nt(order[...], normed[...]).astype(BF16)
    cotangent_t[...] = dot_nt(order[...], cotangent[...]).astype(BF16)


def head_masks(slots):
    lane = lax.broadcasted_iota(jnp.int32, (slots, 2 * HEAD_DIM), 1)
    return lane < HEAD_DIM, lane >= HEAD_DIM


def own_count(counts, image, images):
    return counts[lax.axis_index("tensor") * images + image]


def attend_kernel(layer, slots, counts, normed, weight, bias, joint, attended, lse):
    width = attended.shape[1]
    pairs = width // (2 * HEAD_DIM)
    scale = HEAD_DIM ** (-0.5)
    for member in range(3):
        product = dot(normed[...], weight[layer, member])
        if member == 0:
            product = product + bias[layer, 0:1, :]
        if member == 2:
            product = product + bias[layer, 1:2, :]
        joint[member] = product.astype(BF16)
    masks = head_masks(slots)
    key_index = lax.broadcasted_iota(jnp.int32, (slots, slots), 0)

    def step(index, carry):
        image = index // pairs
        pair = index % pairs
        rows = pl.ds(pl.multiple_of(image * slots, slots), slots)
        lanes = pl.ds(pl.multiple_of(pair * 2 * HEAD_DIM, 2 * HEAD_DIM), 2 * HEAD_DIM)
        queries = joint[0, rows, lanes]
        keys_in = joint[1, rows, lanes] * jnp.asarray(scale, BF16)
        values_t = joint[2, rows, lanes].T
        valid = key_index < own_count(counts, image, normed.shape[0] // slots)
        parts = []
        for side in range(2):
            keys_side = jnp.where(masks[side], keys_in, jnp.zeros_like(keys_in))
            scores = jnp.where(valid, dot_nt(keys_side, queries), NEGATIVE)
            largest = jnp.max(scores, axis=0, keepdims=True)
            exponent = jnp.exp(scores - largest)
            total = jnp.sum(exponent, axis=0, keepdims=True)
            probs = (exponent * (1.0 / total)).astype(BF16)
            parts.append(dot(values_t[side * HEAD_DIM : (side + 1) * HEAD_DIM], probs))
            lse[2 * index + side] = largest + jnp.log(total)
        attended[rows, lanes] = jnp.concatenate(parts, axis=0).T.astype(BF16)
        return carry

    lax.fori_loop(0, (normed.shape[0] // slots) * pairs, step, 0)


def feed_kernel(
    layer,
    slots,
    last_layer,
    counts,
    stream,
    att_own,
    att_far,
    out_own,
    out_far,
    out_bias,
    gain,
    bias,
    order,
    up_own,
    up_far,
    up_bias_own,
    up_bias_far,
    down_own,
    down_far,
    mid,
    normed_t,
    hid_own,
    hid_far,
    slope_own,
    slope_far,
    stream_out,
    *rest,
):
    if last_layer:
        pooled, normed, total, pre = rest
    else:
        next_normed, next_t, normed, total, pre = rest
    step = pl.program_id(0)
    tokens = stream.shape[0]

    @pl.when(step == 0)
    def _():
        total[...] = dot(
            jnp.concatenate([att_own[...], att_far[...]], axis=1),
            jnp.concatenate([out_own[layer], out_far[layer]], axis=0),
        )

        def rows(start):
            here = pl.ds(start, CHUNK)
            value = stream[here, :].astype(F32) + (total[here, :] + out_bias[layer, 0:1, :])
            mid[here, :] = value
            normed[here, :] = normalized(
                value, gain[layer, 1:2, :], bias[layer, 1:2, :]
            ).astype(BF16)

        by_rows(tokens, rows, 4)
        normed_t[...] = dot_nt(order[...], normed[...]).astype(BF16)
        total[...] = jnp.zeros_like(total)

    tile = hid_own.shape[1]
    for weight_up, up_bias, weight_down, hid, slope in (
        (up_own, up_bias_own, down_own, hid_own, slope_own),
        (up_far, up_bias_far, down_far, hid_far, slope_far),
    ):
        pre[...] = dot(normed[...], weight_up[0])
        shift = up_bias[layer : layer + 1, :]

        def rows(start):
            here = pl.ds(start, CHUNK)
            value = pre[here, :] + shift
            cdf = 0.5 * (1.0 + lax.erf(value * (0.5**0.5)))
            hid[here, :] = (value * cdf).astype(BF16)
            density = jnp.exp(-0.5 * value * value) * ((2.0 * math.pi) ** -0.5)
            slope[here, :] = (cdf + value * density).astype(BF16)

        by_rows(tokens, rows)
        total[...] += dot(hid[...], weight_down[0])

    @pl.when(step == pl.num_programs(0) - 1)
    def _():
        def rows(start):
            here = pl.ds(start, CHUNK)
            value = mid[here, :] + (total[here, :] + out_bias[layer, 1:2, :])
            stream_out[here, :] = value
            if not last_layer:
                next_normed[here, :] = normalized(
                    value, gain[layer + 1, 0:1, :], bias[layer + 1, 0:1, :]
                ).astype(BF16)

        by_rows(tokens, rows, 4)
        if last_layer:
            index = lax.broadcasted_iota(jnp.int32, (slots, 1), 0)
            for image in range(tokens // slots):
                block = stream_out[image * slots : (image + 1) * slots, :]
                count = own_count(counts, image, tokens // slots)
                summed = jnp.sum(jnp.where(index < count, block, 0.0), axis=0, keepdims=True)
                pooled[image : image + 1, :] = summed / count.astype(F32)
        else:
            next_t[...] = dot_nt(order[...], next_normed[...]).astype(BF16)


def feed_back_kernel(
    layer,
    grad_in,
    mid,
    gain,
    order,
    down_own,
    down_far,
    up_own,
    up_far,
    slope_own,
    slope_far,
    out_own,
    out_far,
    pre_own,
    pre_far,
    bias_own,
    bias_far,
    grad_mid,
    mid_t,
    att_own,
    att_far,
    sums,
    low,
    total,
    hidden,
    partial,
):
    step = pl.program_id(0)
    tokens = grad_in.shape[0]

    @pl.when(step == 0)
    def _():
        partial[...] = jnp.zeros_like(partial)

        def rows(start):
            here = pl.ds(start, CHUNK)
            value = grad_in[here, :].astype(F32)
            low[here, :] = value.astype(BF16)
            partial[0] += fold_rows(value)

        by_rows(tokens, rows)
        total[...] = jnp.zeros_like(total)

    for weight_down, weight_up, slope, pre, bias in (
        (down_far, up_far, slope_far, pre_far, bias_far),
        (down_own, up_own, slope_own, pre_own, bias_own),
    ):
        hidden[...] = dot_nt(low[...], weight_down[0])

        def rows(index, carry):
            here = pl.ds(pl.multiple_of(index * CHUNK, CHUNK), CHUNK)
            value = hidden[here, :] * slope[here, :].astype(F32)
            pre[here, :] = value.astype(BF16)
            return carry + fold_rows(value)

        summed = lax.fori_loop(
            0, tokens // CHUNK, rows, jnp.zeros((8, hidden.shape[1]), F32), unroll=2
        )
        bias[pl.ds(step, 1), :] = jnp.sum(summed, axis=0, keepdims=True)
        total[...] += dot_nt(pre[...], weight_up[0])

    @pl.when(step == pl.num_programs(0) - 1)
    def _():
        def rows(start):
            here = pl.ds(start, CHUNK)
            normed_grad = total[here, :]
            through, gain_term = norm_backward(mid[here, :], normed_grad, gain[layer, 1:2, :])
            value = grad_in[here, :].astype(F32) + through
            grad_mid[here, :] = value
            low[here, :] = value.astype(BF16)
            partial[1] += fold_rows(value)
            partial[2] += fold_rows(gain_term)
            partial[3] += fold_rows(normed_grad)

        by_rows(tokens, rows, 2)
        sums[...] = jnp.sum(partial[...], axis=1)
        mid_t[...] = dot_nt(order[...], low[...]).astype(BF16)
        att_far[...] = dot_nt(low[...], out_far[layer]).astype(BF16)
        att_own[...] = dot_nt(low[...], out_own[layer]).astype(BF16)


def attend_back_kernel(slots, counts, joint, lse, grad_att, grad_joint, bias_sums):
    width = grad_att.shape[1]
    pairs = width // (2 * HEAD_DIM)
    scale = HEAD_DIM ** (-0.5)
    masks = head_masks(slots)
    key_index = lax.broadcasted_iota(jnp.int32, (slots, slots), 0)
    bias_sums[...] = jnp.zeros_like(bias_sums)

    def step(index, carry):
        image = index // pairs
        pair = index % pairs
        rows = pl.ds(pl.multiple_of(image * slots, slots), slots)
        lanes = pl.ds(pl.multiple_of(pair * 2 * HEAD_DIM, 2 * HEAD_DIM), 2 * HEAD_DIM)
        queries = joint[0, rows, lanes]
        keys_in = joint[1, rows, lanes]
        values_in = joint[2, rows, lanes]
        grads = grad_att[rows, lanes]
        keys_t = keys_in.T
        keys_scaled = keys_in * jnp.asarray(scale, BF16)
        valid = key_index < own_count(counts, image, grad_att.shape[0] // slots)
        zeros = jnp.zeros_like(keys_in)
        query_parts, key_parts, value_parts = [], [], []
        for side in range(2):
            keys_side = jnp.where(masks[side], keys_scaled, zeros)
            values_side = jnp.where(masks[side], values_in, zeros)
            scores = jnp.where(valid, dot_nt(keys_side, queries), NEGATIVE)
            probs = jnp.exp(scores - lse[2 * index + side])
            grad_probs = dot_nt(values_side, grads)
            inner = jnp.sum(grad_probs * probs, axis=0, keepdims=True)
            grad_scores = (probs * (grad_probs - inner)).astype(BF16)
            value_parts.append(dot(probs.astype(BF16), grads))
            key_parts.append(dot(grad_scores, queries))
            query_parts.append(dot(keys_t[side * HEAD_DIM : (side + 1) * HEAD_DIM], grad_scores))
        grad_queries = jnp.concatenate(query_parts, axis=0).T * scale
        grad_keys = jnp.where(masks[0], key_parts[0], key_parts[1]) * scale
        grad_values = jnp.where(masks[0], value_parts[0], value_parts[1])
        bias_sums[0:1, lanes] += jnp.sum(grad_queries, axis=0, keepdims=True)
        value_lanes = pl.ds(
            pl.multiple_of(width + pair * 2 * HEAD_DIM, 2 * HEAD_DIM), 2 * HEAD_DIM
        )
        bias_sums[0:1, value_lanes] += jnp.sum(grad_values, axis=0, keepdims=True)
        grad_joint[0, rows, lanes] = grad_queries.astype(BF16)
        grad_joint[1, rows, lanes] = grad_keys.astype(BF16)
        grad_joint[2, rows, lanes] = grad_values.astype(BF16)
        return carry

    lax.fori_loop(0, (grad_att.shape[0] // slots) * pairs, step, 0)


def entry_back_kernel(
    layer, with_low, joint_own, joint_far, weight_own, weight_far, stream, gain, grad_mid, order, *rest
):
    if with_low:
        grad_out, sums, low_t, total, partial, low = rest
    else:
        grad_out, sums, total, partial = rest
    acc = None
    for member in range(3):
        left = jnp.concatenate([joint_own[member], joint_far[member]], axis=1)
        right = jnp.concatenate([weight_own[layer, member], weight_far[layer, member]], axis=1)
        term = dot_nt(left, right)
        acc = term if acc is None else acc + term
    total[...] = acc
    partial[...] = jnp.zeros_like(partial)

    def rows(start):
        here = pl.ds(start, CHUNK)
        normed_grad = total[here, :]
        through, gain_term = norm_backward(
            stream[here, :].astype(F32), normed_grad, gain[layer, 0:1, :]
        )
        value = grad_mid[here, :] + through
        grad_out[here, :] = value
        if with_low:
            low[here, :] = value.astype(BF16)
        partial[0] += fold_rows(gain_term)
        partial[1] += fold_rows(normed_grad)

    by_rows(stream.shape[0], rows, 2)
    sums[...] = jnp.sum(partial[...], axis=1)
    if with_low:
        low_t[...] = dot_nt(order[...], low[...]).astype(BF16)


def pack_kernel(layers, *refs):
    ins, (own_out, far_out) = refs[:-2], refs[-2:]
    for layer in range(layers):
        sums_mid, sums_in, qv_own, qv_far, upb_own, upb_far = ins[6 * layer : 6 * layer + 6]
        tiles = upb_own.shape[0]
        for ref, qv, upb in ((own_out, qv_own, upb_own), (far_out, qv_far, upb_far)):
            for row, value in (
                (2 * layer, sums_in[0:1, :]),
                (2 * layer + 1, sums_mid[2:3, :]),
                (2 * (layers + layer), sums_in[1:2, :]),
                (2 * (layers + layer) + 1, sums_mid[3:4, :]),
                (2 * (2 * layers + layer), sums_mid[1:2, :]),
                (2 * (2 * layers + layer) + 1, sums_mid[0:1, :]),
                (6 * layers + layer, qv[...]),
            ):
                ref[row : row + 1, :] = value
            start = 7 * layers + tiles * layer
            ref[start : start + tiles, :] = upb[...]


def unpack_kernel(layers, mine, got, gain, bias, out_bias, qv, upb):
    total = mine[...] + got[...]
    half = qv.shape[2]
    tiles = upb.shape[1] // mine.shape[1]
    width = mine.shape[1]
    for layer in range(layers):
        for norm in range(2):
            row = 2 * layer + norm
            gain[layer, norm : norm + 1, :] = total[row : row + 1]
            row += 2 * layers
            bias[layer, norm : norm + 1, :] = total[row : row + 1]
            row += 2 * layers
            out_bias[layer, norm : norm + 1, :] = total[row : row + 1]
        row = 6 * layers + layer
        for kind in range(2):
            qv[layer, kind : kind + 1, :] = total[row : row + 1, kind * half : (kind + 1) * half]
        row = 7 * layers + tiles * layer
        for part in range(tiles):
            upb[layer : layer + 1, part * width : (part + 1) * width] = total[
                row + part : row + part + 1
            ]


def chunk_sources(order):
    first = list(order[:4])
    sources = []
    for target in range(16):
        source = 0
        for place, bit in enumerate(first):
            if (target >> (3 - place)) & 1:
                source |= 1 << (3 - bit)
        sources.append(source)
    return sources


def weight_kernel(sources, tiles, has_extra, *refs):
    if has_extra:
        left_own, left_far, right_own, right_far, lx_own, lx_far, rx_own, rx_far, keep, send = refs
    else:
        left_own, left_far, right_own, right_far, keep, send = refs

    def product(a_own, a_far, b_own, b_far):
        left = jnp.concatenate([a_own[...], a_far[...]], axis=1)
        right = jnp.concatenate([b_own[...].reshape(b_own.shape[-2:]), b_far[...].reshape(b_far.shape[-2:])], axis=0)
        size = left.shape[0] // 16
        low = dot(left, right).astype(BF16)
        for target, source in enumerate(sources):
            ref = keep if target < 8 else send
            ref[(target % 8) * size : (target % 8 + 1) * size, :] = low[
                source * size : (source + 1) * size, :
            ]

    if has_extra:

        @pl.when(pl.program_id(0) < tiles)
        def _():
            product(left_own, left_far, right_own, right_far)

        @pl.when(pl.program_id(0) == tiles)
        def _():
            product(lx_own, lx_far, rx_own, rx_far)

    else:
        product(left_own, left_far, right_own, right_far)


def weight_grad(name, order, left, right, extra=None, tiles=None, first=0):
    left_own, left_far = left
    right_own, right_far = right
    width, tokens = left_own.shape
    if right_own.ndim == 3:
        tile = right_own.shape[2]
        right_spec = pl.BlockSpec(
            (1, tokens, tile), lambda j: (jnp.minimum(j, tiles - 1) + first, 0, 0)
        )
    else:
        tile = 768 if tiles else 512
        tiles = tiles or right_own.shape[1] // tile
        right_spec = pl.BlockSpec((tokens, tile), lambda j: (0, j + first))
    steps = tiles + (1 if extra is not None else 0)
    ins = [left_own, left_far, right_own, right_far]
    specs = [fixed((width, tokens))] * 2 + [right_spec] * 2
    if extra is not None:
        ins += list(extra)
        specs += [fixed((width, tokens))] * 2 + [fixed((tokens, tile))] * 2
    half = out((width // 2, steps * tile), BF16)
    half_spec = pl.BlockSpec((width // 2, tile), lambda j: (0, j))
    return call(
        functools.partial(weight_kernel, chunk_sources(order), tiles, extra is not None),
        name,
        (steps,),
        ins,
        specs,
        [half, half],
        [half_spec, half_spec],
        flops=4 * width * tokens * steps * tile,
    )


def flip(bit):
    size = lax.axis_size("dp")
    return [(index, index ^ (1 << bit)) for index in range(size)]


class DpSum:
    def __init__(self, order, halves=None, units=()):
        self.order = list(order)
        self.incoming = None
        if halves is not None:
            keep, self.outgoing = halves
            self.members = [[keep]]
        else:
            self.members = [parts for unit in units for parts in unit.members]
            self.halve()

    def halve(self):
        rows = self.members[0][0].shape[0] // 2
        sends = [
            sum(part[rows:].astype(F32) for part in parts).astype(BF16) for parts in self.members
        ]
        self.outgoing = sends[0] if len(sends) == 1 else jnp.concatenate(sends, axis=1)
        self.members = [[part[:rows] for part in parts] for parts in self.members]

    def start(self):
        self.incoming = lax.ppermute(self.outgoing, "dp", flip(self.order.pop(0)))

    def turn(self):
        column = 0
        for parts in self.members:
            width = parts[0].shape[1]
            parts.append(self.incoming[:, column : column + width])
            column += width
        self.incoming = None
        if self.order:
            self.halve()
            self.start()

    def results(self):
        return [sum(part.astype(F32) for part in parts) for parts in self.members]


class Everywhere:
    def __init__(self, mine, far, bits):
        self.mine = mine
        self.incoming = swap(far)
        self.bits = list(range(bits))

    def turn(self):
        self.mine = self.mine + self.incoming
        self.incoming = lax.ppermute(self.mine, "dp", flip(self.bits.pop(0)))


def gate(value, starts=(), turns=(), after=()):
    held = [unit.outgoing for unit in starts] + [unit.incoming for unit in turns]
    value, *held = lax.optimization_barrier((value, *held, *after))
    for unit, array in zip(starts, held):
        unit.outgoing = array
        unit.start()
    for unit, array in zip(turns, held[len(starts) :]):
        unit.incoming = array
        unit.turn()
    return value


def swap(values):
    return lax.ppermute(values, "tensor", [(0, 1), (1, 0)])


def shards(
    images,
    valid_count,
    ln_gain,
    ln_bias,
    w_qkv,
    qv_bias,
    w_out,
    out_bias,
    w_up,
    up_bias,
    w_down,
    cotangent,
):
    local_rows, slots, width = images.shape
    tokens = local_rows * slots
    half = w_qkv.shape[3]
    ff_half = w_up.shape[2]
    tile = 768
    steps = ff_half // tile
    heads = half // HEAD_DIM
    dp = lax.axis_size("dp")
    bits = dp.bit_length() - 1
    assert dp == 1 << bits and bits >= 4 and lax.axis_size("tensor") == 2
    tail = tuple(range(4, bits))
    order_a = (0, 1, 2, 3) + tail
    order_b = (1, 0, 2, 3) + tail
    order_c = (2, 3, 0, 1) + tail

    me = lax.axis_index("dp")
    counts = valid_count

    block = width // dp
    row = jnp.arange(width, dtype=jnp.int32)
    index = row // block
    mirrored = jnp.zeros_like(index)
    for bit in range(bits):
        mirrored = mirrored | (((index >> (bits - 1 - bit)) & 1) << bit)
    source = (mirrored ^ me) * block + row % block
    order = (source[:, None] == row[None, :]).astype(BF16)

    w_qkv = jnp.transpose(w_qkv, (0, 2, 1, 3))
    qkv = (w_qkv, swap(w_qkv))
    qv = (qv_bias, swap(qv_bias))
    upb = (up_bias, swap(up_bias))

    images_2d = images.reshape(tokens, width)
    cotangent_2d = cotangent.reshape(tokens, width)
    smem = pl.BlockSpec(memory_space=pltpu.SMEM)
    wide = (tokens, width)
    flops_wide = 2 * width * width * tokens

    normed, normed_t, cotangent_t = call(
        prep_kernel,
        "prep",
        (),
        [images_2d, cotangent_2d, ln_gain, ln_bias, order],
        [whole()] * 5,
        [out(wide, BF16), out((width, tokens), BF16), out((width, tokens), BF16)],
        [whole()] * 3,
        flops=2 * flops_wide,
    )

    wout, wup, wdown = [
        (weight, swap(lax.optimization_barrier((weight, normed))[0]))
        for weight in (w_out, w_up, w_down)
    ]

    def attend(layer, side, normed, counts):
        lse_shape = (local_rows * heads, 1, slots)
        return call(
            functools.partial(attend_kernel, layer, slots),
            "attend",
            (),
            [counts, normed, qkv[side], qv[side]],
            [smem, whole(), whole(), whole()],
            [out((3, tokens, half), BF16), out((tokens, half), BF16), out(lse_shape, F32)],
            [whole()] * 3,
            flops=6 * tokens * width * half + 4 * tokens * slots * half,
        )

    stream = images_2d
    saved = []
    got_cotangent_t = swap(cotangent_t)
    pooled = None
    for layer in range(LAYERS):
        last = layer == LAYERS - 1
        own = attend(layer, 0, normed, counts)
        if layer > 0:
            before = saved[layer - 1]
            names = ("got_normed_t", "got_att", "got_hid")
            far_counts, got_cotangent_t, *got = lax.optimization_barrier(
                (counts, got_cotangent_t, *[before[name] for name in names])
            )
            before.update(zip(names, got))
        else:
            far_counts = counts
        far = attend(layer, 1, normed, far_counts)
        gain_in = ln_gain
        if layer > 0:
            gain_in, before["got_mid_normed_t"] = lax.optimization_barrier(
                (ln_gain, before["got_mid_normed_t"])
            )
        up_spec = pl.BlockSpec((1, width, tile), lambda j, layer=layer: (layer, 0, j))
        down_spec = pl.BlockSpec((1, tile, width), lambda j, layer=layer: (layer, j, 0))
        tile_spec = pl.BlockSpec((tokens, tile), lambda j: (0, j))
        bias_spec = pl.BlockSpec((LAYERS, tile), lambda j: (0, j))
        ff = out((tokens, ff_half), BF16)
        extra = (
            [out((local_rows, width), F32)]
            if last
            else [out(wide, BF16), out((width, tokens), BF16)]
        )
        results = call(
            functools.partial(feed_kernel, layer, slots, last),
            "feed",
            (steps,),
            [
                counts,
                stream,
                own[1],
                far[1],
                wout[0],
                wout[1],
                out_bias,
                gain_in,
                ln_bias,
                order,
                wup[0],
                wup[1],
                upb[0],
                upb[1],
                wdown[0],
                wdown[1],
            ],
            [
                smem,
                *([whole()] * 9),
                up_spec,
                up_spec,
                bias_spec,
                bias_spec,
                down_spec,
                down_spec,
            ],
            [out(wide, F32), out((width, tokens), BF16), ff, ff, ff, ff, out(wide, F32)] + extra,
            [whole()] * 2 + [tile_spec] * 4 + [whole()] + [whole()] * len(extra),
            [pltpu.VMEM(wide, BF16), pltpu.VMEM(wide, F32), pltpu.VMEM((tokens, tile), F32)],
            flops=8 * tokens * width * ff_half + 2 * flops_wide,
        )
        mid, mid_normed_t, hid_own, hid_far, slope_own, slope_far, stream_next = results[:7]
        saved.append(
            dict(
                stream=stream,
                own=own,
                far=far,
                mid=mid,
                slope=(slope_own, slope_far),
                hid=hid_own,
                attended=own[1],
                normed_t=normed_t,
                mid_normed_t=mid_normed_t,
                got_hid=swap(hid_far),
                got_att=swap(far[1]),
                got_normed_t=swap(normed_t),
                got_mid_normed_t=swap(mid_normed_t),
            )
        )
        stream = stream_next
        if last:
            pooled = results[7]
        else:
            normed, normed_t = results[7:9]

    def feed_back(layer, grad, gain_in):
        kept = saved[layer]
        up_spec = pl.BlockSpec((1, width, tile), lambda j: (layer, 0, j))
        down_spec = pl.BlockSpec((1, tile, width), lambda j: (layer, j, 0))
        tile_spec = pl.BlockSpec((tokens, tile), lambda j: (0, j))
        ff = out((tokens, ff_half), BF16)
        bias_shape = out((steps, tile), F32)
        att_shape = out((tokens, half), BF16)
        return call(
            functools.partial(feed_back_kernel, layer),
            "feed_back",
            (steps,),
            [
                grad,
                kept["mid"],
                gain_in,
                order,
                wdown[0],
                wdown[1],
                wup[0],
                wup[1],
                kept["slope"][0],
                kept["slope"][1],
                wout[0],
                wout[1],
            ],
            [
                *([whole()] * 4),
                down_spec,
                down_spec,
                up_spec,
                up_spec,
                tile_spec,
                tile_spec,
                whole(),
                whole(),
            ],
            [
                ff,
                ff,
                bias_shape,
                bias_shape,
                out(wide, F32),
                out((width, tokens), BF16),
                att_shape,
                att_shape,
                out((4, width), F32),
            ],
            [tile_spec, tile_spec, *([whole()] * 7)],
            [
                pltpu.VMEM(wide, BF16),
                pltpu.VMEM(wide, F32),
                pltpu.VMEM((tokens, tile), F32),
                pltpu.VMEM((4, 8, width), F32),
            ],
            flops=8 * tokens * width * ff_half + 2 * flops_wide,
        )

    def attend_back(forward, grad_att, counts_in):
        joint, _, lse = forward
        return call(
            functools.partial(attend_back_kernel, slots),
            "attend_back",
            (),
            [counts_in, joint, lse, grad_att],
            [smem, whole(), whole(), whole()],
            [out(joint.shape, BF16), out((1, 2 * half), F32)],
            [whole()] * 2,
            flops=10 * tokens * slots * half,
        )

    def entry_back(layer, joint_own, joint_far, grad_mid, gain_in):
        with_low = layer > 0
        return call(
            functools.partial(entry_back_kernel, layer, with_low),
            "entry_back",
            (),
            [
                joint_own,
                joint_far,
                qkv[0],
                qkv[1],
                saved[layer]["stream"],
                gain_in,
                grad_mid,
                order,
            ],
            [whole()] * 8,
            [out(wide, F32), out((2, width), F32)]
            + ([out((width, tokens), BF16)] if with_low else []),
            [whole()] * (3 if with_low else 2),
            [pltpu.VMEM(wide, F32), pltpu.VMEM((2, 8, width), F32)]
            + ([pltpu.VMEM(wide, BF16)] if with_low else []),
            flops=12 * tokens * width * half,
        )

    def down_halves(layer, order_of, grad_t, got_grad_t):
        kept = saved[layer]
        return weight_grad(
            "down_grad", order_of, (grad_t, got_grad_t), (kept["hid"], kept["got_hid"])
        )

    def up_halves(layer, order_of, pre_own, got_pre, tiles=None, first=0):
        kept = saved[layer]
        return weight_grad(
            "up_grad",
            order_of,
            (kept["mid_normed_t"], kept["got_mid_normed_t"]),
            (pre_own, got_pre),
            tiles=tiles,
            first=first,
        )

    def lefts(layer):
        return saved[layer]["normed_t"], saved[layer]["got_normed_t"]

    def extras(layer, mid_t, got_mid_t):
        return mid_t, got_mid_t, saved[layer]["attended"], saved[layer]["got_att"]

    small = [None] * LAYERS
    down_1 = DpSum(order_a, down_halves(1, order_a, cotangent_t, got_cotangent_t))
    gain_in = gate(ln_gain, [down_1])
    pre_own, pre_far, upb_own, upb_far, grad_mid, mid_t, att_own, att_far, sums_mid = feed_back(
        1, cotangent_2d, gain_in
    )
    got_pre, got_mid_t = swap(pre_far), swap(mid_t)
    joint_far, qv_far = attend_back(saved[1]["far"], att_far, counts)
    got_joint = swap(joint_far)
    counts_in = gate(counts, [], [down_1], [qv_far])
    joint_own, qv_own = attend_back(saved[1]["own"], att_own, counts_in)
    pre_own = gate(pre_own, after=[qv_own])
    up_1 = DpSum(order_a, up_halves(1, order_a, pre_own, got_pre))
    gain_in = gate(gain_in, [up_1], [down_1])
    grad, sums_in, grad_t = entry_back(1, joint_own, joint_far, grad_mid, gain_in)
    got_grad_t = swap(grad_t)
    small[1] = (sums_mid, sums_in, qv_own, qv_far, upb_own, upb_far)
    joint_own = gate(joint_own, [], [down_1], [sums_in])
    rest_1 = DpSum(
        order_b[:2],
        weight_grad(
            "qkv_out_grad",
            order_b,
            lefts(1),
            (joint_own, got_joint),
            extras(1, mid_t, got_mid_t),
            tiles=3,
        ),
    )
    grad_t = gate(grad_t, [rest_1])
    down_0 = DpSum(order_a[:2], down_halves(0, order_a, grad_t, got_grad_t))

    gain_in = gate(gain_in, [down_0], [up_1, down_1])
    pre_own, pre_far, upb_own, upb_far, grad_mid, mid_t, att_own, att_far, sums_mid = feed_back(
        0, grad, gain_in
    )
    got_pre, got_mid_t = swap(pre_far), swap(mid_t)
    counts_in = gate(counts_in, [], [up_1, rest_1], [sums_mid])
    joint_far, qv_far = attend_back(saved[0]["far"], att_far, counts_in)
    got_joint = swap(joint_far)
    counts_in = gate(counts_in, [], [down_0, up_1], [qv_far])
    joint_own, qv_own = attend_back(saved[0]["own"], att_own, counts_in)
    pre_own = gate(pre_own, [], [rest_1, up_1], [qv_own])
    up_a = DpSum(order_a[:2], up_halves(0, order_a, pre_own, got_pre, tiles=1))
    up_b = DpSum(order_b[:2], up_halves(0, order_b, pre_own, got_pre, tiles=1, first=1))
    joint_low = gate(joint_own, [up_a, up_b])
    one = DpSum(
        order_a[:2],
        weight_grad("qk_grad", order_a, lefts(0), (joint_low, got_joint), tiles=2),
    )
    two = DpSum(
        order_b[:2],
        weight_grad(
            "v_out_grad",
            order_b,
            lefts(0),
            (joint_low, got_joint),
            extras(0, mid_t, got_mid_t),
            tiles=1,
            first=2,
        ),
    )
    gain_in = gate(gain_in, [one, two], [down_0])
    late = DpSum(order_a[2:], units=[down_0, rest_1])
    late.start()
    grad, sums_in = entry_back(0, joint_own, joint_far, grad_mid, gain_in)
    last = gate(sums_in, [], [up_a, up_b, late])
    last = gate(last, [], [one, two, late])
    small[0] = (sums_mid, last, qv_own, qv_far, upb_own, upb_far)
    ins = [array for arrays in small for array in arrays]
    vector_shape = out(((7 + steps) * LAYERS, width), F32)
    mine, far = call(
        functools.partial(pack_kernel, LAYERS),
        "pack_small",
        (),
        ins,
        [whole()] * len(ins),
        [vector_shape] * 2,
        [whole()] * 2,
    )
    vector = Everywhere(mine, far, bits)
    last = gate(last, [], [up_a, up_b, vector])
    up_0 = DpSum(order_a[2:], units=[up_a, up_b])
    up_0.start()
    last = gate(last, [], [one, two, vector])
    join_0 = DpSum(order_a[2:], units=[one, two])
    join_0.start()
    running = [down_1, up_1, late]
    while any(unit.incoming is not None for unit in running):
        last = gate(last, [], [unit for unit in running if unit.incoming is not None])
    while up_0.incoming is not None or join_0.incoming is not None:
        for unit in (up_0, join_0):
            if unit.incoming is not None:
                last = gate(last, [], [unit] + ([vector] if vector.bits else []))

    (down_1_sum,), (up_1_sum,) = down_1.results(), up_1.results()
    down_0_sum, both = late.results()
    one_sum, two_sum = join_0.results()
    summed = [
        (
            jnp.concatenate([one_sum, two_sum[:, :half]], axis=1).reshape(block, 3, half),
            two_sum[:, half:].T,
            jnp.concatenate(up_0.results(), axis=1),
            down_0_sum.T,
        ),
        (
            both[:, : 3 * half].reshape(block, 3, half),
            both[:, 3 * half :].T,
            up_1_sum,
            down_1_sum.T,
        ),
    ]

    while vector.bits:
        vector.turn()
    mine, got = vector.mine, vector.incoming
    gain_grads, shift_grads, outb_grads, qv_grads, upb_grads = call(
        functools.partial(unpack_kernel, LAYERS),
        "unpack_small",
        (),
        [mine, got],
        [whole()] * 2,
        [
            out(ln_gain.shape, F32),
            out(ln_bias.shape, F32),
            out(out_bias.shape, F32),
            out(qv_bias.shape, F32),
            out(up_bias.shape, F32),
        ],
        [whole()] * 5,
    )
    stacked = [jnp.stack([summed[layer][member] for layer in range(LAYERS)]) for member in range(4)]
    return (
        stream.reshape(images.shape),
        pooled,
        grad.reshape(images.shape),
        gain_grads,
        shift_grads,
        stacked[0],
        qv_grads,
        stacked[1],
        outb_grads,
        stacked[2],
        upb_grads,
        stacked[3],
    )


def solution(mesh):
    placed = (
        P(("dp", "tensor"), None, None),
        P("dp"),
        P(),
        P(),
        P(None, None, None, "tensor"),
        P(None, None, "tensor"),
        P(None, "tensor", None),
        P(),
        P(None, None, "tensor"),
        P(None, "tensor"),
        P(None, "tensor", None),
        P(("dp", "tensor"), None, None),
    )
    return jax.shard_map(
        shards,
        mesh=mesh,
        in_specs=placed,
        out_specs=(
            P(("dp", "tensor"), None, None),
            P(("dp", "tensor"), None),
            P(("dp", "tensor"), None, None),
            P(),
            P(),
            P(None, "dp", None, "tensor"),
            P(None, None, "tensor"),
            P(None, "tensor", "dp"),
            P(),
            P(None, "dp", "tensor"),
            P(None, "tensor"),
            P(None, "tensor", "dp"),
        ),
        check_vma=False,
    )
```

```python
import functools
import math

import jax
import jax.numpy as jnp
from jax import lax
from jax.experimental import pallas as pl
from jax.experimental.pallas import tpu as pltpu
from jax.sharding import PartitionSpec as P

HEAD_DIM = 64
LAYERS = 2
EPSILON = 1e-06
NEGATIVE = -1e30
BF16 = jnp.bfloat16
F32 = jnp.float32
CHUNK = 16


def dot(left, right):
    return lax.dot_general(left, right, (((1,), (0,)), ((), ())), preferred_element_type=F32)


def dot_nt(left, right):
    return lax.dot_general(left, right, (((1,), (1,)), ((), ())), preferred_element_type=F32)


def fixed(shape, *lead):
    where = tuple(lead) + (0,) * (len(shape) - len(lead))
    return pl.BlockSpec(shape, lambda *_: where)


def out(shape, dtype):
    return jax.ShapeDtypeStruct(shape, dtype)


def in_hbm(values):
    return pltpu.with_memory_space_constraint(values, pltpu.HBM)


def cost(flops, *arrays):
    total = sum(math.prod(a.shape) * a.dtype.itemsize for a in arrays)
    return pl.CostEstimate(flops=int(flops) // 64, bytes_accessed=int(total) // 64, transcendentals=0)


MIB = 1 << 20


def call(body, name, grid, ins, in_specs, outs, out_specs, scratch=(), flops=0, limit=24):
    return pl.pallas_call(
        body,
        name=name,
        grid=grid,
        in_specs=in_specs,
        out_specs=out_specs,
        out_shape=outs,
        scratch_shapes=list(scratch),
        compiler_params=pltpu.CompilerParams(vmem_limit_bytes=limit * MIB),
        cost_estimate=cost(flops, *ins, *outs),
    )(*ins)


def whole():
    return pl.BlockSpec(memory_space=pltpu.VMEM)


def hbm():
    return pl.BlockSpec(memory_space=pltpu.HBM)


def by_rows(rows, body, unroll=1):
    def step(index, carry):
        for part in range(unroll):
            body(pl.multiple_of((index * unroll + part) * CHUNK, CHUNK))
        return carry

    lax.fori_loop(0, rows // (CHUNK * unroll), step, 0)


def moments(values):
    average = jnp.mean(values, axis=-1, keepdims=True)
    centred = values - average
    variance = jnp.mean(centred * centred, axis=-1, keepdims=True)
    return centred, lax.rsqrt(variance + EPSILON)


def normalized(values, gain, bias):
    centred, scale = moments(values)
    return centred * scale * gain + bias


def norm_backward(values, grad_normed, gain):
    centred, scale = moments(values)
    unit = centred * scale
    grad_unit = grad_normed * gain
    first = jnp.mean(grad_unit, axis=-1, keepdims=True)
    second = jnp.mean(grad_unit * unit, axis=-1, keepdims=True)
    return scale * (grad_unit - first - unit * second), grad_normed * unit


def fold_rows(values):
    total = values[0:8]
    for start in range(8, values.shape[0], 8):
        total = total + values[start : start + 8]
    return total


def prep_kernel(images, cotangent, gain, bias, order, normed, normed_t, cotangent_t):
    def rows(start):
        here = pl.ds(start, CHUNK)
        values = images[here, :].astype(F32)
        normed[here, :] = normalized(values, gain[0, 0:1, :], bias[0, 0:1, :]).astype(BF16)

    by_rows(images.shape[0], rows, 4)
    normed_t[...] = dot_nt(order[...], normed[...]).astype(BF16)
    cotangent_t[...] = dot_nt(order[...], cotangent[...]).astype(BF16)


def head_masks(slots):
    lane = lax.broadcasted_iota(jnp.int32, (slots, 2 * HEAD_DIM), 1)
    return lane < HEAD_DIM, lane >= HEAD_DIM


def own_count(counts, image, images):
    return counts[lax.axis_index("tensor") * images + image]


def attend_kernel(layer, slots, counts, normed, weight, bias, joint, attended, lse):
    width = attended.shape[1]
    pairs = width // (2 * HEAD_DIM)
    scale = HEAD_DIM ** (-0.5)
    member = pl.program_id(0)
    row = jnp.where(member == 0, 0, 1)
    shift = jnp.where(member == 1, 0.0, bias[layer, pl.ds(row, 1), :])
    joint[member] = (dot(normed[...], weight[0, 0]) + shift).astype(BF16)
    masks = head_masks(slots)
    key_index = lax.broadcasted_iota(jnp.int32, (slots, slots), 0)

    def step(index, carry):
        image = index // pairs
        pair = index % pairs
        rows = pl.ds(pl.multiple_of(image * slots, slots), slots)
        lanes = pl.ds(pl.multiple_of(pair * 2 * HEAD_DIM, 2 * HEAD_DIM), 2 * HEAD_DIM)
        queries = joint[0, rows, lanes]
        keys_in = joint[1, rows, lanes] * jnp.asarray(scale, BF16)
        values_t = joint[2, rows, lanes].T
        valid = key_index < own_count(counts, image, normed.shape[0] // slots)
        parts = []
        for side in range(2):
            keys_side = jnp.where(masks[side], keys_in, jnp.zeros_like(keys_in))
            scores = jnp.where(valid, dot_nt(keys_side, queries), NEGATIVE)
            largest = jnp.max(scores, axis=0, keepdims=True)
            exponent = jnp.exp(scores - largest)
            total = jnp.sum(exponent, axis=0, keepdims=True)
            probs = (exponent * (1.0 / total)).astype(BF16)
            parts.append(dot(values_t[side * HEAD_DIM : (side + 1) * HEAD_DIM], probs))
            lse[2 * index + side] = largest + jnp.log(total)
        attended[rows, lanes] = jnp.concatenate(parts, axis=0).T.astype(BF16)
        return carry

    @pl.when(member == 2)
    def _():
        lax.fori_loop(0, (normed.shape[0] // slots) * pairs, step, 0)


def fetch(source, target, sem):
    copy = pltpu.make_async_copy(source, target, sem)
    copy.start()
    return copy


def feed_kernel(
    layer,
    slots,
    last_layer,
    counts,
    stream,
    att_own,
    att_far,
    out_own,
    out_far,
    out_bias,
    gain,
    bias,
    order,
    up_own,
    up_far,
    up_bias_own,
    up_bias_far,
    down_own,
    down_far,
    mid,
    normed_t,
    hid_own,
    hid_far,
    slope_own,
    slope_far,
    stream_out,
    *rest,
):
    if last_layer:
        pooled = rest[0]
    else:
        next_normed, next_t = rest[:2]
    normed, total, pre, w_out, w_up, w_down, hid, slope, in_sem, out_sem = rest[1 if last_layer else 2 :]
    tokens = stream.shape[0]
    half = w_out.shape[0] // 2
    units = w_up.shape[0]
    tile = w_up.shape[2]
    tiles = units // 2
    out_in = [
        fetch(ref.at[layer], w_out.at[pl.ds(side * half, half)], in_sem.at[side])
        for side, ref in enumerate((out_own, out_far))
    ]
    up_in, down_in = [], []
    for unit in range(units):
        side, part = unit // tiles, unit % tiles
        columns = pl.ds(part * tile, tile)
        up_ref, down_ref = ((up_own, down_own), (up_far, down_far))[side]
        up_in.append(fetch(up_ref.at[layer, :, columns], w_up.at[unit], in_sem.at[2 + unit]))
        down_in.append(
            fetch(down_ref.at[layer, columns, :], w_down.at[unit], in_sem.at[2 + units + unit])
        )
    for copy in out_in:
        copy.wait()
    total[...] = dot(jnp.concatenate([att_own[...], att_far[...]], axis=1), w_out[...])

    def enter(start):
        here = pl.ds(start, CHUNK)
        value = stream[here, :].astype(F32) + (total[here, :] + out_bias[layer, 0:1, :])
        mid[here, :] = value
        normed[here, :] = normalized(value, gain[layer, 1:2, :], bias[layer, 1:2, :]).astype(BF16)

    by_rows(tokens, enter, 4)
    up_in[0].wait()
    pre[0] = dot(normed[...], w_up[0])
    normed_t[...] = dot_nt(order[...], normed[...]).astype(BF16)
    rows = 128
    out_copies = []
    for unit in range(units):
        side, part = unit // tiles, unit % tiles
        shift = (up_bias_own, up_bias_far)[side][layer : layer + 1, part * tile : (part + 1) * tile]
        if unit + 1 < units:
            up_in[unit + 1].wait()
        if unit > 0:
            down_in[unit - 1].wait()

        def chunk(index, carry):
            block = pl.ds(pl.multiple_of(index * rows, rows), rows)
            if unit + 1 < units:
                pre[(unit + 1) % 2, block, :] = dot(normed[block, :], w_up[unit + 1])
            if unit == 1:
                total[block, :] = dot(hid[unit - 1, block, :], w_down[unit - 1])
            elif unit > 1:
                total[block, :] += dot(hid[unit - 1, block, :], w_down[unit - 1])
            for sub in range(0, rows, CHUNK):
                here = pl.ds(pl.multiple_of(index * rows + sub, CHUNK), CHUNK)
                value = pre[unit % 2, here, :] + shift
                cdf = 0.5 + 0.5 * lax.erf(value * (0.5**0.5))
                hid[unit, here, :] = (value * cdf).astype(BF16)
                density = jnp.exp(-0.5 * value * value) * ((2.0 * math.pi) ** -0.5)
                slope[unit, here, :] = (cdf + value * density).astype(BF16)
            return carry

        lax.fori_loop(0, tokens // rows, chunk, 0)
        hid_ref, slope_ref = ((hid_own, slope_own), (hid_far, slope_far))[side]
        columns = pl.ds(part * tile, tile)
        out_copies.append(fetch(hid.at[unit], hid_ref.at[:, columns], out_sem.at[unit]))
        out_copies.append(fetch(slope.at[unit], slope_ref.at[:, columns], out_sem.at[units + unit]))
    down_in[units - 1].wait()
    total[...] += dot(hid[units - 1], w_down[units - 1])

    def leave(start):
        here = pl.ds(start, CHUNK)
        value = mid[here, :] + (total[here, :] + out_bias[layer, 1:2, :])
        stream_out[here, :] = value
        if not last_layer:
            next_normed[here, :] = normalized(
                value, gain[layer + 1, 0:1, :], bias[layer + 1, 0:1, :]
            ).astype(BF16)

    by_rows(tokens, leave, 4)
    if last_layer:
        index = lax.broadcasted_iota(jnp.int32, (slots, 1), 0)
        for image in range(tokens // slots):
            block = stream_out[image * slots : (image + 1) * slots, :]
            count = own_count(counts, image, tokens // slots)
            summed = jnp.sum(jnp.where(index < count, block, 0.0), axis=0, keepdims=True)
            pooled[image : image + 1, :] = summed / count.astype(F32)
    else:
        next_t[...] = dot_nt(order[...], next_normed[...]).astype(BF16)
    for copy in out_copies:
        copy.wait()


def feed_back_kernel(
    layer,
    grad_in,
    mid,
    gain,
    order,
    down_own,
    down_far,
    up_own,
    up_far,
    slope_own,
    slope_far,
    out_own,
    out_far,
    pre_own,
    pre_far,
    bias_own,
    bias_far,
    grad_mid,
    mid_t,
    att_own,
    att_far,
    sums,
    low,
    total,
    hidden,
    partial,
):
    step = pl.program_id(0)
    tokens = grad_in.shape[0]

    @pl.when(step == 0)
    def _():
        partial[...] = jnp.zeros_like(partial)

        def rows(start):
            here = pl.ds(start, CHUNK)
            value = grad_in[here, :].astype(F32)
            low[here, :] = value.astype(BF16)
            partial[0] += fold_rows(value)

        by_rows(tokens, rows)
        total[...] = jnp.zeros_like(total)

    for weight_down, weight_up, slope, pre, bias in (
        (down_far, up_far, slope_far, pre_far, bias_far),
        (down_own, up_own, slope_own, pre_own, bias_own),
    ):
        hidden[...] = dot_nt(low[...], weight_down[0])

        def rows(index, carry):
            here = pl.ds(pl.multiple_of(index * CHUNK, CHUNK), CHUNK)
            value = hidden[here, :] * slope[here, :].astype(F32)
            pre[here, :] = value.astype(BF16)
            return carry + fold_rows(value)

        summed = lax.fori_loop(
            0, tokens // CHUNK, rows, jnp.zeros((8, hidden.shape[1]), F32), unroll=2
        )
        bias[pl.ds(step, 1), :] = jnp.sum(summed, axis=0, keepdims=True)
        total[...] += dot_nt(pre[...], weight_up[0])

    @pl.when(step == pl.num_programs(0) - 1)
    def _():
        def rows(start):
            here = pl.ds(start, CHUNK)
            normed_grad = total[here, :]
            through, gain_term = norm_backward(mid[here, :], normed_grad, gain[layer, 1:2, :])
            value = grad_in[here, :].astype(F32) + through
            grad_mid[here, :] = value
            low[here, :] = value.astype(BF16)
            partial[1] += fold_rows(value)
            partial[2] += fold_rows(gain_term)
            partial[3] += fold_rows(normed_grad)

        by_rows(tokens, rows, 2)
        sums[...] = jnp.sum(partial[...], axis=1)
        mid_t[...] = dot_nt(order[...], low[...]).astype(BF16)
        att_far[...] = dot_nt(low[...], out_far[0]).astype(BF16)
        att_own[...] = dot_nt(low[...], out_own[0]).astype(BF16)


def attend_back_kernel(slots, counts, joint, lse, grad_att, grad_joint, bias_sums):
    width = grad_att.shape[1]
    pairs = width // (2 * HEAD_DIM)
    scale = HEAD_DIM ** (-0.5)
    masks = head_masks(slots)
    key_index = lax.broadcasted_iota(jnp.int32, (slots, slots), 0)
    bias_sums[...] = jnp.zeros_like(bias_sums)

    def step(index, carry):
        image = index // pairs
        pair = index % pairs
        rows = pl.ds(pl.multiple_of(image * slots, slots), slots)
        lanes = pl.ds(pl.multiple_of(pair * 2 * HEAD_DIM, 2 * HEAD_DIM), 2 * HEAD_DIM)
        queries = joint[0, rows, lanes]
        keys_in = joint[1, rows, lanes]
        values_in = joint[2, rows, lanes]
        grads = grad_att[rows, lanes]
        keys_t = keys_in.T
        keys_scaled = keys_in * jnp.asarray(scale, BF16)
        valid = key_index < own_count(counts, image, grad_att.shape[0] // slots)
        zeros = jnp.zeros_like(keys_in)
        query_parts, key_parts, value_parts = [], [], []
        for side in range(2):
            keys_side = jnp.where(masks[side], keys_scaled, zeros)
            values_side = jnp.where(masks[side], values_in, zeros)
            scores = jnp.where(valid, dot_nt(keys_side, queries), NEGATIVE)
            probs = jnp.exp(scores - lse[2 * index + side])
            grad_probs = dot_nt(values_side, grads)
            inner = jnp.sum(grad_probs * probs, axis=0, keepdims=True)
            grad_scores = (probs * (grad_probs - inner)).astype(BF16)
            value_parts.append(dot(probs.astype(BF16), grads))
            key_parts.append(dot(grad_scores, queries))
            query_parts.append(dot(keys_t[side * HEAD_DIM : (side + 1) * HEAD_DIM], grad_scores))
        grad_queries = jnp.concatenate(query_parts, axis=0).T * scale
        grad_keys = jnp.where(masks[0], key_parts[0], key_parts[1]) * scale
        grad_values = jnp.where(masks[0], value_parts[0], value_parts[1])
        bias_sums[0:1, lanes] += jnp.sum(grad_queries, axis=0, keepdims=True)
        value_lanes = pl.ds(
            pl.multiple_of(width + pair * 2 * HEAD_DIM, 2 * HEAD_DIM), 2 * HEAD_DIM
        )
        bias_sums[0:1, value_lanes] += jnp.sum(grad_values, axis=0, keepdims=True)
        grad_joint[0, rows, lanes] = grad_queries.astype(BF16)
        grad_joint[1, rows, lanes] = grad_keys.astype(BF16)
        grad_joint[2, rows, lanes] = grad_values.astype(BF16)
        return carry

    lax.fori_loop(0, (grad_att.shape[0] // slots) * pairs, step, 0)


def entry_back_kernel(
    layer, with_low, joint_own, joint_far, weight_own, weight_far, stream, gain, grad_mid, order, *rest
):
    if with_low:
        grad_out, sums, low_t, total, partial, low = rest
    else:
        grad_out, sums, total, partial = rest
    member = pl.program_id(0)

    @pl.when(member == 0)
    def _():
        total[...] = jnp.zeros_like(total)
        partial[...] = jnp.zeros_like(partial)

    left = jnp.concatenate([joint_own[member], joint_far[member]], axis=1)
    right = jnp.concatenate([weight_own[0, 0], weight_far[0, 0]], axis=1)
    total[...] += dot_nt(left, right)

    def rows(start):
        here = pl.ds(start, CHUNK)
        normed_grad = total[here, :]
        through, gain_term = norm_backward(
            stream[here, :].astype(F32), normed_grad, gain[layer, 0:1, :]
        )
        value = grad_mid[here, :] + through
        grad_out[here, :] = value
        if with_low:
            low[here, :] = value.astype(BF16)
        partial[0] += fold_rows(gain_term)
        partial[1] += fold_rows(normed_grad)

    @pl.when(member == 2)
    def _():
        by_rows(stream.shape[0], rows, 2)
        sums[...] = jnp.sum(partial[...], axis=1)
        if with_low:
            low_t[...] = dot_nt(order[...], low[...]).astype(BF16)


def pack_kernel(layers, *refs):
    ins, (own_out, far_out) = refs[:-2], refs[-2:]
    for layer in range(layers):
        sums_mid, sums_in, qv_own, qv_far, upb_own, upb_far = ins[6 * layer : 6 * layer + 6]
        tiles = upb_own.shape[0]
        for ref, qv, upb in ((own_out, qv_own, upb_own), (far_out, qv_far, upb_far)):
            for row, value in (
                (2 * layer, sums_in[0:1, :]),
                (2 * layer + 1, sums_mid[2:3, :]),
                (2 * (layers + layer), sums_in[1:2, :]),
                (2 * (layers + layer) + 1, sums_mid[3:4, :]),
                (2 * (2 * layers + layer), sums_mid[1:2, :]),
                (2 * (2 * layers + layer) + 1, sums_mid[0:1, :]),
                (6 * layers + layer, qv[...]),
            ):
                ref[row : row + 1, :] = value
            start = 7 * layers + tiles * layer
            ref[start : start + tiles, :] = upb[...]


def unpack_kernel(layers, mine, got, gain, bias, out_bias, qv, upb):
    total = mine[...] + got[...]
    half = qv.shape[2]
    tiles = upb.shape[1] // mine.shape[1]
    width = mine.shape[1]
    for layer in range(layers):
        for norm in range(2):
            row = 2 * layer + norm
            gain[layer, norm : norm + 1, :] = total[row : row + 1]
            row += 2 * layers
            bias[layer, norm : norm + 1, :] = total[row : row + 1]
            row += 2 * layers
            out_bias[layer, norm : norm + 1, :] = total[row : row + 1]
        row = 6 * layers + layer
        for kind in range(2):
            qv[layer, kind : kind + 1, :] = total[row : row + 1, kind * half : (kind + 1) * half]
        row = 7 * layers + tiles * layer
        for part in range(tiles):
            upb[layer : layer + 1, part * width : (part + 1) * width] = total[
                row + part : row + part + 1
            ]


def chunk_sources(order):
    first = list(order[:4])
    sources = []
    for target in range(16):
        source = 0
        for place, bit in enumerate(first):
            if (target >> (3 - place)) & 1:
                source |= 1 << (3 - bit)
        sources.append(source)
    return sources


def weight_kernel(sources, tiles, has_extra, *refs):
    if has_extra:
        left_own, left_far, right_own, right_far, lx_own, lx_far, rx_own, rx_far, keep, send = refs
    else:
        left_own, left_far, right_own, right_far, keep, send = refs

    def product(a_own, a_far, b_own, b_far):
        left = jnp.concatenate([a_own[...], a_far[...]], axis=1)
        right = jnp.concatenate([b_own[...].reshape(b_own.shape[-2:]), b_far[...].reshape(b_far.shape[-2:])], axis=0)
        size = left.shape[0] // 16
        low = dot(left, right).astype(BF16)
        for target, source in enumerate(sources):
            ref = keep if target < 8 else send
            ref[(target % 8) * size : (target % 8 + 1) * size, :] = low[
                source * size : (source + 1) * size, :
            ]

    if has_extra:

        @pl.when(pl.program_id(0) < tiles)
        def _():
            product(left_own, left_far, right_own, right_far)

        @pl.when(pl.program_id(0) == tiles)
        def _():
            product(lx_own, lx_far, rx_own, rx_far)

    else:
        product(left_own, left_far, right_own, right_far)


def weight_grad(name, order, left, right, extra=None, tiles=None, first=0):
    left_own, left_far = left
    right_own, right_far = right
    width, tokens = left_own.shape
    if right_own.ndim == 3:
        tile = right_own.shape[2]
        right_spec = pl.BlockSpec(
            (1, tokens, tile), lambda j: (jnp.minimum(j, tiles - 1) + first, 0, 0)
        )
    else:
        tile = 768 if tiles else 512
        tiles = tiles or right_own.shape[1] // tile
        right_spec = pl.BlockSpec((tokens, tile), lambda j: (0, j + first))
    steps = tiles + (1 if extra is not None else 0)
    ins = [left_own, left_far, right_own, right_far]
    specs = [fixed((width, tokens))] * 2 + [right_spec] * 2
    if extra is not None:
        ins += list(extra)
        specs += [fixed((width, tokens))] * 2 + [fixed((tokens, tile))] * 2
    half = out((width // 2, steps * tile), BF16)
    half_spec = pl.BlockSpec((width // 2, tile), lambda j: (0, j))
    return call(
        functools.partial(weight_kernel, chunk_sources(order), tiles, extra is not None),
        name,
        (steps,),
        ins,
        specs,
        [half, half],
        [half_spec, half_spec],
        flops=4 * width * tokens * steps * tile,
    )


def flip(bit):
    size = lax.axis_size("dp")
    return [(index, index ^ (1 << bit)) for index in range(size)]


class DpSum:
    def __init__(self, order, halves=None, units=()):
        self.order = list(order)
        self.incoming = None
        if halves is not None:
            keep, self.outgoing = halves
            self.members = [[keep]]
        else:
            self.members = [parts for unit in units for parts in unit.members]
            self.halve()

    def halve(self):
        rows = self.members[0][0].shape[0] // 2
        sends = [
            sum(part[rows:].astype(F32) for part in parts).astype(BF16) for parts in self.members
        ]
        self.outgoing = sends[0] if len(sends) == 1 else jnp.concatenate(sends, axis=1)
        self.members = [[part[:rows] for part in parts] for parts in self.members]

    def start(self):
        self.incoming = lax.ppermute(self.outgoing, "dp", flip(self.order.pop(0)))

    def turn(self):
        column = 0
        for parts in self.members:
            width = parts[0].shape[1]
            parts.append(self.incoming[:, column : column + width])
            column += width
        self.incoming = None
        if self.order:
            self.halve()
            self.start()

    def results(self):
        return [sum(part.astype(F32) for part in parts) for parts in self.members]


class Everywhere:
    def __init__(self, mine, far, bits):
        self.mine = mine
        self.incoming = swap(far)
        self.bits = list(range(bits))

    def turn(self):
        self.mine = self.mine + self.incoming
        self.incoming = lax.ppermute(self.mine, "dp", flip(self.bits.pop(0)))


def gate(value, starts=(), turns=(), after=()):
    held = [unit.outgoing for unit in starts] + [unit.incoming for unit in turns]
    value, *held = lax.optimization_barrier((value, *held, *after))
    for unit, array in zip(starts, held):
        unit.outgoing = array
        unit.start()
    for unit, array in zip(turns, held[len(starts) :]):
        unit.incoming = array
        unit.turn()
    return value


def swap(values):
    return lax.ppermute(values, "tensor", [(0, 1), (1, 0)])


def shards(
    images,
    valid_count,
    ln_gain,
    ln_bias,
    w_qkv,
    qv_bias,
    w_out,
    out_bias,
    w_up,
    up_bias,
    w_down,
    cotangent,
):
    local_rows, slots, width = images.shape
    tokens = local_rows * slots
    half = w_qkv.shape[3]
    ff_half = w_up.shape[2]
    tile = 768
    steps = ff_half // tile
    heads = half // HEAD_DIM
    dp = lax.axis_size("dp")
    bits = dp.bit_length() - 1
    assert dp == 1 << bits and bits >= 4 and lax.axis_size("tensor") == 2
    tail = tuple(range(4, bits))
    order_a = (0, 1, 2, 3) + tail
    order_b = (1, 0, 2, 3) + tail
    order_c = (2, 3, 0, 1) + tail

    me = lax.axis_index("dp")
    counts = valid_count

    block = width // dp
    row = jnp.arange(width, dtype=jnp.int32)
    index = row // block
    mirrored = jnp.zeros_like(index)
    for bit in range(bits):
        mirrored = mirrored | (((index >> (bits - 1 - bit)) & 1) << bit)
    source = (mirrored ^ me) * block + row % block
    order = (source[:, None] == row[None, :]).astype(BF16)

    w_qkv = jnp.transpose(w_qkv, (0, 2, 1, 3))
    qkv = (w_qkv, swap(w_qkv))
    qv = (qv_bias, swap(qv_bias))

    images_2d = images.reshape(tokens, width)
    cotangent_2d = cotangent.reshape(tokens, width)
    smem = pl.BlockSpec(memory_space=pltpu.SMEM)
    wide = (tokens, width)
    flops_wide = 2 * width * width * tokens

    normed, normed_t, cotangent_t = call(
        prep_kernel,
        "prep",
        (),
        [images_2d, cotangent_2d, ln_gain, ln_bias, order],
        [whole()] * 5,
        [out(wide, BF16), out((width, tokens), BF16), out((width, tokens), BF16)],
        [whole()] * 3,
        flops=2 * flops_wide,
    )

    wout, wup, wdown = [
        (weight, swap(lax.optimization_barrier((weight, normed, qkv[1], qv[1]))[0]))
        for weight in (w_out, w_up, w_down)
    ]

    def attend(layer, side, normed, counts):
        lse_shape = (local_rows * heads, 1, slots)
        return call(
            functools.partial(attend_kernel, layer, slots),
            "attend",
            (3,),
            [counts, normed, in_hbm(qkv[side]), qv[side]],
            [
                smem,
                whole(),
                pl.BlockSpec((1, 1, width, half), lambda c: (layer, c, 0, 0)),
                whole(),
            ],
            [out((3, tokens, half), BF16), out((tokens, half), BF16), out(lse_shape, F32)],
            [whole()] * 3,
            flops=6 * tokens * width * half + 4 * tokens * slots * half,
            limit=48,
        )

    stream = images_2d
    saved = []
    got_cotangent_t = swap(cotangent_t)
    pooled = None
    for layer in range(LAYERS):
        last = layer == LAYERS - 1
        own = attend(layer, 0, normed, counts)
        if layer == 0:
            upb = (up_bias, swap(lax.optimization_barrier((up_bias, own[2]))[0]))
        if layer > 0:
            before = saved[layer - 1]
            names = ("got_normed_t", "got_att", "got_hid")
            far_counts, got_cotangent_t, *got = lax.optimization_barrier(
                (counts, got_cotangent_t, *[before[name] for name in names])
            )
            before.update(zip(names, got))
        else:
            far_counts = counts
        far = attend(layer, 1, normed, far_counts)
        gain_in = ln_gain
        if layer > 0:
            gain_in, before["got_mid_normed_t"] = lax.optimization_barrier(
                (ln_gain, before["got_mid_normed_t"])
            )
        ff = pltpu.HBM((tokens, ff_half), BF16)
        extra = (
            [out((local_rows, width), F32)]
            if last
            else [out(wide, BF16), out((width, tokens), BF16)]
        )
        results = call(
            functools.partial(feed_kernel, layer, slots, last),
            "feed",
            (),
            [
                counts,
                stream,
                own[1],
                far[1],
                in_hbm(wout[0]),
                in_hbm(wout[1]),
                out_bias,
                gain_in,
                ln_bias,
                order,
                in_hbm(wup[0]),
                in_hbm(wup[1]),
                upb[0],
                upb[1],
                in_hbm(wdown[0]),
                in_hbm(wdown[1]),
            ],
            [smem]
            + [whole()] * 3
            + [hbm()] * 2
            + [whole()] * 4
            + [hbm()] * 2
            + [whole()] * 2
            + [hbm()] * 2,
            [out(wide, F32), out((width, tokens), BF16), ff, ff, ff, ff, out(wide, F32)] + extra,
            [whole()] * 2 + [hbm()] * 4 + [whole()] * (1 + len(extra)),
            [
                pltpu.VMEM(wide, BF16),
                pltpu.VMEM(wide, F32),
                pltpu.VMEM((2, tokens, tile), F32),
                pltpu.VMEM((2 * half, width), BF16),
                pltpu.VMEM((2 * steps, width, tile), BF16),
                pltpu.VMEM((2 * steps, tile, width), BF16),
                pltpu.VMEM((2 * steps, tokens, tile), BF16),
                pltpu.VMEM((2 * steps, tokens, tile), BF16),
                pltpu.SemaphoreType.DMA((2 + 4 * steps,)),
                pltpu.SemaphoreType.DMA((4 * steps,)),
            ],
            flops=8 * tokens * width * ff_half + 2 * flops_wide,
            limit=32,
        )
        mid, mid_normed_t, hid_own, hid_far, slope_own, slope_far, stream_next = results[:7]
        saved.append(
            dict(
                stream=stream,
                own=own,
                far=far,
                mid=mid,
                slope=(slope_own, slope_far),
                hid=hid_own,
                attended=own[1],
                normed_t=normed_t,
                mid_normed_t=mid_normed_t,
                got_hid=swap(hid_far),
                got_att=swap(far[1]),
                got_normed_t=swap(normed_t),
                got_mid_normed_t=swap(mid_normed_t),
            )
        )
        stream = stream_next
        if last:
            pooled = results[7]
        else:
            normed, normed_t = results[7:9]

    def feed_back(layer, grad, gain_in):
        kept = saved[layer]
        up_spec = pl.BlockSpec((1, width, tile), lambda j: (layer, 0, j))
        down_spec = pl.BlockSpec((1, tile, width), lambda j: (layer, j, 0))
        tile_spec = pl.BlockSpec((tokens, tile), lambda j: (0, j))
        ff = out((tokens, ff_half), BF16)
        bias_shape = out((steps, tile), F32)
        att_shape = out((tokens, half), BF16)
        return call(
            functools.partial(feed_back_kernel, layer),
            "feed_back",
            (steps,),
            [
                grad,
                kept["mid"],
                gain_in,
                order,
                in_hbm(wdown[0]),
                in_hbm(wdown[1]),
                in_hbm(wup[0]),
                in_hbm(wup[1]),
                kept["slope"][0],
                kept["slope"][1],
                in_hbm(wout[0]),
                in_hbm(wout[1]),
            ],
            [
                *([whole()] * 4),
                down_spec,
                down_spec,
                up_spec,
                up_spec,
                tile_spec,
                tile_spec,
                fixed((1, half, width), layer),
                fixed((1, half, width), layer),
            ],
            [
                ff,
                ff,
                bias_shape,
                bias_shape,
                out(wide, F32),
                out((width, tokens), BF16),
                att_shape,
                att_shape,
                out((4, width), F32),
            ],
            [tile_spec, tile_spec, *([whole()] * 7)],
            [
                pltpu.VMEM(wide, BF16),
                pltpu.VMEM(wide, F32),
                pltpu.VMEM((tokens, tile), F32),
                pltpu.VMEM((4, 8, width), F32),
            ],
            flops=8 * tokens * width * ff_half + 2 * flops_wide,
        )

    def attend_back(forward, grad_att, counts_in):
        joint, _, lse = forward
        return call(
            functools.partial(attend_back_kernel, slots),
            "attend_back",
            (),
            [counts_in, joint, lse, grad_att],
            [smem, whole(), whole(), whole()],
            [out(joint.shape, BF16), out((1, 2 * half), F32)],
            [whole()] * 2,
            flops=10 * tokens * slots * half,
        )

    def entry_back(layer, joint_own, joint_far, grad_mid, gain_in):
        with_low = layer > 0
        return call(
            functools.partial(entry_back_kernel, layer, with_low),
            "entry_back",
            (3,),
            [
                joint_own,
                joint_far,
                in_hbm(qkv[0]),
                in_hbm(qkv[1]),
                saved[layer]["stream"],
                gain_in,
                grad_mid,
                order,
            ],
            [whole()] * 2
            + [pl.BlockSpec((1, 1, width, half), lambda c: (layer, c, 0, 0))] * 2
            + [whole()] * 4,
            [out(wide, F32), out((2, width), F32)]
            + ([out((width, tokens), BF16)] if with_low else []),
            [whole()] * (3 if with_low else 2),
            [pltpu.VMEM(wide, F32), pltpu.VMEM((2, 8, width), F32)]
            + ([pltpu.VMEM(wide, BF16)] if with_low else []),
            flops=12 * tokens * width * half,
        )

    def down_halves(layer, order_of, grad_t, got_grad_t):
        kept = saved[layer]
        return weight_grad(
            "down_grad", order_of, (grad_t, got_grad_t), (kept["hid"], kept["got_hid"])
        )

    def up_halves(layer, order_of, pre_own, got_pre, tiles=None, first=0):
        kept = saved[layer]
        return weight_grad(
            "up_grad",
            order_of,
            (kept["mid_normed_t"], kept["got_mid_normed_t"]),
            (pre_own, got_pre),
            tiles=tiles,
            first=first,
        )

    def lefts(layer):
        return saved[layer]["normed_t"], saved[layer]["got_normed_t"]

    def extras(layer, mid_t, got_mid_t):
        return mid_t, got_mid_t, saved[layer]["attended"], saved[layer]["got_att"]

    small = [None] * LAYERS
    down_1 = DpSum(order_a, down_halves(1, order_a, cotangent_t, got_cotangent_t))
    gain_in = gate(ln_gain, [down_1])
    pre_own, pre_far, upb_own, upb_far, grad_mid, mid_t, att_own, att_far, sums_mid = feed_back(
        1, cotangent_2d, gain_in
    )
    got_pre, got_mid_t = swap(pre_far), swap(mid_t)
    joint_far, qv_far = attend_back(saved[1]["far"], att_far, counts)
    got_joint = swap(joint_far)
    counts_in = gate(counts, [], [down_1], [qv_far])
    joint_own, qv_own = attend_back(saved[1]["own"], att_own, counts_in)
    pre_own = gate(pre_own, after=[qv_own])
    up_1 = DpSum(order_a, up_halves(1, order_a, pre_own, got_pre))
    gain_in = gate(gain_in, [up_1], [down_1])
    grad, sums_in, grad_t = entry_back(1, joint_own, joint_far, grad_mid, gain_in)
    got_grad_t = swap(grad_t)
    small[1] = (sums_mid, sums_in, qv_own, qv_far, upb_own, upb_far)
    joint_own = gate(joint_own, [], [down_1], [sums_in])
    rest_1 = DpSum(
        order_b[:2],
        weight_grad(
            "qkv_out_grad",
            order_b,
            lefts(1),
            (joint_own, got_joint),
            extras(1, mid_t, got_mid_t),
            tiles=3,
        ),
    )
    grad_t = gate(grad_t, [rest_1])
    down_0 = DpSum(order_a[:2], down_halves(0, order_a, grad_t, got_grad_t))

    gain_in = gate(gain_in, [down_0], [up_1, down_1])
    pre_own, pre_far, upb_own, upb_far, grad_mid, mid_t, att_own, att_far, sums_mid = feed_back(
        0, grad, gain_in
    )
    got_pre, got_mid_t = swap(pre_far), swap(mid_t)
    counts_in = gate(counts_in, [], [up_1, rest_1], [sums_mid])
    joint_far, qv_far = attend_back(saved[0]["far"], att_far, counts_in)
    got_joint = swap(joint_far)
    counts_in = gate(counts_in, [], [down_0, up_1], [qv_far])
    joint_own, qv_own = attend_back(saved[0]["own"], att_own, counts_in)
    pre_own = gate(pre_own, [], [rest_1, up_1], [qv_own])
    up_a = DpSum(order_a[:2], up_halves(0, order_a, pre_own, got_pre, tiles=1))
    up_b = DpSum(order_b[:2], up_halves(0, order_b, pre_own, got_pre, tiles=1, first=1))
    joint_low = gate(joint_own, [up_a, up_b])
    one = DpSum(
        order_a[:2],
        weight_grad("qk_grad", order_a, lefts(0), (joint_low, got_joint), tiles=2),
    )
    two = DpSum(
        order_b[:2],
        weight_grad(
            "v_out_grad",
            order_b,
            lefts(0),
            (joint_low, got_joint),
            extras(0, mid_t, got_mid_t),
            tiles=1,
            first=2,
        ),
    )
    gain_in = gate(gain_in, [one, two], [down_0])
    late = DpSum(order_a[2:], units=[down_0, rest_1])
    late.start()
    grad, sums_in = entry_back(0, joint_own, joint_far, grad_mid, gain_in)
    last = gate(sums_in, [], [up_a, up_b, late])
    last = gate(last, [], [one, two, late])
    small[0] = (sums_mid, last, qv_own, qv_far, upb_own, upb_far)
    ins = [array for arrays in small for array in arrays]
    vector_shape = out(((7 + steps) * LAYERS, width), F32)
    mine, far = call(
        functools.partial(pack_kernel, LAYERS),
        "pack_small",
        (),
        ins,
        [whole()] * len(ins),
        [vector_shape] * 2,
        [whole()] * 2,
    )
    vector = Everywhere(mine, far, bits)
    last = gate(last, [], [up_a, up_b, vector])
    up_0 = DpSum(order_a[2:], units=[up_a, up_b])
    up_0.start()
    last = gate(last, [], [one, two, vector])
    join_0 = DpSum(order_a[2:], units=[one, two])
    join_0.start()
    running = [down_1, up_1, late]
    while any(unit.incoming is not None for unit in running):
        last = gate(last, [], [unit for unit in running if unit.incoming is not None])
    while up_0.incoming is not None or join_0.incoming is not None:
        for unit in (up_0, join_0):
            if unit.incoming is not None:
                last = gate(last, [], [unit] + ([vector] if vector.bits else []))

    (down_1_sum,), (up_1_sum,) = down_1.results(), up_1.results()
    down_0_sum, both = late.results()
    one_sum, two_sum = join_0.results()
    summed = [
        (
            jnp.concatenate([one_sum, two_sum[:, :half]], axis=1).reshape(block, 3, half),
            two_sum[:, half:].T,
            jnp.concatenate(up_0.results(), axis=1),
            down_0_sum.T,
        ),
        (
            both[:, : 3 * half].reshape(block, 3, half),
            both[:, 3 * half :].T,
            up_1_sum,
            down_1_sum.T,
        ),
    ]

    while vector.bits:
        vector.turn()
    mine, got = vector.mine, vector.incoming
    gain_grads, shift_grads, outb_grads, qv_grads, upb_grads = call(
        functools.partial(unpack_kernel, LAYERS),
        "unpack_small",
        (),
        [mine, got],
        [whole()] * 2,
        [
            out(ln_gain.shape, F32),
            out(ln_bias.shape, F32),
            out(out_bias.shape, F32),
            out(qv_bias.shape, F32),
            out(up_bias.shape, F32),
        ],
        [whole()] * 5,
    )
    stacked = [jnp.stack([summed[layer][member] for layer in range(LAYERS)]) for member in range(4)]
    return (
        stream.reshape(images.shape),
        pooled,
        grad.reshape(images.shape),
        gain_grads,
        shift_grads,
        stacked[0],
        qv_grads,
        stacked[1],
        outb_grads,
        stacked[2],
        upb_grads,
        stacked[3],
    )


def solution(mesh):
    placed = (
        P(("dp", "tensor"), None, None),
        P("dp"),
        P(),
        P(),
        P(None, None, None, "tensor"),
        P(None, None, "tensor"),
        P(None, "tensor", None),
        P(),
        P(None, None, "tensor"),
        P(None, "tensor"),
        P(None, "tensor", None),
        P(("dp", "tensor"), None, None),
    )
    return jax.shard_map(
        shards,
        mesh=mesh,
        in_specs=placed,
        out_specs=(
            P(("dp", "tensor"), None, None),
            P(("dp", "tensor"), None),
            P(("dp", "tensor"), None, None),
            P(),
            P(),
            P(None, "dp", None, "tensor"),
            P(None, None, "tensor"),
            P(None, "tensor", "dp"),
            P(),
            P(None, "dp", "tensor"),
            P(None, "tensor"),
            P(None, "tensor", "dp"),
        ),
        check_vma=False,
    )
```

```python
import functools
import math

import jax
import jax.numpy as jnp
from jax import lax
from jax.experimental import pallas as pl
from jax.experimental.pallas import tpu as pltpu
from jax.sharding import PartitionSpec as P

HEAD_DIM = 64
LAYERS = 2
EPSILON = 1e-06
NEGATIVE = -1e30
BF16 = jnp.bfloat16
F32 = jnp.float32
CHUNK = 16


def dot(left, right):
    return lax.dot_general(left, right, (((1,), (0,)), ((), ())), preferred_element_type=F32)


def dot_nt(left, right):
    return lax.dot_general(left, right, (((1,), (1,)), ((), ())), preferred_element_type=F32)


def fixed(shape, *lead):
    where = tuple(lead) + (0,) * (len(shape) - len(lead))
    return pl.BlockSpec(shape, lambda *_: where)


def out(shape, dtype):
    return jax.ShapeDtypeStruct(shape, dtype)


def in_hbm(values):
    return pltpu.with_memory_space_constraint(values, pltpu.HBM)


def cost(flops, *arrays):
    total = sum(math.prod(a.shape) * a.dtype.itemsize for a in arrays)
    return pl.CostEstimate(flops=int(flops) // 64, bytes_accessed=int(total) // 64, transcendentals=0)


MIB = 1 << 20


def call(body, name, grid, ins, in_specs, outs, out_specs, scratch=(), flops=0, limit=24):
    return pl.pallas_call(
        body,
        name=name,
        grid=grid,
        in_specs=in_specs,
        out_specs=out_specs,
        out_shape=outs,
        scratch_shapes=list(scratch),
        compiler_params=pltpu.CompilerParams(vmem_limit_bytes=limit * MIB),
        cost_estimate=cost(flops, *ins, *outs),
    )(*ins)


def whole():
    return pl.BlockSpec(memory_space=pltpu.VMEM)


def hbm():
    return pl.BlockSpec(memory_space=pltpu.HBM)


def by_rows(rows, body, unroll=1):
    def step(index, carry):
        for part in range(unroll):
            body(pl.multiple_of((index * unroll + part) * CHUNK, CHUNK))
        return carry

    lax.fori_loop(0, rows // (CHUNK * unroll), step, 0)


def moments(values):
    average = jnp.mean(values, axis=-1, keepdims=True)
    centred = values - average
    variance = jnp.mean(centred * centred, axis=-1, keepdims=True)
    return centred, lax.rsqrt(variance + EPSILON)


def normalized(values, gain, bias):
    centred, scale = moments(values)
    return centred * scale * gain + bias


def norm_backward(values, grad_normed, gain):
    centred, scale = moments(values)
    unit = centred * scale
    grad_unit = grad_normed * gain
    first = jnp.mean(grad_unit, axis=-1, keepdims=True)
    second = jnp.mean(grad_unit * unit, axis=-1, keepdims=True)
    return scale * (grad_unit - first - unit * second), grad_normed * unit


def fold_rows(values):
    total = values[0:8]
    for start in range(8, values.shape[0], 8):
        total = total + values[start : start + 8]
    return total


def prep_kernel(images, cotangent, gain, bias, order, normed, normed_t, cotangent_t):
    def rows(start):
        here = pl.ds(start, CHUNK)
        values = images[here, :].astype(F32)
        normed[here, :] = normalized(values, gain[0, 0:1, :], bias[0, 0:1, :]).astype(BF16)

    by_rows(images.shape[0], rows, 4)
    normed_t[...] = dot_nt(order[...], normed[...]).astype(BF16)
    cotangent_t[...] = dot_nt(order[...], cotangent[...]).astype(BF16)


def head_masks(slots):
    lane = lax.broadcasted_iota(jnp.int32, (slots, 2 * HEAD_DIM), 1)
    return lane < HEAD_DIM, lane >= HEAD_DIM


def own_count(counts, image, images):
    return counts[lax.axis_index("tensor") * images + image]


def attend_kernel(
    layer,
    slots,
    counts,
    normed,
    weight_own,
    weight_far,
    bias_own,
    bias_far,
    joint_own,
    joint_far,
    att_own,
    att_far,
    lse_own,
    lse_far,
    held,
    sem,
):
    width = att_own.shape[1]
    pairs = width // (2 * HEAD_DIM)
    scale = HEAD_DIM ** (-0.5)
    weights = (weight_own, weight_far)
    for side in range(2):
        for member in range(3):
            fetch(weights[side].at[layer, member], held.at[side, member], sem.at[side, member])
    for side, (joint, bias) in enumerate(((joint_own, bias_own), (joint_far, bias_far))):

        def project(member, carry):
            pltpu.make_async_copy(
                weights[side].at[layer, member], held.at[side, member], sem.at[side, member]
            ).wait()
            shift = bias[layer, pl.ds(member // 2, 1), :]
            shift = jnp.where(member == 1, jnp.zeros_like(shift), shift)
            joint[member] = (dot(normed[...], held[side, member]) + shift).astype(BF16)
            return carry

        lax.fori_loop(0, 3, project, 0)
    masks = head_masks(slots)
    key_index = lax.broadcasted_iota(jnp.int32, (slots, slots), 0)

    def step(index, carry):
        image = index // pairs
        pair = index % pairs
        rows = pl.ds(pl.multiple_of(image * slots, slots), slots)
        lanes = pl.ds(pl.multiple_of(pair * 2 * HEAD_DIM, 2 * HEAD_DIM), 2 * HEAD_DIM)
        valid = key_index < own_count(counts, image, normed.shape[0] // slots)
        for joint, attended, lse in (
            (joint_own, att_own, lse_own),
            (joint_far, att_far, lse_far),
        ):
            queries = joint[0, rows, lanes]
            keys_in = joint[1, rows, lanes] * jnp.asarray(scale, BF16)
            values_t = joint[2, rows, lanes].T
            parts = []
            for side in range(2):
                keys_side = jnp.where(masks[side], keys_in, jnp.zeros_like(keys_in))
                scores = jnp.where(valid, dot_nt(keys_side, queries), NEGATIVE)
                largest = jnp.max(scores, axis=0, keepdims=True)
                exponent = jnp.exp(scores - largest)
                total = jnp.sum(exponent, axis=0, keepdims=True)
                probs = (exponent * (1.0 / total)).astype(BF16)
                parts.append(dot(values_t[side * HEAD_DIM : (side + 1) * HEAD_DIM], probs))
                lse[2 * index + side] = largest + jnp.log(total)
            attended[rows, lanes] = jnp.concatenate(parts, axis=0).T.astype(BF16)
        return carry

    lax.fori_loop(0, (normed.shape[0] // slots) * pairs, step, 0)


def fetch(source, target, sem):
    copy = pltpu.make_async_copy(source, target, sem)
    copy.start()
    return copy


def feed_kernel(
    layer,
    slots,
    last_layer,
    counts,
    stream,
    att_own,
    att_far,
    out_own,
    out_far,
    out_bias,
    gain,
    bias,
    order,
    up_own,
    up_far,
    up_bias_own,
    up_bias_far,
    down_own,
    down_far,
    mid,
    normed_t,
    hid_own,
    hid_far,
    slope_own,
    slope_far,
    stream_out,
    *rest,
):
    if last_layer:
        pooled = rest[0]
    else:
        next_normed, next_t = rest[:2]
    normed, total, pre, w_out, w_up, w_down, hid, slope, shift, in_sem, out_sem = rest[
        1 if last_layer else 2 :
    ]
    tokens = stream.shape[0]
    half = w_out.shape[0] // 2
    units = w_up.shape[0]
    tile = w_up.shape[2]
    tiles = units // 2
    out_in = [
        fetch(ref.at[layer], w_out.at[pl.ds(side * half, half)], in_sem.at[side])
        for side, ref in enumerate((out_own, out_far))
    ]
    up_in, down_in = [], []
    for unit in range(units):
        side, part = unit // tiles, unit % tiles
        columns = pl.ds(part * tile, tile)
        up_ref, down_ref = ((up_own, down_own), (up_far, down_far))[side]
        up_in.append(fetch(up_ref.at[layer, :, columns], w_up.at[unit], in_sem.at[2 + unit]))
        down_in.append(
            fetch(down_ref.at[layer, columns, :], w_down.at[unit], in_sem.at[2 + units + unit])
        )
        shift[unit : unit + 1, :] = (up_bias_own, up_bias_far)[side][
            layer : layer + 1, part * tile : (part + 1) * tile
        ]
    for copy in out_in:
        copy.wait()
    total[...] = dot(jnp.concatenate([att_own[...], att_far[...]], axis=1), w_out[...])

    def enter(start):
        here = pl.ds(start, CHUNK)
        value = stream[here, :].astype(F32) + (total[here, :] + out_bias[layer, 0:1, :])
        mid[here, :] = value
        normed[here, :] = normalized(value, gain[layer, 1:2, :], bias[layer, 1:2, :]).astype(BF16)

    by_rows(tokens, enter, 4)
    up_in[0].wait()
    pre[0] = dot(normed[...], w_up[0])
    normed_t[...] = dot_nt(order[...], normed[...]).astype(BF16)
    rows = 128
    total[...] = jnp.zeros_like(total)
    hid[units - 1] = jnp.zeros_like(hid[units - 1])
    hid_refs, slope_refs = (hid_own, hid_far), (slope_own, slope_far)

    def results(unit, side):
        columns = pl.ds(pl.multiple_of(unit % tiles * tile, tile), tile)
        return (
            pltpu.make_async_copy(hid.at[unit], hid_refs[side].at[:, columns], out_sem.at[unit]),
            pltpu.make_async_copy(
                slope.at[unit], slope_refs[side].at[:, columns], out_sem.at[units + unit]
            ),
        )

    def turn(unit, carry):
        after = jnp.minimum(unit + 1, units - 1)
        before = jnp.maximum(unit - 1, 0)

        @pl.when(unit + 1 < units)
        def _():
            pltpu.make_async_copy(
                up_own.at[layer, :, pl.ds(0, tile)], w_up.at[after], in_sem.at[2 + after]
            ).wait()

        @pl.when(unit != 1)
        def _():
            pltpu.make_async_copy(
                down_own.at[layer, pl.ds(0, tile), :],
                w_down.at[before],
                in_sem.at[2 + units + before],
            ).wait()

        row = shift[pl.ds(unit, 1), :]
        idle = (unit + units - 1) % units

        def chunk(index, carry):
            block = pl.ds(pl.multiple_of(index * rows, rows), rows)
            pre[(unit + 1) % 2, block, :] = dot(normed[block, :], w_up[after])
            total[block, :] += dot(hid[idle, block, :], w_down[before])
            for sub in range(0, rows, CHUNK):
                here = pl.ds(pl.multiple_of(index * rows + sub, CHUNK), CHUNK)
                value = pre[unit % 2, here, :] + row
                cdf = 0.5 + 0.5 * lax.erf(value * (0.5**0.5))
                hid[unit, here, :] = (value * cdf).astype(BF16)
                density = jnp.exp(-0.5 * value * value) * ((2.0 * math.pi) ** -0.5)
                slope[unit, here, :] = (cdf + value * density).astype(BF16)
            return carry

        lax.fori_loop(0, tokens // rows, chunk, 0)
        for side in range(2):

            @pl.when(unit // tiles == side)
            def _():
                for copy in results(unit, side):
                    copy.start()

        return carry

    lax.fori_loop(0, units, turn, 0)
    down_in[units - 1].wait()
    total[...] += dot(hid[units - 1], w_down[units - 1])

    def leave(start):
        here = pl.ds(start, CHUNK)
        value = mid[here, :] + (total[here, :] + out_bias[layer, 1:2, :])
        stream_out[here, :] = value
        if not last_layer:
            next_normed[here, :] = normalized(
                value, gain[layer + 1, 0:1, :], bias[layer + 1, 0:1, :]
            ).astype(BF16)

    by_rows(tokens, leave, 4)
    if last_layer:
        index = lax.broadcasted_iota(jnp.int32, (slots, 1), 0)
        for image in range(tokens // slots):
            block = stream_out[image * slots : (image + 1) * slots, :]
            count = own_count(counts, image, tokens // slots)
            summed = jnp.sum(jnp.where(index < count, block, 0.0), axis=0, keepdims=True)
            pooled[image : image + 1, :] = summed / count.astype(F32)
    else:
        next_t[...] = dot_nt(order[...], next_normed[...]).astype(BF16)
    for unit in range(units):
        for copy in results(unit, unit // tiles):
            copy.wait()


def feed_back_kernel(
    layer,
    grad_in,
    mid,
    gain,
    order,
    down_own,
    down_far,
    up_own,
    up_far,
    slope_own,
    slope_far,
    out_own,
    out_far,
    pre_own,
    pre_far,
    bias_own,
    bias_far,
    grad_mid,
    mid_t,
    att_own,
    att_far,
    sums,
    low,
    total,
    hidden,
    partial,
    w_down,
    w_up,
    slope,
    pre,
    w_out,
    in_sem,
    out_sem,
):
    tokens = grad_in.shape[0]
    units = w_up.shape[0]
    tile = w_up.shape[2]
    tiles = units // 2
    down_in, up_in, slope_in = [], [], []
    for unit in range(units):
        columns = pl.ds(unit % tiles * tile, tile)
        down_ref, up_ref, slope_ref = ((down_far, up_far, slope_far), (down_own, up_own, slope_own))[
            unit // tiles
        ]
        down_in.append(fetch(down_ref.at[layer, columns, :], w_down.at[unit], in_sem.at[0, unit]))
        slope_in.append(fetch(slope_ref.at[:, columns], slope.at[unit], in_sem.at[1, unit]))
        up_in.append(fetch(up_ref.at[layer, :, columns], w_up.at[unit], in_sem.at[2, unit]))
    out_in = [
        fetch(ref.at[layer], w_out.at[side], in_sem.at[3, side])
        for side, ref in enumerate((out_far, out_own))
    ]
    partial[...] = jnp.zeros_like(partial)

    def enter(start):
        here = pl.ds(start, CHUNK)
        value = grad_in[here, :].astype(F32)
        low[here, :] = value.astype(BF16)
        partial[0] += fold_rows(value)

    by_rows(tokens, enter)
    down_in[0].wait()
    hidden[0] = dot_nt(low[...], w_down[0])
    rows = 256
    total[...] = jnp.zeros_like(total)
    pre[units - 1] = jnp.zeros_like(pre[units - 1])
    pre_refs = (pre_far, pre_own)

    def result(unit, side):
        columns = pl.ds(pl.multiple_of(unit % tiles * tile, tile), tile)
        return pltpu.make_async_copy(pre.at[unit], pre_refs[side].at[:, columns], out_sem.at[unit])

    def turn(unit, carry):
        after = jnp.minimum(unit + 1, units - 1)
        before = jnp.maximum(unit - 1, 0)

        @pl.when(unit + 1 < units)
        def _():
            pltpu.make_async_copy(
                down_own.at[layer, pl.ds(0, tile), :], w_down.at[after], in_sem.at[0, after]
            ).wait()

        @pl.when(unit != 1)
        def _():
            pltpu.make_async_copy(
                up_own.at[layer, :, pl.ds(0, tile)], w_up.at[before], in_sem.at[2, before]
            ).wait()

        pltpu.make_async_copy(
            slope_own.at[:, pl.ds(0, tile)], slope.at[unit], in_sem.at[1, unit]
        ).wait()
        idle = (unit + units - 1) % units

        def chunk(index, carry):
            block = pl.ds(pl.multiple_of(index * rows, rows), rows)
            hidden[(unit + 1) % 2, block, :] = dot_nt(low[block, :], w_down[after])
            total[block, :] += dot_nt(pre[idle, block, :], w_up[before])
            for sub in range(0, rows, CHUNK):
                here = pl.ds(pl.multiple_of(index * rows + sub, CHUNK), CHUNK)
                value = hidden[unit % 2, here, :] * slope[unit, here, :].astype(F32)
                pre[unit, here, :] = value.astype(BF16)
                carry = carry + fold_rows(value)
            return carry

        summed = lax.fori_loop(0, tokens // rows, chunk, jnp.zeros((8, tile), F32))
        row = jnp.sum(summed, axis=0, keepdims=True)
        for side, bias in enumerate((bias_far, bias_own)):

            @pl.when(unit // tiles == side)
            def _():
                bias[pl.ds(unit % tiles, 1), :] = row
                result(unit, side).start()

        return carry

    lax.fori_loop(0, units, turn, 0)
    up_in[units - 1].wait()
    total[...] += dot_nt(pre[units - 1], w_up[units - 1])

    def leave(start):
        here = pl.ds(start, CHUNK)
        normed_grad = total[here, :]
        through, gain_term = norm_backward(mid[here, :], normed_grad, gain[layer, 1:2, :])
        value = grad_in[here, :].astype(F32) + through
        grad_mid[here, :] = value
        low[here, :] = value.astype(BF16)
        partial[1] += fold_rows(value)
        partial[2] += fold_rows(gain_term)
        partial[3] += fold_rows(normed_grad)

    by_rows(tokens, leave, 2)
    sums[...] = jnp.sum(partial[...], axis=1)
    mid_t[...] = dot_nt(order[...], low[...]).astype(BF16)
    for copy in out_in:
        copy.wait()
    att_far[...] = dot_nt(low[...], w_out[0]).astype(BF16)
    att_own[...] = dot_nt(low[...], w_out[1]).astype(BF16)
    for unit in range(units):
        result(unit, unit // tiles).wait()


def attend_back_kernel(slots, counts, joint, lse, grad_att, grad_joint, bias_sums):
    width = grad_att.shape[1]
    pairs = width // (2 * HEAD_DIM)
    scale = HEAD_DIM ** (-0.5)
    masks = head_masks(slots)
    key_index = lax.broadcasted_iota(jnp.int32, (slots, slots), 0)
    bias_sums[...] = jnp.zeros_like(bias_sums)

    def step(index, carry):
        image = index // pairs
        pair = index % pairs
        rows = pl.ds(pl.multiple_of(image * slots, slots), slots)
        lanes = pl.ds(pl.multiple_of(pair * 2 * HEAD_DIM, 2 * HEAD_DIM), 2 * HEAD_DIM)
        queries = joint[0, rows, lanes]
        keys_in = joint[1, rows, lanes]
        values_in = joint[2, rows, lanes]
        grads = grad_att[rows, lanes]
        keys_t = keys_in.T
        keys_scaled = keys_in * jnp.asarray(scale, BF16)
        valid = key_index < own_count(counts, image, grad_att.shape[0] // slots)
        zeros = jnp.zeros_like(keys_in)
        query_parts, key_parts, value_parts = [], [], []
        for side in range(2):
            keys_side = jnp.where(masks[side], keys_scaled, zeros)
            values_side = jnp.where(masks[side], values_in, zeros)
            scores = jnp.where(valid, dot_nt(keys_side, queries), NEGATIVE)
            probs = jnp.exp(scores - lse[2 * index + side])
            grad_probs = dot_nt(values_side, grads)
            inner = jnp.sum(grad_probs * probs, axis=0, keepdims=True)
            grad_scores = (probs * (grad_probs - inner)).astype(BF16)
            value_parts.append(dot(probs.astype(BF16), grads))
            key_parts.append(dot(grad_scores, queries))
            query_parts.append(dot(keys_t[side * HEAD_DIM : (side + 1) * HEAD_DIM], grad_scores))
        grad_queries = jnp.concatenate(query_parts, axis=0).T * scale
        grad_keys = jnp.where(masks[0], key_parts[0], key_parts[1]) * scale
        grad_values = jnp.where(masks[0], value_parts[0], value_parts[1])
        bias_sums[0:1, lanes] += jnp.sum(grad_queries, axis=0, keepdims=True)
        value_lanes = pl.ds(
            pl.multiple_of(width + pair * 2 * HEAD_DIM, 2 * HEAD_DIM), 2 * HEAD_DIM
        )
        bias_sums[0:1, value_lanes] += jnp.sum(grad_values, axis=0, keepdims=True)
        grad_joint[0, rows, lanes] = grad_queries.astype(BF16)
        grad_joint[1, rows, lanes] = grad_keys.astype(BF16)
        grad_joint[2, rows, lanes] = grad_values.astype(BF16)
        return carry

    lax.fori_loop(0, (grad_att.shape[0] // slots) * pairs, step, 0)


def entry_back_kernel(
    layer, with_low, joint_own, joint_far, weight_own, weight_far, stream, gain, grad_mid, order, *rest
):
    if with_low:
        grad_out, sums, low_t, total, partial, low = rest
    else:
        grad_out, sums, total, partial = rest
    member = pl.program_id(0)

    @pl.when(member == 0)
    def _():
        total[...] = jnp.zeros_like(total)
        partial[...] = jnp.zeros_like(partial)

    left = jnp.concatenate([joint_own[member], joint_far[member]], axis=1)
    right = jnp.concatenate([weight_own[0, 0], weight_far[0, 0]], axis=1)
    total[...] += dot_nt(left, right)

    def rows(start):
        here = pl.ds(start, CHUNK)
        normed_grad = total[here, :]
        through, gain_term = norm_backward(
            stream[here, :].astype(F32), normed_grad, gain[layer, 0:1, :]
        )
        value = grad_mid[here, :] + through
        grad_out[here, :] = value
        if with_low:
            low[here, :] = value.astype(BF16)
        partial[0] += fold_rows(gain_term)
        partial[1] += fold_rows(normed_grad)

    @pl.when(member == 2)
    def _():
        by_rows(stream.shape[0], rows, 2)
        sums[...] = jnp.sum(partial[...], axis=1)
        if with_low:
            low_t[...] = dot_nt(order[...], low[...]).astype(BF16)


def pack_kernel(layers, *refs):
    ins, (own_out, far_out) = refs[:-2], refs[-2:]
    for layer in range(layers):
        sums_mid, sums_in, qv_own, qv_far, upb_own, upb_far = ins[6 * layer : 6 * layer + 6]
        tiles = upb_own.shape[0]
        for ref, qv, upb in ((own_out, qv_own, upb_own), (far_out, qv_far, upb_far)):
            for row, value in (
                (2 * layer, sums_in[0:1, :]),
                (2 * layer + 1, sums_mid[2:3, :]),
                (2 * (layers + layer), sums_in[1:2, :]),
                (2 * (layers + layer) + 1, sums_mid[3:4, :]),
                (2 * (2 * layers + layer), sums_mid[1:2, :]),
                (2 * (2 * layers + layer) + 1, sums_mid[0:1, :]),
                (6 * layers + layer, qv[...]),
            ):
                ref[row : row + 1, :] = value
            start = 7 * layers + tiles * layer
            ref[start : start + tiles, :] = upb[...]


def unpack_kernel(layers, mine, got, gain, bias, out_bias, qv, upb):
    total = mine[...] + got[...]
    half = qv.shape[2]
    tiles = upb.shape[1] // mine.shape[1]
    width = mine.shape[1]
    for layer in range(layers):
        for norm in range(2):
            row = 2 * layer + norm
            gain[layer, norm : norm + 1, :] = total[row : row + 1]
            row += 2 * layers
            bias[layer, norm : norm + 1, :] = total[row : row + 1]
            row += 2 * layers
            out_bias[layer, norm : norm + 1, :] = total[row : row + 1]
        row = 6 * layers + layer
        for kind in range(2):
            qv[layer, kind : kind + 1, :] = total[row : row + 1, kind * half : (kind + 1) * half]
        row = 7 * layers + tiles * layer
        for part in range(tiles):
            upb[layer : layer + 1, part * width : (part + 1) * width] = total[
                row + part : row + part + 1
            ]


def chunk_sources(order):
    first = list(order[:4])
    sources = []
    for target in range(16):
        source = 0
        for place, bit in enumerate(first):
            if (target >> (3 - place)) & 1:
                source |= 1 << (3 - bit)
        sources.append(source)
    return sources


def weight_kernel(sources, tiles, has_extra, *refs):
    if has_extra:
        left_own, left_far, right_own, right_far, lx_own, lx_far, rx_own, rx_far, keep, send = refs
    else:
        left_own, left_far, right_own, right_far, keep, send = refs

    def product(a_own, a_far, b_own, b_far):
        left = jnp.concatenate([a_own[...], a_far[...]], axis=1)
        right = jnp.concatenate([b_own[...].reshape(b_own.shape[-2:]), b_far[...].reshape(b_far.shape[-2:])], axis=0)
        size = left.shape[0] // 16
        low = dot(left, right).astype(BF16)
        for target, source in enumerate(sources):
            ref = keep if target < 8 else send
            ref[(target % 8) * size : (target % 8 + 1) * size, :] = low[
                source * size : (source + 1) * size, :
            ]

    if has_extra:

        @pl.when(pl.program_id(0) < tiles)
        def _():
            product(left_own, left_far, right_own, right_far)

        @pl.when(pl.program_id(0) == tiles)
        def _():
            product(lx_own, lx_far, rx_own, rx_far)

    else:
        product(left_own, left_far, right_own, right_far)


def weight_grad(name, order, left, right, extra=None, tiles=None, first=0):
    left_own, left_far = left
    right_own, right_far = right
    width, tokens = left_own.shape
    if right_own.ndim == 3:
        tile = right_own.shape[2]
        right_spec = pl.BlockSpec(
            (1, tokens, tile), lambda j: (jnp.minimum(j, tiles - 1) + first, 0, 0)
        )
    else:
        tile = 768 if tiles else 384
        tiles = tiles or right_own.shape[1] // tile
        right_spec = pl.BlockSpec((tokens, tile), lambda j: (0, j + first))
    steps = tiles + (1 if extra is not None else 0)
    ins = [left_own, left_far, right_own, right_far]
    specs = [fixed((width, tokens))] * 2 + [right_spec] * 2
    if extra is not None:
        ins += list(extra)
        specs += [fixed((width, tokens))] * 2 + [fixed((tokens, tile))] * 2
    half = out((width // 2, steps * tile), BF16)
    half_spec = pl.BlockSpec((width // 2, tile), lambda j: (0, j))
    return call(
        functools.partial(weight_kernel, chunk_sources(order), tiles, extra is not None),
        name,
        (steps,),
        ins,
        specs,
        [half, half],
        [half_spec, half_spec],
        flops=4 * width * tokens * steps * tile,
    )


def flip(bit):
    size = lax.axis_size("dp")
    return [(index, index ^ (1 << bit)) for index in range(size)]


class DpSum:
    def __init__(self, order, halves=None, units=()):
        self.order = list(order)
        self.incoming = None
        if halves is not None:
            keep, self.outgoing = halves
            self.members = [[keep]]
        else:
            self.members = [parts for unit in units for parts in unit.members]
            self.halve()

    def halve(self):
        rows = self.members[0][0].shape[0] // 2
        sends = [
            sum(part[rows:].astype(F32) for part in parts).astype(BF16) for parts in self.members
        ]
        self.outgoing = sends[0] if len(sends) == 1 else jnp.concatenate(sends, axis=1)
        self.members = [[part[:rows] for part in parts] for parts in self.members]

    def start(self):
        self.incoming = lax.ppermute(self.outgoing, "dp", flip(self.order.pop(0)))

    def turn(self):
        column = 0
        for parts in self.members:
            width = parts[0].shape[1]
            parts.append(self.incoming[:, column : column + width])
            column += width
        self.incoming = None
        if self.order:
            self.halve()
            self.start()

    def results(self):
        return [sum(part.astype(F32) for part in parts) for parts in self.members]


class Everywhere:
    def __init__(self, mine, far, bits):
        self.mine = mine
        self.incoming = swap(far)
        self.bits = list(range(bits))

    def turn(self):
        self.mine = self.mine + self.incoming
        self.incoming = lax.ppermute(self.mine, "dp", flip(self.bits.pop(0)))


def gate(value, starts=(), turns=(), after=()):
    held = [unit.outgoing for unit in starts] + [unit.incoming for unit in turns]
    value, *held = lax.optimization_barrier((value, *held, *after))
    for unit, array in zip(starts, held):
        unit.outgoing = array
        unit.start()
    for unit, array in zip(turns, held[len(starts) :]):
        unit.incoming = array
        unit.turn()
    return value


def swap(values):
    return lax.ppermute(values, "tensor", [(0, 1), (1, 0)])


def shards(
    images,
    valid_count,
    ln_gain,
    ln_bias,
    w_qkv,
    qv_bias,
    w_out,
    out_bias,
    w_up,
    up_bias,
    w_down,
    cotangent,
):
    local_rows, slots, width = images.shape
    tokens = local_rows * slots
    half = w_qkv.shape[3]
    ff_half = w_up.shape[2]
    tile = 768
    steps = ff_half // tile
    heads = half // HEAD_DIM
    dp = lax.axis_size("dp")
    bits = dp.bit_length() - 1
    assert dp == 1 << bits and bits >= 4 and lax.axis_size("tensor") == 2
    tail = tuple(range(4, bits))
    order_a = (0, 1, 2, 3) + tail
    order_b = (1, 0, 2, 3) + tail
    order_c = (2, 3, 0, 1) + tail
    order_d = (0, 2, 3, 1) + tail

    me = lax.axis_index("dp")
    counts = valid_count

    block = width // dp
    row = jnp.arange(width, dtype=jnp.int32)
    index = row // block
    mirrored = jnp.zeros_like(index)
    for bit in range(bits):
        mirrored = mirrored | (((index >> (bits - 1 - bit)) & 1) << bit)
    source = (mirrored ^ me) * block + row % block
    order = (source[:, None] == row[None, :]).astype(BF16)

    w_qkv = jnp.transpose(w_qkv, (0, 2, 1, 3))
    qkv = (w_qkv, swap(w_qkv))
    qv = (qv_bias, swap(qv_bias))

    images_2d = images.reshape(tokens, width)
    cotangent_2d = cotangent.reshape(tokens, width)
    smem = pl.BlockSpec(memory_space=pltpu.SMEM)
    wide = (tokens, width)
    flops_wide = 2 * width * width * tokens

    normed, normed_t, cotangent_t = call(
        prep_kernel,
        "prep",
        (),
        [images_2d, cotangent_2d, ln_gain, ln_bias, order],
        [whole()] * 5,
        [out(wide, BF16), out((width, tokens), BF16), out((width, tokens), BF16)],
        [whole()] * 3,
        flops=2 * flops_wide,
    )

    wout, wup, wdown = [
        (weight, swap(lax.optimization_barrier((weight, normed, qkv[1], qv[1]))[0]))
        for weight in (w_out, w_up, w_down)
    ]

    def attend(layer, normed, counts):
        lse_shape = (local_rows * heads, 1, slots)
        joint_out = out((3, tokens, half), BF16)
        att_out = out((tokens, half), BF16)
        lse_out = out(lse_shape, F32)
        results = call(
            functools.partial(attend_kernel, layer, slots),
            "attend",
            (),
            [counts, normed, in_hbm(qkv[0]), in_hbm(qkv[1]), qv[0], qv[1]],
            [smem, whole(), hbm(), hbm(), whole(), whole()],
            [joint_out, joint_out, att_out, att_out, lse_out, lse_out],
            [whole()] * 6,
            [pltpu.VMEM((2, 3, width, half), BF16), pltpu.SemaphoreType.DMA((2, 3))],
            flops=12 * tokens * width * half + 8 * tokens * slots * half,
            limit=44,
        )
        return results[0::2], results[1::2]

    stream = images_2d
    saved = []
    got_cotangent_t = swap(cotangent_t)
    pooled = None
    for layer in range(LAYERS):
        last = layer == LAYERS - 1
        own, far = attend(layer, normed, counts)
        if layer == 0:
            upb = (up_bias, swap(up_bias))
        gain_in = ln_gain
        if layer > 0:
            before = saved[layer - 1]
            names = ("got_normed_t", "got_att", "got_mid_normed_t", "got_hid")
            gain_in, got_cotangent_t, *got = lax.optimization_barrier(
                (ln_gain, got_cotangent_t, *[before[name] for name in names])
            )
            before.update(zip(names, got))
        ff = pltpu.HBM((tokens, ff_half), BF16)
        extra = (
            [out((local_rows, width), F32)]
            if last
            else [out(wide, BF16), out((width, tokens), BF16)]
        )
        results = call(
            functools.partial(feed_kernel, layer, slots, last),
            "feed",
            (),
            [
                counts,
                stream,
                own[1],
                far[1],
                in_hbm(wout[0]),
                in_hbm(wout[1]),
                out_bias,
                gain_in,
                ln_bias,
                order,
                in_hbm(wup[0]),
                in_hbm(wup[1]),
                upb[0],
                upb[1],
                in_hbm(wdown[0]),
                in_hbm(wdown[1]),
            ],
            [smem]
            + [whole()] * 3
            + [hbm()] * 2
            + [whole()] * 4
            + [hbm()] * 2
            + [whole()] * 2
            + [hbm()] * 2,
            [out(wide, F32), out((width, tokens), BF16), ff, ff, ff, ff, out(wide, F32)] + extra,
            [whole()] * 2 + [hbm()] * 4 + [whole()] * (1 + len(extra)),
            [
                pltpu.VMEM(wide, BF16),
                pltpu.VMEM(wide, F32),
                pltpu.VMEM((2, tokens, tile), F32),
                pltpu.VMEM((2 * half, width), BF16),
                pltpu.VMEM((2 * steps, width, tile), BF16),
                pltpu.VMEM((2 * steps, tile, width), BF16),
                pltpu.VMEM((2 * steps, tokens, tile), BF16),
                pltpu.VMEM((2 * steps, tokens, tile), BF16),
                pltpu.VMEM((2 * steps, tile), F32),
                pltpu.SemaphoreType.DMA((2 + 4 * steps,)),
                pltpu.SemaphoreType.DMA((4 * steps,)),
            ],
            flops=8 * tokens * width * ff_half + 2 * flops_wide,
            limit=32,
        )
        mid, mid_normed_t, hid_own, hid_far, slope_own, slope_far, stream_next = results[:7]
        saved.append(
            dict(
                stream=stream,
                own=own,
                far=far,
                mid=mid,
                slope=(slope_own, slope_far),
                hid=hid_own,
                attended=own[1],
                normed_t=normed_t,
                mid_normed_t=mid_normed_t,
                got_hid=swap(hid_far),
                got_att=swap(far[1]),
                got_normed_t=swap(normed_t),
                got_mid_normed_t=swap(mid_normed_t),
            )
        )
        stream = stream_next
        if last:
            pooled = results[7]
        else:
            normed, normed_t = results[7:9]

    def feed_back(layer, grad, gain_in):
        kept = saved[layer]
        ff = pltpu.HBM((tokens, ff_half), BF16)
        bias_shape = out((steps, tile), F32)
        att_shape = out((tokens, half), BF16)
        return call(
            functools.partial(feed_back_kernel, layer),
            "feed_back",
            (),
            [
                grad,
                kept["mid"],
                gain_in,
                order,
                in_hbm(wdown[0]),
                in_hbm(wdown[1]),
                in_hbm(wup[0]),
                in_hbm(wup[1]),
                kept["slope"][0],
                kept["slope"][1],
                in_hbm(wout[0]),
                in_hbm(wout[1]),
            ],
            [whole()] * 4 + [hbm()] * 8,
            [
                ff,
                ff,
                bias_shape,
                bias_shape,
                out(wide, F32),
                out((width, tokens), BF16),
                att_shape,
                att_shape,
                out((4, width), F32),
            ],
            [hbm()] * 2 + [whole()] * 7,
            [
                pltpu.VMEM(wide, BF16),
                pltpu.VMEM(wide, F32),
                pltpu.VMEM((2, tokens, tile), F32),
                pltpu.VMEM((4, 8, width), F32),
                pltpu.VMEM((2 * steps, tile, width), BF16),
                pltpu.VMEM((2 * steps, width, tile), BF16),
                pltpu.VMEM((2 * steps, tokens, tile), BF16),
                pltpu.VMEM((2 * steps, tokens, tile), BF16),
                pltpu.VMEM((2, half, width), BF16),
                pltpu.SemaphoreType.DMA((4, 2 * steps)),
                pltpu.SemaphoreType.DMA((2 * steps,)),
            ],
            flops=8 * tokens * width * ff_half + 2 * flops_wide,
            limit=32,
        )

    def attend_back(forward, grad_att, counts_in):
        joint, _, lse = forward
        return call(
            functools.partial(attend_back_kernel, slots),
            "attend_back",
            (),
            [counts_in, joint, lse, grad_att],
            [smem, whole(), whole(), whole()],
            [out(joint.shape, BF16), out((1, 2 * half), F32)],
            [whole()] * 2,
            flops=10 * tokens * slots * half,
        )

    def entry_back(layer, joint_own, joint_far, grad_mid, gain_in):
        with_low = layer > 0
        return call(
            functools.partial(entry_back_kernel, layer, with_low),
            "entry_back",
            (3,),
            [
                joint_own,
                joint_far,
                in_hbm(qkv[0]),
                in_hbm(qkv[1]),
                saved[layer]["stream"],
                gain_in,
                grad_mid,
                order,
            ],
            [whole()] * 2
            + [pl.BlockSpec((1, 1, width, half), lambda c: (layer, c, 0, 0))] * 2
            + [whole()] * 4,
            [out(wide, F32), out((2, width), F32)]
            + ([out((width, tokens), BF16)] if with_low else []),
            [whole()] * (3 if with_low else 2),
            [pltpu.VMEM(wide, F32), pltpu.VMEM((2, 8, width), F32)]
            + ([pltpu.VMEM(wide, BF16)] if with_low else []),
            flops=12 * tokens * width * half,
        )

    def down_halves(layer, order_of, grad_t, got_grad_t):
        kept = saved[layer]
        return weight_grad(
            "down_grad", order_of, (grad_t, got_grad_t), (kept["hid"], kept["got_hid"])
        )

    def up_halves(layer, order_of, pre_own, got_pre, tiles=None, first=0):
        kept = saved[layer]
        return weight_grad(
            "up_grad",
            order_of,
            (kept["mid_normed_t"], kept["got_mid_normed_t"]),
            (pre_own, got_pre),
            tiles=tiles,
            first=first,
        )

    def lefts(layer):
        return saved[layer]["normed_t"], saved[layer]["got_normed_t"]

    def extras(layer, mid_t, got_mid_t):
        return mid_t, got_mid_t, saved[layer]["attended"], saved[layer]["got_att"]

    small = [None] * LAYERS
    down_1 = DpSum(order_a, down_halves(1, order_a, cotangent_t, got_cotangent_t))
    gain_in = gate(ln_gain, [down_1])
    pre_own, pre_far, upb_own, upb_far, grad_mid, mid_t, att_own, att_far, sums_mid = feed_back(
        1, cotangent_2d, gain_in
    )
    got_pre, got_mid_t = swap(pre_far), swap(mid_t)
    joint_far, qv_far = attend_back(saved[1]["far"], att_far, counts)
    got_joint = swap(joint_far)
    counts_in = gate(counts, [], [down_1], [qv_far])
    joint_own, qv_own = attend_back(saved[1]["own"], att_own, counts_in)
    pre_own = gate(pre_own, after=[qv_own])
    up_1 = DpSum(order_a, up_halves(1, order_a, pre_own, got_pre))
    gain_in = gate(gain_in, [up_1], [down_1])
    grad, sums_in, grad_t = entry_back(1, joint_own, joint_far, grad_mid, gain_in)
    got_grad_t = swap(grad_t)
    small[1] = (sums_mid, sums_in, qv_own, qv_far, upb_own, upb_far)
    joint_own = gate(joint_own, [], [down_1], [sums_in])
    rest_1 = DpSum(
        order_c,
        weight_grad(
            "qkv_out_grad",
            order_c,
            lefts(1),
            (joint_own, got_joint),
            extras(1, mid_t, got_mid_t),
            tiles=3,
        ),
    )
    grad_t = gate(grad_t, [rest_1])
    down_0 = DpSum(order_a, down_halves(0, order_a, grad_t, got_grad_t))

    gain_in = gate(gain_in, [down_0], [up_1, down_1])
    pre_own, pre_far, upb_own, upb_far, grad_mid, mid_t, att_own, att_far, sums_mid = feed_back(
        0, grad, gain_in
    )
    got_pre, got_mid_t = swap(pre_far), swap(mid_t)
    counts_in = gate(counts_in, [], [up_1, rest_1], [sums_mid])
    joint_far, qv_far = attend_back(saved[0]["far"], att_far, counts_in)
    got_joint = swap(joint_far)
    pre_own = gate(pre_own, [], [down_0, up_1], [qv_far])
    up_0 = DpSum(order_d, up_halves(0, order_d, pre_own, got_pre))
    counts_in = gate(counts_in, [up_0], [], [got_mid_t, got_joint])
    joint_own, qv_own = attend_back(saved[0]["own"], att_own, counts_in)
    rest_0 = DpSum(
        order_b,
        weight_grad(
            "qkv_out_grad",
            order_b,
            lefts(0),
            (joint_own, got_joint),
            extras(0, mid_t, got_mid_t),
            tiles=3,
        ),
    )
    gain_in = gate(gain_in, [rest_0], [down_0, up_1], [qv_own])
    grad, sums_in = entry_back(0, joint_own, joint_far, grad_mid, gain_in)
    small[0] = (sums_mid, sums_in, qv_own, qv_far, upb_own, upb_far)
    ins = [array for arrays in small for array in arrays]
    vector_shape = out(((7 + steps) * LAYERS, width), F32)
    mine, far = call(
        functools.partial(pack_kernel, LAYERS),
        "pack_small",
        (),
        ins,
        [whole()] * len(ins),
        [vector_shape] * 2,
        [whole()] * 2,
    )
    vector = Everywhere(mine, far, bits)
    last = gate(sums_in, [], [up_0, down_0, rest_1, vector])
    last = gate(last, [], [rest_0, up_0, down_0, rest_1, vector])
    last = gate(last, [], [rest_0, up_0, rest_1, vector])
    last = gate(last, [], [rest_0, up_0, vector])
    running = [down_1, up_1, rest_1, down_0, up_0, rest_0]
    while any(unit.incoming is not None for unit in running):
        last = gate(last, [], [unit for unit in running if unit.incoming is not None][:4])

    (down_1_sum,), (up_1_sum,) = down_1.results(), up_1.results()
    (down_0_sum,), (up_0_sum,) = down_0.results(), up_0.results()
    (both,), (first_both,) = rest_1.results(), rest_0.results()
    summed = [
        (
            first_both[:, : 3 * half].reshape(block, 3, half),
            first_both[:, 3 * half :].T,
            up_0_sum,
            down_0_sum.T,
        ),
        (
            both[:, : 3 * half].reshape(block, 3, half),
            both[:, 3 * half :].T,
            up_1_sum,
            down_1_sum.T,
        ),
    ]

    while vector.bits:
        vector.turn()
    mine, got = vector.mine, vector.incoming
    gain_grads, shift_grads, outb_grads, qv_grads, upb_grads = call(
        functools.partial(unpack_kernel, LAYERS),
        "unpack_small",
        (),
        [mine, got],
        [whole()] * 2,
        [
            out(ln_gain.shape, F32),
            out(ln_bias.shape, F32),
            out(out_bias.shape, F32),
            out(qv_bias.shape, F32),
            out(up_bias.shape, F32),
        ],
        [whole()] * 5,
    )
    stacked = [jnp.stack([summed[layer][member] for layer in range(LAYERS)]) for member in range(4)]
    return (
        stream.reshape(images.shape),
        pooled,
        grad.reshape(images.shape),
        gain_grads,
        shift_grads,
        stacked[0],
        qv_grads,
        stacked[1],
        outb_grads,
        stacked[2],
        upb_grads,
        stacked[3],
    )


def solution(mesh):
    placed = (
        P(("dp", "tensor"), None, None),
        P("dp"),
        P(),
        P(),
        P(None, None, None, "tensor"),
        P(None, None, "tensor"),
        P(None, "tensor", None),
        P(),
        P(None, None, "tensor"),
        P(None, "tensor"),
        P(None, "tensor", None),
        P(("dp", "tensor"), None, None),
    )
    return jax.shard_map(
        shards,
        mesh=mesh,
        in_specs=placed,
        out_specs=(
            P(("dp", "tensor"), None, None),
            P(("dp", "tensor"), None),
            P(("dp", "tensor"), None, None),
            P(),
            P(),
            P(None, "dp", None, "tensor"),
            P(None, None, "tensor"),
            P(None, "tensor", "dp"),
            P(),
            P(None, "dp", "tensor"),
            P(None, "tensor"),
            P(None, "tensor", "dp"),
        ),
        check_vma=False,
    )
```

```python
import functools
import math

import jax
import jax.numpy as jnp
from jax import lax
from jax.experimental import pallas as pl
from jax.experimental.pallas import tpu as pltpu
from jax.sharding import PartitionSpec as P

HEAD_DIM = 64
LAYERS = 2
EPSILON = 1e-06
NEGATIVE = -1e30
BF16 = jnp.bfloat16
F32 = jnp.float32
CHUNK = 16


def dot(left, right):
    return lax.dot_general(left, right, (((1,), (0,)), ((), ())), preferred_element_type=F32)


def dot_nt(left, right):
    return lax.dot_general(left, right, (((1,), (1,)), ((), ())), preferred_element_type=F32)


def fixed(shape, *lead):
    where = tuple(lead) + (0,) * (len(shape) - len(lead))
    return pl.BlockSpec(shape, lambda *_: where)


def out(shape, dtype):
    return jax.ShapeDtypeStruct(shape, dtype)


def in_hbm(values):
    return pltpu.with_memory_space_constraint(values, pltpu.HBM)


def cost(flops, *arrays):
    total = sum(math.prod(a.shape) * a.dtype.itemsize for a in arrays)
    return pl.CostEstimate(flops=int(flops) // 64, bytes_accessed=int(total) // 64, transcendentals=0)


MIB = 1 << 20


def call(body, name, grid, ins, in_specs, outs, out_specs, scratch=(), flops=0, limit=24):
    return pl.pallas_call(
        body,
        name=name,
        grid=grid,
        in_specs=in_specs,
        out_specs=out_specs,
        out_shape=outs,
        scratch_shapes=list(scratch),
        compiler_params=pltpu.CompilerParams(vmem_limit_bytes=limit * MIB),
        cost_estimate=cost(flops, *ins, *outs),
    )(*ins)


def whole():
    return pl.BlockSpec(memory_space=pltpu.VMEM)


def by_blocks(target, left, right, product, rows=256, add=False):
    def block(index, carry):
        here = pl.ds(pl.multiple_of(index * rows, rows), rows)
        value = product(left[here, :], right())
        if add:
            value = target[here, :] + value
        target[here, :] = value.astype(target.dtype)
        return carry

    lax.fori_loop(0, left.shape[0] // rows, block, 0)


def hbm():
    return pl.BlockSpec(memory_space=pltpu.HBM)


def by_rows(rows, body, unroll=1):
    def step(index, carry):
        for part in range(unroll):
            body(pl.multiple_of((index * unroll + part) * CHUNK, CHUNK))
        return carry

    lax.fori_loop(0, rows // (CHUNK * unroll), step, 0)


def moments(values):
    average = jnp.mean(values, axis=-1, keepdims=True)
    centred = values - average
    variance = jnp.mean(centred * centred, axis=-1, keepdims=True)
    return centred, lax.rsqrt(variance + EPSILON)


def normalized(values, gain, bias):
    centred, scale = moments(values)
    return centred * scale * gain + bias


def norm_backward(values, grad_normed, gain):
    centred, scale = moments(values)
    unit = centred * scale
    grad_unit = grad_normed * gain
    first = jnp.mean(grad_unit, axis=-1, keepdims=True)
    second = jnp.mean(grad_unit * unit, axis=-1, keepdims=True)
    return scale * (grad_unit - first - unit * second), grad_normed * unit


def fold_rows(values):
    total = values[0:8]
    for start in range(8, values.shape[0], 8):
        total = total + values[start : start + 8]
    return total


def prep_kernel(images, cotangent, gain, bias, order, normed, normed_t, cotangent_t, wide_cotangent):
    def rows(start):
        here = pl.ds(start, CHUNK)
        values = images[here, :].astype(F32)
        normed[here, :] = normalized(values, gain[0, 0:1, :], bias[0, 0:1, :]).astype(BF16)
        wide_cotangent[here, :] = cotangent[here, :].astype(F32)

    by_rows(images.shape[0], rows, 4)
    by_blocks(normed_t, order, lambda: normed[...], dot_nt)
    by_blocks(cotangent_t, order, lambda: cotangent[...], dot_nt)


def head_masks(slots):
    lane = lax.broadcasted_iota(jnp.int32, (slots, 2 * HEAD_DIM), 1)
    return lane < HEAD_DIM, lane >= HEAD_DIM


def own_count(counts, image, images):
    return counts[lax.axis_index("tensor") * images + image]


def attend_kernel(
    slots,
    which,
    counts,
    normed,
    weight_own,
    weight_far,
    bias_own,
    bias_far,
    joint_own,
    joint_far,
    att_own,
    att_far,
    lse_own,
    lse_far,
    held,
    sem,
):
    width = att_own.shape[1]
    pairs = width // (2 * HEAD_DIM)
    scale = HEAD_DIM ** (-0.5)
    layer = which[0]
    weights = (weight_own, weight_far)
    for side in range(2):
        for member in range(3):
            fetch(weights[side].at[layer, member], held.at[side, member], sem.at[side, member])
    for side, (joint, bias) in enumerate(((joint_own, bias_own), (joint_far, bias_far))):

        def project(member, carry):
            pltpu.make_async_copy(
                weights[side].at[layer, member], held.at[side, member], sem.at[side, member]
            ).wait()
            shift = bias[layer, pl.ds(member // 2, 1), :]
            shift = jnp.where(member == 1, jnp.zeros_like(shift), shift)
            joint[member] = (dot(normed[...], held[side, member]) + shift).astype(BF16)
            return carry

        lax.fori_loop(0, 3, project, 0)
    masks = head_masks(slots)
    key_index = lax.broadcasted_iota(jnp.int32, (slots, slots), 0)

    def step(index, carry):
        image = index // pairs
        pair = index % pairs
        rows = pl.ds(pl.multiple_of(image * slots, slots), slots)
        lanes = pl.ds(pl.multiple_of(pair * 2 * HEAD_DIM, 2 * HEAD_DIM), 2 * HEAD_DIM)
        valid = key_index < own_count(counts, image, normed.shape[0] // slots)
        for joint, attended, lse in (
            (joint_own, att_own, lse_own),
            (joint_far, att_far, lse_far),
        ):
            queries = joint[0, rows, lanes]
            keys_in = joint[1, rows, lanes] * jnp.asarray(scale, BF16)
            values_t = joint[2, rows, lanes].T
            parts = []
            for side in range(2):
                keys_side = jnp.where(masks[side], keys_in, jnp.zeros_like(keys_in))
                scores = jnp.where(valid, dot_nt(keys_side, queries), NEGATIVE)
                largest = jnp.max(scores, axis=0, keepdims=True)
                exponent = jnp.exp(scores - largest)
                total = jnp.sum(exponent, axis=0, keepdims=True)
                probs = (exponent * (1.0 / total)).astype(BF16)
                parts.append(dot(values_t[side * HEAD_DIM : (side + 1) * HEAD_DIM], probs))
                lse[2 * index + side] = largest + jnp.log(total)
            attended[rows, lanes] = jnp.concatenate(parts, axis=0).T.astype(BF16)
        return carry

    lax.fori_loop(0, (normed.shape[0] // slots) * pairs, step, 0)


def fetch(source, target, sem):
    copy = pltpu.make_async_copy(source, target, sem)
    copy.start()
    return copy


def feed_kernel(
    layer,
    slots,
    last_layer,
    counts,
    stream,
    att_own,
    att_far,
    out_own,
    out_far,
    out_bias,
    gain,
    bias,
    order,
    up_own,
    up_far,
    up_bias_own,
    up_bias_far,
    down_own,
    down_far,
    mid,
    normed_t,
    hid_own,
    hid_far,
    slope_own,
    slope_far,
    stream_out,
    *rest,
):
    if last_layer:
        pooled = rest[0]
    else:
        next_normed, next_t = rest[:2]
    normed, total, pre, w_out, w_up, w_down, hid, slope, in_sem, out_sem = rest[1 if last_layer else 2 :]
    tokens = stream.shape[0]
    half = w_out.shape[0] // 2
    units = w_up.shape[0]
    tile = w_up.shape[2]
    tiles = units // 2
    out_in = [
        fetch(ref.at[layer], w_out.at[pl.ds(side * half, half)], in_sem.at[side])
        for side, ref in enumerate((out_own, out_far))
    ]
    up_in, down_in = [], []
    for unit in range(units):
        side, part = unit // tiles, unit % tiles
        columns = pl.ds(part * tile, tile)
        up_ref, down_ref = ((up_own, down_own), (up_far, down_far))[side]
        up_in.append(fetch(up_ref.at[layer, :, columns], w_up.at[unit], in_sem.at[2 + unit]))
        down_in.append(
            fetch(down_ref.at[layer, columns, :], w_down.at[unit], in_sem.at[2 + units + unit])
        )
    for copy in out_in:
        copy.wait()
    total[...] = dot(jnp.concatenate([att_own[...], att_far[...]], axis=1), w_out[...])

    def enter(start):
        here = pl.ds(start, CHUNK)
        value = stream[here, :].astype(F32) + (total[here, :] + out_bias[layer, 0:1, :])
        mid[here, :] = value
        normed[here, :] = normalized(value, gain[layer, 1:2, :], bias[layer, 1:2, :]).astype(BF16)

    by_rows(tokens, enter, 4)
    up_in[0].wait()
    by_blocks(pre.at[0], normed, lambda: w_up[0], dot)
    by_blocks(normed_t, order, lambda: normed[...], dot_nt)
    rows = 128
    out_copies = []
    for unit in range(units):
        side, part = unit // tiles, unit % tiles
        shift = (up_bias_own, up_bias_far)[side][layer : layer + 1, part * tile : (part + 1) * tile]
        if unit + 1 < units:
            up_in[unit + 1].wait()
        if unit > 0:
            down_in[unit - 1].wait()

        def chunk(index, carry):
            block = pl.ds(pl.multiple_of(index * rows, rows), rows)
            if unit + 1 < units:
                pre[(unit + 1) % 2, block, :] = dot(normed[block, :], w_up[unit + 1])
            if unit == 1:
                total[block, :] = dot(hid[unit - 1, block, :], w_down[unit - 1])
            elif unit > 1:
                total[block, :] += dot(hid[unit - 1, block, :], w_down[unit - 1])
            for sub in range(0, rows, CHUNK):
                here = pl.ds(pl.multiple_of(index * rows + sub, CHUNK), CHUNK)
                value = pre[unit % 2, here, :] + shift
                cdf = 0.5 + 0.5 * lax.erf(value * (0.5**0.5))
                hid[unit, here, :] = (value * cdf).astype(BF16)
                density = jnp.exp(-0.5 * value * value) * ((2.0 * math.pi) ** -0.5)
                slope[unit, here, :] = (cdf + value * density).astype(BF16)
            return carry

        lax.fori_loop(0, tokens // rows, chunk, 0)
        hid_ref, slope_ref = ((hid_own, slope_own), (hid_far, slope_far))[side]
        columns = pl.ds(part * tile, tile)
        out_copies.append(fetch(hid.at[unit], hid_ref.at[:, columns], out_sem.at[unit]))
        out_copies.append(fetch(slope.at[unit], slope_ref.at[:, columns], out_sem.at[units + unit]))
    down_in[units - 1].wait()
    by_blocks(total, hid.at[units - 1], lambda: w_down[units - 1], dot, add=True)

    def leave(start):
        here = pl.ds(start, CHUNK)
        value = mid[here, :] + (total[here, :] + out_bias[layer, 1:2, :])
        stream_out[here, :] = value
        if not last_layer:
            next_normed[here, :] = normalized(
                value, gain[layer + 1, 0:1, :], bias[layer + 1, 0:1, :]
            ).astype(BF16)

    by_rows(tokens, leave, 4)
    if last_layer:
        index = lax.broadcasted_iota(jnp.int32, (slots, 1), 0)
        for image in range(tokens // slots):
            block = stream_out[image * slots : (image + 1) * slots, :]
            count = own_count(counts, image, tokens // slots)
            summed = jnp.sum(jnp.where(index < count, block, 0.0), axis=0, keepdims=True)
            pooled[image : image + 1, :] = summed / count.astype(F32)
    else:
        by_blocks(next_t, order, lambda: next_normed[...], dot_nt)
    for copy in out_copies:
        copy.wait()


def feed_back_kernel(
    which,
    grad_in,
    mid,
    gain,
    order,
    down_own,
    down_far,
    up_own,
    up_far,
    slope_own,
    slope_far,
    out_own,
    out_far,
    pre_own,
    pre_far,
    bias_own,
    bias_far,
    grad_mid,
    mid_t,
    att_own,
    att_far,
    sums,
    low,
    total,
    hidden,
    partial,
    w_down,
    w_up,
    slope,
    pre,
    w_out,
    in_sem,
    out_sem,
):
    layer = which[0]
    tokens = grad_in.shape[0]
    units = w_up.shape[0]
    tile = w_up.shape[2]
    tiles = units // 2
    down_in, up_in, slope_in = [], [], []
    for unit in range(units):
        columns = pl.ds(unit % tiles * tile, tile)
        down_ref, up_ref, slope_ref = ((down_far, up_far, slope_far), (down_own, up_own, slope_own))[
            unit // tiles
        ]
        down_in.append(fetch(down_ref.at[layer, columns, :], w_down.at[unit], in_sem.at[0, unit]))
        slope_in.append(fetch(slope_ref.at[:, columns], slope.at[unit], in_sem.at[1, unit]))
        up_in.append(fetch(up_ref.at[layer, :, columns], w_up.at[unit], in_sem.at[2, unit]))
    out_in = [
        fetch(ref.at[layer], w_out.at[side], in_sem.at[3, side])
        for side, ref in enumerate((out_far, out_own))
    ]
    partial[...] = jnp.zeros_like(partial)

    def enter(start):
        here = pl.ds(start, CHUNK)
        value = grad_in[here, :].astype(F32)
        low[here, :] = value.astype(BF16)
        partial[0] += fold_rows(value)

    by_rows(tokens, enter)
    down_in[0].wait()
    by_blocks(hidden.at[0], low, lambda: w_down[0], dot_nt)
    rows = 256
    total[...] = jnp.zeros_like(total)
    pre[units - 1] = jnp.zeros_like(pre[units - 1])
    pre_refs = (pre_far, pre_own)

    def result(unit, side):
        columns = pl.ds(pl.multiple_of(unit % tiles * tile, tile), tile)
        return pltpu.make_async_copy(pre.at[unit], pre_refs[side].at[:, columns], out_sem.at[unit])

    def turn(unit, carry):
        after = jnp.minimum(unit + 1, units - 1)
        before = jnp.maximum(unit - 1, 0)

        @pl.when(unit + 1 < units)
        def _():
            pltpu.make_async_copy(
                down_own.at[layer, pl.ds(0, tile), :], w_down.at[after], in_sem.at[0, after]
            ).wait()

        @pl.when(unit != 1)
        def _():
            pltpu.make_async_copy(
                up_own.at[layer, :, pl.ds(0, tile)], w_up.at[before], in_sem.at[2, before]
            ).wait()

        pltpu.make_async_copy(
            slope_own.at[:, pl.ds(0, tile)], slope.at[unit], in_sem.at[1, unit]
        ).wait()
        idle = (unit + units - 1) % units

        def chunk(index, carry):
            block = pl.ds(pl.multiple_of(index * rows, rows), rows)
            hidden[(unit + 1) % 2, block, :] = dot_nt(low[block, :], w_down[after])
            total[block, :] += dot_nt(pre[idle, block, :], w_up[before])
            for sub in range(0, rows, CHUNK):
                here = pl.ds(pl.multiple_of(index * rows + sub, CHUNK), CHUNK)
                value = hidden[unit % 2, here, :] * slope[unit, here, :].astype(F32)
                pre[unit, here, :] = value.astype(BF16)
                carry = carry + fold_rows(value)
            return carry

        summed = lax.fori_loop(0, tokens // rows, chunk, jnp.zeros((8, tile), F32))
        row = jnp.sum(summed, axis=0, keepdims=True)
        for side, bias in enumerate((bias_far, bias_own)):

            @pl.when(unit // tiles == side)
            def _():
                bias[pl.ds(unit % tiles, 1), :] = row
                result(unit, side).start()

        return carry

    lax.fori_loop(0, units, turn, 0)
    up_in[units - 1].wait()
    by_blocks(total, pre.at[units - 1], lambda: w_up[units - 1], dot_nt, add=True)

    def leave(start):
        here = pl.ds(start, CHUNK)
        normed_grad = total[here, :]
        through, gain_term = norm_backward(mid[here, :], normed_grad, gain[layer, 1:2, :])
        value = grad_in[here, :].astype(F32) + through
        grad_mid[here, :] = value
        low[here, :] = value.astype(BF16)
        partial[1] += fold_rows(value)
        partial[2] += fold_rows(gain_term)
        partial[3] += fold_rows(normed_grad)

    by_rows(tokens, leave, 2)
    sums[...] = jnp.sum(partial[...], axis=1)
    by_blocks(mid_t, order, lambda: low[...], dot_nt)
    for copy in out_in:
        copy.wait()
    by_blocks(att_far, low, lambda: w_out[0], dot_nt)
    by_blocks(att_own, low, lambda: w_out[1], dot_nt)
    for unit in range(units):
        result(unit, unit // tiles).wait()


def attend_back_kernel(slots, counts, joint, lse, grad_att, grad_joint, bias_sums):
    width = grad_att.shape[1]
    pairs = width // (2 * HEAD_DIM)
    scale = HEAD_DIM ** (-0.5)
    masks = head_masks(slots)
    key_index = lax.broadcasted_iota(jnp.int32, (slots, slots), 0)
    bias_sums[...] = jnp.zeros_like(bias_sums)

    def step(index, carry):
        image = index // pairs
        pair = index % pairs
        rows = pl.ds(pl.multiple_of(image * slots, slots), slots)
        lanes = pl.ds(pl.multiple_of(pair * 2 * HEAD_DIM, 2 * HEAD_DIM), 2 * HEAD_DIM)
        queries = joint[0, rows, lanes]
        keys_in = joint[1, rows, lanes]
        values_in = joint[2, rows, lanes]
        grads = grad_att[rows, lanes]
        keys_t = keys_in.T
        keys_scaled = keys_in * jnp.asarray(scale, BF16)
        valid = key_index < own_count(counts, image, grad_att.shape[0] // slots)
        zeros = jnp.zeros_like(keys_in)
        query_parts, key_parts, value_parts = [], [], []
        for side in range(2):
            keys_side = jnp.where(masks[side], keys_scaled, zeros)
            values_side = jnp.where(masks[side], values_in, zeros)
            scores = jnp.where(valid, dot_nt(keys_side, queries), NEGATIVE)
            probs = jnp.exp(scores - lse[2 * index + side])
            grad_probs = dot_nt(values_side, grads)
            inner = jnp.sum(grad_probs * probs, axis=0, keepdims=True)
            grad_scores = (probs * (grad_probs - inner)).astype(BF16)
            value_parts.append(dot(probs.astype(BF16), grads))
            key_parts.append(dot(grad_scores, queries))
            query_parts.append(dot(keys_t[side * HEAD_DIM : (side + 1) * HEAD_DIM], grad_scores))
        grad_queries = jnp.concatenate(query_parts, axis=0).T * scale
        grad_keys = jnp.where(masks[0], key_parts[0], key_parts[1]) * scale
        grad_values = jnp.where(masks[0], value_parts[0], value_parts[1])
        bias_sums[0:1, lanes] += jnp.sum(grad_queries, axis=0, keepdims=True)
        value_lanes = pl.ds(
            pl.multiple_of(width + pair * 2 * HEAD_DIM, 2 * HEAD_DIM), 2 * HEAD_DIM
        )
        bias_sums[0:1, value_lanes] += jnp.sum(grad_values, axis=0, keepdims=True)
        grad_joint[0, rows, lanes] = grad_queries.astype(BF16)
        grad_joint[1, rows, lanes] = grad_keys.astype(BF16)
        grad_joint[2, rows, lanes] = grad_values.astype(BF16)
        return carry

    lax.fori_loop(0, (grad_att.shape[0] // slots) * pairs, step, 0)


def entry_back_kernel(
    layer, with_low, joint_own, joint_far, weight_own, weight_far, stream, gain, grad_mid, order, *rest
):
    if with_low:
        grad_out, sums, low_t, total, partial, low = rest
    else:
        grad_out, sums, total, partial = rest
    member = pl.program_id(0)

    @pl.when(member == 0)
    def _():
        total[...] = jnp.zeros_like(total)
        partial[...] = jnp.zeros_like(partial)

    left = jnp.concatenate([joint_own[member], joint_far[member]], axis=1)
    right = jnp.concatenate([weight_own[0, 0], weight_far[0, 0]], axis=1)
    total[...] += dot_nt(left, right)

    def rows(start):
        here = pl.ds(start, CHUNK)
        normed_grad = total[here, :]
        through, gain_term = norm_backward(
            stream[here, :].astype(F32), normed_grad, gain[layer, 0:1, :]
        )
        value = grad_mid[here, :] + through
        grad_out[here, :] = value
        if with_low:
            low[here, :] = value.astype(BF16)
        partial[0] += fold_rows(gain_term)
        partial[1] += fold_rows(normed_grad)

    @pl.when(member == 2)
    def _():
        by_rows(stream.shape[0], rows, 2)
        sums[...] = jnp.sum(partial[...], axis=1)
        if with_low:
            by_blocks(low_t, order, lambda: low[...], dot_nt)


def pack_kernel(layers, *refs):
    ins, (own_out, far_out) = refs[:-2], refs[-2:]
    for layer in range(layers):
        sums_mid, sums_in, qv_own, qv_far, upb_own, upb_far = ins[6 * layer : 6 * layer + 6]
        tiles = upb_own.shape[0]
        for ref, qv, upb in ((own_out, qv_own, upb_own), (far_out, qv_far, upb_far)):
            for row, value in (
                (2 * layer, sums_in[0:1, :]),
                (2 * layer + 1, sums_mid[2:3, :]),
                (2 * (layers + layer), sums_in[1:2, :]),
                (2 * (layers + layer) + 1, sums_mid[3:4, :]),
                (2 * (2 * layers + layer), sums_mid[1:2, :]),
                (2 * (2 * layers + layer) + 1, sums_mid[0:1, :]),
                (6 * layers + layer, qv[...]),
            ):
                ref[row : row + 1, :] = value
            start = 7 * layers + tiles * layer
            ref[start : start + tiles, :] = upb[...]


def unpack_kernel(layers, mine, got, gain, bias, out_bias, qv, upb):
    total = mine[...] + got[...]
    half = qv.shape[2]
    tiles = upb.shape[1] // mine.shape[1]
    width = mine.shape[1]
    for layer in range(layers):
        for norm in range(2):
            row = 2 * layer + norm
            gain[layer, norm : norm + 1, :] = total[row : row + 1]
            row += 2 * layers
            bias[layer, norm : norm + 1, :] = total[row : row + 1]
            row += 2 * layers
            out_bias[layer, norm : norm + 1, :] = total[row : row + 1]
        row = 6 * layers + layer
        for kind in range(2):
            qv[layer, kind : kind + 1, :] = total[row : row + 1, kind * half : (kind + 1) * half]
        row = 7 * layers + tiles * layer
        for part in range(tiles):
            upb[layer : layer + 1, part * width : (part + 1) * width] = total[
                row + part : row + part + 1
            ]


def chunk_sources(order):
    first = list(order[:4])
    sources = []
    for target in range(16):
        source = 0
        for place, bit in enumerate(first):
            if (target >> (3 - place)) & 1:
                source |= 1 << (3 - bit)
        sources.append(source)
    return sources


def weight_kernel(sources, tiles, has_extra, *refs):
    if has_extra:
        left_own, left_far, right_own, right_far, lx_own, lx_far, rx_own, rx_far, keep, send = refs
    else:
        left_own, left_far, right_own, right_far, keep, send = refs

    def product(a_own, a_far, b_own, b_far):
        left = jnp.concatenate([a_own[...], a_far[...]], axis=1)
        right = jnp.concatenate([b_own[...].reshape(b_own.shape[-2:]), b_far[...].reshape(b_far.shape[-2:])], axis=0)
        size = left.shape[0] // 16
        low = dot(left, right).astype(BF16)
        for target, source in enumerate(sources):
            ref = keep if target < 8 else send
            ref[(target % 8) * size : (target % 8 + 1) * size, :] = low[
                source * size : (source + 1) * size, :
            ]

    if has_extra:

        @pl.when(pl.program_id(0) < tiles)
        def _():
            product(left_own, left_far, right_own, right_far)

        @pl.when(pl.program_id(0) == tiles)
        def _():
            product(lx_own, lx_far, rx_own, rx_far)

    else:
        product(left_own, left_far, right_own, right_far)


def weight_grad(name, order, left, right, extra=None, tiles=None, first=0):
    left_own, left_far = left
    right_own, right_far = right
    width, tokens = left_own.shape
    if right_own.ndim == 3:
        tile = right_own.shape[2]
        right_spec = pl.BlockSpec(
            (1, tokens, tile), lambda j: (jnp.minimum(j, tiles - 1) + first, 0, 0)
        )
    else:
        tile = 768 if tiles else 512
        tiles = tiles or right_own.shape[1] // tile
        right_spec = pl.BlockSpec((tokens, tile), lambda j: (0, j + first))
    steps = tiles + (1 if extra is not None else 0)
    ins = [left_own, left_far, right_own, right_far]
    specs = [fixed((width, tokens))] * 2 + [right_spec] * 2
    if extra is not None:
        ins += list(extra)
        specs += [fixed((width, tokens))] * 2 + [fixed((tokens, tile))] * 2
    half = out((width // 2, steps * tile), BF16)
    half_spec = pl.BlockSpec((width // 2, tile), lambda j: (0, j))
    return call(
        functools.partial(weight_kernel, chunk_sources(order), tiles, extra is not None),
        name,
        (steps,),
        ins,
        specs,
        [half, half],
        [half_spec, half_spec],
        flops=4 * width * tokens * steps * tile,
    )


def flip(bit):
    size = lax.axis_size("dp")
    return [(index, index ^ (1 << bit)) for index in range(size)]


class DpSum:
    def __init__(self, order, halves=None, units=()):
        self.order = list(order)
        self.incoming = None
        if halves is not None:
            keep, self.outgoing = halves
            self.members = [[keep]]
        else:
            self.members = [parts for unit in units for parts in unit.members]
            self.halve()

    def halve(self):
        rows = self.members[0][0].shape[0] // 2
        sends = [
            sum(part[rows:].astype(F32) for part in parts).astype(BF16) for parts in self.members
        ]
        self.outgoing = sends[0] if len(sends) == 1 else jnp.concatenate(sends, axis=1)
        self.members = [[part[:rows] for part in parts] for parts in self.members]

    def start(self):
        self.incoming = lax.ppermute(self.outgoing, "dp", flip(self.order.pop(0)))

    def turn(self):
        column = 0
        for parts in self.members:
            width = parts[0].shape[1]
            parts.append(self.incoming[:, column : column + width])
            column += width
        self.incoming = None
        if self.order:
            self.halve()
            self.start()

    def results(self):
        return [sum(part.astype(F32) for part in parts) for parts in self.members]


class Everywhere:
    def __init__(self, mine, far, bits):
        self.mine = mine
        self.incoming = swap(far)
        self.bits = list(range(bits))

    def turn(self):
        self.mine = self.mine + self.incoming
        self.incoming = lax.ppermute(self.mine, "dp", flip(self.bits.pop(0)))


def gate(value, starts=(), turns=(), after=()):
    held = [unit.outgoing for unit in starts] + [unit.incoming for unit in turns]
    value, *held = lax.optimization_barrier((value, *held, *after))
    for unit, array in zip(starts, held):
        unit.outgoing = array
        unit.start()
    for unit, array in zip(turns, held[len(starts) :]):
        unit.incoming = array
        unit.turn()
    return value


def swap(values):
    return lax.ppermute(values, "tensor", [(0, 1), (1, 0)])


def shards(
    images,
    valid_count,
    ln_gain,
    ln_bias,
    w_qkv,
    qv_bias,
    w_out,
    out_bias,
    w_up,
    up_bias,
    w_down,
    cotangent,
):
    local_rows, slots, width = images.shape
    tokens = local_rows * slots
    half = w_qkv.shape[3]
    ff_half = w_up.shape[2]
    tile = 768
    steps = ff_half // tile
    heads = half // HEAD_DIM
    dp = lax.axis_size("dp")
    bits = dp.bit_length() - 1
    assert dp == 1 << bits and bits >= 4 and lax.axis_size("tensor") == 2
    tail = tuple(range(4, bits))
    order_a = (0, 1, 2, 3) + tail
    order_b = (1, 0, 2, 3) + tail
    order_c = (2, 3, 0, 1) + tail
    order_d = (0, 2, 3, 1) + tail

    me = lax.axis_index("dp")
    counts = valid_count

    block = width // dp
    row = jnp.arange(width, dtype=jnp.int32)
    index = row // block
    mirrored = jnp.zeros_like(index)
    for bit in range(bits):
        mirrored = mirrored | (((index >> (bits - 1 - bit)) & 1) << bit)
    source = (mirrored ^ me) * block + row % block
    order = (source[:, None] == row[None, :]).astype(BF16)

    w_qkv = jnp.transpose(w_qkv, (0, 2, 1, 3))
    qkv = (w_qkv, swap(w_qkv))
    qv = (qv_bias, swap(qv_bias))

    images_2d = images.reshape(tokens, width)
    cotangent_2d = cotangent.reshape(tokens, width)
    smem = pl.BlockSpec(memory_space=pltpu.SMEM)
    wide = (tokens, width)
    flops_wide = 2 * width * width * tokens

    normed, normed_t, cotangent_t, wide_cotangent = call(
        prep_kernel,
        "prep",
        (),
        [images_2d, cotangent_2d, ln_gain, ln_bias, order],
        [whole()] * 5,
        [out(wide, BF16), out((width, tokens), BF16), out((width, tokens), BF16), out(wide, F32)],
        [whole()] * 4,
        flops=2 * flops_wide,
    )

    wout, wup, wdown = [
        (weight, swap(lax.optimization_barrier((weight, normed, qkv[1], qv[1]))[0]))
        for weight in (w_out, w_up, w_down)
    ]

    def attend(layer, normed, counts):
        lse_shape = (local_rows * heads, 1, slots)
        joint_out = out((3, tokens, half), BF16)
        att_out = out((tokens, half), BF16)
        lse_out = out(lse_shape, F32)
        results = call(
            functools.partial(attend_kernel, slots),
            "attend",
            (),
            [jnp.full((1,), layer, jnp.int32), counts, normed, in_hbm(qkv[0]), in_hbm(qkv[1]), qv[0], qv[1]],
            [smem, smem, whole(), hbm(), hbm(), whole(), whole()],
            [joint_out, joint_out, att_out, att_out, lse_out, lse_out],
            [whole()] * 6,
            [pltpu.VMEM((2, 3, width, half), BF16), pltpu.SemaphoreType.DMA((2, 3))],
            flops=12 * tokens * width * half + 8 * tokens * slots * half,
            limit=44,
        )
        return results[0::2], results[1::2]

    stream = images_2d
    saved = []
    got_cotangent_t = swap(cotangent_t)
    pooled = None
    for layer in range(LAYERS):
        last = layer == LAYERS - 1
        own, far = attend(layer, normed, counts)
        if layer == 0:
            upb = (up_bias, swap(up_bias))
        gain_in = ln_gain
        if layer > 0:
            before = saved[layer - 1]
            names = ("got_normed_t", "got_att", "got_mid_normed_t", "got_hid")
            gain_in, got_cotangent_t, *got = lax.optimization_barrier(
                (ln_gain, got_cotangent_t, *[before[name] for name in names])
            )
            before.update(zip(names, got))
        ff = pltpu.HBM((tokens, ff_half), BF16)
        extra = (
            [out((local_rows, width), F32)]
            if last
            else [out(wide, BF16), out((width, tokens), BF16)]
        )
        results = call(
            functools.partial(feed_kernel, layer, slots, last),
            "feed",
            (),
            [
                counts,
                stream,
                own[1],
                far[1],
                in_hbm(wout[0]),
                in_hbm(wout[1]),
                out_bias,
                gain_in,
                ln_bias,
                order,
                in_hbm(wup[0]),
                in_hbm(wup[1]),
                upb[0],
                upb[1],
                in_hbm(wdown[0]),
                in_hbm(wdown[1]),
            ],
            [smem]
            + [whole()] * 3
            + [hbm()] * 2
            + [whole()] * 4
            + [hbm()] * 2
            + [whole()] * 2
            + [hbm()] * 2,
            [out(wide, F32), out((width, tokens), BF16), ff, ff, ff, ff, out(wide, F32)] + extra,
            [whole()] * 2 + [hbm()] * 4 + [whole()] * (1 + len(extra)),
            [
                pltpu.VMEM(wide, BF16),
                pltpu.VMEM(wide, F32),
                pltpu.VMEM((2, tokens, tile), F32),
                pltpu.VMEM((2 * half, width), BF16),
                pltpu.VMEM((2 * steps, width, tile), BF16),
                pltpu.VMEM((2 * steps, tile, width), BF16),
                pltpu.VMEM((2 * steps, tokens, tile), BF16),
                pltpu.VMEM((2 * steps, tokens, tile), BF16),
                pltpu.SemaphoreType.DMA((2 + 4 * steps,)),
                pltpu.SemaphoreType.DMA((4 * steps,)),
            ],
            flops=8 * tokens * width * ff_half + 2 * flops_wide,
            limit=32,
        )
        mid, mid_normed_t, hid_own, hid_far, slope_own, slope_far, stream_next = results[:7]
        saved.append(
            dict(
                stream=stream,
                own=own,
                far=far,
                mid=mid,
                slope=(slope_own, slope_far),
                hid=hid_own,
                attended=own[1],
                normed_t=normed_t,
                mid_normed_t=mid_normed_t,
                got_hid=swap(hid_far),
                got_att=swap(far[1]),
                got_normed_t=swap(normed_t),
                got_mid_normed_t=swap(mid_normed_t),
            )
        )
        stream = stream_next
        if last:
            pooled = results[7]
        else:
            normed, normed_t = results[7:9]

    def feed_back(layer, grad, gain_in):
        kept = saved[layer]
        ff = pltpu.HBM((tokens, ff_half), BF16)
        bias_shape = out((steps, tile), F32)
        att_shape = out((tokens, half), BF16)
        return call(
            feed_back_kernel,
            "feed_back",
            (),
            [
                jnp.full((1,), layer, jnp.int32),
                grad,
                kept["mid"],
                gain_in,
                order,
                in_hbm(wdown[0]),
                in_hbm(wdown[1]),
                in_hbm(wup[0]),
                in_hbm(wup[1]),
                kept["slope"][0],
                kept["slope"][1],
                in_hbm(wout[0]),
                in_hbm(wout[1]),
            ],
            [smem] + [whole()] * 4 + [hbm()] * 8,
            [
                ff,
                ff,
                bias_shape,
                bias_shape,
                out(wide, F32),
                out((width, tokens), BF16),
                att_shape,
                att_shape,
                out((4, width), F32),
            ],
            [hbm()] * 2 + [whole()] * 7,
            [
                pltpu.VMEM(wide, BF16),
                pltpu.VMEM(wide, F32),
                pltpu.VMEM((2, tokens, tile), F32),
                pltpu.VMEM((4, 8, width), F32),
                pltpu.VMEM((2 * steps, tile, width), BF16),
                pltpu.VMEM((2 * steps, width, tile), BF16),
                pltpu.VMEM((2 * steps, tokens, tile), BF16),
                pltpu.VMEM((2 * steps, tokens, tile), BF16),
                pltpu.VMEM((2, half, width), BF16),
                pltpu.SemaphoreType.DMA((4, 2 * steps)),
                pltpu.SemaphoreType.DMA((2 * steps,)),
            ],
            flops=8 * tokens * width * ff_half + 2 * flops_wide,
            limit=32,
        )

    def attend_back(forward, grad_att, counts_in):
        joint, _, lse = forward
        return call(
            functools.partial(attend_back_kernel, slots),
            "attend_back",
            (),
            [counts_in, joint, lse, grad_att],
            [smem, whole(), whole(), whole()],
            [out(joint.shape, BF16), out((1, 2 * half), F32)],
            [whole()] * 2,
            flops=10 * tokens * slots * half,
        )

    def entry_back(layer, joint_own, joint_far, grad_mid, gain_in):
        with_low = layer > 0
        return call(
            functools.partial(entry_back_kernel, layer, with_low),
            "entry_back",
            (3,),
            [
                joint_own,
                joint_far,
                in_hbm(qkv[0]),
                in_hbm(qkv[1]),
                saved[layer]["stream"],
                gain_in,
                grad_mid,
                order,
            ],
            [whole()] * 2
            + [pl.BlockSpec((1, 1, width, half), lambda c: (layer, c, 0, 0))] * 2
            + [whole()] * 4,
            [out(wide, F32), out((2, width), F32)]
            + ([out((width, tokens), BF16)] if with_low else []),
            [whole()] * (3 if with_low else 2),
            [pltpu.VMEM(wide, F32), pltpu.VMEM((2, 8, width), F32)]
            + ([pltpu.VMEM(wide, BF16)] if with_low else []),
            flops=12 * tokens * width * half,
        )

    def down_halves(layer, order_of, grad_t, got_grad_t):
        kept = saved[layer]
        return weight_grad(
            "down_grad", order_of, (grad_t, got_grad_t), (in_hbm(kept["hid"]), kept["got_hid"])
        )

    def up_halves(layer, order_of, pre_own, got_pre, tiles=None, first=0):
        kept = saved[layer]
        return weight_grad(
            "up_grad",
            order_of,
            (kept["mid_normed_t"], kept["got_mid_normed_t"]),
            (pre_own, got_pre),
            tiles=tiles,
            first=first,
        )

    def lefts(layer):
        return saved[layer]["normed_t"], saved[layer]["got_normed_t"]

    def extras(layer, mid_t, got_mid_t):
        return mid_t, got_mid_t, saved[layer]["attended"], saved[layer]["got_att"]

    small = [None] * LAYERS
    down_1 = DpSum(order_a, down_halves(1, order_a, cotangent_t, got_cotangent_t))
    gain_in = gate(ln_gain, [down_1])
    pre_own, pre_far, upb_own, upb_far, grad_mid, mid_t, att_own, att_far, sums_mid = feed_back(
        1, wide_cotangent, gain_in
    )
    got_pre, got_mid_t = swap(pre_far), swap(mid_t)
    joint_far, qv_far = attend_back(saved[1]["far"], att_far, counts)
    got_joint = swap(joint_far)
    counts_in = gate(counts, [], [down_1], [qv_far])
    joint_own, qv_own = attend_back(saved[1]["own"], att_own, counts_in)
    pre_own = gate(pre_own, after=[qv_own])
    up_1 = DpSum(order_a, up_halves(1, order_a, pre_own, got_pre))
    gain_in = gate(gain_in, [up_1], [down_1])
    grad, sums_in, grad_t = entry_back(1, joint_own, joint_far, grad_mid, gain_in)
    got_grad_t = swap(grad_t)
    small[1] = (sums_mid, sums_in, qv_own, qv_far, upb_own, upb_far)
    joint_own = gate(joint_own, [], [down_1], [sums_in])
    rest_1 = DpSum(
        order_c,
        weight_grad(
            "qkv_out_grad",
            order_c,
            lefts(1),
            (joint_own, got_joint),
            extras(1, mid_t, got_mid_t),
            tiles=3,
        ),
    )
    grad_t = gate(grad_t, [rest_1])
    down_0 = DpSum(order_a, down_halves(0, order_a, grad_t, got_grad_t))

    gain_in = gate(gain_in, [down_0], [up_1, down_1])
    pre_own, pre_far, upb_own, upb_far, grad_mid, mid_t, att_own, att_far, sums_mid = feed_back(
        0, grad, gain_in
    )
    got_pre, got_mid_t = swap(pre_far), swap(mid_t)
    counts_in = gate(counts_in, [], [up_1, rest_1], [sums_mid])
    joint_far, qv_far = attend_back(saved[0]["far"], att_far, counts_in)
    got_joint = swap(joint_far)
    pre_own = gate(pre_own, [], [down_0, up_1], [qv_far])
    up_0 = DpSum(order_d, up_halves(0, order_d, pre_own, got_pre))
    counts_in = gate(counts_in, [up_0], [], [got_mid_t, got_joint])
    joint_own, qv_own = attend_back(saved[0]["own"], att_own, counts_in)
    rest_0 = DpSum(
        order_b,
        weight_grad(
            "qkv_out_grad",
            order_b,
            lefts(0),
            (joint_own, got_joint),
            extras(0, mid_t, got_mid_t),
            tiles=3,
        ),
    )
    gain_in = gate(gain_in, [rest_0], [down_0], [qv_own])
    grad, sums_in = entry_back(0, joint_own, joint_far, grad_mid, gain_in)
    last = gate(sums_in, [], [up_0, down_0, rest_1, up_1])
    small[0] = (sums_mid, last, qv_own, qv_far, upb_own, upb_far)
    ins = [array for arrays in small for array in arrays]
    vector_shape = out(((7 + steps) * LAYERS, width), F32)
    mine, far = call(
        functools.partial(pack_kernel, LAYERS),
        "pack_small",
        (),
        ins,
        [whole()] * len(ins),
        [vector_shape] * 2,
        [whole()] * 2,
    )
    vector = Everywhere(mine, far, bits)
    last = gate(last, [], [rest_0, up_0, down_0, rest_1, vector])
    last = gate(last, [], [rest_0, up_0, rest_1, vector])
    last = gate(last, [], [rest_0, up_0, vector])
    last = gate(last, [], [rest_0, vector])
    running = [down_1, up_1, rest_1, down_0, up_0, rest_0]
    while any(unit.incoming is not None for unit in running):
        last = gate(last, [], [unit for unit in running if unit.incoming is not None][:4])

    (down_1_sum,), (up_1_sum,) = down_1.results(), up_1.results()
    (down_0_sum,), (up_0_sum,) = down_0.results(), up_0.results()
    (both,), (first_both,) = rest_1.results(), rest_0.results()
    summed = [
        (
            first_both[:, : 3 * half].reshape(block, 3, half),
            first_both[:, 3 * half :].T,
            up_0_sum,
            down_0_sum.T,
        ),
        (
            both[:, : 3 * half].reshape(block, 3, half),
            both[:, 3 * half :].T,
            up_1_sum,
            down_1_sum.T,
        ),
    ]

    while vector.bits:
        vector.turn()
    mine, got = vector.mine, vector.incoming
    gain_grads, shift_grads, outb_grads, qv_grads, upb_grads = call(
        functools.partial(unpack_kernel, LAYERS),
        "unpack_small",
        (),
        [mine, got],
        [whole()] * 2,
        [
            out(ln_gain.shape, F32),
            out(ln_bias.shape, F32),
            out(out_bias.shape, F32),
            out(qv_bias.shape, F32),
            out(up_bias.shape, F32),
        ],
        [whole()] * 5,
    )
    stacked = [jnp.stack([summed[layer][member] for layer in range(LAYERS)]) for member in range(4)]
    return (
        stream.reshape(images.shape),
        pooled,
        grad.reshape(images.shape),
        gain_grads,
        shift_grads,
        stacked[0],
        qv_grads,
        stacked[1],
        outb_grads,
        stacked[2],
        upb_grads,
        stacked[3],
    )


def solution(mesh):
    placed = (
        P(("dp", "tensor"), None, None),
        P("dp"),
        P(),
        P(),
        P(None, None, None, "tensor"),
        P(None, None, "tensor"),
        P(None, "tensor", None),
        P(),
        P(None, None, "tensor"),
        P(None, "tensor"),
        P(None, "tensor", None),
        P(("dp", "tensor"), None, None),
    )
    return jax.shard_map(
        shards,
        mesh=mesh,
        in_specs=placed,
        out_specs=(
            P(("dp", "tensor"), None, None),
            P(("dp", "tensor"), None),
            P(("dp", "tensor"), None, None),
            P(),
            P(),
            P(None, "dp", None, "tensor"),
            P(None, None, "tensor"),
            P(None, "tensor", "dp"),
            P(),
            P(None, "dp", "tensor"),
            P(None, "tensor"),
            P(None, "tensor", "dp"),
        ),
        check_vma=False,
    )
```

```python
import functools
import math

import jax
import jax.numpy as jnp
from jax import lax
from jax.experimental import pallas as pl
from jax.experimental.pallas import tpu as pltpu
from jax.sharding import PartitionSpec as P

HEAD_DIM = 64
LAYERS = 2
EPSILON = 1e-06
NEGATIVE = -1e30
BF16 = jnp.bfloat16
F32 = jnp.float32
CHUNK = 16


def dot(left, right):
    return lax.dot_general(left, right, (((1,), (0,)), ((), ())), preferred_element_type=F32)


def dot_nt(left, right):
    return lax.dot_general(left, right, (((1,), (1,)), ((), ())), preferred_element_type=F32)


def fixed(shape, *lead):
    where = tuple(lead) + (0,) * (len(shape) - len(lead))
    return pl.BlockSpec(shape, lambda *_: where)


def out(shape, dtype):
    return jax.ShapeDtypeStruct(shape, dtype)


def in_hbm(values):
    return pltpu.with_memory_space_constraint(values, pltpu.HBM)


def cost(flops, *arrays):
    total = sum(math.prod(a.shape) * a.dtype.itemsize for a in arrays)
    return pl.CostEstimate(flops=int(flops) // 64, bytes_accessed=int(total) // 64, transcendentals=0)


MIB = 1 << 20


def call(body, name, grid, ins, in_specs, outs, out_specs, scratch=(), flops=0, limit=24):
    return pl.pallas_call(
        body,
        name=name,
        grid=grid,
        in_specs=in_specs,
        out_specs=out_specs,
        out_shape=outs,
        scratch_shapes=list(scratch),
        compiler_params=pltpu.CompilerParams(vmem_limit_bytes=limit * MIB),
        cost_estimate=cost(flops, *ins, *outs),
    )(*ins)


def whole():
    return pl.BlockSpec(memory_space=pltpu.VMEM)


def by_blocks(target, left, right, product, rows=256, add=False):
    def block(index, carry):
        here = pl.ds(pl.multiple_of(index * rows, rows), rows)
        value = product(left[here, :], right())
        if add:
            value = target[here, :] + value
        target[here, :] = value.astype(target.dtype)
        return carry

    lax.fori_loop(0, left.shape[0] // rows, block, 0)


def hbm():
    return pl.BlockSpec(memory_space=pltpu.HBM)


def by_rows(rows, body, unroll=1):
    def step(index, carry):
        for part in range(unroll):
            body(pl.multiple_of((index * unroll + part) * CHUNK, CHUNK))
        return carry

    lax.fori_loop(0, rows // (CHUNK * unroll), step, 0)


def moments(values):
    average = jnp.mean(values, axis=-1, keepdims=True)
    centred = values - average
    variance = jnp.mean(centred * centred, axis=-1, keepdims=True)
    return centred, lax.rsqrt(variance + EPSILON)


def normalized(values, gain, bias):
    centred, scale = moments(values)
    return centred * scale * gain + bias


def norm_backward(values, grad_normed, gain):
    centred, scale = moments(values)
    unit = centred * scale
    grad_unit = grad_normed * gain
    first = jnp.mean(grad_unit, axis=-1, keepdims=True)
    second = jnp.mean(grad_unit * unit, axis=-1, keepdims=True)
    return scale * (grad_unit - first - unit * second), grad_normed * unit


def fold_rows(values):
    total = values[0:8]
    for start in range(8, values.shape[0], 8):
        total = total + values[start : start + 8]
    return total


def prep_kernel(images, cotangent, gain, bias, order, normed, normed_t, cotangent_t, wide_cotangent):
    def rows(start):
        here = pl.ds(start, CHUNK)
        values = images[here, :].astype(F32)
        normed[here, :] = normalized(values, gain[0, 0:1, :], bias[0, 0:1, :]).astype(BF16)
        wide_cotangent[here, :] = cotangent[here, :].astype(F32)

    by_rows(images.shape[0], rows, 4)
    by_blocks(normed_t, order, lambda: normed[...], dot_nt)
    by_blocks(cotangent_t, order, lambda: cotangent[...], dot_nt)


def head_masks(slots):
    lane = lax.broadcasted_iota(jnp.int32, (slots, 2 * HEAD_DIM), 1)
    return lane < HEAD_DIM, lane >= HEAD_DIM


def own_count(counts, image, images):
    return counts[lax.axis_index("tensor") * images + image]


def attend_kernel(
    slots,
    which,
    counts,
    normed,
    weight_own,
    weight_far,
    bias_own,
    bias_far,
    joint_own,
    joint_far,
    att_own,
    att_far,
    lse_own,
    lse_far,
    held,
    sem,
):
    width = att_own.shape[1]
    pairs = width // (2 * HEAD_DIM)
    scale = HEAD_DIM ** (-0.5)
    layer = which[0]
    weights = (weight_own, weight_far)
    for side in range(2):
        for member in range(3):
            fetch(weights[side].at[layer, member], held.at[side, member], sem.at[side, member])
    for side, (joint, bias) in enumerate(((joint_own, bias_own), (joint_far, bias_far))):

        def project(member, carry):
            pltpu.make_async_copy(
                weights[side].at[layer, member], held.at[side, member], sem.at[side, member]
            ).wait()
            shift = bias[layer, pl.ds(member // 2, 1), :]
            shift = jnp.where(member == 1, jnp.zeros_like(shift), shift)
            joint[member] = (dot(normed[...], held[side, member]) + shift).astype(BF16)
            return carry

        lax.fori_loop(0, 3, project, 0)
    masks = head_masks(slots)
    key_index = lax.broadcasted_iota(jnp.int32, (slots, slots), 0)

    def step(index, carry):
        image = index // pairs
        pair = index % pairs
        rows = pl.ds(pl.multiple_of(image * slots, slots), slots)
        lanes = pl.ds(pl.multiple_of(pair * 2 * HEAD_DIM, 2 * HEAD_DIM), 2 * HEAD_DIM)
        valid = key_index < own_count(counts, image, normed.shape[0] // slots)
        for joint, attended, lse in (
            (joint_own, att_own, lse_own),
            (joint_far, att_far, lse_far),
        ):
            queries = joint[0, rows, lanes]
            keys_in = joint[1, rows, lanes] * jnp.asarray(scale, BF16)
            values_t = joint[2, rows, lanes].T
            parts = []
            for side in range(2):
                keys_side = jnp.where(masks[side], keys_in, jnp.zeros_like(keys_in))
                scores = jnp.where(valid, dot_nt(keys_side, queries), NEGATIVE)
                largest = jnp.max(scores, axis=0, keepdims=True)
                exponent = jnp.exp(scores - largest)
                total = jnp.sum(exponent, axis=0, keepdims=True)
                probs = (exponent * (1.0 / total)).astype(BF16)
                parts.append(dot(values_t[side * HEAD_DIM : (side + 1) * HEAD_DIM], probs))
                lse[2 * index + side] = largest + jnp.log(total)
            attended[rows, lanes] = jnp.concatenate(parts, axis=0).T.astype(BF16)
        return carry

    lax.fori_loop(0, (normed.shape[0] // slots) * pairs, step, 0)


def fetch(source, target, sem):
    copy = pltpu.make_async_copy(source, target, sem)
    copy.start()
    return copy


def feed_kernel(
    layer,
    slots,
    last_layer,
    counts,
    stream,
    att_own,
    att_far,
    out_own,
    out_far,
    out_bias,
    gain,
    bias,
    order,
    up_own,
    up_far,
    up_bias_own,
    up_bias_far,
    down_own,
    down_far,
    mid,
    normed_t,
    hid_own,
    hid_far,
    slope_own,
    slope_far,
    stream_out,
    *rest,
):
    if last_layer:
        pooled = rest[0]
    else:
        next_normed, next_t = rest[:2]
    normed, total, pre, w_out, w_up, w_down, hid, slope, in_sem, out_sem = rest[1 if last_layer else 2 :]
    tokens = stream.shape[0]
    half = w_out.shape[0] // 2
    units = w_up.shape[0]
    tile = w_up.shape[2]
    tiles = units // 2
    out_in = [
        fetch(ref.at[layer], w_out.at[pl.ds(side * half, half)], in_sem.at[side])
        for side, ref in enumerate((out_own, out_far))
    ]
    up_in, down_in = [], []
    for unit in range(units):
        side, part = unit // tiles, unit % tiles
        columns = pl.ds(part * tile, tile)
        up_ref, down_ref = ((up_own, down_own), (up_far, down_far))[side]
        up_in.append(fetch(up_ref.at[layer, :, columns], w_up.at[unit], in_sem.at[2 + unit]))
        down_in.append(
            fetch(down_ref.at[layer, columns, :], w_down.at[unit], in_sem.at[2 + units + unit])
        )
    for copy in out_in:
        copy.wait()
    total[...] = dot(jnp.concatenate([att_own[...], att_far[...]], axis=1), w_out[...])

    def enter(start):
        here = pl.ds(start, CHUNK)
        value = stream[here, :].astype(F32) + (total[here, :] + out_bias[layer, 0:1, :])
        mid[here, :] = value
        normed[here, :] = normalized(value, gain[layer, 1:2, :], bias[layer, 1:2, :]).astype(BF16)

    by_rows(tokens, enter, 4)
    up_in[0].wait()
    by_blocks(pre.at[0], normed, lambda: w_up[0], dot)
    by_blocks(normed_t, order, lambda: normed[...], dot_nt)
    rows = 128
    out_copies = []
    for unit in range(units):
        side, part = unit // tiles, unit % tiles
        shift = (up_bias_own, up_bias_far)[side][layer : layer + 1, part * tile : (part + 1) * tile]
        if unit + 1 < units:
            up_in[unit + 1].wait()
        if unit > 0:
            down_in[unit - 1].wait()

        def chunk(index, carry):
            block = pl.ds(pl.multiple_of(index * rows, rows), rows)
            if unit + 1 < units:
                pre[(unit + 1) % 2, block, :] = dot(normed[block, :], w_up[unit + 1])
            if unit == 1:
                total[block, :] = dot(hid[unit - 1, block, :], w_down[unit - 1])
            elif unit > 1:
                total[block, :] += dot(hid[unit - 1, block, :], w_down[unit - 1])
            for sub in range(0, rows, CHUNK):
                here = pl.ds(pl.multiple_of(index * rows + sub, CHUNK), CHUNK)
                value = pre[unit % 2, here, :] + shift
                cdf = 0.5 + 0.5 * lax.erf(value * (0.5**0.5))
                hid[unit, here, :] = (value * cdf).astype(BF16)
                density = jnp.exp(-0.5 * value * value) * ((2.0 * math.pi) ** -0.5)
                slope[unit, here, :] = (cdf + value * density).astype(BF16)
            return carry

        lax.fori_loop(0, tokens // rows, chunk, 0)
        hid_ref, slope_ref = ((hid_own, slope_own), (hid_far, slope_far))[side]
        columns = pl.ds(part * tile, tile)
        out_copies.append(fetch(hid.at[unit], hid_ref.at[:, columns], out_sem.at[unit]))
        out_copies.append(fetch(slope.at[unit], slope_ref.at[:, columns], out_sem.at[units + unit]))
    down_in[units - 1].wait()
    by_blocks(total, hid.at[units - 1], lambda: w_down[units - 1], dot, add=True)

    def leave(start):
        here = pl.ds(start, CHUNK)
        value = mid[here, :] + (total[here, :] + out_bias[layer, 1:2, :])
        stream_out[here, :] = value
        if not last_layer:
            next_normed[here, :] = normalized(
                value, gain[layer + 1, 0:1, :], bias[layer + 1, 0:1, :]
            ).astype(BF16)

    by_rows(tokens, leave, 4)
    if last_layer:
        index = lax.broadcasted_iota(jnp.int32, (slots, 1), 0)
        for image in range(tokens // slots):
            block = stream_out[image * slots : (image + 1) * slots, :]
            count = own_count(counts, image, tokens // slots)
            summed = jnp.sum(jnp.where(index < count, block, 0.0), axis=0, keepdims=True)
            pooled[image : image + 1, :] = summed / count.astype(F32)
    else:
        by_blocks(next_t, order, lambda: next_normed[...], dot_nt)
    for copy in out_copies:
        copy.wait()


def feed_back_kernel(
    which,
    grad_in,
    mid,
    gain,
    order,
    down_own,
    down_far,
    up_own,
    up_far,
    slope_own,
    slope_far,
    out_own,
    out_far,
    pre_own,
    pre_far,
    bias_own,
    bias_far,
    grad_mid,
    mid_t,
    att_own,
    att_far,
    sums,
    low,
    total,
    hidden,
    partial,
    w_down,
    w_up,
    slope,
    pre,
    w_out,
    in_sem,
    out_sem,
):
    layer = which[0]
    tokens = grad_in.shape[0]
    units = w_up.shape[0]
    tile = w_up.shape[2]
    tiles = units // 2
    down_in, up_in, slope_in = [], [], []
    for unit in range(units):
        columns = pl.ds(unit % tiles * tile, tile)
        down_ref, up_ref, slope_ref = ((down_far, up_far, slope_far), (down_own, up_own, slope_own))[
            unit // tiles
        ]
        down_in.append(fetch(down_ref.at[layer, columns, :], w_down.at[unit], in_sem.at[0, unit]))
        slope_in.append(fetch(slope_ref.at[:, columns], slope.at[unit], in_sem.at[1, unit]))
        up_in.append(fetch(up_ref.at[layer, :, columns], w_up.at[unit], in_sem.at[2, unit]))
    out_in = [
        fetch(ref.at[layer], w_out.at[side], in_sem.at[3, side])
        for side, ref in enumerate((out_far, out_own))
    ]
    partial[...] = jnp.zeros_like(partial)

    def enter(start):
        here = pl.ds(start, CHUNK)
        value = grad_in[here, :].astype(F32)
        low[here, :] = value.astype(BF16)
        partial[0] += fold_rows(value)

    by_rows(tokens, enter)
    down_in[0].wait()
    by_blocks(hidden.at[0], low, lambda: w_down[0], dot_nt)
    rows = 256
    total[...] = jnp.zeros_like(total)
    pre[units - 1] = jnp.zeros_like(pre[units - 1])
    pre_refs = (pre_far, pre_own)

    def result(unit, side):
        columns = pl.ds(pl.multiple_of(unit % tiles * tile, tile), tile)
        return pltpu.make_async_copy(pre.at[unit], pre_refs[side].at[:, columns], out_sem.at[unit])

    def turn(unit, carry):
        after = jnp.minimum(unit + 1, units - 1)
        before = jnp.maximum(unit - 1, 0)

        @pl.when(unit + 1 < units)
        def _():
            pltpu.make_async_copy(
                down_own.at[layer, pl.ds(0, tile), :], w_down.at[after], in_sem.at[0, after]
            ).wait()

        @pl.when(unit != 1)
        def _():
            pltpu.make_async_copy(
                up_own.at[layer, :, pl.ds(0, tile)], w_up.at[before], in_sem.at[2, before]
            ).wait()

        pltpu.make_async_copy(
            slope_own.at[:, pl.ds(0, tile)], slope.at[unit], in_sem.at[1, unit]
        ).wait()
        idle = (unit + units - 1) % units

        def chunk(index, carry):
            block = pl.ds(pl.multiple_of(index * rows, rows), rows)
            hidden[(unit + 1) % 2, block, :] = dot_nt(low[block, :], w_down[after])
            total[block, :] += dot_nt(pre[idle, block, :], w_up[before])
            for sub in range(0, rows, CHUNK):
                here = pl.ds(pl.multiple_of(index * rows + sub, CHUNK), CHUNK)
                value = hidden[unit % 2, here, :] * slope[unit, here, :].astype(F32)
                pre[unit, here, :] = value.astype(BF16)
                carry = carry + fold_rows(value)
            return carry

        summed = lax.fori_loop(0, tokens // rows, chunk, jnp.zeros((8, tile), F32))
        row = jnp.sum(summed, axis=0, keepdims=True)
        for side, bias in enumerate((bias_far, bias_own)):

            @pl.when(unit // tiles == side)
            def _():
                bias[pl.ds(unit % tiles, 1), :] = row
                result(unit, side).start()

        return carry

    lax.fori_loop(0, units, turn, 0)
    up_in[units - 1].wait()
    by_blocks(total, pre.at[units - 1], lambda: w_up[units - 1], dot_nt, add=True)

    def leave(start):
        here = pl.ds(start, CHUNK)
        normed_grad = total[here, :]
        through, gain_term = norm_backward(mid[here, :], normed_grad, gain[layer, 1:2, :])
        value = grad_in[here, :].astype(F32) + through
        grad_mid[here, :] = value
        low[here, :] = value.astype(BF16)
        partial[1] += fold_rows(value)
        partial[2] += fold_rows(gain_term)
        partial[3] += fold_rows(normed_grad)

    by_rows(tokens, leave, 2)
    sums[...] = jnp.sum(partial[...], axis=1)
    by_blocks(mid_t, order, lambda: low[...], dot_nt)
    for copy in out_in:
        copy.wait()
    by_blocks(att_far, low, lambda: w_out[0], dot_nt)
    by_blocks(att_own, low, lambda: w_out[1], dot_nt)
    for unit in range(units):
        result(unit, unit // tiles).wait()


def attend_back_kernel(slots, counts, joint, lse, grad_att, grad_joint, bias_sums):
    width = grad_att.shape[1]
    pairs = width // (2 * HEAD_DIM)
    scale = HEAD_DIM ** (-0.5)
    masks = head_masks(slots)
    key_index = lax.broadcasted_iota(jnp.int32, (slots, slots), 0)
    bias_sums[...] = jnp.zeros_like(bias_sums)

    def step(index, carry):
        image = index // pairs
        pair = index % pairs
        rows = pl.ds(pl.multiple_of(image * slots, slots), slots)
        lanes = pl.ds(pl.multiple_of(pair * 2 * HEAD_DIM, 2 * HEAD_DIM), 2 * HEAD_DIM)
        queries = joint[0, rows, lanes]
        keys_in = joint[1, rows, lanes]
        values_in = joint[2, rows, lanes]
        grads = grad_att[rows, lanes]
        keys_t = keys_in.T
        keys_scaled = keys_in * jnp.asarray(scale, BF16)
        valid = key_index < own_count(counts, image, grad_att.shape[0] // slots)
        zeros = jnp.zeros_like(keys_in)
        query_parts, key_parts, value_parts = [], [], []
        for side in range(2):
            keys_side = jnp.where(masks[side], keys_scaled, zeros)
            values_side = jnp.where(masks[side], values_in, zeros)
            scores = jnp.where(valid, dot_nt(keys_side, queries), NEGATIVE)
            probs = jnp.exp(scores - lse[2 * index + side])
            grad_probs = dot_nt(values_side, grads)
            inner = jnp.sum(grad_probs * probs, axis=0, keepdims=True)
            grad_scores = (probs * (grad_probs - inner)).astype(BF16)
            value_parts.append(dot(probs.astype(BF16), grads))
            key_parts.append(dot(grad_scores, queries))
            query_parts.append(dot(keys_t[side * HEAD_DIM : (side + 1) * HEAD_DIM], grad_scores))
        grad_queries = jnp.concatenate(query_parts, axis=0).T * scale
        grad_keys = jnp.where(masks[0], key_parts[0], key_parts[1]) * scale
        grad_values = jnp.where(masks[0], value_parts[0], value_parts[1])
        bias_sums[0:1, lanes] += jnp.sum(grad_queries, axis=0, keepdims=True)
        value_lanes = pl.ds(
            pl.multiple_of(width + pair * 2 * HEAD_DIM, 2 * HEAD_DIM), 2 * HEAD_DIM
        )
        bias_sums[0:1, value_lanes] += jnp.sum(grad_values, axis=0, keepdims=True)
        grad_joint[0, rows, lanes] = grad_queries.astype(BF16)
        grad_joint[1, rows, lanes] = grad_keys.astype(BF16)
        grad_joint[2, rows, lanes] = grad_values.astype(BF16)
        return carry

    lax.fori_loop(0, (grad_att.shape[0] // slots) * pairs, step, 0)


def entry_back_kernel(
    layer, with_low, joint_own, joint_far, weight_own, weight_far, stream, gain, grad_mid, order, *rest
):
    if with_low:
        grad_out, sums, low_t, total, partial, low = rest
    else:
        grad_out, sums, total, partial = rest
    member = pl.program_id(0)

    @pl.when(member == 0)
    def _():
        total[...] = jnp.zeros_like(total)
        partial[...] = jnp.zeros_like(partial)

    left = jnp.concatenate([joint_own[member], joint_far[member]], axis=1)
    right = jnp.concatenate([weight_own[0, 0], weight_far[0, 0]], axis=1)
    total[...] += dot_nt(left, right)

    def rows(start):
        here = pl.ds(start, CHUNK)
        normed_grad = total[here, :]
        through, gain_term = norm_backward(
            stream[here, :].astype(F32), normed_grad, gain[layer, 0:1, :]
        )
        value = grad_mid[here, :] + through
        grad_out[here, :] = value
        if with_low:
            low[here, :] = value.astype(BF16)
        partial[0] += fold_rows(gain_term)
        partial[1] += fold_rows(normed_grad)

    @pl.when(member == 2)
    def _():
        by_rows(stream.shape[0], rows, 2)
        sums[...] = jnp.sum(partial[...], axis=1)
        if with_low:
            by_blocks(low_t, order, lambda: low[...], dot_nt)


def pack_kernel(layers, *refs):
    ins, (own_out, far_out) = refs[:-2], refs[-2:]
    for layer in range(layers):
        sums_mid, sums_in, qv_own, qv_far, upb_own, upb_far = ins[6 * layer : 6 * layer + 6]
        tiles = upb_own.shape[0]
        for ref, qv, upb in ((own_out, qv_own, upb_own), (far_out, qv_far, upb_far)):
            for row, value in (
                (2 * layer, sums_in[0:1, :]),
                (2 * layer + 1, sums_mid[2:3, :]),
                (2 * (layers + layer), sums_in[1:2, :]),
                (2 * (layers + layer) + 1, sums_mid[3:4, :]),
                (2 * (2 * layers + layer), sums_mid[1:2, :]),
                (2 * (2 * layers + layer) + 1, sums_mid[0:1, :]),
                (6 * layers + layer, qv[...]),
            ):
                ref[row : row + 1, :] = value
            start = 7 * layers + tiles * layer
            ref[start : start + tiles, :] = upb[...]


def unpack_kernel(layers, mine, gain, bias, out_bias, qv, upb):
    total = mine[...]
    half = qv.shape[2]
    tiles = upb.shape[1] // mine.shape[1]
    width = mine.shape[1]
    for layer in range(layers):
        for norm in range(2):
            row = 2 * layer + norm
            gain[layer, norm : norm + 1, :] = total[row : row + 1]
            row += 2 * layers
            bias[layer, norm : norm + 1, :] = total[row : row + 1]
            row += 2 * layers
            out_bias[layer, norm : norm + 1, :] = total[row : row + 1]
        row = 6 * layers + layer
        for kind in range(2):
            qv[layer, kind : kind + 1, :] = total[row : row + 1, kind * half : (kind + 1) * half]
        row = 7 * layers + tiles * layer
        for part in range(tiles):
            upb[layer : layer + 1, part * width : (part + 1) * width] = total[
                row + part : row + part + 1
            ]


def finish_kernel(parts, *refs):
    layers = len(refs) // parts
    outs = refs[layers * parts :]
    for layer in range(layers):
        total = refs[layer * parts][...].astype(F32)
        for ref in refs[layer * parts + 1 : (layer + 1) * parts]:
            total = total + ref[...].astype(F32)
        column = 0
        for ref in outs:
            size = ref.shape[3]
            for member in range(ref.shape[1]):
                ref[layer, member] = total[:, column : column + size]
                column += size


def chunk_sources(order):
    first = list(order[:4])
    sources = []
    for target in range(16):
        source = 0
        for place, bit in enumerate(first):
            if (target >> (3 - place)) & 1:
                source |= 1 << (3 - bit)
        sources.append(source)
    return sources


def weight_kernel(sources, tiles, has_extra, *refs):
    if has_extra:
        left_own, left_far, right_own, right_far, lx_own, lx_far, rx_own, rx_far, keep, send = refs
    else:
        left_own, left_far, right_own, right_far, keep, send = refs

    def product(a_own, a_far, b_own, b_far):
        left = jnp.concatenate([a_own[...], a_far[...]], axis=1)
        right = jnp.concatenate([b_own[...].reshape(b_own.shape[-2:]), b_far[...].reshape(b_far.shape[-2:])], axis=0)
        size = left.shape[0] // 16
        low = dot(left, right).astype(BF16)
        for target, source in enumerate(sources):
            ref = keep if target < 8 else send
            ref[(target % 8) * size : (target % 8 + 1) * size, :] = low[
                source * size : (source + 1) * size, :
            ]

    if has_extra:

        @pl.when(pl.program_id(0) < tiles)
        def _():
            product(left_own, left_far, right_own, right_far)

        @pl.when(pl.program_id(0) == tiles)
        def _():
            product(lx_own, lx_far, rx_own, rx_far)

    else:
        product(left_own, left_far, right_own, right_far)


def weight_grad(name, order, left, right, extra=None, tiles=None, first=0):
    left_own, left_far = left
    right_own, right_far = right
    width, tokens = left_own.shape
    if right_own.ndim == 3:
        tile = right_own.shape[2]
        right_spec = pl.BlockSpec(
            (1, tokens, tile), lambda j: (jnp.minimum(j, tiles - 1) + first, 0, 0)
        )
    else:
        tile = 768 if tiles else 512
        tiles = tiles or right_own.shape[1] // tile
        right_spec = pl.BlockSpec((tokens, tile), lambda j: (0, j + first))
    steps = tiles + (1 if extra is not None else 0)
    ins = [left_own, left_far, right_own, right_far]
    specs = [fixed((width, tokens))] * 2 + [right_spec] * 2
    if extra is not None:
        ins += list(extra)
        specs += [fixed((width, tokens))] * 2 + [fixed((tokens, tile))] * 2
    half = out((width // 2, steps * tile), BF16)
    half_spec = pl.BlockSpec((width // 2, tile), lambda j: (0, j))
    return call(
        functools.partial(weight_kernel, chunk_sources(order), tiles, extra is not None),
        name,
        (steps,),
        ins,
        specs,
        [half, half],
        [half_spec, half_spec],
        flops=4 * width * tokens * steps * tile,
    )


def flip(bit):
    size = lax.axis_size("dp")
    return [(index, index ^ (1 << bit)) for index in range(size)]


class DpSum:
    def __init__(self, order, halves=None, units=()):
        self.order = list(order)
        self.incoming = None
        if halves is not None:
            keep, self.outgoing = halves
            self.members = [[keep]]
        else:
            self.members = [parts for unit in units for parts in unit.members]
            self.halve()

    def halve(self):
        rows = self.members[0][0].shape[0] // 2
        sends = [
            sum(part[rows:].astype(F32) for part in parts).astype(BF16) for parts in self.members
        ]
        self.outgoing = sends[0] if len(sends) == 1 else jnp.concatenate(sends, axis=1)
        self.members = [[part[:rows] for part in parts] for parts in self.members]

    def start(self):
        self.incoming = lax.ppermute(self.outgoing, "dp", flip(self.order.pop(0)))

    def turn(self, go=True):
        column = 0
        for parts in self.members:
            width = parts[0].shape[1]
            parts.append(self.incoming[:, column : column + width])
            column += width
        self.incoming = None
        if self.order:
            self.halve()
            if go:
                self.start()

    def flying(self):
        return [self.incoming]

    def land(self, arrays):
        (self.incoming,) = arrays


class Everywhere:
    def __init__(self, mine, far, groups):
        self.mine = mine
        self.incoming = [swap(far)]
        self.groups = list(groups)

    def flying(self):
        return self.incoming

    def land(self, arrays):
        self.incoming = arrays

    def turn(self):
        if len(self.incoming) == 1:
            self.mine = self.mine + self.incoming[0]
        else:
            near, far, across = self.incoming
            self.mine = (self.mine + near) + (far + across)
        self.incoming = []
        if self.groups:
            group = self.groups.pop(0)
            masks = [1 << bit for bit in group]
            if len(masks) == 2:
                masks.append(masks[0] | masks[1])
            size = lax.axis_size("dp")
            self.incoming = [
                lax.ppermute(self.mine, "dp", [(index, index ^ mask) for index in range(size)])
                for mask in masks
            ]


def gate(value, starts=(), turns=(), after=(), holds=()):
    ends = [*turns, *holds]
    held = [unit.outgoing for unit in starts] + [array for unit in ends for array in unit.flying()]
    value, *held = lax.optimization_barrier((value, *held, *after))
    for unit in starts:
        unit.outgoing = held.pop(0)
        unit.start()
    for unit in ends:
        unit.land([held.pop(0) for _ in unit.flying()])
    for unit in turns:
        unit.turn()
    for unit in holds:
        unit.turn(go=False)
    return value


def swap(values):
    return lax.ppermute(values, "tensor", [(0, 1), (1, 0)])


def shards(
    images,
    valid_count,
    ln_gain,
    ln_bias,
    w_qkv,
    qv_bias,
    w_out,
    out_bias,
    w_up,
    up_bias,
    w_down,
    cotangent,
):
    local_rows, slots, width = images.shape
    tokens = local_rows * slots
    half = w_qkv.shape[3]
    ff_half = w_up.shape[2]
    tile = 768
    steps = ff_half // tile
    heads = half // HEAD_DIM
    dp = lax.axis_size("dp")
    bits = dp.bit_length() - 1
    assert dp == 1 << bits and bits >= 4 and lax.axis_size("tensor") == 2
    tail = tuple(range(4, bits))
    order_a = (0, 1, 2, 3) + tail
    order_b = (1, 0, 2, 3) + tail
    order_e = (2, 0, 1, 3) + tail
    order_d = (0, 2, 3, 1) + tail

    me = lax.axis_index("dp")
    counts = valid_count

    block = width // dp
    row = jnp.arange(width, dtype=jnp.int32)
    index = row // block
    mirrored = jnp.zeros_like(index)
    for bit in range(bits):
        mirrored = mirrored | (((index >> (bits - 1 - bit)) & 1) << bit)
    source = (mirrored ^ me) * block + row % block
    order = (source[:, None] == row[None, :]).astype(BF16)

    w_qkv = jnp.transpose(w_qkv, (0, 2, 1, 3))
    qkv = (w_qkv, swap(w_qkv))
    qv = (qv_bias, swap(qv_bias))

    images_2d = images.reshape(tokens, width)
    cotangent_2d = cotangent.reshape(tokens, width)
    smem = pl.BlockSpec(memory_space=pltpu.SMEM)
    wide = (tokens, width)
    flops_wide = 2 * width * width * tokens

    normed, normed_t, cotangent_t, wide_cotangent = call(
        prep_kernel,
        "prep",
        (),
        [images_2d, cotangent_2d, ln_gain, ln_bias, order],
        [whole()] * 5,
        [out(wide, BF16), out((width, tokens), BF16), out((width, tokens), BF16), out(wide, F32)],
        [whole()] * 4,
        flops=2 * flops_wide,
    )

    wout, wup, wdown = [
        (weight, swap(lax.optimization_barrier((weight, normed, qkv[1], qv[1]))[0]))
        for weight in (w_out, w_up, w_down)
    ]

    def attend(layer, normed, counts):
        lse_shape = (local_rows * heads, 1, slots)
        joint_out = out((3, tokens, half), BF16)
        att_out = out((tokens, half), BF16)
        lse_out = out(lse_shape, F32)
        results = call(
            functools.partial(attend_kernel, slots),
            "attend",
            (),
            [jnp.full((1,), layer, jnp.int32), counts, normed, in_hbm(qkv[0]), in_hbm(qkv[1]), qv[0], qv[1]],
            [smem, smem, whole(), hbm(), hbm(), whole(), whole()],
            [joint_out, joint_out, att_out, att_out, lse_out, lse_out],
            [whole()] * 6,
            [pltpu.VMEM((2, 3, width, half), BF16), pltpu.SemaphoreType.DMA((2, 3))],
            flops=12 * tokens * width * half + 8 * tokens * slots * half,
            limit=44,
        )
        return results[0::2], results[1::2]

    stream = images_2d
    saved = []
    got_cotangent_t = swap(cotangent_t)
    pooled = None
    for layer in range(LAYERS):
        last = layer == LAYERS - 1
        own, far = attend(layer, normed, counts)
        if layer == 0:
            upb = (up_bias, swap(up_bias))
        gain_in = ln_gain
        if layer > 0:
            before = saved[layer - 1]
            names = ("got_normed_t", "got_att", "got_mid_normed_t", "got_hid")
            gain_in, got_cotangent_t, *got = lax.optimization_barrier(
                (ln_gain, got_cotangent_t, *[before[name] for name in names])
            )
            before.update(zip(names, got))
        ff = pltpu.HBM((tokens, ff_half), BF16)
        extra = (
            [out((local_rows, width), F32)]
            if last
            else [out(wide, BF16), out((width, tokens), BF16)]
        )
        results = call(
            functools.partial(feed_kernel, layer, slots, last),
            "feed",
            (),
            [
                counts,
                stream,
                own[1],
                far[1],
                in_hbm(wout[0]),
                in_hbm(wout[1]),
                out_bias,
                gain_in,
                ln_bias,
                order,
                in_hbm(wup[0]),
                in_hbm(wup[1]),
                upb[0],
                upb[1],
                in_hbm(wdown[0]),
                in_hbm(wdown[1]),
            ],
            [smem]
            + [whole()] * 3
            + [hbm()] * 2
            + [whole()] * 4
            + [hbm()] * 2
            + [whole()] * 2
            + [hbm()] * 2,
            [out(wide, F32), out((width, tokens), BF16), ff, ff, ff, ff, out(wide, F32)] + extra,
            [whole()] * 2 + [hbm()] * 4 + [whole()] * (1 + len(extra)),
            [
                pltpu.VMEM(wide, BF16),
                pltpu.VMEM(wide, F32),
                pltpu.VMEM((2, tokens, tile), F32),
                pltpu.VMEM((2 * half, width), BF16),
                pltpu.VMEM((2 * steps, width, tile), BF16),
                pltpu.VMEM((2 * steps, tile, width), BF16),
                pltpu.VMEM((2 * steps, tokens, tile), BF16),
                pltpu.VMEM((2 * steps, tokens, tile), BF16),
                pltpu.SemaphoreType.DMA((2 + 4 * steps,)),
                pltpu.SemaphoreType.DMA((4 * steps,)),
            ],
            flops=8 * tokens * width * ff_half + 2 * flops_wide,
            limit=32,
        )
        mid, mid_normed_t, hid_own, hid_far, slope_own, slope_far, stream_next = results[:7]
        saved.append(
            dict(
                stream=stream,
                own=own,
                far=far,
                mid=mid,
                slope=(slope_own, slope_far),
                hid=hid_own,
                attended=own[1],
                normed_t=normed_t,
                mid_normed_t=mid_normed_t,
                got_hid=swap(hid_far),
                got_att=swap(far[1]),
                got_normed_t=swap(normed_t),
                got_mid_normed_t=swap(mid_normed_t),
            )
        )
        stream = stream_next
        if last:
            pooled = results[7]
        else:
            normed, normed_t = results[7:9]

    def feed_back(layer, grad, gain_in):
        kept = saved[layer]
        ff = pltpu.HBM((tokens, ff_half), BF16)
        bias_shape = out((steps, tile), F32)
        att_shape = out((tokens, half), BF16)
        return call(
            feed_back_kernel,
            "feed_back",
            (),
            [
                jnp.full((1,), layer, jnp.int32),
                grad,
                kept["mid"],
                gain_in,
                order,
                in_hbm(wdown[0]),
                in_hbm(wdown[1]),
                in_hbm(wup[0]),
                in_hbm(wup[1]),
                kept["slope"][0],
                kept["slope"][1],
                in_hbm(wout[0]),
                in_hbm(wout[1]),
            ],
            [smem] + [whole()] * 4 + [hbm()] * 8,
            [
                ff,
                ff,
                bias_shape,
                bias_shape,
                out(wide, F32),
                out((width, tokens), BF16),
                att_shape,
                att_shape,
                out((4, width), F32),
            ],
            [hbm()] * 2 + [whole()] * 7,
            [
                pltpu.VMEM(wide, BF16),
                pltpu.VMEM(wide, F32),
                pltpu.VMEM((2, tokens, tile), F32),
                pltpu.VMEM((4, 8, width), F32),
                pltpu.VMEM((2 * steps, tile, width), BF16),
                pltpu.VMEM((2 * steps, width, tile), BF16),
                pltpu.VMEM((2 * steps, tokens, tile), BF16),
                pltpu.VMEM((2 * steps, tokens, tile), BF16),
                pltpu.VMEM((2, half, width), BF16),
                pltpu.SemaphoreType.DMA((4, 2 * steps)),
                pltpu.SemaphoreType.DMA((2 * steps,)),
            ],
            flops=8 * tokens * width * ff_half + 2 * flops_wide,
            limit=32,
        )

    def attend_back(forward, grad_att, counts_in):
        joint, _, lse = forward
        return call(
            functools.partial(attend_back_kernel, slots),
            "attend_back",
            (),
            [counts_in, joint, lse, grad_att],
            [smem, whole(), whole(), whole()],
            [out(joint.shape, BF16), out((1, 2 * half), F32)],
            [whole()] * 2,
            flops=10 * tokens * slots * half,
        )

    def entry_back(layer, joint_own, joint_far, grad_mid, gain_in):
        with_low = layer > 0
        return call(
            functools.partial(entry_back_kernel, layer, with_low),
            "entry_back",
            (3,),
            [
                joint_own,
                joint_far,
                in_hbm(qkv[0]),
                in_hbm(qkv[1]),
                saved[layer]["stream"],
                gain_in,
                grad_mid,
                order,
            ],
            [whole()] * 2
            + [pl.BlockSpec((1, 1, width, half), lambda c: (layer, c, 0, 0))] * 2
            + [whole()] * 4,
            [out(wide, F32), out((2, width), F32)]
            + ([out((width, tokens), BF16)] if with_low else []),
            [whole()] * (3 if with_low else 2),
            [pltpu.VMEM(wide, F32), pltpu.VMEM((2, 8, width), F32)]
            + ([pltpu.VMEM(wide, BF16)] if with_low else []),
            flops=12 * tokens * width * half,
        )

    def down_halves(layer, order_of, grad_t, got_grad_t):
        kept = saved[layer]
        return weight_grad(
            "down_grad", order_of, (grad_t, got_grad_t), (in_hbm(kept["hid"]), kept["got_hid"])
        )

    def up_halves(layer, order_of, pre_own, got_pre, tiles=None, first=0):
        kept = saved[layer]
        return weight_grad(
            "up_grad",
            order_of,
            (kept["mid_normed_t"], kept["got_mid_normed_t"]),
            (pre_own, got_pre),
            tiles=tiles,
            first=first,
        )

    def lefts(layer):
        return saved[layer]["normed_t"], saved[layer]["got_normed_t"]

    def extras(layer, mid_t, got_mid_t):
        return mid_t, got_mid_t, saved[layer]["attended"], saved[layer]["got_att"]

    small = [None] * LAYERS
    down_1 = DpSum(order_a, down_halves(1, order_a, cotangent_t, got_cotangent_t))
    gain_in = gate(ln_gain, [down_1])
    pre_own, pre_far, upb_own, upb_far, grad_mid, mid_t, att_own, att_far, sums_mid = feed_back(
        1, wide_cotangent, gain_in
    )
    got_pre, got_mid_t = swap(pre_far), swap(mid_t)
    joint_far, qv_far = attend_back(saved[1]["far"], att_far, counts)
    got_joint = swap(joint_far)
    counts_in = gate(counts, [], [down_1], [qv_far])
    joint_own, qv_own = attend_back(saved[1]["own"], att_own, counts_in)
    pre_own = gate(pre_own, after=[qv_own])
    up_1 = DpSum(order_a, up_halves(1, order_a, pre_own, got_pre))
    gain_in = gate(gain_in, [up_1])
    grad, sums_in, grad_t = entry_back(1, joint_own, joint_far, grad_mid, gain_in)
    got_grad_t = swap(grad_t)
    small[1] = (sums_mid, sums_in, qv_own, qv_far, upb_own, upb_far)
    joint_own = gate(joint_own, [], [down_1], [sums_in])
    rest_1 = DpSum(
        order_e,
        weight_grad(
            "qkv_out_grad",
            order_e,
            lefts(1),
            (joint_own, got_joint),
            extras(1, mid_t, got_mid_t),
            tiles=3,
        ),
    )
    grad_t = gate(grad_t, [rest_1])
    down_0 = DpSum(order_a, down_halves(0, order_a, grad_t, got_grad_t))

    gain_in = gate(gain_in, [down_0], [up_1], holds=[down_1])
    pre_own, pre_far, upb_own, upb_far, grad_mid, mid_t, att_own, att_far, sums_mid = feed_back(
        0, grad, gain_in
    )
    got_pre, got_mid_t = swap(pre_far), swap(mid_t)
    counts_in = gate(counts_in, [], [], [sums_mid], [up_1, rest_1])
    joint_far, qv_far = attend_back(saved[0]["far"], att_far, counts_in)
    got_joint = swap(joint_far)
    pre_own = gate(pre_own, [down_1, up_1], [down_0], [qv_far])
    up_0 = DpSum(order_d, up_halves(0, order_d, pre_own, got_pre))
    counts_in = gate(counts_in, [up_0], [], [got_mid_t, got_joint])
    joint_own, qv_own = attend_back(saved[0]["own"], att_own, counts_in)
    rest_0 = DpSum(
        order_b,
        weight_grad(
            "qkv_out_grad",
            order_b,
            lefts(0),
            (joint_own, got_joint),
            extras(0, mid_t, got_mid_t),
            tiles=3,
        ),
    )
    gain_in = gate(gain_in, [rest_0], [down_0, up_1, down_1], [qv_own])
    grad, sums_in = entry_back(0, joint_own, joint_far, grad_mid, gain_in)
    last = gate(sums_in, [rest_1], [up_0, down_0, up_1])
    small[0] = (sums_mid, last, qv_own, qv_far, upb_own, upb_far)
    ins = [array for arrays in small for array in arrays]
    vector_shape = out(((7 + steps) * LAYERS, width), F32)
    mine, far = call(
        functools.partial(pack_kernel, LAYERS),
        "pack_small",
        (),
        ins,
        [whole()] * len(ins),
        [vector_shape] * 2,
        [whole()] * 2,
    )
    vector = Everywhere(mine, far, [(1,), (0,), (2, 3), *[(bit,) for bit in tail]])
    last = gate(last, [], [rest_0, up_0, down_0, rest_1, vector])
    last = gate(last, [], [rest_0, up_0, rest_1, vector])
    last = gate(last, [], [rest_0, up_0, rest_1, vector])
    last = gate(last, [], [rest_0, vector])
    while vector.flying():
        vector.turn()
    running = [down_1, up_1, rest_1, down_0, up_0, rest_0]
    while any(unit.incoming is not None for unit in running):
        last = gate(last, [], [unit for unit in running if unit.incoming is not None][:4])

    def finish(first, second, shapes):
        ins = [*first.members[0], *second.members[0]]
        return call(
            functools.partial(finish_kernel, len(first.members[0])),
            "finish",
            (),
            ins,
            [whole()] * len(ins),
            [out((LAYERS,) + shape, F32) for shape in shapes],
            [whole()] * len(shapes),
        )

    (down_grad,) = finish(down_0, down_1, [(1, block, ff_half)])
    (up_grad,) = finish(up_0, up_1, [(1, block, ff_half)])
    qkv_grad, out_grad = finish(rest_0, rest_1, [(3, block, half), (1, block, half)])
    gain_grads, shift_grads, outb_grads, qv_grads, upb_grads = call(
        functools.partial(unpack_kernel, LAYERS),
        "unpack_small",
        (),
        [vector.mine],
        [whole()],
        [
            out(ln_gain.shape, F32),
            out(ln_bias.shape, F32),
            out(out_bias.shape, F32),
            out(qv_bias.shape, F32),
            out(up_bias.shape, F32),
        ],
        [whole()] * 5,
    )
    return (
        stream.reshape(images.shape),
        pooled,
        grad.reshape(images.shape),
        gain_grads,
        shift_grads,
        jnp.transpose(qkv_grad, (0, 2, 1, 3)),
        qv_grads,
        jnp.transpose(out_grad[:, 0], (0, 2, 1)),
        outb_grads,
        up_grad[:, 0],
        upb_grads,
        jnp.transpose(down_grad[:, 0], (0, 2, 1)),
    )


def solution(mesh):
    placed = (
        P(("dp", "tensor"), None, None),
        P("dp"),
        P(),
        P(),
        P(None, None, None, "tensor"),
        P(None, None, "tensor"),
        P(None, "tensor", None),
        P(),
        P(None, None, "tensor"),
        P(None, "tensor"),
        P(None, "tensor", None),
        P(("dp", "tensor"), None, None),
    )
    return jax.shard_map(
        shards,
        mesh=mesh,
        in_specs=placed,
        out_specs=(
            P(("dp", "tensor"), None, None),
            P(("dp", "tensor"), None),
            P(("dp", "tensor"), None, None),
            P(),
            P(),
            P(None, "dp", None, "tensor"),
            P(None, None, "tensor"),
            P(None, "tensor", "dp"),
            P(),
            P(None, "dp", "tensor"),
            P(None, "tensor"),
            P(None, "tensor", "dp"),
        ),
        check_vma=False,
    )
```

```python
import functools
import math

import jax
import jax.numpy as jnp
from jax import lax
from jax.experimental import pallas as pl
from jax.experimental.pallas import tpu as pltpu
from jax.sharding import PartitionSpec as P

HEAD_DIM = 64
LAYERS = 2
EPSILON = 1e-06
NEGATIVE = -1e30
BF16 = jnp.bfloat16
F32 = jnp.float32
CHUNK = 16


def dot(left, right):
    return lax.dot_general(left, right, (((1,), (0,)), ((), ())), preferred_element_type=F32)


def dot_nt(left, right):
    return lax.dot_general(left, right, (((1,), (1,)), ((), ())), preferred_element_type=F32)


def fixed(shape, *lead):
    where = tuple(lead) + (0,) * (len(shape) - len(lead))
    return pl.BlockSpec(shape, lambda *_: where)


def out(shape, dtype):
    return jax.ShapeDtypeStruct(shape, dtype)


def in_hbm(values):
    return pltpu.with_memory_space_constraint(values, pltpu.HBM)


def cost(flops, *arrays):
    total = sum(math.prod(a.shape) * a.dtype.itemsize for a in arrays)
    return pl.CostEstimate(flops=int(flops) // 64, bytes_accessed=int(total) // 64, transcendentals=0)


MIB = 1 << 20


def call(body, name, grid, ins, in_specs, outs, out_specs, scratch=(), flops=0, limit=24):
    return pl.pallas_call(
        body,
        name=name,
        grid=grid,
        in_specs=in_specs,
        out_specs=out_specs,
        out_shape=outs,
        scratch_shapes=list(scratch),
        compiler_params=pltpu.CompilerParams(vmem_limit_bytes=limit * MIB),
        cost_estimate=cost(flops, *ins, *outs),
    )(*ins)


def whole():
    return pl.BlockSpec(memory_space=pltpu.VMEM)


def by_blocks(target, left, right, product, rows=256, add=False):
    def block(index, carry):
        here = pl.ds(pl.multiple_of(index * rows, rows), rows)
        value = product(left[here, :], right())
        if add:
            value = target[here, :] + value
        target[here, :] = value.astype(target.dtype)
        return carry

    lax.fori_loop(0, left.shape[0] // rows, block, 0)


def hbm():
    return pl.BlockSpec(memory_space=pltpu.HBM)


def by_rows(rows, body, unroll=1):
    def step(index, carry):
        for part in range(unroll):
            body(pl.multiple_of((index * unroll + part) * CHUNK, CHUNK))
        return carry

    lax.fori_loop(0, rows // (CHUNK * unroll), step, 0)


def moments(values):
    average = jnp.mean(values, axis=-1, keepdims=True)
    centred = values - average
    variance = jnp.mean(centred * centred, axis=-1, keepdims=True)
    return centred, lax.rsqrt(variance + EPSILON)


def normalized(values, gain, bias):
    centred, scale = moments(values)
    return centred * scale * gain + bias


def norm_backward(values, grad_normed, gain):
    centred, scale = moments(values)
    unit = centred * scale
    grad_unit = grad_normed * gain
    first = jnp.mean(grad_unit, axis=-1, keepdims=True)
    second = jnp.mean(grad_unit * unit, axis=-1, keepdims=True)
    return scale * (grad_unit - first - unit * second), grad_normed * unit


def fold_rows(values):
    total = values[0:8]
    for start in range(8, values.shape[0], 8):
        total = total + values[start : start + 8]
    return total


def prep_kernel(images, cotangent, gain, bias, order, normed, normed_t, cotangent_t, wide_cotangent):
    def rows(start):
        here = pl.ds(start, CHUNK)
        values = images[here, :].astype(F32)
        normed[here, :] = normalized(values, gain[0, 0:1, :], bias[0, 0:1, :]).astype(BF16)
        wide_cotangent[here, :] = cotangent[here, :].astype(F32)

    by_rows(images.shape[0], rows, 4)
    by_blocks(normed_t, order, lambda: normed[...], dot_nt)
    by_blocks(cotangent_t, order, lambda: cotangent[...], dot_nt)


def head_masks(slots):
    lane = lax.broadcasted_iota(jnp.int32, (slots, 2 * HEAD_DIM), 1)
    return lane < HEAD_DIM, lane >= HEAD_DIM


def own_count(counts, image, images):
    return counts[lax.axis_index("tensor") * images + image]


def attend_kernel(
    slots,
    which,
    counts,
    normed,
    weight_own,
    weight_far,
    bias_own,
    bias_far,
    joint_own,
    joint_far,
    att_own,
    att_far,
    lse_own,
    lse_far,
    held,
    sem,
):
    width = att_own.shape[1]
    pairs = width // (2 * HEAD_DIM)
    scale = HEAD_DIM ** (-0.5)
    layer = which[0]
    weights = (weight_own, weight_far)
    for side in range(2):
        for member in range(3):
            fetch(weights[side].at[layer, member], held.at[side, member], sem.at[side, member])
    for side, (joint, bias) in enumerate(((joint_own, bias_own), (joint_far, bias_far))):

        def project(member, carry):
            pltpu.make_async_copy(
                weights[side].at[layer, member], held.at[side, member], sem.at[side, member]
            ).wait()
            shift = bias[layer, pl.ds(member // 2, 1), :]
            shift = jnp.where(member == 1, jnp.zeros_like(shift), shift)
            joint[member] = (dot(normed[...], held[side, member]) + shift).astype(BF16)
            return carry

        lax.fori_loop(0, 3, project, 0)
    masks = head_masks(slots)
    key_index = lax.broadcasted_iota(jnp.int32, (slots, slots), 0)

    def step(index, carry):
        image = index // pairs
        pair = index % pairs
        rows = pl.ds(pl.multiple_of(image * slots, slots), slots)
        lanes = pl.ds(pl.multiple_of(pair * 2 * HEAD_DIM, 2 * HEAD_DIM), 2 * HEAD_DIM)
        valid = key_index < own_count(counts, image, normed.shape[0] // slots)
        for joint, attended, lse in (
            (joint_own, att_own, lse_own),
            (joint_far, att_far, lse_far),
        ):
            queries = joint[0, rows, lanes]
            keys_in = joint[1, rows, lanes] * jnp.asarray(scale, BF16)
            values_t = joint[2, rows, lanes].T
            parts = []
            for side in range(2):
                keys_side = jnp.where(masks[side], keys_in, jnp.zeros_like(keys_in))
                scores = jnp.where(valid, dot_nt(keys_side, queries), NEGATIVE)
                largest = jnp.max(scores, axis=0, keepdims=True)
                exponent = jnp.exp(scores - largest)
                total = jnp.sum(exponent, axis=0, keepdims=True)
                probs = (exponent * (1.0 / total)).astype(BF16)
                parts.append(dot(values_t[side * HEAD_DIM : (side + 1) * HEAD_DIM], probs))
                lse[2 * index + side] = largest + jnp.log(total)
            attended[rows, lanes] = jnp.concatenate(parts, axis=0).T.astype(BF16)
        return carry

    lax.fori_loop(0, (normed.shape[0] // slots) * pairs, step, 0)


def fetch(source, target, sem):
    copy = pltpu.make_async_copy(source, target, sem)
    copy.start()
    return copy


def feed_kernel(
    layer,
    slots,
    last_layer,
    counts,
    stream,
    att_own,
    att_far,
    out_own,
    out_far,
    out_bias,
    gain,
    bias,
    order,
    up_own,
    up_far,
    up_bias_own,
    up_bias_far,
    down_own,
    down_far,
    mid,
    normed_t,
    hid_own,
    hid_far,
    slope_own,
    slope_far,
    stream_out,
    *rest,
):
    if last_layer:
        pooled = rest[0]
    else:
        next_normed, next_t = rest[:2]
    normed, total, pre, w_out, w_up, w_down, hid, slope, in_sem, out_sem = rest[1 if last_layer else 2 :]
    tokens = stream.shape[0]
    half = w_out.shape[0] // 2
    units = w_up.shape[0]
    tile = w_up.shape[2]
    tiles = units // 2
    out_in = [
        fetch(ref.at[layer], w_out.at[pl.ds(side * half, half)], in_sem.at[side])
        for side, ref in enumerate((out_own, out_far))
    ]
    up_in, down_in = [], []
    for unit in range(units):
        side, part = unit // tiles, unit % tiles
        columns = pl.ds(part * tile, tile)
        up_ref, down_ref = ((up_own, down_own), (up_far, down_far))[side]
        up_in.append(fetch(up_ref.at[layer, :, columns], w_up.at[unit], in_sem.at[2 + unit]))
        down_in.append(
            fetch(down_ref.at[layer, columns, :], w_down.at[unit], in_sem.at[2 + units + unit])
        )
    for copy in out_in:
        copy.wait()
    total[...] = dot(jnp.concatenate([att_own[...], att_far[...]], axis=1), w_out[...])

    def enter(start):
        here = pl.ds(start, CHUNK)
        value = stream[here, :].astype(F32) + (total[here, :] + out_bias[layer, 0:1, :])
        mid[here, :] = value
        normed[here, :] = normalized(value, gain[layer, 1:2, :], bias[layer, 1:2, :]).astype(BF16)

    by_rows(tokens, enter, 4)
    up_in[0].wait()
    by_blocks(pre.at[0], normed, lambda: w_up[0], dot)
    by_blocks(normed_t, order, lambda: normed[...], dot_nt)
    rows = 128
    out_copies = []
    for unit in range(units):
        side, part = unit // tiles, unit % tiles
        shift = (up_bias_own, up_bias_far)[side][layer : layer + 1, part * tile : (part + 1) * tile]
        if unit + 1 < units:
            up_in[unit + 1].wait()
        if unit > 0:
            down_in[unit - 1].wait()

        def chunk(index, carry):
            block = pl.ds(pl.multiple_of(index * rows, rows), rows)
            if unit + 1 < units:
                pre[(unit + 1) % 2, block, :] = dot(normed[block, :], w_up[unit + 1])
            if unit == 1:
                total[block, :] = dot(hid[unit - 1, block, :], w_down[unit - 1])
            elif unit > 1:
                total[block, :] += dot(hid[unit - 1, block, :], w_down[unit - 1])
            for sub in range(0, rows, CHUNK):
                here = pl.ds(pl.multiple_of(index * rows + sub, CHUNK), CHUNK)
                value = pre[unit % 2, here, :] + shift
                cdf = 0.5 + 0.5 * lax.erf(value * (0.5**0.5))
                hid[unit, here, :] = (value * cdf).astype(BF16)
                density = jnp.exp(-0.5 * value * value) * ((2.0 * math.pi) ** -0.5)
                slope[unit, here, :] = (cdf + value * density).astype(BF16)
            return carry

        lax.fori_loop(0, tokens // rows, chunk, 0)
        hid_ref, slope_ref = ((hid_own, slope_own), (hid_far, slope_far))[side]
        columns = pl.ds(part * tile, tile)
        out_copies.append(fetch(hid.at[unit], hid_ref.at[:, columns], out_sem.at[unit]))
        out_copies.append(fetch(slope.at[unit], slope_ref.at[:, columns], out_sem.at[units + unit]))
    down_in[units - 1].wait()
    by_blocks(total, hid.at[units - 1], lambda: w_down[units - 1], dot, add=True)

    def leave(start):
        here = pl.ds(start, CHUNK)
        value = mid[here, :] + (total[here, :] + out_bias[layer, 1:2, :])
        stream_out[here, :] = value
        if not last_layer:
            next_normed[here, :] = normalized(
                value, gain[layer + 1, 0:1, :], bias[layer + 1, 0:1, :]
            ).astype(BF16)

    by_rows(tokens, leave, 4)
    if last_layer:
        index = lax.broadcasted_iota(jnp.int32, (slots, 1), 0)
        for image in range(tokens // slots):
            block = stream_out[image * slots : (image + 1) * slots, :]
            count = own_count(counts, image, tokens // slots)
            summed = jnp.sum(jnp.where(index < count, block, 0.0), axis=0, keepdims=True)
            pooled[image : image + 1, :] = summed / count.astype(F32)
    else:
        by_blocks(next_t, order, lambda: next_normed[...], dot_nt)
    for copy in out_copies:
        copy.wait()


def feed_back_kernel(
    which,
    grad_in,
    mid,
    gain,
    order,
    down_own,
    down_far,
    up_own,
    up_far,
    slope_own,
    slope_far,
    out_own,
    out_far,
    pre_own,
    pre_far,
    bias_own,
    bias_far,
    grad_mid,
    mid_t,
    att_own,
    att_far,
    sums,
    low,
    total,
    hidden,
    partial,
    w_down,
    w_up,
    slope,
    pre,
    w_out,
    in_sem,
    out_sem,
):
    layer = which[0]
    tokens = grad_in.shape[0]
    units = w_up.shape[0]
    tile = w_up.shape[2]
    tiles = units // 2
    down_in, up_in, slope_in = [], [], []
    for unit in range(units):
        columns = pl.ds(unit % tiles * tile, tile)
        down_ref, up_ref, slope_ref = ((down_far, up_far, slope_far), (down_own, up_own, slope_own))[
            unit // tiles
        ]
        down_in.append(fetch(down_ref.at[layer, columns, :], w_down.at[unit], in_sem.at[0, unit]))
        slope_in.append(fetch(slope_ref.at[:, columns], slope.at[unit], in_sem.at[1, unit]))
        up_in.append(fetch(up_ref.at[layer, :, columns], w_up.at[unit], in_sem.at[2, unit]))
    out_in = [
        fetch(ref.at[layer], w_out.at[side], in_sem.at[3, side])
        for side, ref in enumerate((out_far, out_own))
    ]
    partial[...] = jnp.zeros_like(partial)

    def enter(start):
        here = pl.ds(start, CHUNK)
        value = grad_in[here, :].astype(F32)
        low[here, :] = value.astype(BF16)
        partial[0] += fold_rows(value)

    by_rows(tokens, enter)
    down_in[0].wait()
    by_blocks(hidden.at[0], low, lambda: w_down[0], dot_nt)
    rows = 256
    total[...] = jnp.zeros_like(total)
    pre[units - 1] = jnp.zeros_like(pre[units - 1])
    pre_refs = (pre_far, pre_own)

    def result(unit, side):
        columns = pl.ds(pl.multiple_of(unit % tiles * tile, tile), tile)
        return pltpu.make_async_copy(pre.at[unit], pre_refs[side].at[:, columns], out_sem.at[unit])

    def turn(unit, carry):
        after = jnp.minimum(unit + 1, units - 1)
        before = jnp.maximum(unit - 1, 0)

        @pl.when(unit + 1 < units)
        def _():
            pltpu.make_async_copy(
                down_own.at[layer, pl.ds(0, tile), :], w_down.at[after], in_sem.at[0, after]
            ).wait()

        @pl.when(unit != 1)
        def _():
            pltpu.make_async_copy(
                up_own.at[layer, :, pl.ds(0, tile)], w_up.at[before], in_sem.at[2, before]
            ).wait()

        pltpu.make_async_copy(
            slope_own.at[:, pl.ds(0, tile)], slope.at[unit], in_sem.at[1, unit]
        ).wait()
        idle = (unit + units - 1) % units

        def chunk(index, carry):
            block = pl.ds(pl.multiple_of(index * rows, rows), rows)
            hidden[(unit + 1) % 2, block, :] = dot_nt(low[block, :], w_down[after])
            total[block, :] += dot_nt(pre[idle, block, :], w_up[before])
            for sub in range(0, rows, CHUNK):
                here = pl.ds(pl.multiple_of(index * rows + sub, CHUNK), CHUNK)
                value = hidden[unit % 2, here, :] * slope[unit, here, :].astype(F32)
                pre[unit, here, :] = value.astype(BF16)
                carry = carry + fold_rows(value)
            return carry

        summed = lax.fori_loop(0, tokens // rows, chunk, jnp.zeros((8, tile), F32))
        row = jnp.sum(summed, axis=0, keepdims=True)
        for side, bias in enumerate((bias_far, bias_own)):

            @pl.when(unit // tiles == side)
            def _():
                bias[pl.ds(unit % tiles, 1), :] = row
                result(unit, side).start()

        return carry

    lax.fori_loop(0, units, turn, 0)
    up_in[units - 1].wait()
    by_blocks(total, pre.at[units - 1], lambda: w_up[units - 1], dot_nt, add=True)

    def leave(start):
        here = pl.ds(start, CHUNK)
        normed_grad = total[here, :]
        through, gain_term = norm_backward(mid[here, :], normed_grad, gain[layer, 1:2, :])
        value = grad_in[here, :].astype(F32) + through
        grad_mid[here, :] = value
        low[here, :] = value.astype(BF16)
        partial[1] += fold_rows(value)
        partial[2] += fold_rows(gain_term)
        partial[3] += fold_rows(normed_grad)

    by_rows(tokens, leave, 2)
    sums[...] = jnp.sum(partial[...], axis=1)
    by_blocks(mid_t, order, lambda: low[...], dot_nt)
    for copy in out_in:
        copy.wait()
    by_blocks(att_far, low, lambda: w_out[0], dot_nt)
    by_blocks(att_own, low, lambda: w_out[1], dot_nt)
    for unit in range(units):
        result(unit, unit // tiles).wait()


def attend_back_kernel(slots, counts, joint, lse, grad_att, grad_joint, bias_sums):
    width = grad_att.shape[1]
    pairs = width // (2 * HEAD_DIM)
    scale = HEAD_DIM ** (-0.5)
    masks = head_masks(slots)
    key_index = lax.broadcasted_iota(jnp.int32, (slots, slots), 0)
    bias_sums[...] = jnp.zeros_like(bias_sums)

    def step(index, carry):
        image = index // pairs
        pair = index % pairs
        rows = pl.ds(pl.multiple_of(image * slots, slots), slots)
        lanes = pl.ds(pl.multiple_of(pair * 2 * HEAD_DIM, 2 * HEAD_DIM), 2 * HEAD_DIM)
        queries = joint[0, rows, lanes]
        keys_in = joint[1, rows, lanes]
        values_in = joint[2, rows, lanes]
        grads = grad_att[rows, lanes]
        keys_t = keys_in.T
        keys_scaled = keys_in * jnp.asarray(scale, BF16)
        valid = key_index < own_count(counts, image, grad_att.shape[0] // slots)
        zeros = jnp.zeros_like(keys_in)
        query_parts, key_parts, value_parts = [], [], []
        for side in range(2):
            keys_side = jnp.where(masks[side], keys_scaled, zeros)
            values_side = jnp.where(masks[side], values_in, zeros)
            scores = jnp.where(valid, dot_nt(keys_side, queries), NEGATIVE)
            probs = jnp.exp(scores - lse[2 * index + side])
            grad_probs = dot_nt(values_side, grads)
            inner = jnp.sum(grad_probs * probs, axis=0, keepdims=True)
            grad_scores = (probs * (grad_probs - inner)).astype(BF16)
            value_parts.append(dot(probs.astype(BF16), grads))
            key_parts.append(dot(grad_scores, queries))
            query_parts.append(dot(keys_t[side * HEAD_DIM : (side + 1) * HEAD_DIM], grad_scores))
        grad_queries = jnp.concatenate(query_parts, axis=0).T * scale
        grad_keys = jnp.where(masks[0], key_parts[0], key_parts[1]) * scale
        grad_values = jnp.where(masks[0], value_parts[0], value_parts[1])
        bias_sums[0:1, lanes] += jnp.sum(grad_queries, axis=0, keepdims=True)
        value_lanes = pl.ds(
            pl.multiple_of(width + pair * 2 * HEAD_DIM, 2 * HEAD_DIM), 2 * HEAD_DIM
        )
        bias_sums[0:1, value_lanes] += jnp.sum(grad_values, axis=0, keepdims=True)
        grad_joint[0, rows, lanes] = grad_queries.astype(BF16)
        grad_joint[1, rows, lanes] = grad_keys.astype(BF16)
        grad_joint[2, rows, lanes] = grad_values.astype(BF16)
        return carry

    lax.fori_loop(0, (grad_att.shape[0] // slots) * pairs, step, 0)


def entry_back_kernel(
    layer, with_low, joint_own, joint_far, weight_own, weight_far, stream, gain, grad_mid, order, *rest
):
    if with_low:
        grad_out, sums, low_t, total, partial, low = rest
    else:
        grad_out, sums, total, partial = rest
    member = pl.program_id(0)

    @pl.when(member == 0)
    def _():
        total[...] = jnp.zeros_like(total)
        partial[...] = jnp.zeros_like(partial)

    left = jnp.concatenate([joint_own[member], joint_far[member]], axis=1)
    right = jnp.concatenate([weight_own[0, 0], weight_far[0, 0]], axis=1)
    total[...] += dot_nt(left, right)

    def rows(start):
        here = pl.ds(start, CHUNK)
        normed_grad = total[here, :]
        through, gain_term = norm_backward(
            stream[here, :].astype(F32), normed_grad, gain[layer, 0:1, :]
        )
        value = grad_mid[here, :] + through
        grad_out[here, :] = value
        if with_low:
            low[here, :] = value.astype(BF16)
        partial[0] += fold_rows(gain_term)
        partial[1] += fold_rows(normed_grad)

    @pl.when(member == 2)
    def _():
        by_rows(stream.shape[0], rows, 2)
        sums[...] = jnp.sum(partial[...], axis=1)
        if with_low:
            by_blocks(low_t, order, lambda: low[...], dot_nt)


def pack_kernel(layers, *refs):
    ins, (own_out, far_out) = refs[:-2], refs[-2:]
    for layer in range(layers):
        sums_mid, sums_in, qv_own, qv_far, upb_own, upb_far = ins[6 * layer : 6 * layer + 6]
        tiles = upb_own.shape[0]
        for ref, qv, upb in ((own_out, qv_own, upb_own), (far_out, qv_far, upb_far)):
            for row, value in (
                (2 * layer, sums_in[0:1, :]),
                (2 * layer + 1, sums_mid[2:3, :]),
                (2 * (layers + layer), sums_in[1:2, :]),
                (2 * (layers + layer) + 1, sums_mid[3:4, :]),
                (2 * (2 * layers + layer), sums_mid[1:2, :]),
                (2 * (2 * layers + layer) + 1, sums_mid[0:1, :]),
                (6 * layers + layer, qv[...]),
            ):
                ref[row : row + 1, :] = value
            start = 7 * layers + tiles * layer
            ref[start : start + tiles, :] = upb[...]


def unpack_kernel(layers, mine, gain, bias, out_bias, qv, upb):
    total = mine[...]
    half = qv.shape[2]
    tiles = upb.shape[1] // mine.shape[1]
    width = mine.shape[1]
    for layer in range(layers):
        for norm in range(2):
            row = 2 * layer + norm
            gain[layer, norm : norm + 1, :] = total[row : row + 1]
            row += 2 * layers
            bias[layer, norm : norm + 1, :] = total[row : row + 1]
            row += 2 * layers
            out_bias[layer, norm : norm + 1, :] = total[row : row + 1]
        row = 6 * layers + layer
        for kind in range(2):
            qv[layer, kind : kind + 1, :] = total[row : row + 1, kind * half : (kind + 1) * half]
        row = 7 * layers + tiles * layer
        for part in range(tiles):
            upb[layer : layer + 1, part * width : (part + 1) * width] = total[
                row + part : row + part + 1
            ]


def finish_kernel(parts, *refs):
    layers = len(refs) // parts
    outs = refs[layers * parts :]
    for layer in range(layers):
        total = refs[layer * parts][...].astype(F32)
        for ref in refs[layer * parts + 1 : (layer + 1) * parts]:
            total = total + ref[...].astype(F32)
        column = 0
        for ref in outs:
            size = ref.shape[3]
            for member in range(ref.shape[1]):
                ref[layer, member] = total[:, column : column + size]
                column += size


def chunk_sources(order):
    first = list(order[:4])
    sources = []
    for target in range(16):
        source = 0
        for place, bit in enumerate(first):
            if (target >> (3 - place)) & 1:
                source |= 1 << (3 - bit)
        sources.append(source)
    return sources


def weight_kernel(sources, tiles, has_extra, *refs):
    if has_extra:
        left_own, left_far, right_own, right_far, lx_own, lx_far, rx_own, rx_far, keep, send = refs
    else:
        left_own, left_far, right_own, right_far, keep, send = refs

    def product(a_own, a_far, b_own, b_far):
        left = jnp.concatenate([a_own[...], a_far[...]], axis=1)
        right = jnp.concatenate([b_own[...].reshape(b_own.shape[-2:]), b_far[...].reshape(b_far.shape[-2:])], axis=0)
        size = left.shape[0] // 16
        low = dot(left, right).astype(BF16)
        for target, source in enumerate(sources):
            ref = keep if target < 8 else send
            ref[(target % 8) * size : (target % 8 + 1) * size, :] = low[
                source * size : (source + 1) * size, :
            ]

    if has_extra:

        @pl.when(pl.program_id(0) < tiles)
        def _():
            product(left_own, left_far, right_own, right_far)

        @pl.when(pl.program_id(0) == tiles)
        def _():
            product(lx_own, lx_far, rx_own, rx_far)

    else:
        product(left_own, left_far, right_own, right_far)


def weight_grad(name, order, left, right, extra=None, tiles=None, first=0):
    left_own, left_far = left
    right_own, right_far = right
    width, tokens = left_own.shape
    if right_own.ndim == 3:
        tile = right_own.shape[2]
        right_spec = pl.BlockSpec(
            (1, tokens, tile), lambda j: (jnp.minimum(j, tiles - 1) + first, 0, 0)
        )
    else:
        tile = 768 if tiles else 512
        tiles = tiles or right_own.shape[1] // tile
        right_spec = pl.BlockSpec((tokens, tile), lambda j: (0, j + first))
    steps = tiles + (1 if extra is not None else 0)
    ins = [left_own, left_far, right_own, right_far]
    specs = [fixed((width, tokens))] * 2 + [right_spec] * 2
    if extra is not None:
        ins += list(extra)
        specs += [fixed((width, tokens))] * 2 + [fixed((tokens, tile))] * 2
    half = out((width // 2, steps * tile), BF16)
    half_spec = pl.BlockSpec((width // 2, tile), lambda j: (0, j))
    return call(
        functools.partial(weight_kernel, chunk_sources(order), tiles, extra is not None),
        name,
        (steps,),
        ins,
        specs,
        [half, half],
        [half_spec, half_spec],
        flops=4 * width * tokens * steps * tile,
    )


def flip(bit):
    size = lax.axis_size("dp")
    return [(index, index ^ (1 << bit)) for index in range(size)]


class DpSum:
    def __init__(self, order, halves=None, units=()):
        self.order = list(order)
        self.incoming = None
        if halves is not None:
            keep, self.outgoing = halves
            self.members = [[keep]]
        else:
            self.members = [parts for unit in units for parts in unit.members]
            self.halve()

    def halve(self):
        rows = self.members[0][0].shape[0] // 2
        sends = [
            sum(part[rows:].astype(F32) for part in parts).astype(BF16) for parts in self.members
        ]
        self.outgoing = sends[0] if len(sends) == 1 else jnp.concatenate(sends, axis=1)
        self.members = [[part[:rows] for part in parts] for parts in self.members]

    def start(self):
        self.incoming = lax.ppermute(self.outgoing, "dp", flip(self.order.pop(0)))

    def turn(self, go=True):
        column = 0
        for parts in self.members:
            width = parts[0].shape[1]
            parts.append(self.incoming[:, column : column + width])
            column += width
        self.incoming = None
        if self.order:
            self.halve()
            if go:
                self.start()

    def flying(self):
        return [self.incoming]

    def land(self, arrays):
        (self.incoming,) = arrays


class Everywhere:
    def __init__(self, mine, far, groups):
        self.mine = mine
        self.incoming = [swap(far)]
        self.groups = list(groups)

    def flying(self):
        return self.incoming

    def land(self, arrays):
        self.incoming = arrays

    def turn(self):
        if len(self.incoming) == 1:
            self.mine = self.mine + self.incoming[0]
        else:
            near, far, across = self.incoming
            self.mine = (self.mine + near) + (far + across)
        self.incoming = []
        if self.groups:
            group = self.groups.pop(0)
            masks = [1 << bit for bit in group]
            if len(masks) == 2:
                masks.append(masks[0] | masks[1])
            size = lax.axis_size("dp")
            self.incoming = [
                lax.ppermute(self.mine, "dp", [(index, index ^ mask) for index in range(size)])
                for mask in masks
            ]


def gate(value, starts=(), turns=(), after=(), holds=()):
    ends = [*turns, *holds]
    held = [unit.outgoing for unit in starts] + [array for unit in ends for array in unit.flying()]
    value, *held = lax.optimization_barrier((value, *held, *after))
    for unit in starts:
        unit.outgoing = held.pop(0)
        unit.start()
    for unit in ends:
        unit.land([held.pop(0) for _ in unit.flying()])
    for unit in turns:
        unit.turn()
    for unit in holds:
        unit.turn(go=False)
    return value


def swap(values):
    return lax.ppermute(values, "tensor", [(0, 1), (1, 0)])


def shards(
    images,
    valid_count,
    ln_gain,
    ln_bias,
    w_qkv,
    qv_bias,
    w_out,
    out_bias,
    w_up,
    up_bias,
    w_down,
    cotangent,
):
    local_rows, slots, width = images.shape
    tokens = local_rows * slots
    half = w_qkv.shape[3]
    ff_half = w_up.shape[2]
    tile = 768
    steps = ff_half // tile
    heads = half // HEAD_DIM
    dp = lax.axis_size("dp")
    bits = dp.bit_length() - 1
    assert dp == 1 << bits and bits >= 4 and lax.axis_size("tensor") == 2
    tail = tuple(range(4, bits))
    order_a = (0, 1, 2, 3) + tail
    order_b = (1, 0, 2, 3) + tail
    order_e = (2, 0, 1, 3) + tail
    order_d = (0, 2, 3, 1) + tail

    me = lax.axis_index("dp")
    counts = valid_count

    block = width // dp
    row = jnp.arange(width, dtype=jnp.int32)
    index = row // block
    mirrored = jnp.zeros_like(index)
    for bit in range(bits):
        mirrored = mirrored | (((index >> (bits - 1 - bit)) & 1) << bit)
    source = (mirrored ^ me) * block + row % block
    order = (source[:, None] == row[None, :]).astype(BF16)

    w_qkv = jnp.transpose(w_qkv, (0, 2, 1, 3))
    qkv = (w_qkv, swap(w_qkv))
    qv = (qv_bias, swap(qv_bias))

    images_2d = images.reshape(tokens, width)
    cotangent_2d = cotangent.reshape(tokens, width)
    smem = pl.BlockSpec(memory_space=pltpu.SMEM)
    wide = (tokens, width)
    flops_wide = 2 * width * width * tokens

    normed, normed_t, cotangent_t, wide_cotangent = call(
        prep_kernel,
        "prep",
        (),
        [images_2d, cotangent_2d, ln_gain, ln_bias, order],
        [whole()] * 5,
        [out(wide, BF16), out((width, tokens), BF16), out((width, tokens), BF16), out(wide, F32)],
        [whole()] * 4,
        flops=2 * flops_wide,
    )

    wout, wup, wdown = [
        (weight, swap(lax.optimization_barrier((weight, normed, qkv[1], qv[1]))[0]))
        for weight in (w_out, w_up, w_down)
    ]

    def attend(layer, normed, counts):
        lse_shape = (local_rows * heads, 1, slots)
        joint_out = out((3, tokens, half), BF16)
        att_out = out((tokens, half), BF16)
        lse_out = out(lse_shape, F32)
        results = call(
            functools.partial(attend_kernel, slots),
            "attend",
            (),
            [jnp.full((1,), layer, jnp.int32), counts, normed, in_hbm(qkv[0]), in_hbm(qkv[1]), qv[0], qv[1]],
            [smem, smem, whole(), hbm(), hbm(), whole(), whole()],
            [joint_out, joint_out, att_out, att_out, lse_out, lse_out],
            [whole()] * 6,
            [pltpu.VMEM((2, 3, width, half), BF16), pltpu.SemaphoreType.DMA((2, 3))],
            flops=12 * tokens * width * half + 8 * tokens * slots * half,
            limit=44,
        )
        return results[0::2], results[1::2]

    stream = images_2d
    saved = []
    got_cotangent_t = swap(cotangent_t)
    pooled = None
    for layer in range(LAYERS):
        last = layer == LAYERS - 1
        own, far = attend(layer, normed, counts)
        if layer == 0:
            upb = (up_bias, swap(up_bias))
        gain_in = ln_gain
        if layer > 0:
            before = saved[layer - 1]
            names = ("got_normed_t", "got_att", "got_mid_normed_t", "got_hid")
            gain_in, got_cotangent_t, *got = lax.optimization_barrier(
                (ln_gain, got_cotangent_t, *[before[name] for name in names])
            )
            before.update(zip(names, got))
        ff = pltpu.HBM((tokens, ff_half), BF16)
        extra = (
            [out((local_rows, width), F32)]
            if last
            else [out(wide, BF16), out((width, tokens), BF16)]
        )
        results = call(
            functools.partial(feed_kernel, layer, slots, last),
            "feed",
            (),
            [
                counts,
                stream,
                own[1],
                far[1],
                in_hbm(wout[0]),
                in_hbm(wout[1]),
                out_bias,
                gain_in,
                ln_bias,
                order,
                in_hbm(wup[0]),
                in_hbm(wup[1]),
                upb[0],
                upb[1],
                in_hbm(wdown[0]),
                in_hbm(wdown[1]),
            ],
            [smem]
            + [whole()] * 3
            + [hbm()] * 2
            + [whole()] * 4
            + [hbm()] * 2
            + [whole()] * 2
            + [hbm()] * 2,
            [out(wide, F32), out((width, tokens), BF16), ff, ff, ff, ff, out(wide, F32)] + extra,
            [whole()] * 2 + [hbm()] * 4 + [whole()] * (1 + len(extra)),
            [
                pltpu.VMEM(wide, BF16),
                pltpu.VMEM(wide, F32),
                pltpu.VMEM((2, tokens, tile), F32),
                pltpu.VMEM((2 * half, width), BF16),
                pltpu.VMEM((2 * steps, width, tile), BF16),
                pltpu.VMEM((2 * steps, tile, width), BF16),
                pltpu.VMEM((2 * steps, tokens, tile), BF16),
                pltpu.VMEM((2 * steps, tokens, tile), BF16),
                pltpu.SemaphoreType.DMA((2 + 4 * steps,)),
                pltpu.SemaphoreType.DMA((4 * steps,)),
            ],
            flops=8 * tokens * width * ff_half + 2 * flops_wide,
            limit=32,
        )
        mid, mid_normed_t, hid_own, hid_far, slope_own, slope_far, stream_next = results[:7]
        saved.append(
            dict(
                stream=stream,
                own=own,
                far=far,
                mid=mid,
                slope=(slope_own, slope_far),
                hid=hid_own,
                attended=own[1],
                normed_t=normed_t,
                mid_normed_t=mid_normed_t,
                got_hid=swap(hid_far),
                got_att=swap(far[1]),
                got_normed_t=swap(normed_t),
                got_mid_normed_t=swap(mid_normed_t),
            )
        )
        stream = stream_next
        if last:
            pooled = results[7]
        else:
            normed, normed_t = results[7:9]

    def feed_back(layer, grad, gain_in):
        kept = saved[layer]
        ff = pltpu.HBM((tokens, ff_half), BF16)
        bias_shape = out((steps, tile), F32)
        att_shape = out((tokens, half), BF16)
        return call(
            feed_back_kernel,
            "feed_back",
            (),
            [
                jnp.full((1,), layer, jnp.int32),
                grad,
                kept["mid"],
                gain_in,
                order,
                in_hbm(wdown[0]),
                in_hbm(wdown[1]),
                in_hbm(wup[0]),
                in_hbm(wup[1]),
                kept["slope"][0],
                kept["slope"][1],
                in_hbm(wout[0]),
                in_hbm(wout[1]),
            ],
            [smem] + [whole()] * 4 + [hbm()] * 8,
            [
                ff,
                ff,
                bias_shape,
                bias_shape,
                out(wide, F32),
                out((width, tokens), BF16),
                att_shape,
                att_shape,
                out((4, width), F32),
            ],
            [hbm()] * 2 + [whole()] * 7,
            [
                pltpu.VMEM(wide, BF16),
                pltpu.VMEM(wide, F32),
                pltpu.VMEM((2, tokens, tile), F32),
                pltpu.VMEM((4, 8, width), F32),
                pltpu.VMEM((2 * steps, tile, width), BF16),
                pltpu.VMEM((2 * steps, width, tile), BF16),
                pltpu.VMEM((2 * steps, tokens, tile), BF16),
                pltpu.VMEM((2 * steps, tokens, tile), BF16),
                pltpu.VMEM((2, half, width), BF16),
                pltpu.SemaphoreType.DMA((4, 2 * steps)),
                pltpu.SemaphoreType.DMA((2 * steps,)),
            ],
            flops=8 * tokens * width * ff_half + 2 * flops_wide,
            limit=32,
        )

    def attend_back(forward, grad_att, counts_in):
        joint, _, lse = forward
        return call(
            functools.partial(attend_back_kernel, slots),
            "attend_back",
            (),
            [counts_in, joint, lse, grad_att],
            [smem, whole(), whole(), whole()],
            [out(joint.shape, BF16), out((1, 2 * half), F32)],
            [whole()] * 2,
            flops=10 * tokens * slots * half,
        )

    def entry_back(layer, joint_own, joint_far, grad_mid, gain_in):
        with_low = layer > 0
        return call(
            functools.partial(entry_back_kernel, layer, with_low),
            "entry_back",
            (3,),
            [
                joint_own,
                joint_far,
                in_hbm(qkv[0]),
                in_hbm(qkv[1]),
                saved[layer]["stream"],
                gain_in,
                grad_mid,
                order,
            ],
            [whole()] * 2
            + [pl.BlockSpec((1, 1, width, half), lambda c: (layer, c, 0, 0))] * 2
            + [whole()] * 4,
            [out(wide, F32), out((2, width), F32)]
            + ([out((width, tokens), BF16)] if with_low else []),
            [whole()] * (3 if with_low else 2),
            [pltpu.VMEM(wide, F32), pltpu.VMEM((2, 8, width), F32)]
            + ([pltpu.VMEM(wide, BF16)] if with_low else []),
            flops=12 * tokens * width * half,
        )

    def down_halves(layer, order_of, grad_t, got_grad_t):
        kept = saved[layer]
        return weight_grad(
            "down_grad", order_of, (grad_t, got_grad_t), (in_hbm(kept["hid"]), kept["got_hid"])
        )

    def up_halves(layer, order_of, pre_own, got_pre, tiles=None, first=0):
        kept = saved[layer]
        return weight_grad(
            "up_grad",
            order_of,
            (kept["mid_normed_t"], kept["got_mid_normed_t"]),
            (pre_own, got_pre),
            tiles=tiles,
            first=first,
        )

    def lefts(layer):
        return saved[layer]["normed_t"], saved[layer]["got_normed_t"]

    def extras(layer, mid_t, got_mid_t):
        return mid_t, got_mid_t, saved[layer]["attended"], saved[layer]["got_att"]

    small = [None] * LAYERS
    down_1 = DpSum(order_a, down_halves(1, order_a, cotangent_t, got_cotangent_t))
    gain_in = gate(ln_gain, [down_1])
    pre_own, pre_far, upb_own, upb_far, grad_mid, mid_t, att_own, att_far, sums_mid = feed_back(
        1, wide_cotangent, gain_in
    )
    got_pre, got_mid_t = swap(pre_far), swap(mid_t)
    joint_far, qv_far = attend_back(saved[1]["far"], att_far, counts)
    got_joint = swap(joint_far)
    pre_own = gate(pre_own, [], [], [qv_far], [down_1])
    pre_own = gate(pre_own, [down_1])
    up_1 = DpSum(order_a, up_halves(1, order_a, pre_own, got_pre))
    counts_in = gate(counts, [up_1])
    joint_own, qv_own = attend_back(saved[1]["own"], att_own, counts_in)
    gain_in = gate(gain_in, after=[qv_own])
    grad, sums_in, grad_t = entry_back(1, joint_own, joint_far, grad_mid, gain_in)
    got_grad_t = swap(grad_t)
    small[1] = (sums_mid, sums_in, qv_own, qv_far, upb_own, upb_far)
    joint_own = gate(joint_own, [], [down_1], [sums_in])
    rest_1 = DpSum(
        order_e,
        weight_grad(
            "qkv_out_grad",
            order_e,
            lefts(1),
            (joint_own, got_joint),
            extras(1, mid_t, got_mid_t),
            tiles=3,
        ),
    )
    grad_t = gate(grad_t, [rest_1])
    down_0 = DpSum(order_a, down_halves(0, order_a, grad_t, got_grad_t))

    gain_in = gate(gain_in, [down_0], [up_1], holds=[down_1])
    pre_own, pre_far, upb_own, upb_far, grad_mid, mid_t, att_own, att_far, sums_mid = feed_back(
        0, grad, gain_in
    )
    got_pre, got_mid_t = swap(pre_far), swap(mid_t)
    counts_in = gate(counts_in, [], [up_1], [sums_mid], [rest_1])
    joint_far, qv_far = attend_back(saved[0]["far"], att_far, counts_in)
    got_joint = swap(joint_far)
    pre_own = gate(pre_own, [], [], [qv_far], [down_0, up_1])
    pre_own = gate(pre_own, [down_0, up_1, down_1])
    up_0 = DpSum(order_d, up_halves(0, order_d, pre_own, got_pre))
    counts_in = gate(counts_in, [up_0], [], [got_mid_t, got_joint])
    joint_own, qv_own = attend_back(saved[0]["own"], att_own, counts_in)
    rest_0 = DpSum(
        order_b,
        weight_grad(
            "qkv_out_grad",
            order_b,
            lefts(0),
            (joint_own, got_joint),
            extras(0, mid_t, got_mid_t),
            tiles=3,
        ),
    )
    gain_in = gate(gain_in, [rest_0], [down_0, up_1, down_1], [qv_own])
    grad, sums_in = entry_back(0, joint_own, joint_far, grad_mid, gain_in)
    last = gate(sums_in, [rest_1], [up_0])
    small[0] = (sums_mid, last, qv_own, qv_far, upb_own, upb_far)
    ins = [array for arrays in small for array in arrays]
    vector_shape = out(((7 + steps) * LAYERS, width), F32)
    mine, far = call(
        functools.partial(pack_kernel, LAYERS),
        "pack_small",
        (),
        ins,
        [whole()] * len(ins),
        [vector_shape] * 2,
        [whole()] * 2,
    )
    vector = Everywhere(mine, far, [(0, 1), (2,), (3,), *[(bit,) for bit in tail]])
    last = gate(last, holds=[down_0])
    last = gate(last, [], [rest_0, up_0, vector], [down_0.outgoing], [rest_1])
    last = gate(last, [down_0, rest_1], [rest_0, up_0, vector])
    last = gate(last, [], [rest_0, up_0, down_0, rest_1, vector])
    last = gate(last, [], [rest_0, rest_1])
    last = gate(last, [], [vector])
    while vector.flying():
        vector.turn()
    running = [down_1, up_1, rest_1, down_0, up_0, rest_0]
    while any(unit.incoming is not None for unit in running):
        last = gate(last, [], [unit for unit in running if unit.incoming is not None][:4])

    def finish(first, second, shapes):
        ins = [*first.members[0], *second.members[0]]
        return call(
            functools.partial(finish_kernel, len(first.members[0])),
            "finish",
            (),
            ins,
            [whole()] * len(ins),
            [out((LAYERS,) + shape, F32) for shape in shapes],
            [whole()] * len(shapes),
        )

    (down_grad,) = finish(down_0, down_1, [(1, block, ff_half)])
    (up_grad,) = finish(up_0, up_1, [(1, block, ff_half)])
    qkv_grad, out_grad = finish(rest_0, rest_1, [(3, block, half), (1, block, half)])
    total, qkv_grad = lax.optimization_barrier((vector.mine, qkv_grad))
    gain_grads, shift_grads, outb_grads, qv_grads, upb_grads = call(
        functools.partial(unpack_kernel, LAYERS),
        "unpack_small",
        (),
        [total],
        [whole()],
        [
            out(ln_gain.shape, F32),
            out(ln_bias.shape, F32),
            out(out_bias.shape, F32),
            out(qv_bias.shape, F32),
            out(up_bias.shape, F32),
        ],
        [whole()] * 5,
    )
    return (
        stream.reshape(images.shape),
        pooled,
        grad.reshape(images.shape),
        gain_grads,
        shift_grads,
        jnp.transpose(qkv_grad, (0, 2, 1, 3)),
        qv_grads,
        jnp.transpose(out_grad[:, 0], (0, 2, 1)),
        outb_grads,
        up_grad[:, 0],
        upb_grads,
        jnp.transpose(down_grad[:, 0], (0, 2, 1)),
    )


def solution(mesh):
    placed = (
        P(("dp", "tensor"), None, None),
        P("dp"),
        P(),
        P(),
        P(None, None, None, "tensor"),
        P(None, None, "tensor"),
        P(None, "tensor", None),
        P(),
        P(None, None, "tensor"),
        P(None, "tensor"),
        P(None, "tensor", None),
        P(("dp", "tensor"), None, None),
    )
    return jax.shard_map(
        shards,
        mesh=mesh,
        in_specs=placed,
        out_specs=(
            P(("dp", "tensor"), None, None),
            P(("dp", "tensor"), None),
            P(("dp", "tensor"), None, None),
            P(),
            P(),
            P(None, "dp", None, "tensor"),
            P(None, None, "tensor"),
            P(None, "tensor", "dp"),
            P(),
            P(None, "dp", "tensor"),
            P(None, "tensor"),
            P(None, "tensor", "dp"),
        ),
        check_vma=False,
    )
```

```python
import functools
import math

import jax
import jax.numpy as jnp
from jax import lax
from jax.experimental import pallas as pl
from jax.experimental.pallas import tpu as pltpu
from jax.sharding import PartitionSpec as P

HEAD_DIM = 64
LAYERS = 2
EPSILON = 1e-06
NEGATIVE = -1e30
BF16 = jnp.bfloat16
F32 = jnp.float32
CHUNK = 16


def dot(left, right):
    return lax.dot_general(left, right, (((1,), (0,)), ((), ())), preferred_element_type=F32)


def dot_nt(left, right):
    return lax.dot_general(left, right, (((1,), (1,)), ((), ())), preferred_element_type=F32)


def fixed(shape, *lead):
    where = tuple(lead) + (0,) * (len(shape) - len(lead))
    return pl.BlockSpec(shape, lambda *_: where)


def out(shape, dtype):
    return jax.ShapeDtypeStruct(shape, dtype)


def in_hbm(values):
    return pltpu.with_memory_space_constraint(values, pltpu.HBM)


def cost(flops, *arrays):
    total = sum(math.prod(a.shape) * a.dtype.itemsize for a in arrays)
    return pl.CostEstimate(flops=int(flops) // 64, bytes_accessed=int(total) // 64, transcendentals=0)


MIB = 1 << 20


def call(body, name, grid, ins, in_specs, outs, out_specs, scratch=(), flops=0, limit=24):
    return pl.pallas_call(
        body,
        name=name,
        grid=grid,
        in_specs=in_specs,
        out_specs=out_specs,
        out_shape=outs,
        scratch_shapes=list(scratch),
        compiler_params=pltpu.CompilerParams(vmem_limit_bytes=limit * MIB),
        cost_estimate=cost(flops, *ins, *outs),
    )(*ins)


def whole():
    return pl.BlockSpec(memory_space=pltpu.VMEM)


def by_blocks(target, left, right, product, rows=256, add=False):
    def block(index, carry):
        here = pl.ds(pl.multiple_of(index * rows, rows), rows)
        value = product(left[here, :], right())
        if add:
            value = target[here, :] + value
        target[here, :] = value.astype(target.dtype)
        return carry

    lax.fori_loop(0, left.shape[0] // rows, block, 0)


def hbm():
    return pl.BlockSpec(memory_space=pltpu.HBM)


def by_rows(rows, body, unroll=1):
    def step(index, carry):
        for part in range(unroll):
            body(pl.multiple_of((index * unroll + part) * CHUNK, CHUNK))
        return carry

    lax.fori_loop(0, rows // (CHUNK * unroll), step, 0)


def moments(values):
    average = jnp.mean(values, axis=-1, keepdims=True)
    centred = values - average
    variance = jnp.mean(centred * centred, axis=-1, keepdims=True)
    return centred, lax.rsqrt(variance + EPSILON)


def normalized(values, gain, bias):
    centred, scale = moments(values)
    return centred * scale * gain + bias


def norm_backward(values, grad_normed, gain):
    centred, scale = moments(values)
    unit = centred * scale
    grad_unit = grad_normed * gain
    first = jnp.mean(grad_unit, axis=-1, keepdims=True)
    second = jnp.mean(grad_unit * unit, axis=-1, keepdims=True)
    return scale * (grad_unit - first - unit * second), grad_normed * unit


def fold_rows(values):
    total = values[0:8]
    for start in range(8, values.shape[0], 8):
        total = total + values[start : start + 8]
    return total


def prep_kernel(images, cotangent, gain, bias, order, normed, normed_t, cotangent_t, wide_cotangent):
    def rows(start):
        here = pl.ds(start, CHUNK)
        values = images[here, :].astype(F32)
        normed[here, :] = normalized(values, gain[0, 0:1, :], bias[0, 0:1, :]).astype(BF16)
        wide_cotangent[here, :] = cotangent[here, :].astype(F32)

    by_rows(images.shape[0], rows, 4)
    by_blocks(normed_t, order, lambda: normed[...], dot_nt)
    by_blocks(cotangent_t, order, lambda: cotangent[...], dot_nt)


def head_masks(slots):
    lane = lax.broadcasted_iota(jnp.int32, (slots, 2 * HEAD_DIM), 1)
    return lane < HEAD_DIM, lane >= HEAD_DIM


def own_count(counts, image, images):
    return counts[lax.axis_index("tensor") * images + image]


def attend_kernel(
    slots,
    which,
    counts,
    normed,
    weight_own,
    weight_far,
    bias_own,
    bias_far,
    joint_own,
    joint_far,
    att_own,
    att_far,
    lse_own,
    lse_far,
    held,
    sem,
):
    width = att_own.shape[1]
    pairs = width // (2 * HEAD_DIM)
    scale = HEAD_DIM ** (-0.5)
    layer = which[0]
    weights = (weight_own, weight_far)
    for side in range(2):
        for member in range(3):
            fetch(weights[side].at[layer, member], held.at[side, member], sem.at[side, member])
    for side, (joint, bias) in enumerate(((joint_own, bias_own), (joint_far, bias_far))):

        def project(member, carry):
            pltpu.make_async_copy(
                weights[side].at[layer, member], held.at[side, member], sem.at[side, member]
            ).wait()
            shift = bias[layer, pl.ds(member // 2, 1), :]
            shift = jnp.where(member == 1, jnp.zeros_like(shift), shift)
            joint[member] = (dot(normed[...], held[side, member]) + shift).astype(BF16)
            return carry

        lax.fori_loop(0, 3, project, 0)
    masks = head_masks(slots)
    key_index = lax.broadcasted_iota(jnp.int32, (slots, slots), 0)

    def step(index, carry):
        image = index // pairs
        pair = index % pairs
        rows = pl.ds(pl.multiple_of(image * slots, slots), slots)
        lanes = pl.ds(pl.multiple_of(pair * 2 * HEAD_DIM, 2 * HEAD_DIM), 2 * HEAD_DIM)
        valid = key_index < own_count(counts, image, normed.shape[0] // slots)
        sets = ((joint_own, att_own, lse_own), (joint_far, att_far, lse_far))
        heads = []
        for joint, _, _ in sets:
            queries = joint[0, rows, lanes]
            keys_in = joint[1, rows, lanes] * jnp.asarray(scale, BF16)
            for side in range(2):
                keys_side = jnp.where(masks[side], keys_in, jnp.zeros_like(keys_in))
                heads.append(dot_nt(keys_side, queries))
        values_t = [joint[2, rows, lanes].T for joint, _, _ in sets]
        heads = [jnp.where(valid, scores, NEGATIVE) for scores in heads]
        largest = [jnp.max(scores, axis=0, keepdims=True) for scores in heads]
        heads = [jnp.exp(scores - top) for scores, top in zip(heads, largest)]
        totals = [jnp.sum(exponent, axis=0, keepdims=True) for exponent in heads]
        heads = [(exponent * (1.0 / total)).astype(BF16) for exponent, total in zip(heads, totals)]
        for which_set, (_, attended, lse) in enumerate(sets):
            parts = []
            for side in range(2):
                head = 2 * which_set + side
                lse[2 * index + side] = largest[head] + jnp.log(totals[head])
                parts.append(
                    dot(values_t[which_set][side * HEAD_DIM : (side + 1) * HEAD_DIM], heads[head])
                )
            attended[rows, lanes] = jnp.concatenate(parts, axis=0).T.astype(BF16)
        return carry

    lax.fori_loop(0, (normed.shape[0] // slots) * pairs, step, 0)


def fetch(source, target, sem):
    copy = pltpu.make_async_copy(source, target, sem)
    copy.start()
    return copy


def feed_kernel(
    layer,
    slots,
    last_layer,
    counts,
    stream,
    att_own,
    att_far,
    out_own,
    out_far,
    out_bias,
    gain,
    bias,
    order,
    up_own,
    up_far,
    up_bias_own,
    up_bias_far,
    down_own,
    down_far,
    mid,
    normed_t,
    hid_own,
    hid_far,
    slope_own,
    slope_far,
    stream_out,
    *rest,
):
    if last_layer:
        pooled = rest[0]
    else:
        next_normed, next_t = rest[:2]
    normed, total, pre, w_out, w_up, w_down, hid, slope, in_sem, out_sem = rest[1 if last_layer else 2 :]
    tokens = stream.shape[0]
    half = w_out.shape[0] // 2
    units = w_up.shape[0]
    tile = w_up.shape[2]
    tiles = units // 2
    out_in = [
        fetch(ref.at[layer], w_out.at[pl.ds(side * half, half)], in_sem.at[side])
        for side, ref in enumerate((out_own, out_far))
    ]
    up_in, down_in = [], []
    for unit in range(units):
        side, part = unit // tiles, unit % tiles
        columns = pl.ds(part * tile, tile)
        up_ref, down_ref = ((up_own, down_own), (up_far, down_far))[side]
        up_in.append(fetch(up_ref.at[layer, :, columns], w_up.at[unit], in_sem.at[2 + unit]))
        down_in.append(
            fetch(down_ref.at[layer, columns, :], w_down.at[unit], in_sem.at[2 + units + unit])
        )
    for copy in out_in:
        copy.wait()
    total[...] = dot(jnp.concatenate([att_own[...], att_far[...]], axis=1), w_out[...])

    def enter(start):
        here = pl.ds(start, CHUNK)
        value = stream[here, :].astype(F32) + (total[here, :] + out_bias[layer, 0:1, :])
        mid[here, :] = value
        normed[here, :] = normalized(value, gain[layer, 1:2, :], bias[layer, 1:2, :]).astype(BF16)

    by_rows(tokens, enter, 4)
    up_in[0].wait()
    by_blocks(pre.at[0], normed, lambda: w_up[0], dot)
    by_blocks(normed_t, order, lambda: normed[...], dot_nt)
    rows = 256
    out_copies = []
    for unit in range(units):
        side, part = unit // tiles, unit % tiles
        shift = (up_bias_own, up_bias_far)[side][layer : layer + 1, part * tile : (part + 1) * tile]
        if unit + 1 < units:
            up_in[unit + 1].wait()
        if unit > 0:
            down_in[unit - 1].wait()

        def chunk(index, carry):
            block = pl.ds(pl.multiple_of(index * rows, rows), rows)
            if unit + 1 < units:
                pre[(unit + 1) % 2, block, :] = dot(normed[block, :], w_up[unit + 1])
            if unit == 1:
                total[block, :] = dot(hid[unit - 1, block, :], w_down[unit - 1])
            elif unit > 1:
                total[block, :] += dot(hid[unit - 1, block, :], w_down[unit - 1])
            for sub in range(0, rows, CHUNK):
                here = pl.ds(pl.multiple_of(index * rows + sub, CHUNK), CHUNK)
                value = pre[unit % 2, here, :] + shift
                cdf = 0.5 + 0.5 * lax.erf(value * (0.5**0.5))
                hid[unit, here, :] = (value * cdf).astype(BF16)
                density = jnp.exp(-0.5 * value * value) * ((2.0 * math.pi) ** -0.5)
                slope[unit, here, :] = (cdf + value * density).astype(BF16)
            return carry

        lax.fori_loop(0, tokens // rows, chunk, 0)
        hid_ref, slope_ref = ((hid_own, slope_own), (hid_far, slope_far))[side]
        columns = pl.ds(part * tile, tile)
        out_copies.append(fetch(hid.at[unit], hid_ref.at[:, columns], out_sem.at[unit]))
        out_copies.append(fetch(slope.at[unit], slope_ref.at[:, columns], out_sem.at[units + unit]))
    down_in[units - 1].wait()
    by_blocks(total, hid.at[units - 1], lambda: w_down[units - 1], dot, add=True)

    def leave(start):
        here = pl.ds(start, CHUNK)
        value = mid[here, :] + (total[here, :] + out_bias[layer, 1:2, :])
        stream_out[here, :] = value
        if not last_layer:
            next_normed[here, :] = normalized(
                value, gain[layer + 1, 0:1, :], bias[layer + 1, 0:1, :]
            ).astype(BF16)

    by_rows(tokens, leave, 4)
    if last_layer:
        index = lax.broadcasted_iota(jnp.int32, (slots, 1), 0)
        for image in range(tokens // slots):
            block = stream_out[image * slots : (image + 1) * slots, :]
            count = own_count(counts, image, tokens // slots)
            summed = jnp.sum(jnp.where(index < count, block, 0.0), axis=0, keepdims=True)
            pooled[image : image + 1, :] = summed / count.astype(F32)
    else:
        by_blocks(next_t, order, lambda: next_normed[...], dot_nt)
    for copy in out_copies:
        copy.wait()


def feed_back_kernel(
    which,
    grad_in,
    mid,
    gain,
    order,
    down_own,
    down_far,
    up_own,
    up_far,
    slope_own,
    slope_far,
    out_own,
    out_far,
    pre_own,
    pre_far,
    bias_own,
    bias_far,
    grad_mid,
    mid_t,
    att_own,
    att_far,
    sums,
    low,
    total,
    hidden,
    partial,
    w_down,
    w_up,
    slope,
    pre,
    w_out,
    in_sem,
    out_sem,
):
    layer = which[0]
    tokens = grad_in.shape[0]
    units = w_up.shape[0]
    tile = w_up.shape[2]
    tiles = units // 2
    down_in, up_in, slope_in = [], [], []
    for unit in range(units):
        columns = pl.ds(unit % tiles * tile, tile)
        down_ref, up_ref, slope_ref = ((down_far, up_far, slope_far), (down_own, up_own, slope_own))[
            unit // tiles
        ]
        down_in.append(fetch(down_ref.at[layer, columns, :], w_down.at[unit], in_sem.at[0, unit]))
        slope_in.append(fetch(slope_ref.at[:, columns], slope.at[unit], in_sem.at[1, unit]))
        up_in.append(fetch(up_ref.at[layer, :, columns], w_up.at[unit], in_sem.at[2, unit]))
    out_in = [
        fetch(ref.at[layer], w_out.at[side], in_sem.at[3, side])
        for side, ref in enumerate((out_far, out_own))
    ]
    partial[...] = jnp.zeros_like(partial)

    def enter(start):
        here = pl.ds(start, CHUNK)
        value = grad_in[here, :].astype(F32)
        low[here, :] = value.astype(BF16)
        partial[0] += fold_rows(value)

    by_rows(tokens, enter)
    down_in[0].wait()
    by_blocks(hidden.at[0], low, lambda: w_down[0], dot_nt)
    rows = 256
    total[...] = jnp.zeros_like(total)
    pre[units - 1] = jnp.zeros_like(pre[units - 1])
    pre_refs = (pre_far, pre_own)

    def result(unit, side):
        columns = pl.ds(pl.multiple_of(unit % tiles * tile, tile), tile)
        return pltpu.make_async_copy(pre.at[unit], pre_refs[side].at[:, columns], out_sem.at[unit])

    def turn(unit, carry):
        after = jnp.minimum(unit + 1, units - 1)
        before = jnp.maximum(unit - 1, 0)

        @pl.when(unit + 1 < units)
        def _():
            pltpu.make_async_copy(
                down_own.at[layer, pl.ds(0, tile), :], w_down.at[after], in_sem.at[0, after]
            ).wait()

        @pl.when(unit != 1)
        def _():
            pltpu.make_async_copy(
                up_own.at[layer, :, pl.ds(0, tile)], w_up.at[before], in_sem.at[2, before]
            ).wait()

        pltpu.make_async_copy(
            slope_own.at[:, pl.ds(0, tile)], slope.at[unit], in_sem.at[1, unit]
        ).wait()
        idle = (unit + units - 1) % units

        def chunk(index, carry):
            block = pl.ds(pl.multiple_of(index * rows, rows), rows)
            hidden[(unit + 1) % 2, block, :] = dot_nt(low[block, :], w_down[after])
            total[block, :] += dot_nt(pre[idle, block, :], w_up[before])
            for sub in range(0, rows, CHUNK):
                here = pl.ds(pl.multiple_of(index * rows + sub, CHUNK), CHUNK)
                value = hidden[unit % 2, here, :] * slope[unit, here, :].astype(F32)
                pre[unit, here, :] = value.astype(BF16)
                carry = carry + fold_rows(value)
            return carry

        summed = lax.fori_loop(0, tokens // rows, chunk, jnp.zeros((8, tile), F32))
        row = jnp.sum(summed, axis=0, keepdims=True)
        for side, bias in enumerate((bias_far, bias_own)):

            @pl.when(unit // tiles == side)
            def _():
                bias[pl.ds(unit % tiles, 1), :] = row
                result(unit, side).start()

        return carry

    lax.fori_loop(0, units, turn, 0)
    up_in[units - 1].wait()
    by_blocks(total, pre.at[units - 1], lambda: w_up[units - 1], dot_nt, add=True)

    def leave(start):
        here = pl.ds(start, CHUNK)
        normed_grad = total[here, :]
        through, gain_term = norm_backward(mid[here, :], normed_grad, gain[layer, 1:2, :])
        value = grad_in[here, :].astype(F32) + through
        grad_mid[here, :] = value
        low[here, :] = value.astype(BF16)
        partial[1] += fold_rows(value)
        partial[2] += fold_rows(gain_term)
        partial[3] += fold_rows(normed_grad)

    by_rows(tokens, leave, 2)
    sums[...] = jnp.sum(partial[...], axis=1)
    by_blocks(mid_t, order, lambda: low[...], dot_nt)
    for copy in out_in:
        copy.wait()
    by_blocks(att_far, low, lambda: w_out[0], dot_nt)
    by_blocks(att_own, low, lambda: w_out[1], dot_nt)
    for unit in range(units):
        result(unit, unit // tiles).wait()


def attend_back_kernel(slots, counts, joint, lse, grad_att, grad_joint, bias_sums):
    width = grad_att.shape[1]
    pairs = width // (2 * HEAD_DIM)
    scale = HEAD_DIM ** (-0.5)
    masks = head_masks(slots)
    key_index = lax.broadcasted_iota(jnp.int32, (slots, slots), 0)
    bias_sums[...] = jnp.zeros_like(bias_sums)

    def step(index, carry):
        image = index // pairs
        pair = index % pairs
        rows = pl.ds(pl.multiple_of(image * slots, slots), slots)
        lanes = pl.ds(pl.multiple_of(pair * 2 * HEAD_DIM, 2 * HEAD_DIM), 2 * HEAD_DIM)
        queries = joint[0, rows, lanes]
        keys_in = joint[1, rows, lanes]
        values_in = joint[2, rows, lanes]
        grads = grad_att[rows, lanes]
        keys_t = keys_in.T
        keys_scaled = keys_in * jnp.asarray(scale, BF16)
        valid = key_index < own_count(counts, image, grad_att.shape[0] // slots)
        zeros = jnp.zeros_like(keys_in)
        scores = [
            dot_nt(jnp.where(masks[side], keys_scaled, zeros), queries) for side in range(2)
        ]
        grad_probs = [dot_nt(jnp.where(masks[side], values_in, zeros), grads) for side in range(2)]
        probs = [
            jnp.exp(jnp.where(valid, scores[side], NEGATIVE) - lse[2 * index + side])
            for side in range(2)
        ]
        value_parts = [dot(weights.astype(BF16), grads) for weights in probs]
        inner = [
            jnp.sum(back * weights, axis=0, keepdims=True) for back, weights in zip(grad_probs, probs)
        ]
        grad_scores = [
            (weights * (back - total)).astype(BF16)
            for weights, back, total in zip(probs, grad_probs, inner)
        ]
        key_parts = [dot(back, queries) for back in grad_scores]
        query_parts = [
            dot(keys_t[side * HEAD_DIM : (side + 1) * HEAD_DIM], grad_scores[side])
            for side in range(2)
        ]
        grad_queries = jnp.concatenate(query_parts, axis=0).T * scale
        grad_keys = jnp.where(masks[0], key_parts[0], key_parts[1]) * scale
        grad_values = jnp.where(masks[0], value_parts[0], value_parts[1])
        bias_sums[0:1, lanes] += jnp.sum(grad_queries, axis=0, keepdims=True)
        value_lanes = pl.ds(
            pl.multiple_of(width + pair * 2 * HEAD_DIM, 2 * HEAD_DIM), 2 * HEAD_DIM
        )
        bias_sums[0:1, value_lanes] += jnp.sum(grad_values, axis=0, keepdims=True)
        grad_joint[0, rows, lanes] = grad_queries.astype(BF16)
        grad_joint[1, rows, lanes] = grad_keys.astype(BF16)
        grad_joint[2, rows, lanes] = grad_values.astype(BF16)
        return carry

    lax.fori_loop(0, (grad_att.shape[0] // slots) * pairs, step, 0)


def entry_back_kernel(
    layer, with_low, joint_own, joint_far, weight_own, weight_far, stream, gain, grad_mid, order, *rest
):
    if with_low:
        grad_out, sums, low_t, total, partial, low = rest
    else:
        grad_out, sums, total, partial = rest
    member = pl.program_id(0)

    @pl.when(member == 0)
    def _():
        total[...] = jnp.zeros_like(total)
        partial[...] = jnp.zeros_like(partial)

    left = jnp.concatenate([joint_own[member], joint_far[member]], axis=1)
    right = jnp.concatenate([weight_own[0, 0], weight_far[0, 0]], axis=1)
    total[...] += dot_nt(left, right)

    def rows(start):
        here = pl.ds(start, CHUNK)
        normed_grad = total[here, :]
        through, gain_term = norm_backward(
            stream[here, :].astype(F32), normed_grad, gain[layer, 0:1, :]
        )
        value = grad_mid[here, :] + through
        grad_out[here, :] = value
        if with_low:
            low[here, :] = value.astype(BF16)
        partial[0] += fold_rows(gain_term)
        partial[1] += fold_rows(normed_grad)

    @pl.when(member == 2)
    def _():
        by_rows(stream.shape[0], rows, 2)
        sums[...] = jnp.sum(partial[...], axis=1)
        if with_low:
            by_blocks(low_t, order, lambda: low[...], dot_nt)


def pack_kernel(layers, *refs):
    ins, (own_out, far_out) = refs[:-2], refs[-2:]
    for layer in range(layers):
        sums_mid, sums_in, qv_own, qv_far, upb_own, upb_far = ins[6 * layer : 6 * layer + 6]
        tiles = upb_own.shape[0]
        for ref, qv, upb in ((own_out, qv_own, upb_own), (far_out, qv_far, upb_far)):
            for row, value in (
                (2 * layer, sums_in[0:1, :]),
                (2 * layer + 1, sums_mid[2:3, :]),
                (2 * (layers + layer), sums_in[1:2, :]),
                (2 * (layers + layer) + 1, sums_mid[3:4, :]),
                (2 * (2 * layers + layer), sums_mid[1:2, :]),
                (2 * (2 * layers + layer) + 1, sums_mid[0:1, :]),
                (6 * layers + layer, qv[...]),
            ):
                ref[row : row + 1, :] = value
            start = 7 * layers + tiles * layer
            ref[start : start + tiles, :] = upb[...]


def unpack_kernel(layers, mine, gain, bias, out_bias, qv, upb):
    total = mine[...]
    half = qv.shape[2]
    tiles = upb.shape[1] // mine.shape[1]
    width = mine.shape[1]
    for layer in range(layers):
        for norm in range(2):
            row = 2 * layer + norm
            gain[layer, norm : norm + 1, :] = total[row : row + 1]
            row += 2 * layers
            bias[layer, norm : norm + 1, :] = total[row : row + 1]
            row += 2 * layers
            out_bias[layer, norm : norm + 1, :] = total[row : row + 1]
        row = 6 * layers + layer
        for kind in range(2):
            qv[layer, kind : kind + 1, :] = total[row : row + 1, kind * half : (kind + 1) * half]
        row = 7 * layers + tiles * layer
        for part in range(tiles):
            upb[layer : layer + 1, part * width : (part + 1) * width] = total[
                row + part : row + part + 1
            ]


def finish_kernel(parts, *refs):
    layers = len(refs) // parts
    outs = refs[layers * parts :]
    for layer in range(layers):
        total = refs[layer * parts][...].astype(F32)
        for ref in refs[layer * parts + 1 : (layer + 1) * parts]:
            total = total + ref[...].astype(F32)
        column = 0
        for ref in outs:
            size = ref.shape[3]
            for member in range(ref.shape[1]):
                ref[layer, member] = total[:, column : column + size]
                column += size


def chunk_sources(order):
    first = list(order[:4])
    sources = []
    for target in range(16):
        source = 0
        for place, bit in enumerate(first):
            if (target >> (3 - place)) & 1:
                source |= 1 << (3 - bit)
        sources.append(source)
    return sources


def weight_kernel(sources, tiles, has_extra, *refs):
    if has_extra:
        left_own, left_far, right_own, right_far, lx_own, lx_far, rx_own, rx_far, keep, send = refs
    else:
        left_own, left_far, right_own, right_far, keep, send = refs

    def product(a_own, a_far, b_own, b_far):
        left = jnp.concatenate([a_own[...], a_far[...]], axis=1)
        right = jnp.concatenate([b_own[...].reshape(b_own.shape[-2:]), b_far[...].reshape(b_far.shape[-2:])], axis=0)
        size = left.shape[0] // 16
        low = dot(left, right).astype(BF16)
        for target, source in enumerate(sources):
            ref = keep if target < 8 else send
            ref[(target % 8) * size : (target % 8 + 1) * size, :] = low[
                source * size : (source + 1) * size, :
            ]

    if has_extra:

        @pl.when(pl.program_id(0) < tiles)
        def _():
            product(left_own, left_far, right_own, right_far)

        @pl.when(pl.program_id(0) == tiles)
        def _():
            product(lx_own, lx_far, rx_own, rx_far)

    else:
        product(left_own, left_far, right_own, right_far)


def weight_grad(name, order, left, right, extra=None, tiles=None, first=0):
    left_own, left_far = left
    right_own, right_far = right
    width, tokens = left_own.shape
    if right_own.ndim == 3:
        tile = right_own.shape[2]
        right_spec = pl.BlockSpec(
            (1, tokens, tile), lambda j: (jnp.minimum(j, tiles - 1) + first, 0, 0)
        )
    else:
        tile = 768 if tiles else 512
        tiles = tiles or right_own.shape[1] // tile
        right_spec = pl.BlockSpec((tokens, tile), lambda j: (0, j + first))
    steps = tiles + (1 if extra is not None else 0)
    ins = [left_own, left_far, right_own, right_far]
    specs = [fixed((width, tokens))] * 2 + [right_spec] * 2
    if extra is not None:
        ins += list(extra)
        specs += [fixed((width, tokens))] * 2 + [fixed((tokens, tile))] * 2
    half = out((width // 2, steps * tile), BF16)
    half_spec = pl.BlockSpec((width // 2, tile), lambda j: (0, j))
    return call(
        functools.partial(weight_kernel, chunk_sources(order), tiles, extra is not None),
        name,
        (steps,),
        ins,
        specs,
        [half, half],
        [half_spec, half_spec],
        flops=4 * width * tokens * steps * tile,
    )


def flip(bit):
    size = lax.axis_size("dp")
    return [(index, index ^ (1 << bit)) for index in range(size)]


class DpSum:
    def __init__(self, order, halves=None, units=()):
        self.order = list(order)
        self.incoming = None
        if halves is not None:
            keep, self.outgoing = halves
            self.members = [[keep]]
        else:
            self.members = [parts for unit in units for parts in unit.members]
            self.halve()

    def halve(self):
        rows = self.members[0][0].shape[0] // 2
        sends = [
            sum(part[rows:].astype(F32) for part in parts).astype(BF16) for parts in self.members
        ]
        self.outgoing = sends[0] if len(sends) == 1 else jnp.concatenate(sends, axis=1)
        self.members = [[part[:rows] for part in parts] for parts in self.members]

    @classmethod
    def joined(cls, units):
        whole_unit = cls(units[0].order, (None, jnp.concatenate([u.outgoing for u in units], axis=1)))
        whole_unit.members = [parts for unit in units for parts in unit.members]
        return whole_unit

    def start(self):
        self.incoming = lax.ppermute(self.outgoing, "dp", flip(self.order.pop(0)))

    def turn(self, go=True):
        column = 0
        for parts in self.members:
            width = parts[0].shape[1]
            parts.append(self.incoming[:, column : column + width])
            column += width
        self.incoming = None
        if self.order:
            self.halve()
            if go:
                self.start()

    def flying(self):
        return [self.incoming]

    def land(self, arrays):
        (self.incoming,) = arrays


class Everywhere:
    def __init__(self, mine, far, groups):
        self.mine = mine
        self.incoming = [swap(far)]
        self.groups = list(groups)

    def flying(self):
        return self.incoming

    def land(self, arrays):
        self.incoming = arrays

    def turn(self):
        if len(self.incoming) == 1:
            self.mine = self.mine + self.incoming[0]
        else:
            near, far, across = self.incoming
            self.mine = (self.mine + near) + (far + across)
        self.incoming = []
        if self.groups:
            group = self.groups.pop(0)
            masks = [1 << bit for bit in group]
            if len(masks) == 2:
                masks.append(masks[0] | masks[1])
            size = lax.axis_size("dp")
            self.incoming = [
                lax.ppermute(self.mine, "dp", [(index, index ^ mask) for index in range(size)])
                for mask in masks
            ]


def gate(value, starts=(), turns=(), after=(), holds=()):
    ends = [*turns, *holds]
    held = [unit.outgoing for unit in starts] + [array for unit in ends for array in unit.flying()]
    value, *held = lax.optimization_barrier((value, *held, *after))
    for unit in starts:
        unit.outgoing = held.pop(0)
        unit.start()
    for unit in ends:
        unit.land([held.pop(0) for _ in unit.flying()])
    for unit in turns:
        unit.turn()
    for unit in holds:
        unit.turn(go=False)
    return value


def swap(values):
    return lax.ppermute(values, "tensor", [(0, 1), (1, 0)])


def shards(
    images,
    valid_count,
    ln_gain,
    ln_bias,
    w_qkv,
    qv_bias,
    w_out,
    out_bias,
    w_up,
    up_bias,
    w_down,
    cotangent,
):
    local_rows, slots, width = images.shape
    tokens = local_rows * slots
    half = w_qkv.shape[3]
    ff_half = w_up.shape[2]
    tile = 768
    steps = ff_half // tile
    heads = half // HEAD_DIM
    dp = lax.axis_size("dp")
    bits = dp.bit_length() - 1
    assert dp == 1 << bits and bits >= 4 and lax.axis_size("tensor") == 2
    tail = tuple(range(4, bits))
    order_a = (0, 1, 2, 3) + tail
    order_b = (1, 0, 2, 3) + tail
    order_e = (2, 0, 1, 3) + tail
    order_d = (0, 2, 3, 1) + tail

    me = lax.axis_index("dp")
    counts = valid_count

    block = width // dp
    row = jnp.arange(width, dtype=jnp.int32)
    index = row // block
    mirrored = jnp.zeros_like(index)
    for bit in range(bits):
        mirrored = mirrored | (((index >> (bits - 1 - bit)) & 1) << bit)
    source = (mirrored ^ me) * block + row % block
    order = (source[:, None] == row[None, :]).astype(BF16)

    w_qkv = jnp.transpose(w_qkv, (0, 2, 1, 3))
    qkv = (w_qkv, swap(w_qkv))
    qv = (qv_bias, swap(qv_bias))

    images_2d = images.reshape(tokens, width)
    cotangent_2d = cotangent.reshape(tokens, width)
    smem = pl.BlockSpec(memory_space=pltpu.SMEM)
    wide = (tokens, width)
    flops_wide = 2 * width * width * tokens

    normed, normed_t, cotangent_t, wide_cotangent = call(
        prep_kernel,
        "prep",
        (),
        [images_2d, cotangent_2d, ln_gain, ln_bias, order],
        [whole()] * 5,
        [out(wide, BF16), out((width, tokens), BF16), out((width, tokens), BF16), out(wide, F32)],
        [whole()] * 4,
        flops=2 * flops_wide,
    )

    wout, wup, wdown = [
        (weight, swap(lax.optimization_barrier((weight, normed, qkv[1], qv[1]))[0]))
        for weight in (w_out, w_up, w_down)
    ]

    def attend(layer, normed, counts):
        lse_shape = (local_rows * heads, 1, slots)
        joint_out = out((3, tokens, half), BF16)
        att_out = out((tokens, half), BF16)
        lse_out = out(lse_shape, F32)
        results = call(
            functools.partial(attend_kernel, slots),
            "attend",
            (),
            [jnp.full((1,), layer, jnp.int32), counts, normed, in_hbm(qkv[0]), in_hbm(qkv[1]), qv[0], qv[1]],
            [smem, smem, whole(), hbm(), hbm(), whole(), whole()],
            [joint_out, joint_out, att_out, att_out, lse_out, lse_out],
            [whole()] * 6,
            [pltpu.VMEM((2, 3, width, half), BF16), pltpu.SemaphoreType.DMA((2, 3))],
            flops=12 * tokens * width * half + 8 * tokens * slots * half,
            limit=44,
        )
        return results[0::2], results[1::2]

    stream = images_2d
    saved = []
    got_cotangent_t = swap(cotangent_t)
    pooled = None
    for layer in range(LAYERS):
        last = layer == LAYERS - 1
        own, far = attend(layer, normed, counts)
        if layer == 0:
            upb = (up_bias, swap(up_bias))
        gain_in = ln_gain
        if layer > 0:
            before = saved[layer - 1]
            names = ("got_normed_t", "got_att", "got_mid_normed_t", "got_hid")
            gain_in, got_cotangent_t, *got = lax.optimization_barrier(
                (ln_gain, got_cotangent_t, *[before[name] for name in names])
            )
            before.update(zip(names, got))
        ff = pltpu.HBM((tokens, ff_half), BF16)
        extra = (
            [out((local_rows, width), F32)]
            if last
            else [out(wide, BF16), out((width, tokens), BF16)]
        )
        results = call(
            functools.partial(feed_kernel, layer, slots, last),
            "feed",
            (),
            [
                counts,
                stream,
                own[1],
                far[1],
                in_hbm(wout[0]),
                in_hbm(wout[1]),
                out_bias,
                gain_in,
                ln_bias,
                order,
                in_hbm(wup[0]),
                in_hbm(wup[1]),
                upb[0],
                upb[1],
                in_hbm(wdown[0]),
                in_hbm(wdown[1]),
            ],
            [smem]
            + [whole()] * 3
            + [hbm()] * 2
            + [whole()] * 4
            + [hbm()] * 2
            + [whole()] * 2
            + [hbm()] * 2,
            [out(wide, F32), out((width, tokens), BF16), ff, ff, ff, ff, out(wide, F32)] + extra,
            [whole()] * 2 + [hbm()] * 4 + [whole()] * (1 + len(extra)),
            [
                pltpu.VMEM(wide, BF16),
                pltpu.VMEM(wide, F32),
                pltpu.VMEM((2, tokens, tile), F32),
                pltpu.VMEM((2 * half, width), BF16),
                pltpu.VMEM((2 * steps, width, tile), BF16),
                pltpu.VMEM((2 * steps, tile, width), BF16),
                pltpu.VMEM((2 * steps, tokens, tile), BF16),
                pltpu.VMEM((2 * steps, tokens, tile), BF16),
                pltpu.SemaphoreType.DMA((2 + 4 * steps,)),
                pltpu.SemaphoreType.DMA((4 * steps,)),
            ],
            flops=8 * tokens * width * ff_half + 2 * flops_wide,
            limit=32,
        )
        mid, mid_normed_t, hid_own, hid_far, slope_own, slope_far, stream_next = results[:7]
        saved.append(
            dict(
                stream=stream,
                own=own,
                far=far,
                mid=mid,
                slope=(slope_own, slope_far),
                hid=hid_own,
                attended=own[1],
                normed_t=normed_t,
                mid_normed_t=mid_normed_t,
                got_hid=swap(hid_far),
                got_att=swap(far[1]),
                got_normed_t=swap(normed_t),
                got_mid_normed_t=swap(mid_normed_t),
            )
        )
        stream = stream_next
        if last:
            pooled = results[7]
        else:
            normed, normed_t = results[7:9]

    def feed_back(layer, grad, gain_in):
        kept = saved[layer]
        ff = pltpu.HBM((tokens, ff_half), BF16)
        bias_shape = out((steps, tile), F32)
        att_shape = out((tokens, half), BF16)
        return call(
            feed_back_kernel,
            "feed_back",
            (),
            [
                jnp.full((1,), layer, jnp.int32),
                grad,
                kept["mid"],
                gain_in,
                order,
                in_hbm(wdown[0]),
                in_hbm(wdown[1]),
                in_hbm(wup[0]),
                in_hbm(wup[1]),
                kept["slope"][0],
                kept["slope"][1],
                in_hbm(wout[0]),
                in_hbm(wout[1]),
            ],
            [smem] + [whole()] * 4 + [hbm()] * 8,
            [
                ff,
                ff,
                bias_shape,
                bias_shape,
                out(wide, F32),
                out((width, tokens), BF16),
                att_shape,
                att_shape,
                out((4, width), F32),
            ],
            [hbm()] * 2 + [whole()] * 7,
            [
                pltpu.VMEM(wide, BF16),
                pltpu.VMEM(wide, F32),
                pltpu.VMEM((2, tokens, tile), F32),
                pltpu.VMEM((4, 8, width), F32),
                pltpu.VMEM((2 * steps, tile, width), BF16),
                pltpu.VMEM((2 * steps, width, tile), BF16),
                pltpu.VMEM((2 * steps, tokens, tile), BF16),
                pltpu.VMEM((2 * steps, tokens, tile), BF16),
                pltpu.VMEM((2, half, width), BF16),
                pltpu.SemaphoreType.DMA((4, 2 * steps)),
                pltpu.SemaphoreType.DMA((2 * steps,)),
            ],
            flops=8 * tokens * width * ff_half + 2 * flops_wide,
            limit=32,
        )

    def attend_back(forward, grad_att, counts_in):
        joint, _, lse = forward
        return call(
            functools.partial(attend_back_kernel, slots),
            "attend_back",
            (),
            [counts_in, joint, lse, grad_att],
            [smem, whole(), whole(), whole()],
            [out(joint.shape, BF16), out((1, 2 * half), F32)],
            [whole()] * 2,
            flops=10 * tokens * slots * half,
        )

    def entry_back(layer, joint_own, joint_far, grad_mid, gain_in):
        with_low = layer > 0
        return call(
            functools.partial(entry_back_kernel, layer, with_low),
            "entry_back",
            (3,),
            [
                joint_own,
                joint_far,
                in_hbm(qkv[0]),
                in_hbm(qkv[1]),
                saved[layer]["stream"],
                gain_in,
                grad_mid,
                order,
            ],
            [whole()] * 2
            + [pl.BlockSpec((1, 1, width, half), lambda c: (layer, c, 0, 0))] * 2
            + [whole()] * 4,
            [out(wide, F32), out((2, width), F32)]
            + ([out((width, tokens), BF16)] if with_low else []),
            [whole()] * (3 if with_low else 2),
            [pltpu.VMEM(wide, F32), pltpu.VMEM((2, 8, width), F32)]
            + ([pltpu.VMEM(wide, BF16)] if with_low else []),
            flops=12 * tokens * width * half,
        )

    def down_halves(layer, order_of, grad_t, got_grad_t):
        kept = saved[layer]
        return weight_grad(
            "down_grad", order_of, (grad_t, got_grad_t), (in_hbm(kept["hid"]) if layer else kept["hid"], kept["got_hid"])
        )

    def up_halves(layer, order_of, pre_own, got_pre, tiles=None, first=0):
        kept = saved[layer]
        return weight_grad(
            "up_grad",
            order_of,
            (kept["mid_normed_t"], kept["got_mid_normed_t"]),
            (pre_own, got_pre),
            tiles=tiles,
            first=first,
        )

    def lefts(layer):
        return saved[layer]["normed_t"], saved[layer]["got_normed_t"]

    def extras(layer, mid_t, got_mid_t):
        return mid_t, got_mid_t, saved[layer]["attended"], saved[layer]["got_att"]

    small = [None] * LAYERS
    down_1 = DpSum(order_a, down_halves(1, order_a, cotangent_t, got_cotangent_t))
    gain_in = gate(ln_gain, [down_1])
    pre_own, pre_far, upb_own, upb_far, grad_mid, mid_t, att_own, att_far, sums_mid = feed_back(
        1, wide_cotangent, gain_in
    )
    got_pre, got_mid_t = swap(pre_far), swap(mid_t)
    joint_far, qv_far = attend_back(saved[1]["far"], att_far, counts)
    got_joint = swap(joint_far)
    pre_own = gate(pre_own, [], [], [qv_far], [down_1])
    pre_own = gate(pre_own, [down_1])
    up_1 = DpSum(order_a, up_halves(1, order_a, pre_own, got_pre))
    counts_in = gate(counts, [up_1])
    joint_own, qv_own = attend_back(saved[1]["own"], att_own, counts_in)
    gain_in = gate(gain_in, after=[qv_own])
    grad, sums_in, grad_t = entry_back(1, joint_own, joint_far, grad_mid, gain_in)
    got_grad_t = swap(grad_t)
    small[1] = (sums_mid, sums_in, qv_own, qv_far, upb_own, upb_far)
    joint_own = gate(joint_own, [], [down_1], [sums_in])
    rest_1 = DpSum(
        order_e,
        weight_grad(
            "qkv_out_grad",
            order_e,
            lefts(1),
            (joint_own, got_joint),
            extras(1, mid_t, got_mid_t),
            tiles=3,
        ),
    )
    grad_t = gate(grad_t, [rest_1])
    down_0 = DpSum(order_a, down_halves(0, order_a, grad_t, got_grad_t))

    gain_in = gate(gain_in, [down_0], [up_1], holds=[down_1])
    pre_own, pre_far, upb_own, upb_far, grad_mid, mid_t, att_own, att_far, sums_mid = feed_back(
        0, grad, gain_in
    )
    got_pre, got_mid_t = swap(pre_far), swap(mid_t)
    counts_in = gate(counts_in, [], [up_1], [sums_mid], [rest_1])
    joint_far, qv_far = attend_back(saved[0]["far"], att_far, counts_in)
    got_joint = swap(joint_far)
    pre_own = gate(pre_own, [], [], [qv_far], [down_0, up_1])
    late_1 = DpSum.joined([up_1, down_1])
    pre_own = gate(pre_own, [down_0, late_1])
    up_0 = DpSum(order_d, up_halves(0, order_d, pre_own, got_pre))
    counts_in = gate(counts_in, [up_0], [], [got_mid_t, got_joint])
    joint_own, qv_own = attend_back(saved[0]["own"], att_own, counts_in)
    rest_0 = DpSum(
        order_b,
        weight_grad(
            "qkv_out_grad",
            order_b,
            lefts(0),
            (joint_own, got_joint),
            extras(0, mid_t, got_mid_t),
            tiles=3,
        ),
    )
    gain_in = gate(gain_in, [rest_0], [down_0, late_1], [qv_own])
    grad, sums_in = entry_back(0, joint_own, joint_far, grad_mid, gain_in)
    last = gate(sums_in, [rest_1], [up_0])
    small[0] = (sums_mid, last, qv_own, qv_far, upb_own, upb_far)
    ins = [array for arrays in small for array in arrays]
    vector_shape = out(((7 + steps) * LAYERS, width), F32)
    mine, far = call(
        functools.partial(pack_kernel, LAYERS),
        "pack_small",
        (),
        ins,
        [whole()] * len(ins),
        [vector_shape] * 2,
        [whole()] * 2,
    )
    vector = Everywhere(mine, far, [(0, 1), (2,), (3,), *[(bit,) for bit in tail]])
    last = gate(last, holds=[down_0])
    last = gate(last, [], [rest_0, up_0, vector], [down_0.outgoing], [rest_1])
    last = gate(last, holds=[rest_0, up_0])
    last = gate(last, [rest_0, up_0, down_0, rest_1], [vector])
    last = gate(last, [], [rest_0, up_0, down_0, rest_1, vector])
    last = gate(last, [], [rest_0, rest_1])
    last = gate(last, [], [vector])
    while vector.flying():
        vector.turn()
    running = [late_1, rest_1, down_0, up_0, rest_0]
    while any(unit.incoming is not None for unit in running):
        last = gate(last, [], [unit for unit in running if unit.incoming is not None][:4])

    def finish(first, second, shapes):
        ins = [*first, *second]
        return call(
            functools.partial(finish_kernel, len(first)),
            "finish",
            (),
            ins,
            [whole()] * len(ins),
            [out((LAYERS,) + shape, F32) for shape in shapes],
            [whole()] * len(shapes),
        )

    (down_grad,) = finish(down_0.members[0], late_1.members[1], [(1, block, ff_half)])
    (up_grad,) = finish(up_0.members[0], late_1.members[0], [(1, block, ff_half)])
    qkv_grad, out_grad = finish(rest_0.members[0], rest_1.members[0], [(3, block, half), (1, block, half)])
    total, qkv_grad = lax.optimization_barrier((vector.mine, qkv_grad))
    gain_grads, shift_grads, outb_grads, qv_grads, upb_grads = call(
        functools.partial(unpack_kernel, LAYERS),
        "unpack_small",
        (),
        [total],
        [whole()],
        [
            out(ln_gain.shape, F32),
            out(ln_bias.shape, F32),
            out(out_bias.shape, F32),
            out(qv_bias.shape, F32),
            out(up_bias.shape, F32),
        ],
        [whole()] * 5,
    )
    return (
        stream.reshape(images.shape),
        pooled,
        grad.reshape(images.shape),
        gain_grads,
        shift_grads,
        jnp.transpose(qkv_grad, (0, 2, 1, 3)),
        qv_grads,
        jnp.transpose(out_grad[:, 0], (0, 2, 1)),
        outb_grads,
        up_grad[:, 0],
        upb_grads,
        jnp.transpose(down_grad[:, 0], (0, 2, 1)),
    )


def solution(mesh):
    placed = (
        P(("dp", "tensor"), None, None),
        P("dp"),
        P(),
        P(),
        P(None, None, None, "tensor"),
        P(None, None, "tensor"),
        P(None, "tensor", None),
        P(),
        P(None, None, "tensor"),
        P(None, "tensor"),
        P(None, "tensor", None),
        P(("dp", "tensor"), None, None),
    )
    return jax.shard_map(
        shards,
        mesh=mesh,
        in_specs=placed,
        out_specs=(
            P(("dp", "tensor"), None, None),
            P(("dp", "tensor"), None),
            P(("dp", "tensor"), None, None),
            P(),
            P(),
            P(None, "dp", None, "tensor"),
            P(None, None, "tensor"),
            P(None, "tensor", "dp"),
            P(),
            P(None, "dp", "tensor"),
            P(None, "tensor"),
            P(None, "tensor", "dp"),
        ),
        check_vma=False,
    )
```

```python
import functools
import math

import jax
import jax.numpy as jnp
from jax import lax
from jax.experimental import pallas as pl
from jax.experimental.pallas import tpu as pltpu
from jax.sharding import PartitionSpec as P

HEAD_DIM = 64
LAYERS = 2
EPSILON = 1e-06
NEGATIVE = -1e30
BF16 = jnp.bfloat16
F32 = jnp.float32
CHUNK = 16
BAND = 64


def dot(left, right):
    return lax.dot_general(left, right, (((1,), (0,)), ((), ())), preferred_element_type=F32)


def dot_nt(left, right):
    return lax.dot_general(left, right, (((1,), (1,)), ((), ())), preferred_element_type=F32)


def fixed(shape, *lead):
    where = tuple(lead) + (0,) * (len(shape) - len(lead))
    return pl.BlockSpec(shape, lambda *_: where)


def out(shape, dtype):
    return jax.ShapeDtypeStruct(shape, dtype)


def in_hbm(values):
    return pltpu.with_memory_space_constraint(values, pltpu.HBM)


def cost(flops, *arrays):
    total = sum(math.prod(a.shape) * a.dtype.itemsize for a in arrays)
    return pl.CostEstimate(flops=int(flops) // 64, bytes_accessed=int(total) // 64, transcendentals=0)


MIB = 1 << 20


def call(body, name, grid, ins, in_specs, outs, out_specs, scratch=(), flops=0, limit=24):
    return pl.pallas_call(
        body,
        name=name,
        grid=grid,
        in_specs=in_specs,
        out_specs=out_specs,
        out_shape=outs,
        scratch_shapes=list(scratch),
        compiler_params=pltpu.CompilerParams(vmem_limit_bytes=limit * MIB),
        cost_estimate=cost(flops, *ins, *outs),
    )(*ins)


def whole():
    return pl.BlockSpec(memory_space=pltpu.VMEM)


def by_blocks(target, left, right, product, rows=256, add=False):
    def block(index, carry):
        here = pl.ds(pl.multiple_of(index * rows, rows), rows)
        value = product(left[here, :], right())
        if add:
            value = target[here, :] + value
        target[here, :] = value.astype(target.dtype)
        return carry

    lax.fori_loop(0, left.shape[0] // rows, block, 0)


def hbm():
    return pl.BlockSpec(memory_space=pltpu.HBM)


def by_rows(rows, body, unroll=1):
    def step(index, carry):
        for part in range(unroll):
            body(pl.multiple_of((index * unroll + part) * BAND, BAND))
        return carry

    lax.fori_loop(0, rows // (BAND * unroll), step, 0)


def moments(values):
    average = jnp.mean(values, axis=-1, keepdims=True)
    centred = values - average
    variance = jnp.mean(centred * centred, axis=-1, keepdims=True)
    return centred, lax.rsqrt(variance + EPSILON)


def normalized(values, gain, bias):
    centred, scale = moments(values)
    return centred * scale * gain + bias


def norm_backward(values, grad_normed, gain):
    centred, scale = moments(values)
    unit = centred * scale
    grad_unit = grad_normed * gain
    first = jnp.mean(grad_unit, axis=-1, keepdims=True)
    second = jnp.mean(grad_unit * unit, axis=-1, keepdims=True)
    return scale * (grad_unit - first - unit * second), grad_normed * unit


def fold_rows(values):
    total = values[0:8]
    for start in range(8, values.shape[0], 8):
        total = total + values[start : start + 8]
    return total


def prep_kernel(images, cotangent, gain, bias, order, normed, normed_t, cotangent_t, wide_cotangent):
    def rows(start):
        here = pl.ds(start, BAND)
        values = images[here, :].astype(F32)
        normed[here, :] = normalized(values, gain[0, 0:1, :], bias[0, 0:1, :]).astype(BF16)
        wide_cotangent[here, :] = cotangent[here, :].astype(F32)

    by_rows(images.shape[0], rows, 1)
    by_blocks(normed_t, order, lambda: normed[...], dot_nt)
    by_blocks(cotangent_t, order, lambda: cotangent[...], dot_nt)


def head_masks(slots):
    lane = lax.broadcasted_iota(jnp.int32, (slots, 2 * HEAD_DIM), 1)
    return lane < HEAD_DIM, lane >= HEAD_DIM


def own_count(counts, image, images):
    return counts[lax.axis_index("tensor") * images + image]


def attend_kernel(
    slots,
    which,
    counts,
    normed,
    weight_own,
    weight_far,
    bias_own,
    bias_far,
    joint_own,
    joint_far,
    att_own,
    att_far,
    lse_own,
    lse_far,
    held,
    sem,
):
    width = att_own.shape[1]
    pairs = width // (2 * HEAD_DIM)
    scale = HEAD_DIM ** (-0.5)
    layer = which[0]
    weights = (weight_own, weight_far)
    for side in range(2):
        for member in range(3):
            fetch(weights[side].at[layer, member], held.at[side, member], sem.at[side, member])
    for side, (joint, bias) in enumerate(((joint_own, bias_own), (joint_far, bias_far))):

        def project(member, carry):
            pltpu.make_async_copy(
                weights[side].at[layer, member], held.at[side, member], sem.at[side, member]
            ).wait()
            shift = bias[layer, pl.ds(member // 2, 1), :]
            shift = jnp.where(member == 1, jnp.zeros_like(shift), shift)
            joint[member] = (dot(normed[...], held[side, member]) + shift).astype(BF16)
            return carry

        lax.fori_loop(0, 3, project, 0)
    masks = head_masks(slots)
    key_index = lax.broadcasted_iota(jnp.int32, (slots, slots), 0)

    def step(index, carry):
        image = index // pairs
        pair = index % pairs
        rows = pl.ds(pl.multiple_of(image * slots, slots), slots)
        lanes = pl.ds(pl.multiple_of(pair * 2 * HEAD_DIM, 2 * HEAD_DIM), 2 * HEAD_DIM)
        valid = key_index < own_count(counts, image, normed.shape[0] // slots)
        sets = ((joint_own, att_own, lse_own), (joint_far, att_far, lse_far))
        heads = []
        for joint, _, _ in sets:
            queries = joint[0, rows, lanes]
            keys_in = joint[1, rows, lanes] * jnp.asarray(scale, BF16)
            for side in range(2):
                keys_side = jnp.where(masks[side], keys_in, jnp.zeros_like(keys_in))
                heads.append(dot_nt(keys_side, queries))
        values_t = [joint[2, rows, lanes].T for joint, _, _ in sets]
        heads = [jnp.where(valid, scores, NEGATIVE) for scores in heads]
        largest = [jnp.max(scores, axis=0, keepdims=True) for scores in heads]
        heads = [jnp.exp(scores - top) for scores, top in zip(heads, largest)]
        totals = [jnp.sum(exponent, axis=0, keepdims=True) for exponent in heads]
        heads = [(exponent * (1.0 / total)).astype(BF16) for exponent, total in zip(heads, totals)]
        for which_set, (_, attended, lse) in enumerate(sets):
            parts = []
            for side in range(2):
                head = 2 * which_set + side
                lse[2 * index + side] = largest[head] + jnp.log(totals[head])
                parts.append(
                    dot(values_t[which_set][side * HEAD_DIM : (side + 1) * HEAD_DIM], heads[head])
                )
            attended[rows, lanes] = jnp.concatenate(parts, axis=0).T.astype(BF16)
        return carry

    lax.fori_loop(0, (normed.shape[0] // slots) * pairs, step, 0)


def fetch(source, target, sem):
    copy = pltpu.make_async_copy(source, target, sem)
    copy.start()
    return copy


def feed_kernel(
    layer,
    slots,
    last_layer,
    counts,
    stream,
    att_own,
    att_far,
    out_own,
    out_far,
    out_bias,
    gain,
    bias,
    order,
    up_own,
    up_far,
    up_bias_own,
    up_bias_far,
    down_own,
    down_far,
    mid,
    normed_t,
    hid_own,
    hid_far,
    slope_own,
    slope_far,
    stream_out,
    *rest,
):
    if last_layer:
        pooled = rest[0]
    else:
        next_normed, next_t = rest[:2]
    normed, total, pre, w_out, w_up, w_down, hid, slope, in_sem, out_sem = rest[1 if last_layer else 2 :]
    tokens = stream.shape[0]
    half = w_out.shape[0] // 2
    units = w_up.shape[0]
    tile = w_up.shape[2]
    tiles = units // 2
    out_in = [
        fetch(ref.at[layer], w_out.at[pl.ds(side * half, half)], in_sem.at[side])
        for side, ref in enumerate((out_own, out_far))
    ]
    up_in, down_in = [], []
    for unit in range(units):
        side, part = unit // tiles, unit % tiles
        columns = pl.ds(part * tile, tile)
        up_ref, down_ref = ((up_own, down_own), (up_far, down_far))[side]
        up_in.append(fetch(up_ref.at[layer, :, columns], w_up.at[unit], in_sem.at[2 + unit]))
        down_in.append(
            fetch(down_ref.at[layer, columns, :], w_down.at[unit], in_sem.at[2 + units + unit])
        )
    for copy in out_in:
        copy.wait()
    total[...] = dot(jnp.concatenate([att_own[...], att_far[...]], axis=1), w_out[...])

    def enter(start):
        here = pl.ds(start, BAND)
        value = stream[here, :].astype(F32) + (total[here, :] + out_bias[layer, 0:1, :])
        mid[here, :] = value
        normed[here, :] = normalized(value, gain[layer, 1:2, :], bias[layer, 1:2, :]).astype(BF16)

    by_rows(tokens, enter, 1)
    up_in[0].wait()
    by_blocks(pre.at[0], normed, lambda: w_up[0], dot)
    by_blocks(normed_t, order, lambda: normed[...], dot_nt)
    rows = 256
    out_copies = []
    for unit in range(units):
        side, part = unit // tiles, unit % tiles
        shift = (up_bias_own, up_bias_far)[side][layer : layer + 1, part * tile : (part + 1) * tile]
        if unit + 1 < units:
            up_in[unit + 1].wait()
        if unit > 0:
            down_in[unit - 1].wait()

        def chunk(index, carry):
            block = pl.ds(pl.multiple_of(index * rows, rows), rows)
            if unit + 1 < units:
                pre[(unit + 1) % 2, block, :] = dot(normed[block, :], w_up[unit + 1])
            if unit == 1:
                total[block, :] = dot(hid[unit - 1, block, :], w_down[unit - 1])
            elif unit > 1:
                total[block, :] += dot(hid[unit - 1, block, :], w_down[unit - 1])
            for sub in range(0, rows, CHUNK):
                here = pl.ds(pl.multiple_of(index * rows + sub, CHUNK), CHUNK)
                value = pre[unit % 2, here, :] + shift
                cdf = 0.5 + 0.5 * lax.erf(value * (0.5**0.5))
                hid[unit, here, :] = (value * cdf).astype(BF16)
                density = jnp.exp(-0.5 * value * value) * ((2.0 * math.pi) ** -0.5)
                slope[unit, here, :] = (cdf + value * density).astype(BF16)
            return carry

        lax.fori_loop(0, tokens // rows, chunk, 0)
        hid_ref, slope_ref = ((hid_own, slope_own), (hid_far, slope_far))[side]
        columns = pl.ds(part * tile, tile)
        out_copies.append(fetch(hid.at[unit], hid_ref.at[:, columns], out_sem.at[unit]))
        out_copies.append(fetch(slope.at[unit], slope_ref.at[:, columns], out_sem.at[units + unit]))
    down_in[units - 1].wait()
    by_blocks(total, hid.at[units - 1], lambda: w_down[units - 1], dot, add=True)

    def leave(start):
        here = pl.ds(start, BAND)
        value = mid[here, :] + (total[here, :] + out_bias[layer, 1:2, :])
        stream_out[here, :] = value
        if not last_layer:
            next_normed[here, :] = normalized(
                value, gain[layer + 1, 0:1, :], bias[layer + 1, 0:1, :]
            ).astype(BF16)

    by_rows(tokens, leave, 1)
    if last_layer:
        index = lax.broadcasted_iota(jnp.int32, (slots, 1), 0)
        for image in range(tokens // slots):
            block = stream_out[image * slots : (image + 1) * slots, :]
            count = own_count(counts, image, tokens // slots)
            summed = jnp.sum(jnp.where(index < count, block, 0.0), axis=0, keepdims=True)
            pooled[image : image + 1, :] = summed / count.astype(F32)
    else:
        by_blocks(next_t, order, lambda: next_normed[...], dot_nt)
    for copy in out_copies:
        copy.wait()


def feed_back_kernel(
    which,
    grad_in,
    mid,
    gain,
    order,
    down_own,
    down_far,
    up_own,
    up_far,
    slope_own,
    slope_far,
    out_own,
    out_far,
    pre_own,
    pre_far,
    bias_own,
    bias_far,
    grad_mid,
    mid_t,
    att_own,
    att_far,
    sums,
    low,
    total,
    hidden,
    partial,
    w_down,
    w_up,
    slope,
    pre,
    w_out,
    in_sem,
    out_sem,
):
    layer = which[0]
    tokens = grad_in.shape[0]
    units = w_up.shape[0]
    tile = w_up.shape[2]
    tiles = units // 2
    down_in, up_in, slope_in = [], [], []
    for unit in range(units):
        columns = pl.ds(unit % tiles * tile, tile)
        down_ref, up_ref, slope_ref = ((down_far, up_far, slope_far), (down_own, up_own, slope_own))[
            unit // tiles
        ]
        down_in.append(fetch(down_ref.at[layer, columns, :], w_down.at[unit], in_sem.at[0, unit]))
        slope_in.append(fetch(slope_ref.at[:, columns], slope.at[unit], in_sem.at[1, unit]))
        up_in.append(fetch(up_ref.at[layer, :, columns], w_up.at[unit], in_sem.at[2, unit]))
    out_in = [
        fetch(ref.at[layer], w_out.at[side], in_sem.at[3, side])
        for side, ref in enumerate((out_far, out_own))
    ]
    partial[...] = jnp.zeros_like(partial)

    def enter(start):
        here = pl.ds(start, BAND)
        value = grad_in[here, :].astype(F32)
        low[here, :] = value.astype(BF16)
        partial[0] += fold_rows(value)

    by_rows(tokens, enter)
    down_in[0].wait()
    by_blocks(hidden.at[0], low, lambda: w_down[0], dot_nt)
    rows = 256
    total[...] = jnp.zeros_like(total)
    pre[units - 1] = jnp.zeros_like(pre[units - 1])
    pre_refs = (pre_far, pre_own)

    def result(unit, side):
        columns = pl.ds(pl.multiple_of(unit % tiles * tile, tile), tile)
        return pltpu.make_async_copy(pre.at[unit], pre_refs[side].at[:, columns], out_sem.at[unit])

    def turn(unit, carry):
        after = jnp.minimum(unit + 1, units - 1)
        before = jnp.maximum(unit - 1, 0)

        @pl.when(unit + 1 < units)
        def _():
            pltpu.make_async_copy(
                down_own.at[layer, pl.ds(0, tile), :], w_down.at[after], in_sem.at[0, after]
            ).wait()

        @pl.when(unit != 1)
        def _():
            pltpu.make_async_copy(
                up_own.at[layer, :, pl.ds(0, tile)], w_up.at[before], in_sem.at[2, before]
            ).wait()

        pltpu.make_async_copy(
            slope_own.at[:, pl.ds(0, tile)], slope.at[unit], in_sem.at[1, unit]
        ).wait()
        idle = (unit + units - 1) % units

        def chunk(index, carry):
            block = pl.ds(pl.multiple_of(index * rows, rows), rows)
            hidden[(unit + 1) % 2, block, :] = dot_nt(low[block, :], w_down[after])
            total[block, :] += dot_nt(pre[idle, block, :], w_up[before])
            for sub in range(0, rows, CHUNK):
                here = pl.ds(pl.multiple_of(index * rows + sub, CHUNK), CHUNK)
                value = hidden[unit % 2, here, :] * slope[unit, here, :].astype(F32)
                pre[unit, here, :] = value.astype(BF16)
                carry = carry + fold_rows(value)
            return carry

        summed = lax.fori_loop(0, tokens // rows, chunk, jnp.zeros((8, tile), F32))
        row = jnp.sum(summed, axis=0, keepdims=True)
        for side, bias in enumerate((bias_far, bias_own)):

            @pl.when(unit // tiles == side)
            def _():
                bias[pl.ds(unit % tiles, 1), :] = row
                result(unit, side).start()

        return carry

    lax.fori_loop(0, units, turn, 0)
    up_in[units - 1].wait()
    by_blocks(total, pre.at[units - 1], lambda: w_up[units - 1], dot_nt, add=True)

    def leave(start):
        here = pl.ds(start, BAND)
        normed_grad = total[here, :]
        through, gain_term = norm_backward(mid[here, :], normed_grad, gain[layer, 1:2, :])
        value = grad_in[here, :].astype(F32) + through
        grad_mid[here, :] = value
        low[here, :] = value.astype(BF16)
        partial[1] += fold_rows(value)
        partial[2] += fold_rows(gain_term)
        partial[3] += fold_rows(normed_grad)

    by_rows(tokens, leave, 1)
    sums[...] = jnp.sum(partial[...], axis=1)
    by_blocks(mid_t, order, lambda: low[...], dot_nt)
    for copy in out_in:
        copy.wait()
    by_blocks(att_far, low, lambda: w_out[0], dot_nt)
    by_blocks(att_own, low, lambda: w_out[1], dot_nt)
    for unit in range(units):
        result(unit, unit // tiles).wait()


def attend_back_kernel(slots, counts, joint, lse, grad_att, grad_joint, bias_sums):
    width = grad_att.shape[1]
    pairs = width // (2 * HEAD_DIM)
    scale = HEAD_DIM ** (-0.5)
    masks = head_masks(slots)
    key_index = lax.broadcasted_iota(jnp.int32, (slots, slots), 0)
    bias_sums[...] = jnp.zeros_like(bias_sums)

    def step(index, carry):
        image = index // pairs
        pair = index % pairs
        rows = pl.ds(pl.multiple_of(image * slots, slots), slots)
        lanes = pl.ds(pl.multiple_of(pair * 2 * HEAD_DIM, 2 * HEAD_DIM), 2 * HEAD_DIM)
        queries = joint[0, rows, lanes]
        keys_in = joint[1, rows, lanes]
        values_in = joint[2, rows, lanes]
        grads = grad_att[rows, lanes]
        keys_t = keys_in.T
        keys_scaled = keys_in * jnp.asarray(scale, BF16)
        valid = key_index < own_count(counts, image, grad_att.shape[0] // slots)
        zeros = jnp.zeros_like(keys_in)
        scores = [
            dot_nt(jnp.where(masks[side], keys_scaled, zeros), queries) for side in range(2)
        ]
        grad_probs = [dot_nt(jnp.where(masks[side], values_in, zeros), grads) for side in range(2)]
        probs = [
            jnp.exp(jnp.where(valid, scores[side], NEGATIVE) - lse[2 * index + side])
            for side in range(2)
        ]
        value_parts = [dot(weights.astype(BF16), grads) for weights in probs]
        inner = [
            jnp.sum(back * weights, axis=0, keepdims=True) for back, weights in zip(grad_probs, probs)
        ]
        grad_scores = [
            (weights * (back - total)).astype(BF16)
            for weights, back, total in zip(probs, grad_probs, inner)
        ]
        key_parts = [dot(back, queries) for back in grad_scores]
        query_parts = [
            dot(keys_t[side * HEAD_DIM : (side + 1) * HEAD_DIM], grad_scores[side])
            for side in range(2)
        ]
        grad_queries = jnp.concatenate(query_parts, axis=0).T * scale
        grad_keys = jnp.where(masks[0], key_parts[0], key_parts[1]) * scale
        grad_values = jnp.where(masks[0], value_parts[0], value_parts[1])
        bias_sums[0:1, lanes] += jnp.sum(grad_queries, axis=0, keepdims=True)
        value_lanes = pl.ds(
            pl.multiple_of(width + pair * 2 * HEAD_DIM, 2 * HEAD_DIM), 2 * HEAD_DIM
        )
        bias_sums[0:1, value_lanes] += jnp.sum(grad_values, axis=0, keepdims=True)
        grad_joint[0, rows, lanes] = grad_queries.astype(BF16)
        grad_joint[1, rows, lanes] = grad_keys.astype(BF16)
        grad_joint[2, rows, lanes] = grad_values.astype(BF16)
        return carry

    lax.fori_loop(0, (grad_att.shape[0] // slots) * pairs, step, 0)


def entry_back_kernel(
    layer, with_low, joint_own, joint_far, weight_own, weight_far, stream, gain, grad_mid, order, *rest
):
    if with_low:
        grad_out, sums, low_t, total, partial, low = rest
    else:
        grad_out, sums, total, partial = rest
    member = pl.program_id(0)

    @pl.when(member == 0)
    def _():
        total[...] = jnp.zeros_like(total)
        partial[...] = jnp.zeros_like(partial)

    left = jnp.concatenate([joint_own[member], joint_far[member]], axis=1)
    right = jnp.concatenate([weight_own[0, 0], weight_far[0, 0]], axis=1)
    total[...] += dot_nt(left, right)

    def rows(start):
        here = pl.ds(start, BAND)
        normed_grad = total[here, :]
        through, gain_term = norm_backward(
            stream[here, :].astype(F32), normed_grad, gain[layer, 0:1, :]
        )
        value = grad_mid[here, :] + through
        grad_out[here, :] = value
        if with_low:
            low[here, :] = value.astype(BF16)
        partial[0] += fold_rows(gain_term)
        partial[1] += fold_rows(normed_grad)

    @pl.when(member == 2)
    def _():
        by_rows(stream.shape[0], rows, 1)
        sums[...] = jnp.sum(partial[...], axis=1)
        if with_low:
            by_blocks(low_t, order, lambda: low[...], dot_nt)


def pack_kernel(layers, *refs):
    ins, (own_out, far_out) = refs[:-2], refs[-2:]
    for layer in range(layers):
        sums_mid, sums_in, qv_own, qv_far, upb_own, upb_far = ins[6 * layer : 6 * layer + 6]
        tiles = upb_own.shape[0]
        for ref, qv, upb in ((own_out, qv_own, upb_own), (far_out, qv_far, upb_far)):
            for row, value in (
                (2 * layer, sums_in[0:1, :]),
                (2 * layer + 1, sums_mid[2:3, :]),
                (2 * (layers + layer), sums_in[1:2, :]),
                (2 * (layers + layer) + 1, sums_mid[3:4, :]),
                (2 * (2 * layers + layer), sums_mid[1:2, :]),
                (2 * (2 * layers + layer) + 1, sums_mid[0:1, :]),
                (6 * layers + layer, qv[...]),
            ):
                ref[row : row + 1, :] = value
            start = 7 * layers + tiles * layer
            ref[start : start + tiles, :] = upb[...]


def unpack_kernel(layers, mine, gain, bias, out_bias, qv, upb):
    total = mine[...]
    half = qv.shape[2]
    tiles = upb.shape[1] // mine.shape[1]
    width = mine.shape[1]
    for layer in range(layers):
        for norm in range(2):
            row = 2 * layer + norm
            gain[layer, norm : norm + 1, :] = total[row : row + 1]
            row += 2 * layers
            bias[layer, norm : norm + 1, :] = total[row : row + 1]
            row += 2 * layers
            out_bias[layer, norm : norm + 1, :] = total[row : row + 1]
        row = 6 * layers + layer
        for kind in range(2):
            qv[layer, kind : kind + 1, :] = total[row : row + 1, kind * half : (kind + 1) * half]
        row = 7 * layers + tiles * layer
        for part in range(tiles):
            upb[layer : layer + 1, part * width : (part + 1) * width] = total[
                row + part : row + part + 1
            ]


def finish_kernel(parts, *refs):
    layers = len(refs) // parts
    outs = refs[layers * parts :]
    for layer in range(layers):
        total = refs[layer * parts][...].astype(F32)
        for ref in refs[layer * parts + 1 : (layer + 1) * parts]:
            total = total + ref[...].astype(F32)
        column = 0
        for ref in outs:
            size = ref.shape[3]
            for member in range(ref.shape[1]):
                ref[layer, member] = total[:, column : column + size]
                column += size


def chunk_sources(order):
    first = list(order[:4])
    sources = []
    for target in range(16):
        source = 0
        for place, bit in enumerate(first):
            if (target >> (3 - place)) & 1:
                source |= 1 << (3 - bit)
        sources.append(source)
    return sources


def weight_kernel(sources, tiles, has_extra, *refs):
    if has_extra:
        left_own, left_far, right_own, right_far, lx_own, lx_far, rx_own, rx_far, keep, send = refs
    else:
        left_own, left_far, right_own, right_far, keep, send = refs

    def product(a_own, a_far, b_own, b_far):
        left = jnp.concatenate([a_own[...], a_far[...]], axis=1)
        right = jnp.concatenate([b_own[...].reshape(b_own.shape[-2:]), b_far[...].reshape(b_far.shape[-2:])], axis=0)
        size = left.shape[0] // 16
        low = dot(left, right).astype(BF16)
        for target, source in enumerate(sources):
            ref = keep if target < 8 else send
            ref[(target % 8) * size : (target % 8 + 1) * size, :] = low[
                source * size : (source + 1) * size, :
            ]

    if has_extra:

        @pl.when(pl.program_id(0) < tiles)
        def _():
            product(left_own, left_far, right_own, right_far)

        @pl.when(pl.program_id(0) == tiles)
        def _():
            product(lx_own, lx_far, rx_own, rx_far)

    else:
        product(left_own, left_far, right_own, right_far)


def weight_grad(name, order, left, right, extra=None, tiles=None, first=0):
    left_own, left_far = left
    right_own, right_far = right
    width, tokens = left_own.shape
    if right_own.ndim == 3:
        tile = right_own.shape[2]
        right_spec = pl.BlockSpec(
            (1, tokens, tile), lambda j: (jnp.minimum(j, tiles - 1) + first, 0, 0)
        )
    else:
        tile = 768 if tiles else 512
        tiles = tiles or right_own.shape[1] // tile
        right_spec = pl.BlockSpec((tokens, tile), lambda j: (0, j + first))
    steps = tiles + (1 if extra is not None else 0)
    ins = [left_own, left_far, right_own, right_far]
    specs = [fixed((width, tokens))] * 2 + [right_spec] * 2
    if extra is not None:
        ins += list(extra)
        specs += [fixed((width, tokens))] * 2 + [fixed((tokens, tile))] * 2
    half = out((width // 2, steps * tile), BF16)
    half_spec = pl.BlockSpec((width // 2, tile), lambda j: (0, j))
    return call(
        functools.partial(weight_kernel, chunk_sources(order), tiles, extra is not None),
        name,
        (steps,),
        ins,
        specs,
        [half, half],
        [half_spec, half_spec],
        flops=4 * width * tokens * steps * tile,
    )


def flip(bit):
    size = lax.axis_size("dp")
    return [(index, index ^ (1 << bit)) for index in range(size)]


class DpSum:
    def __init__(self, order, halves=None, units=()):
        self.order = list(order)
        self.incoming = None
        if halves is not None:
            keep, self.outgoing = halves
            self.members = [[keep]]
        else:
            self.members = [parts for unit in units for parts in unit.members]
            self.halve()

    def halve(self):
        rows = self.members[0][0].shape[0] // 2
        sends = [
            sum(part[rows:].astype(F32) for part in parts).astype(BF16) for parts in self.members
        ]
        self.outgoing = sends[0] if len(sends) == 1 else jnp.concatenate(sends, axis=1)
        self.members = [[part[:rows] for part in parts] for parts in self.members]

    @classmethod
    def joined(cls, units):
        whole_unit = cls(units[0].order, (None, jnp.concatenate([u.outgoing for u in units], axis=1)))
        whole_unit.members = [parts for unit in units for parts in unit.members]
        return whole_unit

    def start(self):
        self.incoming = lax.ppermute(self.outgoing, "dp", flip(self.order.pop(0)))

    def turn(self, go=True):
        column = 0
        for parts in self.members:
            width = parts[0].shape[1]
            parts.append(self.incoming[:, column : column + width])
            column += width
        self.incoming = None
        if self.order:
            self.halve()
            if go:
                self.start()

    def flying(self):
        return [self.incoming]

    def land(self, arrays):
        (self.incoming,) = arrays


class Everywhere:
    def __init__(self, mine, far, groups):
        self.mine = mine
        self.incoming = [swap(far)]
        self.groups = list(groups)

    def flying(self):
        return self.incoming

    def land(self, arrays):
        self.incoming = arrays

    def turn(self):
        if len(self.incoming) == 1:
            self.mine = self.mine + self.incoming[0]
        else:
            near, far, across = self.incoming
            self.mine = (self.mine + near) + (far + across)
        self.incoming = []
        if self.groups:
            group = self.groups.pop(0)
            masks = [1 << bit for bit in group]
            if len(masks) == 2:
                masks.append(masks[0] | masks[1])
            size = lax.axis_size("dp")
            self.incoming = [
                lax.ppermute(self.mine, "dp", [(index, index ^ mask) for index in range(size)])
                for mask in masks
            ]


def gate(value, starts=(), turns=(), after=(), holds=()):
    ends = [*turns, *holds]
    held = [unit.outgoing for unit in starts] + [array for unit in ends for array in unit.flying()]
    value, *held = lax.optimization_barrier((value, *held, *after))
    for unit in starts:
        unit.outgoing = held.pop(0)
        unit.start()
    for unit in ends:
        unit.land([held.pop(0) for _ in unit.flying()])
    for unit in turns:
        unit.turn()
    for unit in holds:
        unit.turn(go=False)
    return value


def swap(values):
    return lax.ppermute(values, "tensor", [(0, 1), (1, 0)])


def shards(
    images,
    valid_count,
    ln_gain,
    ln_bias,
    w_qkv,
    qv_bias,
    w_out,
    out_bias,
    w_up,
    up_bias,
    w_down,
    cotangent,
):
    local_rows, slots, width = images.shape
    tokens = local_rows * slots
    half = w_qkv.shape[3]
    ff_half = w_up.shape[2]
    tile = 768
    steps = ff_half // tile
    heads = half // HEAD_DIM
    dp = lax.axis_size("dp")
    bits = dp.bit_length() - 1
    assert dp == 1 << bits and bits >= 4 and lax.axis_size("tensor") == 2
    tail = tuple(range(4, bits))
    order_a = (0, 1, 2, 3) + tail
    order_b = (1, 0, 2, 3) + tail
    order_e = (2, 0, 1, 3) + tail
    order_d = (0, 2, 3, 1) + tail

    me = lax.axis_index("dp")
    counts = valid_count

    block = width // dp
    row = jnp.arange(width, dtype=jnp.int32)
    index = row // block
    mirrored = jnp.zeros_like(index)
    for bit in range(bits):
        mirrored = mirrored | (((index >> (bits - 1 - bit)) & 1) << bit)
    source = (mirrored ^ me) * block + row % block
    order = (source[:, None] == row[None, :]).astype(BF16)

    w_qkv = jnp.transpose(w_qkv, (0, 2, 1, 3))
    qkv = (w_qkv, swap(w_qkv))
    qv = (qv_bias, swap(qv_bias))

    images_2d = images.reshape(tokens, width)
    cotangent_2d = cotangent.reshape(tokens, width)
    smem = pl.BlockSpec(memory_space=pltpu.SMEM)
    wide = (tokens, width)
    flops_wide = 2 * width * width * tokens

    normed, normed_t, cotangent_t, wide_cotangent = call(
        prep_kernel,
        "prep",
        (),
        [images_2d, cotangent_2d, ln_gain, ln_bias, order],
        [whole()] * 5,
        [out(wide, BF16), out((width, tokens), BF16), out((width, tokens), BF16), out(wide, F32)],
        [whole()] * 4,
        flops=2 * flops_wide,
    )

    wout, wup, wdown = [
        (weight, swap(lax.optimization_barrier((weight, normed, qkv[1], qv[1]))[0]))
        for weight in (w_out, w_up, w_down)
    ]

    def attend(layer, normed, counts):
        lse_shape = (local_rows * heads, 1, slots)
        joint_out = out((3, tokens, half), BF16)
        att_out = out((tokens, half), BF16)
        lse_out = out(lse_shape, F32)
        results = call(
            functools.partial(attend_kernel, slots),
            "attend",
            (),
            [jnp.full((1,), layer, jnp.int32), counts, normed, in_hbm(qkv[0]), in_hbm(qkv[1]), qv[0], qv[1]],
            [smem, smem, whole(), hbm(), hbm(), whole(), whole()],
            [joint_out, joint_out, att_out, att_out, lse_out, lse_out],
            [whole()] * 6,
            [pltpu.VMEM((2, 3, width, half), BF16), pltpu.SemaphoreType.DMA((2, 3))],
            flops=12 * tokens * width * half + 8 * tokens * slots * half,
            limit=44,
        )
        return results[0::2], results[1::2]

    stream = images_2d
    saved = []
    got_cotangent_t = swap(cotangent_t)
    pooled = None
    for layer in range(LAYERS):
        last = layer == LAYERS - 1
        own, far = attend(layer, normed, counts)
        if layer == 0:
            upb = (up_bias, swap(up_bias))
        gain_in = ln_gain
        if layer > 0:
            before = saved[layer - 1]
            names = ("got_normed_t", "got_att", "got_mid_normed_t", "got_hid")
            gain_in, got_cotangent_t, *got = lax.optimization_barrier(
                (ln_gain, got_cotangent_t, *[before[name] for name in names])
            )
            before.update(zip(names, got))
        ff = pltpu.HBM((tokens, ff_half), BF16)
        extra = (
            [out((local_rows, width), F32)]
            if last
            else [out(wide, BF16), out((width, tokens), BF16)]
        )
        results = call(
            functools.partial(feed_kernel, layer, slots, last),
            "feed",
            (),
            [
                counts,
                stream,
                own[1],
                far[1],
                in_hbm(wout[0]),
                in_hbm(wout[1]),
                out_bias,
                gain_in,
                ln_bias,
                order,
                in_hbm(wup[0]),
                in_hbm(wup[1]),
                upb[0],
                upb[1],
                in_hbm(wdown[0]),
                in_hbm(wdown[1]),
            ],
            [smem]
            + [whole()] * 3
            + [hbm()] * 2
            + [whole()] * 4
            + [hbm()] * 2
            + [whole()] * 2
            + [hbm()] * 2,
            [out(wide, F32), out((width, tokens), BF16), ff, ff, ff, ff, out(wide, F32)] + extra,
            [whole()] * 2 + [hbm()] * 4 + [whole()] * (1 + len(extra)),
            [
                pltpu.VMEM(wide, BF16),
                pltpu.VMEM(wide, F32),
                pltpu.VMEM((2, tokens, tile), F32),
                pltpu.VMEM((2 * half, width), BF16),
                pltpu.VMEM((2 * steps, width, tile), BF16),
                pltpu.VMEM((2 * steps, tile, width), BF16),
                pltpu.VMEM((2 * steps, tokens, tile), BF16),
                pltpu.VMEM((2 * steps, tokens, tile), BF16),
                pltpu.SemaphoreType.DMA((2 + 4 * steps,)),
                pltpu.SemaphoreType.DMA((4 * steps,)),
            ],
            flops=8 * tokens * width * ff_half + 2 * flops_wide,
            limit=32,
        )
        mid, mid_normed_t, hid_own, hid_far, slope_own, slope_far, stream_next = results[:7]
        saved.append(
            dict(
                stream=stream,
                own=own,
                far=far,
                mid=mid,
                slope=(slope_own, slope_far),
                hid=hid_own,
                attended=own[1],
                normed_t=normed_t,
                mid_normed_t=mid_normed_t,
                got_hid=swap(hid_far),
                got_att=swap(far[1]),
                got_normed_t=swap(normed_t),
                got_mid_normed_t=swap(mid_normed_t),
            )
        )
        stream = stream_next
        if last:
            pooled = results[7]
        else:
            normed, normed_t = results[7:9]

    def feed_back(layer, grad, gain_in):
        kept = saved[layer]
        ff = pltpu.HBM((tokens, ff_half), BF16)
        bias_shape = out((steps, tile), F32)
        att_shape = out((tokens, half), BF16)
        return call(
            feed_back_kernel,
            "feed_back",
            (),
            [
                jnp.full((1,), layer, jnp.int32),
                grad,
                kept["mid"],
                gain_in,
                order,
                in_hbm(wdown[0]),
                in_hbm(wdown[1]),
                in_hbm(wup[0]),
                in_hbm(wup[1]),
                kept["slope"][0],
                kept["slope"][1],
                in_hbm(wout[0]),
                in_hbm(wout[1]),
            ],
            [smem] + [whole()] * 4 + [hbm()] * 8,
            [
                ff,
                ff,
                bias_shape,
                bias_shape,
                out(wide, F32),
                out((width, tokens), BF16),
                att_shape,
                att_shape,
                out((4, width), F32),
            ],
            [hbm()] * 2 + [whole()] * 7,
            [
                pltpu.VMEM(wide, BF16),
                pltpu.VMEM(wide, F32),
                pltpu.VMEM((2, tokens, tile), F32),
                pltpu.VMEM((4, 8, width), F32),
                pltpu.VMEM((2 * steps, tile, width), BF16),
                pltpu.VMEM((2 * steps, width, tile), BF16),
                pltpu.VMEM((2 * steps, tokens, tile), BF16),
                pltpu.VMEM((2 * steps, tokens, tile), BF16),
                pltpu.VMEM((2, half, width), BF16),
                pltpu.SemaphoreType.DMA((4, 2 * steps)),
                pltpu.SemaphoreType.DMA((2 * steps,)),
            ],
            flops=8 * tokens * width * ff_half + 2 * flops_wide,
            limit=32,
        )

    def attend_back(forward, grad_att, counts_in):
        joint, _, lse = forward
        return call(
            functools.partial(attend_back_kernel, slots),
            "attend_back",
            (),
            [counts_in, joint, lse, grad_att],
            [smem, whole(), whole(), whole()],
            [out(joint.shape, BF16), out((1, 2 * half), F32)],
            [whole()] * 2,
            flops=10 * tokens * slots * half,
        )

    def entry_back(layer, joint_own, joint_far, grad_mid, gain_in):
        with_low = layer > 0
        return call(
            functools.partial(entry_back_kernel, layer, with_low),
            "entry_back",
            (3,),
            [
                joint_own,
                joint_far,
                in_hbm(qkv[0]),
                in_hbm(qkv[1]),
                saved[layer]["stream"],
                gain_in,
                grad_mid,
                order,
            ],
            [whole()] * 2
            + [pl.BlockSpec((1, 1, width, half), lambda c: (layer, c, 0, 0))] * 2
            + [whole()] * 4,
            [out(wide, F32), out((2, width), F32)]
            + ([out((width, tokens), BF16)] if with_low else []),
            [whole()] * (3 if with_low else 2),
            [pltpu.VMEM(wide, F32), pltpu.VMEM((2, 8, width), F32)]
            + ([pltpu.VMEM(wide, BF16)] if with_low else []),
            flops=12 * tokens * width * half,
        )

    def down_halves(layer, order_of, grad_t, got_grad_t):
        kept = saved[layer]
        return weight_grad(
            "down_grad", order_of, (grad_t, got_grad_t), (in_hbm(kept["hid"]) if layer else kept["hid"], kept["got_hid"])
        )

    def up_halves(layer, order_of, pre_own, got_pre, tiles=None, first=0):
        kept = saved[layer]
        return weight_grad(
            "up_grad",
            order_of,
            (kept["mid_normed_t"], kept["got_mid_normed_t"]),
            (pre_own, got_pre),
            tiles=tiles,
            first=first,
        )

    def lefts(layer):
        return saved[layer]["normed_t"], saved[layer]["got_normed_t"]

    def extras(layer, mid_t, got_mid_t):
        return mid_t, got_mid_t, saved[layer]["attended"], saved[layer]["got_att"]

    small = [None] * LAYERS
    down_1 = DpSum(order_a, down_halves(1, order_a, cotangent_t, got_cotangent_t))
    gain_in = gate(ln_gain, [down_1])
    pre_own, pre_far, upb_own, upb_far, grad_mid, mid_t, att_own, att_far, sums_mid = feed_back(
        1, wide_cotangent, gain_in
    )
    got_pre, got_mid_t = swap(pre_far), swap(mid_t)
    joint_far, qv_far = attend_back(saved[1]["far"], att_far, counts)
    got_joint = swap(joint_far)
    pre_own = gate(pre_own, [], [], [qv_far], [down_1])
    pre_own = gate(pre_own, [down_1])
    up_1 = DpSum(order_a, up_halves(1, order_a, pre_own, got_pre))
    counts_in = gate(counts, [up_1])
    joint_own, qv_own = attend_back(saved[1]["own"], att_own, counts_in)
    gain_in = gate(gain_in, after=[qv_own])
    grad, sums_in, grad_t = entry_back(1, joint_own, joint_far, grad_mid, gain_in)
    got_grad_t = swap(grad_t)
    small[1] = (sums_mid, sums_in, qv_own, qv_far, upb_own, upb_far)
    joint_own = gate(joint_own, [], [down_1], [sums_in])
    rest_1 = DpSum(
        order_e,
        weight_grad(
            "qkv_out_grad",
            order_e,
            lefts(1),
            (joint_own, got_joint),
            extras(1, mid_t, got_mid_t),
            tiles=3,
        ),
    )
    grad_t = gate(grad_t, [rest_1])
    down_0 = DpSum(order_a, down_halves(0, order_a, grad_t, got_grad_t))

    gain_in = gate(gain_in, [down_0], [up_1], holds=[down_1])
    pre_own, pre_far, upb_own, upb_far, grad_mid, mid_t, att_own, att_far, sums_mid = feed_back(
        0, grad, gain_in
    )
    got_pre, got_mid_t = swap(pre_far), swap(mid_t)
    counts_in = gate(counts_in, [], [up_1], [sums_mid], [rest_1])
    joint_far, qv_far = attend_back(saved[0]["far"], att_far, counts_in)
    got_joint = swap(joint_far)
    pre_own = gate(pre_own, [], [], [qv_far], [down_0, up_1])
    late_1 = DpSum.joined([up_1, down_1])
    pre_own = gate(pre_own, [down_0, late_1])
    up_0 = DpSum(order_d, up_halves(0, order_d, pre_own, got_pre))
    counts_in = gate(counts_in, [up_0], [], [got_mid_t, got_joint])
    joint_own, qv_own = attend_back(saved[0]["own"], att_own, counts_in)
    rest_0 = DpSum(
        order_b,
        weight_grad(
            "qkv_out_grad",
            order_b,
            lefts(0),
            (joint_own, got_joint),
            extras(0, mid_t, got_mid_t),
            tiles=3,
        ),
    )
    gain_in = gate(gain_in, [rest_0], [down_0, late_1], [qv_own])
    grad, sums_in = entry_back(0, joint_own, joint_far, grad_mid, gain_in)
    last = gate(sums_in, [rest_1], [up_0])
    small[0] = (sums_mid, last, qv_own, qv_far, upb_own, upb_far)
    ins = [array for arrays in small for array in arrays]
    vector_shape = out(((7 + steps) * LAYERS, width), F32)
    mine, far = call(
        functools.partial(pack_kernel, LAYERS),
        "pack_small",
        (),
        ins,
        [whole()] * len(ins),
        [vector_shape] * 2,
        [whole()] * 2,
    )
    vector = Everywhere(mine, far, [(0, 1), (2,), (3,), *[(bit,) for bit in tail]])
    last = gate(last, holds=[down_0])
    last = gate(last, [], [rest_0, up_0, vector], [down_0.outgoing], [rest_1])
    last = gate(last, holds=[rest_0, up_0])
    last = gate(last, [rest_0, up_0, down_0, rest_1], [vector])
    last = gate(last, holds=[rest_0, rest_1])
    late_0 = DpSum.joined([rest_0, rest_1])
    last = gate(last, [late_0], [up_0, down_0, vector])
    last = gate(last, [], [late_0])
    last = gate(last, [], [vector])
    while vector.flying():
        vector.turn()
    running = [late_1, late_0, down_0, up_0]
    while any(unit.incoming is not None for unit in running):
        last = gate(last, [], [unit for unit in running if unit.incoming is not None][:4])

    def finish(first, second, shapes):
        ins = [*first, *second]
        return call(
            functools.partial(finish_kernel, len(first)),
            "finish",
            (),
            ins,
            [whole()] * len(ins),
            [out((LAYERS,) + shape, F32) for shape in shapes],
            [whole()] * len(shapes),
        )

    (down_grad,) = finish(down_0.members[0], late_1.members[1], [(1, block, ff_half)])
    (up_grad,) = finish(up_0.members[0], late_1.members[0], [(1, block, ff_half)])
    qkv_grad, out_grad = finish(late_0.members[0], late_0.members[1], [(3, block, half), (1, block, half)])
    total, qkv_grad = lax.optimization_barrier((vector.mine, qkv_grad))
    gain_grads, shift_grads, outb_grads, qv_grads, upb_grads = call(
        functools.partial(unpack_kernel, LAYERS),
        "unpack_small",
        (),
        [total],
        [whole()],
        [
            out(ln_gain.shape, F32),
            out(ln_bias.shape, F32),
            out(out_bias.shape, F32),
            out(qv_bias.shape, F32),
            out(up_bias.shape, F32),
        ],
        [whole()] * 5,
    )
    return (
        stream.reshape(images.shape),
        pooled,
        grad.reshape(images.shape),
        gain_grads,
        shift_grads,
        jnp.transpose(qkv_grad, (0, 2, 1, 3)),
        qv_grads,
        jnp.transpose(out_grad[:, 0], (0, 2, 1)),
        outb_grads,
        up_grad[:, 0],
        upb_grads,
        jnp.transpose(down_grad[:, 0], (0, 2, 1)),
    )


def solution(mesh):
    placed = (
        P(("dp", "tensor"), None, None),
        P("dp"),
        P(),
        P(),
        P(None, None, None, "tensor"),
        P(None, None, "tensor"),
        P(None, "tensor", None),
        P(),
        P(None, None, "tensor"),
        P(None, "tensor"),
        P(None, "tensor", None),
        P(("dp", "tensor"), None, None),
    )
    return jax.shard_map(
        shards,
        mesh=mesh,
        in_specs=placed,
        out_specs=(
            P(("dp", "tensor"), None, None),
            P(("dp", "tensor"), None),
            P(("dp", "tensor"), None, None),
            P(),
            P(),
            P(None, "dp", None, "tensor"),
            P(None, None, "tensor"),
            P(None, "tensor", "dp"),
            P(),
            P(None, "dp", "tensor"),
            P(None, "tensor"),
            P(None, "tensor", "dp"),
        ),
        check_vma=False,
    )
```

```python
import functools
import math

import jax
import jax.numpy as jnp
from jax import lax
from jax.experimental import pallas as pl
from jax.experimental.pallas import tpu as pltpu
from jax.sharding import PartitionSpec as P

HEAD_DIM = 64
LAYERS = 2
EPSILON = 1e-06
NEGATIVE = -1e30
BF16 = jnp.bfloat16
F32 = jnp.float32
CHUNK = 16
BAND = 64


def dot(left, right):
    return lax.dot_general(left, right, (((1,), (0,)), ((), ())), preferred_element_type=F32)


def dot_nt(left, right):
    return lax.dot_general(left, right, (((1,), (1,)), ((), ())), preferred_element_type=F32)


def fixed(shape, *lead):
    where = tuple(lead) + (0,) * (len(shape) - len(lead))
    return pl.BlockSpec(shape, lambda *_: where)


def out(shape, dtype):
    return jax.ShapeDtypeStruct(shape, dtype)


def in_hbm(values):
    return pltpu.with_memory_space_constraint(values, pltpu.HBM)


def cost(flops, *arrays):
    total = sum(math.prod(a.shape) * a.dtype.itemsize for a in arrays)
    return pl.CostEstimate(flops=int(flops) // 64, bytes_accessed=int(total) // 64, transcendentals=0)


MIB = 1 << 20


def call(body, name, grid, ins, in_specs, outs, out_specs, scratch=(), flops=0, limit=24):
    return pl.pallas_call(
        body,
        name=name,
        grid=grid,
        in_specs=in_specs,
        out_specs=out_specs,
        out_shape=outs,
        scratch_shapes=list(scratch),
        compiler_params=pltpu.CompilerParams(vmem_limit_bytes=limit * MIB),
        cost_estimate=cost(flops, *ins, *outs),
    )(*ins)


def whole():
    return pl.BlockSpec(memory_space=pltpu.VMEM)


def by_blocks(target, left, right, product, rows=256, add=False):
    def block(index, carry):
        here = pl.ds(pl.multiple_of(index * rows, rows), rows)
        value = product(left[here, :], right())
        if add:
            value = target[here, :] + value
        target[here, :] = value.astype(target.dtype)
        return carry

    lax.fori_loop(0, left.shape[0] // rows, block, 0)


def hbm():
    return pl.BlockSpec(memory_space=pltpu.HBM)


def by_rows(rows, body, unroll=1):
    def step(index, carry):
        for part in range(unroll):
            body(pl.multiple_of((index * unroll + part) * BAND, BAND))
        return carry

    lax.fori_loop(0, rows // (BAND * unroll), step, 0)


def moments(values):
    average = jnp.mean(values, axis=-1, keepdims=True)
    centred = values - average
    variance = jnp.mean(centred * centred, axis=-1, keepdims=True)
    return centred, lax.rsqrt(variance + EPSILON)


def normalized(values, gain, bias):
    centred, scale = moments(values)
    return centred * scale * gain + bias


def norm_backward(values, grad_normed, gain):
    centred, scale = moments(values)
    unit = centred * scale
    grad_unit = grad_normed * gain
    first = jnp.mean(grad_unit, axis=-1, keepdims=True)
    second = jnp.mean(grad_unit * unit, axis=-1, keepdims=True)
    return scale * (grad_unit - first - unit * second), grad_normed * unit


def fold_rows(values):
    total = values[0:8]
    for start in range(8, values.shape[0], 8):
        total = total + values[start : start + 8]
    return total


def prep_kernel(images, cotangent, gain, bias, order, normed, normed_t, cotangent_t, wide_cotangent):
    def rows(start):
        here = pl.ds(start, BAND)
        values = images[here, :].astype(F32)
        normed[here, :] = normalized(values, gain[0, 0:1, :], bias[0, 0:1, :]).astype(BF16)
        wide_cotangent[here, :] = cotangent[here, :].astype(F32)

    by_rows(images.shape[0], rows, 1)
    by_blocks(normed_t, order, lambda: normed[...], dot_nt)
    by_blocks(cotangent_t, order, lambda: cotangent[...], dot_nt)


def head_masks(slots):
    lane = lax.broadcasted_iota(jnp.int32, (slots, 2 * HEAD_DIM), 1)
    return lane < HEAD_DIM, lane >= HEAD_DIM


def own_count(counts, image, images):
    return counts[lax.axis_index("tensor") * images + image]


def attend_kernel(
    slots,
    which,
    counts,
    normed,
    weight_own,
    weight_far,
    bias_own,
    bias_far,
    joint_own,
    joint_far,
    att_own,
    att_far,
    lse_own,
    lse_far,
    held,
    sem,
):
    width = att_own.shape[1]
    pairs = width // (2 * HEAD_DIM)
    scale = HEAD_DIM ** (-0.5)
    layer = which[0]
    weights = (weight_own, weight_far)
    for side in range(2):
        for member in range(3):
            fetch(weights[side].at[layer, member], held.at[side, member], sem.at[side, member])
    for side, (joint, bias) in enumerate(((joint_own, bias_own), (joint_far, bias_far))):

        def project(member, carry):
            pltpu.make_async_copy(
                weights[side].at[layer, member], held.at[side, member], sem.at[side, member]
            ).wait()
            shift = bias[layer, pl.ds(member // 2, 1), :]
            shift = jnp.where(member == 1, jnp.zeros_like(shift), shift)
            joint[member] = (dot(normed[...], held[side, member]) + shift).astype(BF16)
            return carry

        lax.fori_loop(0, 3, project, 0)
    masks = head_masks(slots)
    key_index = lax.broadcasted_iota(jnp.int32, (slots, slots), 0)

    def step(index, carry):
        image = index // pairs
        pair = index % pairs
        rows = pl.ds(pl.multiple_of(image * slots, slots), slots)
        lanes = pl.ds(pl.multiple_of(pair * 2 * HEAD_DIM, 2 * HEAD_DIM), 2 * HEAD_DIM)
        valid = key_index < own_count(counts, image, normed.shape[0] // slots)
        sets = ((joint_own, att_own, lse_own), (joint_far, att_far, lse_far))
        heads = []
        for joint, _, _ in sets:
            queries = joint[0, rows, lanes]
            keys_in = joint[1, rows, lanes] * jnp.asarray(scale, BF16)
            for side in range(2):
                keys_side = jnp.where(masks[side], keys_in, jnp.zeros_like(keys_in))
                heads.append(dot_nt(keys_side, queries))
        values_t = [joint[2, rows, lanes].T for joint, _, _ in sets]
        heads = [jnp.where(valid, scores, NEGATIVE) for scores in heads]
        largest = [jnp.max(scores, axis=0, keepdims=True) for scores in heads]
        heads = [jnp.exp(scores - top) for scores, top in zip(heads, largest)]
        totals = [jnp.sum(exponent, axis=0, keepdims=True) for exponent in heads]
        heads = [(exponent * (1.0 / total)).astype(BF16) for exponent, total in zip(heads, totals)]
        for which_set, (_, attended, lse) in enumerate(sets):
            parts = []
            for side in range(2):
                head = 2 * which_set + side
                lse[2 * index + side] = largest[head] + jnp.log(totals[head])
                parts.append(
                    dot(values_t[which_set][side * HEAD_DIM : (side + 1) * HEAD_DIM], heads[head])
                )
            attended[rows, lanes] = jnp.concatenate(parts, axis=0).T.astype(BF16)
        return carry

    lax.fori_loop(0, (normed.shape[0] // slots) * pairs, step, 0)


def fetch(source, target, sem):
    copy = pltpu.make_async_copy(source, target, sem)
    copy.start()
    return copy


def feed_kernel(
    layer,
    slots,
    last_layer,
    counts,
    stream,
    att_own,
    att_far,
    out_own,
    out_far,
    out_bias,
    gain,
    bias,
    order,
    up_own,
    up_far,
    up_bias_own,
    up_bias_far,
    down_own,
    down_far,
    mid,
    normed_t,
    hid_own,
    hid_far,
    slope_own,
    slope_far,
    stream_out,
    *rest,
):
    if last_layer:
        pooled = rest[0]
    else:
        next_normed, next_t = rest[:2]
    normed, total, pre, w_out, w_up, w_down, hid, slope, in_sem, out_sem = rest[1 if last_layer else 2 :]
    tokens = stream.shape[0]
    half = w_out.shape[0] // 2
    units = w_up.shape[0]
    tile = w_up.shape[2]
    tiles = units // 2
    out_in = [
        fetch(ref.at[layer], w_out.at[pl.ds(side * half, half)], in_sem.at[side])
        for side, ref in enumerate((out_own, out_far))
    ]
    up_in, down_in = [], []
    for unit in range(units):
        side, part = unit // tiles, unit % tiles
        columns = pl.ds(part * tile, tile)
        up_ref, down_ref = ((up_own, down_own), (up_far, down_far))[side]
        up_in.append(fetch(up_ref.at[layer, :, columns], w_up.at[unit], in_sem.at[2 + unit]))
        down_in.append(
            fetch(down_ref.at[layer, columns, :], w_down.at[unit], in_sem.at[2 + units + unit])
        )
    for copy in out_in:
        copy.wait()
    total[...] = dot(jnp.concatenate([att_own[...], att_far[...]], axis=1), w_out[...])

    def enter(start):
        here = pl.ds(start, BAND)
        value = stream[here, :].astype(F32) + (total[here, :] + out_bias[layer, 0:1, :])
        mid[here, :] = value
        normed[here, :] = normalized(value, gain[layer, 1:2, :], bias[layer, 1:2, :]).astype(BF16)

    by_rows(tokens, enter, 1)
    up_in[0].wait()
    by_blocks(pre.at[0], normed, lambda: w_up[0], dot)
    by_blocks(normed_t, order, lambda: normed[...], dot_nt)
    rows = 256
    out_copies = []
    for unit in range(units):
        side, part = unit // tiles, unit % tiles
        shift = (up_bias_own, up_bias_far)[side][layer : layer + 1, part * tile : (part + 1) * tile]
        if unit + 1 < units:
            up_in[unit + 1].wait()
        if unit > 0:
            down_in[unit - 1].wait()

        def chunk(index, carry):
            block = pl.ds(pl.multiple_of(index * rows, rows), rows)
            if unit + 1 < units:
                pre[(unit + 1) % 2, block, :] = dot(normed[block, :], w_up[unit + 1])
            if unit == 1:
                total[block, :] = dot(hid[unit - 1, block, :], w_down[unit - 1])
            elif unit > 1:
                total[block, :] += dot(hid[unit - 1, block, :], w_down[unit - 1])
            for sub in range(0, rows, CHUNK):
                here = pl.ds(pl.multiple_of(index * rows + sub, CHUNK), CHUNK)
                value = pre[unit % 2, here, :] + shift
                cdf = 0.5 + 0.5 * lax.erf(value * (0.5**0.5))
                hid[unit, here, :] = (value * cdf).astype(BF16)
                density = jnp.exp(-0.5 * value * value) * ((2.0 * math.pi) ** -0.5)
                slope[unit, here, :] = (cdf + value * density).astype(BF16)
            return carry

        lax.fori_loop(0, tokens // rows, chunk, 0)
        hid_ref, slope_ref = ((hid_own, slope_own), (hid_far, slope_far))[side]
        columns = pl.ds(part * tile, tile)
        out_copies.append(fetch(hid.at[unit], hid_ref.at[:, columns], out_sem.at[unit]))
        out_copies.append(fetch(slope.at[unit], slope_ref.at[:, columns], out_sem.at[units + unit]))
    down_in[units - 1].wait()
    by_blocks(total, hid.at[units - 1], lambda: w_down[units - 1], dot, add=True)

    def leave(start):
        here = pl.ds(start, BAND)
        value = mid[here, :] + (total[here, :] + out_bias[layer, 1:2, :])
        stream_out[here, :] = value
        if not last_layer:
            next_normed[here, :] = normalized(
                value, gain[layer + 1, 0:1, :], bias[layer + 1, 0:1, :]
            ).astype(BF16)

    by_rows(tokens, leave, 1)
    if last_layer:
        index = lax.broadcasted_iota(jnp.int32, (slots, 1), 0)
        for image in range(tokens // slots):
            block = stream_out[image * slots : (image + 1) * slots, :]
            count = own_count(counts, image, tokens // slots)
            summed = jnp.sum(jnp.where(index < count, block, 0.0), axis=0, keepdims=True)
            pooled[image : image + 1, :] = summed / count.astype(F32)
    else:
        by_blocks(next_t, order, lambda: next_normed[...], dot_nt)
    for copy in out_copies:
        copy.wait()


def feed_back_kernel(
    which,
    grad_in,
    mid,
    gain,
    order,
    down_own,
    down_far,
    up_own,
    up_far,
    slope_own,
    slope_far,
    out_own,
    out_far,
    pre_own,
    pre_far,
    bias_own,
    bias_far,
    grad_mid,
    mid_t,
    att_own,
    att_far,
    sums,
    low,
    total,
    hidden,
    partial,
    w_down,
    w_up,
    slope,
    pre,
    w_out,
    in_sem,
    out_sem,
):
    layer = which[0]
    tokens = grad_in.shape[0]
    units = w_up.shape[0]
    tile = w_up.shape[2]
    tiles = units // 2
    down_in, up_in, slope_in = [], [], []
    for unit in range(units):
        columns = pl.ds(unit % tiles * tile, tile)
        down_ref, up_ref, slope_ref = ((down_far, up_far, slope_far), (down_own, up_own, slope_own))[
            unit // tiles
        ]
        down_in.append(fetch(down_ref.at[layer, columns, :], w_down.at[unit], in_sem.at[0, unit]))
        slope_in.append(fetch(slope_ref.at[:, columns], slope.at[unit], in_sem.at[1, unit]))
        up_in.append(fetch(up_ref.at[layer, :, columns], w_up.at[unit], in_sem.at[2, unit]))
    out_in = [
        fetch(ref.at[layer], w_out.at[side], in_sem.at[3, side])
        for side, ref in enumerate((out_far, out_own))
    ]
    partial[...] = jnp.zeros_like(partial)

    def enter(start):
        here = pl.ds(start, BAND)
        value = grad_in[here, :].astype(F32)
        low[here, :] = value.astype(BF16)
        partial[0] += fold_rows(value)

    by_rows(tokens, enter)
    down_in[0].wait()
    by_blocks(hidden.at[0], low, lambda: w_down[0], dot_nt)
    rows = 256
    total[...] = jnp.zeros_like(total)
    pre[units - 1] = jnp.zeros_like(pre[units - 1])
    pre_refs = (pre_far, pre_own)

    def result(unit, side):
        columns = pl.ds(pl.multiple_of(unit % tiles * tile, tile), tile)
        return pltpu.make_async_copy(pre.at[unit], pre_refs[side].at[:, columns], out_sem.at[unit])

    def turn(unit, carry):
        after = jnp.minimum(unit + 1, units - 1)
        before = jnp.maximum(unit - 1, 0)

        @pl.when(unit + 1 < units)
        def _():
            pltpu.make_async_copy(
                down_own.at[layer, pl.ds(0, tile), :], w_down.at[after], in_sem.at[0, after]
            ).wait()

        @pl.when(unit != 1)
        def _():
            pltpu.make_async_copy(
                up_own.at[layer, :, pl.ds(0, tile)], w_up.at[before], in_sem.at[2, before]
            ).wait()

        pltpu.make_async_copy(
            slope_own.at[:, pl.ds(0, tile)], slope.at[unit], in_sem.at[1, unit]
        ).wait()
        idle = (unit + units - 1) % units

        def chunk(index, carry):
            block = pl.ds(pl.multiple_of(index * rows, rows), rows)
            hidden[(unit + 1) % 2, block, :] = dot_nt(low[block, :], w_down[after])
            total[block, :] += dot_nt(pre[idle, block, :], w_up[before])
            for sub in range(0, rows, CHUNK):
                here = pl.ds(pl.multiple_of(index * rows + sub, CHUNK), CHUNK)
                value = hidden[unit % 2, here, :] * slope[unit, here, :].astype(F32)
                pre[unit, here, :] = value.astype(BF16)
                carry = carry + fold_rows(value)
            return carry

        summed = lax.fori_loop(0, tokens // rows, chunk, jnp.zeros((8, tile), F32))
        row = jnp.sum(summed, axis=0, keepdims=True)
        for side, bias in enumerate((bias_far, bias_own)):

            @pl.when(unit // tiles == side)
            def _():
                bias[pl.ds(unit % tiles, 1), :] = row
                result(unit, side).start()

        return carry

    lax.fori_loop(0, units, turn, 0)
    up_in[units - 1].wait()
    by_blocks(total, pre.at[units - 1], lambda: w_up[units - 1], dot_nt, add=True)

    def leave(start):
        here = pl.ds(start, BAND)
        normed_grad = total[here, :]
        through, gain_term = norm_backward(mid[here, :], normed_grad, gain[layer, 1:2, :])
        value = grad_in[here, :].astype(F32) + through
        grad_mid[here, :] = value
        low[here, :] = value.astype(BF16)
        partial[1] += fold_rows(value)
        partial[2] += fold_rows(gain_term)
        partial[3] += fold_rows(normed_grad)

    by_rows(tokens, leave, 1)
    sums[...] = jnp.sum(partial[...], axis=1)
    by_blocks(mid_t, order, lambda: low[...], dot_nt)
    for copy in out_in:
        copy.wait()
    by_blocks(att_far, low, lambda: w_out[0], dot_nt)
    by_blocks(att_own, low, lambda: w_out[1], dot_nt)
    for unit in range(units):
        result(unit, unit // tiles).wait()


def attend_back_kernel(slots, counts, joint, lse, grad_att, grad_joint, bias_sums):
    width = grad_att.shape[1]
    pairs = width // (2 * HEAD_DIM)
    scale = HEAD_DIM ** (-0.5)
    masks = head_masks(slots)
    key_index = lax.broadcasted_iota(jnp.int32, (slots, slots), 0)
    bias_sums[...] = jnp.zeros_like(bias_sums)

    def step(index, carry):
        image = index // pairs
        pair = index % pairs
        rows = pl.ds(pl.multiple_of(image * slots, slots), slots)
        lanes = pl.ds(pl.multiple_of(pair * 2 * HEAD_DIM, 2 * HEAD_DIM), 2 * HEAD_DIM)
        queries = joint[0, rows, lanes]
        keys_in = joint[1, rows, lanes]
        values_in = joint[2, rows, lanes]
        grads = grad_att[rows, lanes]
        keys_t = keys_in.T
        keys_scaled = keys_in * jnp.asarray(scale, BF16)
        valid = key_index < own_count(counts, image, grad_att.shape[0] // slots)
        zeros = jnp.zeros_like(keys_in)
        scores = [
            dot_nt(jnp.where(masks[side], keys_scaled, zeros), queries) for side in range(2)
        ]
        grad_probs = [dot_nt(jnp.where(masks[side], values_in, zeros), grads) for side in range(2)]
        probs = [
            jnp.exp(jnp.where(valid, scores[side], NEGATIVE) - lse[2 * index + side])
            for side in range(2)
        ]
        value_parts = [dot(weights.astype(BF16), grads) for weights in probs]
        inner = [
            jnp.sum(back * weights, axis=0, keepdims=True) for back, weights in zip(grad_probs, probs)
        ]
        grad_scores = [
            (weights * (back - total)).astype(BF16)
            for weights, back, total in zip(probs, grad_probs, inner)
        ]
        key_parts = [dot(back, queries) for back in grad_scores]
        query_parts = [
            dot(keys_t[side * HEAD_DIM : (side + 1) * HEAD_DIM], grad_scores[side])
            for side in range(2)
        ]
        grad_queries = jnp.concatenate(query_parts, axis=0).T * scale
        grad_keys = jnp.where(masks[0], key_parts[0], key_parts[1]) * scale
        grad_values = jnp.where(masks[0], value_parts[0], value_parts[1])
        bias_sums[0:1, lanes] += jnp.sum(grad_queries, axis=0, keepdims=True)
        value_lanes = pl.ds(
            pl.multiple_of(width + pair * 2 * HEAD_DIM, 2 * HEAD_DIM), 2 * HEAD_DIM
        )
        bias_sums[0:1, value_lanes] += jnp.sum(grad_values, axis=0, keepdims=True)
        grad_joint[0, rows, lanes] = grad_queries.astype(BF16)
        grad_joint[1, rows, lanes] = grad_keys.astype(BF16)
        grad_joint[2, rows, lanes] = grad_values.astype(BF16)
        return carry

    lax.fori_loop(0, (grad_att.shape[0] // slots) * pairs, step, 0)


def entry_back_kernel(
    layer, with_low, joint_own, joint_far, weight_own, weight_far, stream, gain, grad_mid, order, *rest
):
    if with_low:
        grad_out, sums, low_t, total, partial, low = rest
    else:
        grad_out, sums, total, partial = rest
    member = pl.program_id(0)

    @pl.when(member == 0)
    def _():
        total[...] = jnp.zeros_like(total)
        partial[...] = jnp.zeros_like(partial)

    left = jnp.concatenate([joint_own[member], joint_far[member]], axis=1)
    right = jnp.concatenate([weight_own[0, 0], weight_far[0, 0]], axis=1)
    total[...] += dot_nt(left, right)

    def rows(start):
        here = pl.ds(start, BAND)
        normed_grad = total[here, :]
        through, gain_term = norm_backward(
            stream[here, :].astype(F32), normed_grad, gain[layer, 0:1, :]
        )
        value = grad_mid[here, :] + through
        grad_out[here, :] = value
        if with_low:
            low[here, :] = value.astype(BF16)
        partial[0] += fold_rows(gain_term)
        partial[1] += fold_rows(normed_grad)

    @pl.when(member == 2)
    def _():
        by_rows(stream.shape[0], rows, 1)
        sums[...] = jnp.sum(partial[...], axis=1)
        if with_low:
            by_blocks(low_t, order, lambda: low[...], dot_nt)


def pack_kernel(layers, *refs):
    ins, (own_out, far_out) = refs[:-2], refs[-2:]
    for layer in range(layers):
        sums_mid, sums_in, qv_own, qv_far, upb_own, upb_far = ins[6 * layer : 6 * layer + 6]
        tiles = upb_own.shape[0]
        for ref, qv, upb in ((own_out, qv_own, upb_own), (far_out, qv_far, upb_far)):
            for row, value in (
                (2 * layer, sums_in[0:1, :]),
                (2 * layer + 1, sums_mid[2:3, :]),
                (2 * (layers + layer), sums_in[1:2, :]),
                (2 * (layers + layer) + 1, sums_mid[3:4, :]),
                (2 * (2 * layers + layer), sums_mid[1:2, :]),
                (2 * (2 * layers + layer) + 1, sums_mid[0:1, :]),
                (6 * layers + layer, qv[...]),
            ):
                ref[row : row + 1, :] = value
            start = 7 * layers + tiles * layer
            ref[start : start + tiles, :] = upb[...]


def unpack_kernel(layers, mine, gain, bias, out_bias, qv, upb):
    total = mine[...]
    half = qv.shape[2]
    tiles = upb.shape[1] // mine.shape[1]
    width = mine.shape[1]
    for layer in range(layers):
        for norm in range(2):
            row = 2 * layer + norm
            gain[layer, norm : norm + 1, :] = total[row : row + 1]
            row += 2 * layers
            bias[layer, norm : norm + 1, :] = total[row : row + 1]
            row += 2 * layers
            out_bias[layer, norm : norm + 1, :] = total[row : row + 1]
        row = 6 * layers + layer
        for kind in range(2):
            qv[layer, kind : kind + 1, :] = total[row : row + 1, kind * half : (kind + 1) * half]
        row = 7 * layers + tiles * layer
        for part in range(tiles):
            upb[layer : layer + 1, part * width : (part + 1) * width] = total[
                row + part : row + part + 1
            ]


def finish_kernel(parts, *refs):
    layers = len(refs) // parts
    outs = refs[layers * parts :]
    for layer in range(layers):
        total = refs[layer * parts][...].astype(F32)
        for ref in refs[layer * parts + 1 : (layer + 1) * parts]:
            total = total + ref[...].astype(F32)
        column = 0
        for ref in outs:
            size = ref.shape[3]
            for member in range(ref.shape[1]):
                ref[layer, member] = total[:, column : column + size]
                column += size


def chunk_sources(order):
    first = list(order[:4])
    sources = []
    for target in range(16):
        source = 0
        for place, bit in enumerate(first):
            if (target >> (3 - place)) & 1:
                source |= 1 << (3 - bit)
        sources.append(source)
    return sources


def weight_kernel(sources, tiles, has_extra, *refs):
    if has_extra:
        left_own, left_far, right_own, right_far, lx_own, lx_far, rx_own, rx_far, keep, send = refs
    else:
        left_own, left_far, right_own, right_far, keep, send = refs

    def product(a_own, a_far, b_own, b_far):
        left = jnp.concatenate([a_own[...], a_far[...]], axis=1)
        right = jnp.concatenate([b_own[...].reshape(b_own.shape[-2:]), b_far[...].reshape(b_far.shape[-2:])], axis=0)
        size = left.shape[0] // 16
        low = dot(left, right).astype(BF16)
        for target, source in enumerate(sources):
            ref = keep if target < 8 else send
            ref[(target % 8) * size : (target % 8 + 1) * size, :] = low[
                source * size : (source + 1) * size, :
            ]

    if has_extra:

        @pl.when(pl.program_id(0) < tiles)
        def _():
            product(left_own, left_far, right_own, right_far)

        @pl.when(pl.program_id(0) == tiles)
        def _():
            product(lx_own, lx_far, rx_own, rx_far)

    else:
        product(left_own, left_far, right_own, right_far)


def weight_grad(name, order, left, right, extra=None, tiles=None, first=0):
    left_own, left_far = left
    right_own, right_far = right
    width, tokens = left_own.shape
    if right_own.ndim == 3:
        tile = right_own.shape[2]
        right_spec = pl.BlockSpec(
            (1, tokens, tile), lambda j: (jnp.minimum(j, tiles - 1) + first, 0, 0)
        )
    else:
        tile = 768 if tiles else 512
        tiles = tiles or right_own.shape[1] // tile
        right_spec = pl.BlockSpec((tokens, tile), lambda j: (0, j + first))
    steps = tiles + (1 if extra is not None else 0)
    ins = [left_own, left_far, right_own, right_far]
    specs = [fixed((width, tokens))] * 2 + [right_spec] * 2
    if extra is not None:
        ins += list(extra)
        specs += [fixed((width, tokens))] * 2 + [fixed((tokens, tile))] * 2
    half = out((width // 2, steps * tile), BF16)
    half_spec = pl.BlockSpec((width // 2, tile), lambda j: (0, j))
    return call(
        functools.partial(weight_kernel, chunk_sources(order), tiles, extra is not None),
        name,
        (steps,),
        ins,
        specs,
        [half, half],
        [half_spec, half_spec],
        flops=4 * width * tokens * steps * tile,
    )


def flip(bit):
    size = lax.axis_size("dp")
    return [(index, index ^ (1 << bit)) for index in range(size)]


class DpSum:
    def __init__(self, order, halves=None, units=()):
        self.order = list(order)
        self.incoming = None
        if halves is not None:
            keep, self.outgoing = halves
            self.members = [[keep]]
        else:
            self.members = [parts for unit in units for parts in unit.members]
            self.halve()

    def halve(self):
        rows = self.members[0][0].shape[0] // 2
        sends = [
            sum(part[rows:].astype(F32) for part in parts).astype(BF16) for parts in self.members
        ]
        self.outgoing = sends[0] if len(sends) == 1 else jnp.concatenate(sends, axis=1)
        self.members = [[part[:rows] for part in parts] for parts in self.members]

    @classmethod
    def joined(cls, units):
        whole_unit = cls(units[0].order, (None, jnp.concatenate([u.outgoing for u in units], axis=1)))
        whole_unit.members = [parts for unit in units for parts in unit.members]
        return whole_unit

    def start(self):
        self.incoming = lax.ppermute(self.outgoing, "dp", flip(self.order.pop(0)))

    def turn(self, go=True):
        column = 0
        for parts in self.members:
            width = parts[0].shape[1]
            parts.append(self.incoming[:, column : column + width])
            column += width
        self.incoming = None
        if self.order:
            self.halve()
            if go:
                self.start()

    def flying(self):
        return [self.incoming]

    def land(self, arrays):
        (self.incoming,) = arrays


class Everywhere:
    def __init__(self, mine, far, groups):
        self.mine = mine
        self.incoming = [swap(far)]
        self.groups = list(groups)

    def flying(self):
        return self.incoming

    def land(self, arrays):
        self.incoming = arrays

    def turn(self):
        if len(self.incoming) == 1:
            self.mine = self.mine + self.incoming[0]
        else:
            near, far, across = self.incoming
            self.mine = (self.mine + near) + (far + across)
        self.incoming = []
        if self.groups:
            group = self.groups.pop(0)
            masks = [1 << bit for bit in group]
            if len(masks) == 2:
                masks.append(masks[0] | masks[1])
            size = lax.axis_size("dp")
            self.incoming = [
                lax.ppermute(self.mine, "dp", [(index, index ^ mask) for index in range(size)])
                for mask in masks
            ]


def gate(value, starts=(), turns=(), after=(), holds=()):
    ends = [*turns, *holds]
    held = [unit.outgoing for unit in starts] + [array for unit in ends for array in unit.flying()]
    value, *held = lax.optimization_barrier((value, *held, *after))
    for unit in starts:
        unit.outgoing = held.pop(0)
        unit.start()
    for unit in ends:
        unit.land([held.pop(0) for _ in unit.flying()])
    for unit in turns:
        unit.turn()
    for unit in holds:
        unit.turn(go=False)
    return value


def swap(values):
    return lax.ppermute(values, "tensor", [(0, 1), (1, 0)])


def shards(
    images,
    valid_count,
    ln_gain,
    ln_bias,
    w_qkv,
    qv_bias,
    w_out,
    out_bias,
    w_up,
    up_bias,
    w_down,
    cotangent,
):
    local_rows, slots, width = images.shape
    tokens = local_rows * slots
    half = w_qkv.shape[3]
    ff_half = w_up.shape[2]
    tile = 768
    steps = ff_half // tile
    heads = half // HEAD_DIM
    dp = lax.axis_size("dp")
    bits = dp.bit_length() - 1
    assert dp == 1 << bits and bits >= 4 and lax.axis_size("tensor") == 2
    tail = tuple(range(4, bits))
    order_a = (0, 1, 2, 3) + tail
    order_b = (1, 0, 2, 3) + tail
    order_e = (2, 0, 1, 3) + tail
    order_d = (0, 2, 3, 1) + tail

    me = lax.axis_index("dp")
    counts = valid_count

    block = width // dp
    row = jnp.arange(width, dtype=jnp.int32)
    index = row // block
    mirrored = jnp.zeros_like(index)
    for bit in range(bits):
        mirrored = mirrored | (((index >> (bits - 1 - bit)) & 1) << bit)
    source = (mirrored ^ me) * block + row % block
    order = (source[:, None] == row[None, :]).astype(BF16)

    w_qkv = jnp.transpose(w_qkv, (0, 2, 1, 3))
    qkv = (w_qkv, swap(w_qkv))
    qv = (qv_bias, swap(qv_bias))

    images_2d = images.reshape(tokens, width)
    cotangent_2d = cotangent.reshape(tokens, width)
    smem = pl.BlockSpec(memory_space=pltpu.SMEM)
    wide = (tokens, width)
    flops_wide = 2 * width * width * tokens

    normed, normed_t, cotangent_t, wide_cotangent = call(
        prep_kernel,
        "prep",
        (),
        [images_2d, cotangent_2d, ln_gain, ln_bias, order],
        [whole()] * 5,
        [out(wide, BF16), out((width, tokens), BF16), out((width, tokens), BF16), out(wide, F32)],
        [whole()] * 4,
        flops=2 * flops_wide,
    )

    wout, wup, wdown = [
        (weight, swap(lax.optimization_barrier((weight, normed, qkv[1], qv[1]))[0]))
        for weight in (w_out, w_up, w_down)
    ]

    def attend(layer, normed, counts):
        lse_shape = (local_rows * heads, 1, slots)
        joint_out = out((3, tokens, half), BF16)
        att_out = out((tokens, half), BF16)
        lse_out = out(lse_shape, F32)
        results = call(
            functools.partial(attend_kernel, slots),
            "attend",
            (),
            [jnp.full((1,), layer, jnp.int32), counts, normed, in_hbm(qkv[0]), in_hbm(qkv[1]), qv[0], qv[1]],
            [smem, smem, whole(), hbm(), hbm(), whole(), whole()],
            [joint_out, joint_out, att_out, att_out, lse_out, lse_out],
            [whole()] * 6,
            [pltpu.VMEM((2, 3, width, half), BF16), pltpu.SemaphoreType.DMA((2, 3))],
            flops=12 * tokens * width * half + 8 * tokens * slots * half,
            limit=32,
        )
        return results[0::2], results[1::2]

    stream = images_2d
    saved = []
    got_cotangent_t = swap(cotangent_t)
    pooled = None
    for layer in range(LAYERS):
        last = layer == LAYERS - 1
        own, far = attend(layer, normed, counts)
        if layer == 0:
            upb = (up_bias, swap(up_bias))
        gain_in = ln_gain
        if layer > 0:
            before = saved[layer - 1]
            names = ("got_normed_t", "got_att", "got_mid_normed_t", "got_hid")
            gain_in, got_cotangent_t, *got = lax.optimization_barrier(
                (ln_gain, got_cotangent_t, *[before[name] for name in names])
            )
            before.update(zip(names, got))
        ff = pltpu.HBM((tokens, ff_half), BF16)
        extra = (
            [out((local_rows, width), F32)]
            if last
            else [out(wide, BF16), out((width, tokens), BF16)]
        )
        results = call(
            functools.partial(feed_kernel, layer, slots, last),
            "feed",
            (),
            [
                counts,
                stream,
                own[1],
                far[1],
                in_hbm(wout[0]),
                in_hbm(wout[1]),
                out_bias,
                gain_in,
                ln_bias,
                order,
                in_hbm(wup[0]),
                in_hbm(wup[1]),
                upb[0],
                upb[1],
                in_hbm(wdown[0]),
                in_hbm(wdown[1]),
            ],
            [smem]
            + [whole()] * 3
            + [hbm()] * 2
            + [whole()] * 4
            + [hbm()] * 2
            + [whole()] * 2
            + [hbm()] * 2,
            [out(wide, F32), out((width, tokens), BF16), ff, ff, ff, ff, out(wide, F32)] + extra,
            [whole()] * 2 + [hbm()] * 4 + [whole()] * (1 + len(extra)),
            [
                pltpu.VMEM(wide, BF16),
                pltpu.VMEM(wide, F32),
                pltpu.VMEM((2, tokens, tile), F32),
                pltpu.VMEM((2 * half, width), BF16),
                pltpu.VMEM((2 * steps, width, tile), BF16),
                pltpu.VMEM((2 * steps, tile, width), BF16),
                pltpu.VMEM((2 * steps, tokens, tile), BF16),
                pltpu.VMEM((2 * steps, tokens, tile), BF16),
                pltpu.SemaphoreType.DMA((2 + 4 * steps,)),
                pltpu.SemaphoreType.DMA((4 * steps,)),
            ],
            flops=8 * tokens * width * ff_half + 2 * flops_wide,
            limit=32,
        )
        mid, mid_normed_t, hid_own, hid_far, slope_own, slope_far, stream_next = results[:7]
        saved.append(
            dict(
                stream=stream,
                own=own,
                far=far,
                mid=mid,
                slope=(slope_own, slope_far),
                hid=hid_own,
                attended=own[1],
                normed_t=normed_t,
                mid_normed_t=mid_normed_t,
                got_hid=swap(hid_far),
                got_att=swap(far[1]),
                got_normed_t=swap(normed_t),
                got_mid_normed_t=swap(mid_normed_t),
            )
        )
        stream = stream_next
        if last:
            pooled = results[7]
        else:
            normed, normed_t = results[7:9]

    def feed_back(layer, grad, gain_in):
        kept = saved[layer]
        ff = pltpu.HBM((tokens, ff_half), BF16)
        bias_shape = out((steps, tile), F32)
        att_shape = out((tokens, half), BF16)
        return call(
            feed_back_kernel,
            "feed_back",
            (),
            [
                jnp.full((1,), layer, jnp.int32),
                grad,
                kept["mid"],
                gain_in,
                order,
                in_hbm(wdown[0]),
                in_hbm(wdown[1]),
                in_hbm(wup[0]),
                in_hbm(wup[1]),
                kept["slope"][0],
                kept["slope"][1],
                in_hbm(wout[0]),
                in_hbm(wout[1]),
            ],
            [smem] + [whole()] * 4 + [hbm()] * 8,
            [
                ff,
                ff,
                bias_shape,
                bias_shape,
                out(wide, F32),
                out((width, tokens), BF16),
                att_shape,
                att_shape,
                out((4, width), F32),
            ],
            [hbm()] * 2 + [whole()] * 7,
            [
                pltpu.VMEM(wide, BF16),
                pltpu.VMEM(wide, F32),
                pltpu.VMEM((2, tokens, tile), F32),
                pltpu.VMEM((4, 8, width), F32),
                pltpu.VMEM((2 * steps, tile, width), BF16),
                pltpu.VMEM((2 * steps, width, tile), BF16),
                pltpu.VMEM((2 * steps, tokens, tile), BF16),
                pltpu.VMEM((2 * steps, tokens, tile), BF16),
                pltpu.VMEM((2, half, width), BF16),
                pltpu.SemaphoreType.DMA((4, 2 * steps)),
                pltpu.SemaphoreType.DMA((2 * steps,)),
            ],
            flops=8 * tokens * width * ff_half + 2 * flops_wide,
            limit=32,
        )

    def attend_back(forward, grad_att, counts_in):
        joint, _, lse = forward
        return call(
            functools.partial(attend_back_kernel, slots),
            "attend_back",
            (),
            [counts_in, joint, lse, grad_att],
            [smem, whole(), whole(), whole()],
            [out(joint.shape, BF16), out((1, 2 * half), F32)],
            [whole()] * 2,
            flops=10 * tokens * slots * half,
        )

    def entry_back(layer, joint_own, joint_far, grad_mid, gain_in):
        with_low = layer > 0
        return call(
            functools.partial(entry_back_kernel, layer, with_low),
            "entry_back",
            (3,),
            [
                joint_own,
                joint_far,
                in_hbm(qkv[0]),
                in_hbm(qkv[1]),
                saved[layer]["stream"],
                gain_in,
                grad_mid,
                order,
            ],
            [whole()] * 2
            + [pl.BlockSpec((1, 1, width, half), lambda c: (layer, c, 0, 0))] * 2
            + [whole()] * 4,
            [out(wide, F32), out((2, width), F32)]
            + ([out((width, tokens), BF16)] if with_low else []),
            [whole()] * (3 if with_low else 2),
            [pltpu.VMEM(wide, F32), pltpu.VMEM((2, 8, width), F32)]
            + ([pltpu.VMEM(wide, BF16)] if with_low else []),
            flops=12 * tokens * width * half,
        )

    def down_halves(layer, order_of, grad_t, got_grad_t):
        kept = saved[layer]
        return weight_grad(
            "down_grad", order_of, (grad_t, got_grad_t), (in_hbm(kept["hid"]) if layer else kept["hid"], kept["got_hid"])
        )

    def up_halves(layer, order_of, pre_own, got_pre, tiles=None, first=0):
        kept = saved[layer]
        return weight_grad(
            "up_grad",
            order_of,
            (kept["mid_normed_t"], kept["got_mid_normed_t"]),
            (pre_own, got_pre),
            tiles=tiles,
            first=first,
        )

    def lefts(layer):
        return saved[layer]["normed_t"], saved[layer]["got_normed_t"]

    def extras(layer, mid_t, got_mid_t):
        return mid_t, got_mid_t, saved[layer]["attended"], saved[layer]["got_att"]

    small = [None] * LAYERS
    down_1 = DpSum(order_a, down_halves(1, order_a, cotangent_t, got_cotangent_t))
    gain_in = gate(ln_gain, [down_1])
    pre_own, pre_far, upb_own, upb_far, grad_mid, mid_t, att_own, att_far, sums_mid = feed_back(
        1, wide_cotangent, gain_in
    )
    got_pre, got_mid_t = swap(pre_far), swap(mid_t)
    joint_far, qv_far = attend_back(saved[1]["far"], att_far, counts)
    got_joint = swap(joint_far)
    pre_own = gate(pre_own, [], [], [qv_far], [down_1])
    pre_own = gate(pre_own, [down_1])
    up_1 = DpSum(order_a, up_halves(1, order_a, pre_own, got_pre))
    counts_in = gate(counts, [up_1])
    joint_own, qv_own = attend_back(saved[1]["own"], att_own, counts_in)
    gain_in = gate(gain_in, after=[qv_own])
    grad, sums_in, grad_t = entry_back(1, joint_own, joint_far, grad_mid, gain_in)
    got_grad_t = swap(grad_t)
    small[1] = (sums_mid, sums_in, qv_own, qv_far, upb_own, upb_far)
    joint_own = gate(joint_own, [], [down_1], [sums_in])
    rest_1 = DpSum(
        order_e,
        weight_grad(
            "qkv_out_grad",
            order_e,
            lefts(1),
            (joint_own, got_joint),
            extras(1, mid_t, got_mid_t),
            tiles=3,
        ),
    )
    grad_t = gate(grad_t, [rest_1])
    down_0 = DpSum(order_a, down_halves(0, order_a, grad_t, got_grad_t))

    gain_in = gate(gain_in, [down_0], [up_1], holds=[down_1])
    pre_own, pre_far, upb_own, upb_far, grad_mid, mid_t, att_own, att_far, sums_mid = feed_back(
        0, grad, gain_in
    )
    got_pre, got_mid_t = swap(pre_far), swap(mid_t)
    counts_in = gate(counts_in, [], [up_1], [sums_mid], [rest_1])
    joint_far, qv_far = attend_back(saved[0]["far"], att_far, counts_in)
    got_joint = swap(joint_far)
    pre_own = gate(pre_own, [], [], [qv_far], [down_0, up_1])
    late_1 = DpSum.joined([up_1, down_1])
    pre_own = gate(pre_own, [down_0, late_1])
    up_0 = DpSum(order_d, up_halves(0, order_d, pre_own, got_pre))
    counts_in = gate(counts_in, [up_0], [], [got_mid_t, got_joint])
    joint_own, qv_own = attend_back(saved[0]["own"], att_own, counts_in)
    rest_0 = DpSum(
        order_b,
        weight_grad(
            "qkv_out_grad",
            order_b,
            lefts(0),
            (joint_own, got_joint),
            extras(0, mid_t, got_mid_t),
            tiles=3,
        ),
    )
    gain_in = gate(gain_in, [rest_0], [down_0, late_1], [qv_own])
    grad, sums_in = entry_back(0, joint_own, joint_far, grad_mid, gain_in)
    last = gate(sums_in, [rest_1], [up_0])
    small[0] = (sums_mid, last, qv_own, qv_far, upb_own, upb_far)
    ins = [array for arrays in small for array in arrays]
    vector_shape = out(((7 + steps) * LAYERS, width), F32)
    mine, far = call(
        functools.partial(pack_kernel, LAYERS),
        "pack_small",
        (),
        ins,
        [whole()] * len(ins),
        [vector_shape] * 2,
        [whole()] * 2,
    )
    vector = Everywhere(mine, far, [(0, 1), (2,), (3,), *[(bit,) for bit in tail]])
    last = gate(last, holds=[down_0])
    last = gate(last, [], [rest_0, up_0, vector], [down_0.outgoing], [rest_1])
    last = gate(last, holds=[rest_0, up_0])
    last = gate(last, [rest_0, up_0, down_0, rest_1], [vector])
    last = gate(last, holds=[rest_0, rest_1])
    late_0 = DpSum.joined([rest_0, rest_1])
    last = gate(last, [late_0], [up_0, down_0, vector])
    last = gate(last, [], [late_0])
    last = gate(last, [], [vector])
    while vector.flying():
        vector.turn()
    running = [late_1, late_0, down_0, up_0]
    while any(unit.incoming is not None for unit in running):
        last = gate(last, [], [unit for unit in running if unit.incoming is not None][:4])

    def finish(first, second, shapes):
        ins = [*first, *second]
        return call(
            functools.partial(finish_kernel, len(first)),
            "finish",
            (),
            ins,
            [whole()] * len(ins),
            [out((LAYERS,) + shape, F32) for shape in shapes],
            [whole()] * len(shapes),
        )

    (down_grad,) = finish(down_0.members[0], late_1.members[1], [(1, block, ff_half)])
    (up_grad,) = finish(up_0.members[0], late_1.members[0], [(1, block, ff_half)])
    qkv_grad, out_grad = finish(late_0.members[0], late_0.members[1], [(3, block, half), (1, block, half)])
    total, qkv_grad = lax.optimization_barrier((vector.mine, qkv_grad))
    gain_grads, shift_grads, outb_grads, qv_grads, upb_grads = call(
        functools.partial(unpack_kernel, LAYERS),
        "unpack_small",
        (),
        [total],
        [whole()],
        [
            out(ln_gain.shape, F32),
            out(ln_bias.shape, F32),
            out(out_bias.shape, F32),
            out(qv_bias.shape, F32),
            out(up_bias.shape, F32),
        ],
        [whole()] * 5,
    )
    return (
        stream.reshape(images.shape),
        pooled,
        grad.reshape(images.shape),
        gain_grads,
        shift_grads,
        jnp.transpose(qkv_grad, (0, 2, 1, 3)),
        qv_grads,
        jnp.transpose(out_grad[:, 0], (0, 2, 1)),
        outb_grads,
        up_grad[:, 0],
        upb_grads,
        jnp.transpose(down_grad[:, 0], (0, 2, 1)),
    )


def solution(mesh):
    placed = (
        P(("dp", "tensor"), None, None),
        P("dp"),
        P(),
        P(),
        P(None, None, None, "tensor"),
        P(None, None, "tensor"),
        P(None, "tensor", None),
        P(),
        P(None, None, "tensor"),
        P(None, "tensor"),
        P(None, "tensor", None),
        P(("dp", "tensor"), None, None),
    )
    return jax.shard_map(
        shards,
        mesh=mesh,
        in_specs=placed,
        out_specs=(
            P(("dp", "tensor"), None, None),
            P(("dp", "tensor"), None),
            P(("dp", "tensor"), None, None),
            P(),
            P(),
            P(None, "dp", None, "tensor"),
            P(None, None, "tensor"),
            P(None, "tensor", "dp"),
            P(),
            P(None, "dp", "tensor"),
            P(None, "tensor"),
            P(None, "tensor", "dp"),
        ),
        check_vma=False,
    )
```

```python
import functools
import math

import jax
import jax.numpy as jnp
from jax import lax
from jax.experimental import pallas as pl
from jax.experimental.pallas import tpu as pltpu
from jax.sharding import PartitionSpec as P

HEAD_DIM = 64
LAYERS = 2
EPSILON = 1e-06
NEGATIVE = -1e30
BF16 = jnp.bfloat16
F32 = jnp.float32
CHUNK = 16
BAND = 64


def dot(left, right):
    return lax.dot_general(left, right, (((1,), (0,)), ((), ())), preferred_element_type=F32)


def dot_nt(left, right):
    return lax.dot_general(left, right, (((1,), (1,)), ((), ())), preferred_element_type=F32)


def fixed(shape, *lead):
    where = tuple(lead) + (0,) * (len(shape) - len(lead))
    return pl.BlockSpec(shape, lambda *_: where)


def out(shape, dtype):
    return jax.ShapeDtypeStruct(shape, dtype)


def in_hbm(values):
    return pltpu.with_memory_space_constraint(values, pltpu.HBM)


def cost(flops, *arrays):
    total = sum(math.prod(a.shape) * a.dtype.itemsize for a in arrays)
    return pl.CostEstimate(flops=int(flops) // 64, bytes_accessed=int(total) // 64, transcendentals=0)


MIB = 1 << 20


def call(body, name, grid, ins, in_specs, outs, out_specs, scratch=(), flops=0, limit=24):
    return pl.pallas_call(
        body,
        name=name,
        grid=grid,
        in_specs=in_specs,
        out_specs=out_specs,
        out_shape=outs,
        scratch_shapes=list(scratch),
        compiler_params=pltpu.CompilerParams(vmem_limit_bytes=limit * MIB),
        cost_estimate=cost(flops, *ins, *outs),
    )(*ins)


def whole():
    return pl.BlockSpec(memory_space=pltpu.VMEM)


def by_blocks(target, left, right, product, rows=256, add=False):
    def block(index, carry):
        here = pl.ds(pl.multiple_of(index * rows, rows), rows)
        value = product(left[here, :], right())
        if add:
            value = target[here, :] + value
        target[here, :] = value.astype(target.dtype)
        return carry

    lax.fori_loop(0, left.shape[0] // rows, block, 0)


def hbm():
    return pl.BlockSpec(memory_space=pltpu.HBM)


def by_rows(rows, body, unroll=1):
    def step(index, carry):
        for part in range(unroll):
            body(pl.multiple_of((index * unroll + part) * BAND, BAND))
        return carry

    lax.fori_loop(0, rows // (BAND * unroll), step, 0)


def moments(values):
    average = jnp.mean(values, axis=-1, keepdims=True)
    centred = values - average
    variance = jnp.mean(centred * centred, axis=-1, keepdims=True)
    return centred, lax.rsqrt(variance + EPSILON)


def normalized(values, gain, bias):
    centred, scale = moments(values)
    return centred * scale * gain + bias


def norm_backward(values, grad_normed, gain):
    centred, scale = moments(values)
    unit = centred * scale
    grad_unit = grad_normed * gain
    first = jnp.mean(grad_unit, axis=-1, keepdims=True)
    second = jnp.mean(grad_unit * unit, axis=-1, keepdims=True)
    return scale * (grad_unit - first - unit * second), grad_normed * unit


def fold_rows(values):
    total = values[0:8]
    for start in range(8, values.shape[0], 8):
        total = total + values[start : start + 8]
    return total


def prep_kernel(images, cotangent, gain, bias, order, normed, normed_t, cotangent_t, wide_cotangent):
    def rows(start):
        here = pl.ds(start, BAND)
        values = images[here, :].astype(F32)
        normed[here, :] = normalized(values, gain[0, 0:1, :], bias[0, 0:1, :]).astype(BF16)
        wide_cotangent[here, :] = cotangent[here, :].astype(F32)

    by_rows(images.shape[0], rows, 1)
    by_blocks(normed_t, order, lambda: normed[...], dot_nt)
    by_blocks(cotangent_t, order, lambda: cotangent[...], dot_nt)


def head_masks(slots):
    lane = lax.broadcasted_iota(jnp.int32, (slots, 2 * HEAD_DIM), 1)
    return lane < HEAD_DIM, lane >= HEAD_DIM


def own_count(counts, image, images):
    return counts[lax.axis_index("tensor") * images + image]


def attend_kernel(
    slots,
    which,
    counts,
    normed,
    weight_own,
    weight_far,
    bias_own,
    bias_far,
    joint_own,
    joint_far,
    att_own,
    att_far,
    lse_own,
    lse_far,
    held,
    sem,
):
    width = att_own.shape[1]
    pairs = width // (2 * HEAD_DIM)
    scale = HEAD_DIM ** (-0.5)
    layer = which[0]
    weights = (weight_own, weight_far)
    for side in range(2):
        for member in range(3):
            fetch(weights[side].at[layer, member], held.at[side, member], sem.at[side, member])
    for side, (joint, bias) in enumerate(((joint_own, bias_own), (joint_far, bias_far))):

        def project(member, carry):
            pltpu.make_async_copy(
                weights[side].at[layer, member], held.at[side, member], sem.at[side, member]
            ).wait()
            shift = bias[layer, pl.ds(member // 2, 1), :]
            shift = jnp.where(member == 1, jnp.zeros_like(shift), shift)
            joint[member] = (dot(normed[...], held[side, member]) + shift).astype(BF16)
            return carry

        lax.fori_loop(0, 3, project, 0)
    masks = head_masks(slots)
    key_index = lax.broadcasted_iota(jnp.int32, (slots, slots), 0)

    def step(index, carry):
        image = index // pairs
        pair = index % pairs
        rows = pl.ds(pl.multiple_of(image * slots, slots), slots)
        lanes = pl.ds(pl.multiple_of(pair * 2 * HEAD_DIM, 2 * HEAD_DIM), 2 * HEAD_DIM)
        valid = key_index < own_count(counts, image, normed.shape[0] // slots)
        sets = ((joint_own, att_own, lse_own), (joint_far, att_far, lse_far))
        heads = []
        for joint, _, _ in sets:
            queries = joint[0, rows, lanes]
            keys_in = joint[1, rows, lanes] * jnp.asarray(scale, BF16)
            for side in range(2):
                keys_side = jnp.where(masks[side], keys_in, jnp.zeros_like(keys_in))
                heads.append(dot_nt(keys_side, queries))
        values_t = [joint[2, rows, lanes].T for joint, _, _ in sets]
        heads = [jnp.where(valid, scores, NEGATIVE) for scores in heads]
        largest = [jnp.max(scores, axis=0, keepdims=True) for scores in heads]
        heads = [jnp.exp(scores - top) for scores, top in zip(heads, largest)]
        totals = [jnp.sum(exponent, axis=0, keepdims=True) for exponent in heads]
        heads = [(exponent * (1.0 / total)).astype(BF16) for exponent, total in zip(heads, totals)]
        for which_set, (_, attended, lse) in enumerate(sets):
            parts = []
            for side in range(2):
                head = 2 * which_set + side
                lse[2 * index + side] = largest[head] + jnp.log(totals[head])
                parts.append(
                    dot(values_t[which_set][side * HEAD_DIM : (side + 1) * HEAD_DIM], heads[head])
                )
            attended[rows, lanes] = jnp.concatenate(parts, axis=0).T.astype(BF16)
        return carry

    lax.fori_loop(0, (normed.shape[0] // slots) * pairs, step, 0)


def fetch(source, target, sem):
    copy = pltpu.make_async_copy(source, target, sem)
    copy.start()
    return copy


def feed_kernel(
    layer,
    slots,
    last_layer,
    counts,
    stream,
    att_own,
    att_far,
    out_own,
    out_far,
    out_bias,
    gain,
    bias,
    order,
    up_own,
    up_far,
    up_bias_own,
    up_bias_far,
    down_own,
    down_far,
    mid,
    normed_t,
    hid_own,
    hid_far,
    slope_own,
    slope_far,
    stream_out,
    *rest,
):
    if last_layer:
        pooled = rest[0]
    else:
        next_normed, next_t = rest[:2]
    normed, total, pre, w_out, w_up, w_down, hid, slope, in_sem, out_sem = rest[1 if last_layer else 2 :]
    tokens = stream.shape[0]
    half = w_out.shape[0] // 2
    units = w_up.shape[0]
    tile = w_up.shape[2]
    tiles = units // 2
    out_in = [
        fetch(ref.at[layer], w_out.at[pl.ds(side * half, half)], in_sem.at[side])
        for side, ref in enumerate((out_own, out_far))
    ]
    up_in, down_in = [], []
    for unit in range(units):
        side, part = unit // tiles, unit % tiles
        columns = pl.ds(part * tile, tile)
        up_ref, down_ref = ((up_own, down_own), (up_far, down_far))[side]
        up_in.append(fetch(up_ref.at[layer, :, columns], w_up.at[unit], in_sem.at[2 + unit]))
        down_in.append(
            fetch(down_ref.at[layer, columns, :], w_down.at[unit], in_sem.at[2 + units + unit])
        )
    for copy in out_in:
        copy.wait()
    total[...] = dot(jnp.concatenate([att_own[...], att_far[...]], axis=1), w_out[...])

    def enter(start):
        here = pl.ds(start, BAND)
        value = stream[here, :].astype(F32) + (total[here, :] + out_bias[layer, 0:1, :])
        mid[here, :] = value
        normed[here, :] = normalized(value, gain[layer, 1:2, :], bias[layer, 1:2, :]).astype(BF16)

    by_rows(tokens, enter, 1)
    up_in[0].wait()
    by_blocks(pre.at[0], normed, lambda: w_up[0], dot)
    by_blocks(normed_t, order, lambda: normed[...], dot_nt)
    rows = 256
    out_copies = []
    for unit in range(units):
        side, part = unit // tiles, unit % tiles
        shift = (up_bias_own, up_bias_far)[side][layer : layer + 1, part * tile : (part + 1) * tile]
        if unit + 1 < units:
            up_in[unit + 1].wait()
        if unit > 0:
            down_in[unit - 1].wait()

        def chunk(index, carry):
            block = pl.ds(pl.multiple_of(index * rows, rows), rows)
            if unit + 1 < units:
                pre[(unit + 1) % 2, block, :] = dot(normed[block, :], w_up[unit + 1])
            if unit == 1:
                total[block, :] = dot(hid[unit - 1, block, :], w_down[unit - 1])
            elif unit > 1:
                total[block, :] += dot(hid[unit - 1, block, :], w_down[unit - 1])
            for sub in range(0, rows, CHUNK):
                here = pl.ds(pl.multiple_of(index * rows + sub, CHUNK), CHUNK)
                value = pre[unit % 2, here, :] + shift
                cdf = 0.5 + 0.5 * lax.erf(value * (0.5**0.5))
                hid[unit, here, :] = (value * cdf).astype(BF16)
                density = jnp.exp(-0.5 * value * value) * ((2.0 * math.pi) ** -0.5)
                slope[unit, here, :] = (cdf + value * density).astype(BF16)
            return carry

        lax.fori_loop(0, tokens // rows, chunk, 0)
        hid_ref, slope_ref = ((hid_own, slope_own), (hid_far, slope_far))[side]
        columns = pl.ds(part * tile, tile)
        out_copies.append(fetch(hid.at[unit], hid_ref.at[:, columns], out_sem.at[unit]))
        out_copies.append(fetch(slope.at[unit], slope_ref.at[:, columns], out_sem.at[units + unit]))
    down_in[units - 1].wait()
    by_blocks(total, hid.at[units - 1], lambda: w_down[units - 1], dot, add=True)

    def leave(start):
        here = pl.ds(start, BAND)
        value = mid[here, :] + (total[here, :] + out_bias[layer, 1:2, :])
        stream_out[here, :] = value
        if not last_layer:
            next_normed[here, :] = normalized(
                value, gain[layer + 1, 0:1, :], bias[layer + 1, 0:1, :]
            ).astype(BF16)

    by_rows(tokens, leave, 1)
    if last_layer:
        index = lax.broadcasted_iota(jnp.int32, (slots, 1), 0)
        for image in range(tokens // slots):
            block = stream_out[image * slots : (image + 1) * slots, :]
            count = own_count(counts, image, tokens // slots)
            summed = jnp.sum(jnp.where(index < count, block, 0.0), axis=0, keepdims=True)
            pooled[image : image + 1, :] = summed / count.astype(F32)
    else:
        by_blocks(next_t, order, lambda: next_normed[...], dot_nt)
    for copy in out_copies:
        copy.wait()


def feed_back_kernel(
    which,
    grad_in,
    mid,
    gain,
    order,
    down_own,
    down_far,
    up_own,
    up_far,
    slope_own,
    slope_far,
    out_own,
    out_far,
    pre_own,
    pre_far,
    bias_own,
    bias_far,
    grad_mid,
    mid_t,
    att_own,
    att_far,
    sums,
    low,
    total,
    hidden,
    partial,
    w_down,
    w_up,
    slope,
    pre,
    w_out,
    in_sem,
    out_sem,
):
    layer = which[0]
    tokens = grad_in.shape[0]
    units = w_up.shape[0]
    tile = w_up.shape[2]
    tiles = units // 2
    down_in, up_in, slope_in = [], [], []
    for unit in range(units):
        columns = pl.ds(unit % tiles * tile, tile)
        down_ref, up_ref, slope_ref = ((down_far, up_far, slope_far), (down_own, up_own, slope_own))[
            unit // tiles
        ]
        down_in.append(fetch(down_ref.at[layer, columns, :], w_down.at[unit], in_sem.at[0, unit]))
        slope_in.append(fetch(slope_ref.at[:, columns], slope.at[unit], in_sem.at[1, unit]))
        up_in.append(fetch(up_ref.at[layer, :, columns], w_up.at[unit], in_sem.at[2, unit]))
    out_in = [
        fetch(ref.at[layer], w_out.at[side], in_sem.at[3, side])
        for side, ref in enumerate((out_far, out_own))
    ]
    partial[...] = jnp.zeros_like(partial)

    def enter(start):
        here = pl.ds(start, BAND)
        value = grad_in[here, :].astype(F32)
        low[here, :] = value.astype(BF16)
        partial[0] += fold_rows(value)

    by_rows(tokens, enter)
    down_in[0].wait()
    by_blocks(hidden.at[0], low, lambda: w_down[0], dot_nt)
    rows = 256
    total[...] = jnp.zeros_like(total)
    pre[units - 1] = jnp.zeros_like(pre[units - 1])
    pre_refs = (pre_far, pre_own)

    def result(unit, side):
        columns = pl.ds(pl.multiple_of(unit % tiles * tile, tile), tile)
        return pltpu.make_async_copy(pre.at[unit], pre_refs[side].at[:, columns], out_sem.at[unit])

    def turn(unit, carry):
        after = jnp.minimum(unit + 1, units - 1)
        before = jnp.maximum(unit - 1, 0)

        @pl.when(unit + 1 < units)
        def _():
            pltpu.make_async_copy(
                down_own.at[layer, pl.ds(0, tile), :], w_down.at[after], in_sem.at[0, after]
            ).wait()

        @pl.when(unit != 1)
        def _():
            pltpu.make_async_copy(
                up_own.at[layer, :, pl.ds(0, tile)], w_up.at[before], in_sem.at[2, before]
            ).wait()

        pltpu.make_async_copy(
            slope_own.at[:, pl.ds(0, tile)], slope.at[unit], in_sem.at[1, unit]
        ).wait()
        idle = (unit + units - 1) % units

        def chunk(index, carry):
            block = pl.ds(pl.multiple_of(index * rows, rows), rows)
            hidden[(unit + 1) % 2, block, :] = dot_nt(low[block, :], w_down[after])
            total[block, :] += dot_nt(pre[idle, block, :], w_up[before])
            for sub in range(0, rows, CHUNK):
                here = pl.ds(pl.multiple_of(index * rows + sub, CHUNK), CHUNK)
                value = hidden[unit % 2, here, :] * slope[unit, here, :].astype(F32)
                pre[unit, here, :] = value.astype(BF16)
                carry = carry + fold_rows(value)
            return carry

        summed = lax.fori_loop(0, tokens // rows, chunk, jnp.zeros((8, tile), F32))
        row = jnp.sum(summed, axis=0, keepdims=True)
        for side, bias in enumerate((bias_far, bias_own)):

            @pl.when(unit // tiles == side)
            def _():
                bias[pl.ds(unit % tiles, 1), :] = row
                result(unit, side).start()

        return carry

    lax.fori_loop(0, units, turn, 0)
    up_in[units - 1].wait()
    by_blocks(total, pre.at[units - 1], lambda: w_up[units - 1], dot_nt, add=True)

    def leave(start):
        here = pl.ds(start, BAND)
        normed_grad = total[here, :]
        through, gain_term = norm_backward(mid[here, :], normed_grad, gain[layer, 1:2, :])
        value = grad_in[here, :].astype(F32) + through
        grad_mid[here, :] = value
        low[here, :] = value.astype(BF16)
        partial[1] += fold_rows(value)
        partial[2] += fold_rows(gain_term)
        partial[3] += fold_rows(normed_grad)

    by_rows(tokens, leave, 1)
    sums[...] = jnp.sum(partial[...], axis=1)
    by_blocks(mid_t, order, lambda: low[...], dot_nt)
    for copy in out_in:
        copy.wait()
    by_blocks(att_far, low, lambda: w_out[0], dot_nt)
    by_blocks(att_own, low, lambda: w_out[1], dot_nt)
    for unit in range(units):
        result(unit, unit // tiles).wait()


def attend_back_kernel(slots, counts, joint, lse, grad_att, grad_joint, bias_sums):
    width = grad_att.shape[1]
    pairs = width // (2 * HEAD_DIM)
    scale = HEAD_DIM ** (-0.5)
    masks = head_masks(slots)
    key_index = lax.broadcasted_iota(jnp.int32, (slots, slots), 0)
    bias_sums[...] = jnp.zeros_like(bias_sums)

    def step(index, carry):
        image = index // pairs
        pair = index % pairs
        rows = pl.ds(pl.multiple_of(image * slots, slots), slots)
        lanes = pl.ds(pl.multiple_of(pair * 2 * HEAD_DIM, 2 * HEAD_DIM), 2 * HEAD_DIM)
        queries = joint[0, rows, lanes]
        keys_in = joint[1, rows, lanes]
        values_in = joint[2, rows, lanes]
        grads = grad_att[rows, lanes]
        keys_t = keys_in.T
        keys_scaled = keys_in * jnp.asarray(scale, BF16)
        valid = key_index < own_count(counts, image, grad_att.shape[0] // slots)
        zeros = jnp.zeros_like(keys_in)
        scores = [
            dot_nt(jnp.where(masks[side], keys_scaled, zeros), queries) for side in range(2)
        ]
        grad_probs = [dot_nt(jnp.where(masks[side], values_in, zeros), grads) for side in range(2)]
        probs = [
            jnp.exp(jnp.where(valid, scores[side], NEGATIVE) - lse[2 * index + side])
            for side in range(2)
        ]
        value_parts = [dot(weights.astype(BF16), grads) for weights in probs]
        inner = [
            jnp.sum(back * weights, axis=0, keepdims=True) for back, weights in zip(grad_probs, probs)
        ]
        grad_scores = [
            (weights * (back - total)).astype(BF16)
            for weights, back, total in zip(probs, grad_probs, inner)
        ]
        key_parts = [dot(back, queries) for back in grad_scores]
        query_parts = [
            dot(keys_t[side * HEAD_DIM : (side + 1) * HEAD_DIM], grad_scores[side])
            for side in range(2)
        ]
        grad_queries = jnp.concatenate(query_parts, axis=0).T * scale
        grad_keys = jnp.where(masks[0], key_parts[0], key_parts[1]) * scale
        grad_values = jnp.where(masks[0], value_parts[0], value_parts[1])
        bias_sums[0:1, lanes] += jnp.sum(grad_queries, axis=0, keepdims=True)
        value_lanes = pl.ds(
            pl.multiple_of(width + pair * 2 * HEAD_DIM, 2 * HEAD_DIM), 2 * HEAD_DIM
        )
        bias_sums[0:1, value_lanes] += jnp.sum(grad_values, axis=0, keepdims=True)
        grad_joint[0, rows, lanes] = grad_queries.astype(BF16)
        grad_joint[1, rows, lanes] = grad_keys.astype(BF16)
        grad_joint[2, rows, lanes] = grad_values.astype(BF16)
        return carry

    lax.fori_loop(0, (grad_att.shape[0] // slots) * pairs, step, 0)


def entry_back_kernel(
    layer, with_low, joint_own, joint_far, weight_own, weight_far, stream, gain, grad_mid, order, *rest
):
    if with_low:
        grad_out, sums, low_t, total, partial, low = rest
    else:
        grad_out, sums, total, partial = rest
    member = pl.program_id(0)

    @pl.when(member == 0)
    def _():
        total[...] = jnp.zeros_like(total)
        partial[...] = jnp.zeros_like(partial)

    left = jnp.concatenate([joint_own[member], joint_far[member]], axis=1)
    right = jnp.concatenate([weight_own[0, 0], weight_far[0, 0]], axis=1)
    total[...] += dot_nt(left, right)

    def rows(start):
        here = pl.ds(start, BAND)
        normed_grad = total[here, :]
        through, gain_term = norm_backward(
            stream[here, :].astype(F32), normed_grad, gain[layer, 0:1, :]
        )
        value = grad_mid[here, :] + through
        grad_out[here, :] = value
        if with_low:
            low[here, :] = value.astype(BF16)
        partial[0] += fold_rows(gain_term)
        partial[1] += fold_rows(normed_grad)

    @pl.when(member == 2)
    def _():
        by_rows(stream.shape[0], rows, 1)
        sums[...] = jnp.sum(partial[...], axis=1)
        if with_low:
            by_blocks(low_t, order, lambda: low[...], dot_nt)


def pack_kernel(layers, *refs):
    ins, (own_out, far_out) = refs[:-2], refs[-2:]
    for layer in range(layers):
        sums_mid, sums_in, qv_own, qv_far, upb_own, upb_far = ins[6 * layer : 6 * layer + 6]
        tiles = upb_own.shape[0]
        for ref, qv, upb in ((own_out, qv_own, upb_own), (far_out, qv_far, upb_far)):
            for row, value in (
                (2 * layer, sums_in[0:1, :]),
                (2 * layer + 1, sums_mid[2:3, :]),
                (2 * (layers + layer), sums_in[1:2, :]),
                (2 * (layers + layer) + 1, sums_mid[3:4, :]),
                (2 * (2 * layers + layer), sums_mid[1:2, :]),
                (2 * (2 * layers + layer) + 1, sums_mid[0:1, :]),
                (6 * layers + layer, qv[...]),
            ):
                ref[row : row + 1, :] = value
            start = 7 * layers + tiles * layer
            ref[start : start + tiles, :] = upb[...]


def unpack_kernel(layers, mine, gain, bias, out_bias, qv, upb):
    total = mine[...]
    half = qv.shape[2]
    tiles = upb.shape[1] // mine.shape[1]
    width = mine.shape[1]
    for layer in range(layers):
        for norm in range(2):
            row = 2 * layer + norm
            gain[layer, norm : norm + 1, :] = total[row : row + 1]
            row += 2 * layers
            bias[layer, norm : norm + 1, :] = total[row : row + 1]
            row += 2 * layers
            out_bias[layer, norm : norm + 1, :] = total[row : row + 1]
        row = 6 * layers + layer
        for kind in range(2):
            qv[layer, kind : kind + 1, :] = total[row : row + 1, kind * half : (kind + 1) * half]
        row = 7 * layers + tiles * layer
        for part in range(tiles):
            upb[layer : layer + 1, part * width : (part + 1) * width] = total[
                row + part : row + part + 1
            ]


def finish_kernel(parts, *refs):
    layers = len(refs) // parts
    outs = refs[layers * parts :]
    for layer in range(layers):
        total = refs[layer * parts][...].astype(F32)
        for ref in refs[layer * parts + 1 : (layer + 1) * parts]:
            total = total + ref[...].astype(F32)
        column = 0
        for ref in outs:
            size = ref.shape[3]
            for member in range(ref.shape[1]):
                ref[layer, member] = total[:, column : column + size]
                column += size


def chunk_sources(order):
    first = list(order[:4])
    sources = []
    for target in range(16):
        source = 0
        for place, bit in enumerate(first):
            if (target >> (3 - place)) & 1:
                source |= 1 << (3 - bit)
        sources.append(source)
    return sources


def weight_kernel(sources, tiles, has_extra, *refs):
    if has_extra:
        left_own, left_far, right_own, right_far, lx_own, lx_far, rx_own, rx_far, keep, send = refs
    else:
        left_own, left_far, right_own, right_far, keep, send = refs

    def product(a_own, a_far, b_own, b_far):
        left = jnp.concatenate([a_own[...], a_far[...]], axis=1)
        right = jnp.concatenate([b_own[...].reshape(b_own.shape[-2:]), b_far[...].reshape(b_far.shape[-2:])], axis=0)
        size = left.shape[0] // 16
        low = dot(left, right).astype(BF16)
        for target, source in enumerate(sources):
            ref = keep if target < 8 else send
            ref[(target % 8) * size : (target % 8 + 1) * size, :] = low[
                source * size : (source + 1) * size, :
            ]

    if has_extra:

        @pl.when(pl.program_id(0) < tiles)
        def _():
            product(left_own, left_far, right_own, right_far)

        @pl.when(pl.program_id(0) == tiles)
        def _():
            product(lx_own, lx_far, rx_own, rx_far)

    else:
        product(left_own, left_far, right_own, right_far)


def weight_grad(name, order, left, right, extra=None, tiles=None, first=0):
    left_own, left_far = left
    right_own, right_far = right
    width, tokens = left_own.shape
    if right_own.ndim == 3:
        tile = right_own.shape[2]
        right_spec = pl.BlockSpec(
            (1, tokens, tile), lambda j: (jnp.minimum(j, tiles - 1) + first, 0, 0)
        )
    else:
        tile = 768 if tiles else 512
        tiles = tiles or right_own.shape[1] // tile
        right_spec = pl.BlockSpec((tokens, tile), lambda j: (0, j + first))
    steps = tiles + (1 if extra is not None else 0)
    ins = [left_own, left_far, right_own, right_far]
    specs = [fixed((width, tokens))] * 2 + [right_spec] * 2
    if extra is not None:
        ins += list(extra)
        specs += [fixed((width, tokens))] * 2 + [fixed((tokens, tile))] * 2
    half = out((width // 2, steps * tile), BF16)
    half_spec = pl.BlockSpec((width // 2, tile), lambda j: (0, j))
    return call(
        functools.partial(weight_kernel, chunk_sources(order), tiles, extra is not None),
        name,
        (steps,),
        ins,
        specs,
        [half, half],
        [half_spec, half_spec],
        flops=4 * width * tokens * steps * tile,
    )


def flip(bit):
    size = lax.axis_size("dp")
    return [(index, index ^ (1 << bit)) for index in range(size)]


class DpSum:
    def __init__(self, order, halves=None, units=()):
        self.order = list(order)
        self.incoming = None
        if halves is not None:
            keep, self.outgoing = halves
            self.members = [[keep]]
        else:
            self.members = [parts for unit in units for parts in unit.members]
            self.halve()

    def halve(self):
        rows = self.members[0][0].shape[0] // 2
        sends = [
            sum(part[rows:].astype(F32) for part in parts).astype(BF16) for parts in self.members
        ]
        self.outgoing = sends[0] if len(sends) == 1 else jnp.concatenate(sends, axis=1)
        self.members = [[part[:rows] for part in parts] for parts in self.members]

    @classmethod
    def joined(cls, units):
        whole_unit = cls(units[0].order, (None, jnp.concatenate([u.outgoing for u in units], axis=1)))
        whole_unit.members = [parts for unit in units for parts in unit.members]
        return whole_unit

    def start(self):
        self.incoming = lax.ppermute(self.outgoing, "dp", flip(self.order.pop(0)))

    def turn(self, go=True):
        column = 0
        for parts in self.members:
            width = parts[0].shape[1]
            parts.append(self.incoming[:, column : column + width])
            column += width
        self.incoming = None
        if self.order:
            self.halve()
            if go:
                self.start()

    def flying(self):
        return [self.incoming]

    def land(self, arrays):
        (self.incoming,) = arrays


class Everywhere:
    def __init__(self, mine, far, groups):
        self.mine = mine
        self.incoming = [swap(far)]
        self.groups = list(groups)

    def flying(self):
        return self.incoming

    def land(self, arrays):
        self.incoming = arrays

    def turn(self):
        if len(self.incoming) == 1:
            self.mine = self.mine + self.incoming[0]
        else:
            near, far, across = self.incoming
            self.mine = (self.mine + near) + (far + across)
        self.incoming = []
        if self.groups:
            group = self.groups.pop(0)
            masks = [1 << bit for bit in group]
            if len(masks) == 2:
                masks.append(masks[0] | masks[1])
            size = lax.axis_size("dp")
            self.incoming = [
                lax.ppermute(self.mine, "dp", [(index, index ^ mask) for index in range(size)])
                for mask in masks
            ]


def gate(value, starts=(), turns=(), after=(), holds=()):
    ends = [*turns, *holds]
    held = [unit.outgoing for unit in starts] + [array for unit in ends for array in unit.flying()]
    value, *held = lax.optimization_barrier((value, *held, *after))
    for unit in starts:
        unit.outgoing = held.pop(0)
        unit.start()
    for unit in ends:
        unit.land([held.pop(0) for _ in unit.flying()])
    for unit in turns:
        unit.turn()
    for unit in holds:
        unit.turn(go=False)
    return value


def swap(values):
    return lax.ppermute(values, "tensor", [(0, 1), (1, 0)])


def shards(
    images,
    valid_count,
    ln_gain,
    ln_bias,
    w_qkv,
    qv_bias,
    w_out,
    out_bias,
    w_up,
    up_bias,
    w_down,
    cotangent,
):
    local_rows, slots, width = images.shape
    tokens = local_rows * slots
    half = w_qkv.shape[3]
    ff_half = w_up.shape[2]
    tile = 768
    steps = ff_half // tile
    heads = half // HEAD_DIM
    dp = lax.axis_size("dp")
    bits = dp.bit_length() - 1
    assert dp == 1 << bits and bits >= 4 and lax.axis_size("tensor") == 2
    tail = tuple(range(4, bits))
    order_a = (0, 1, 2, 3) + tail
    order_b = (1, 0, 2, 3) + tail
    order_e = (2, 0, 1, 3) + tail
    order_d = (0, 2, 3, 1) + tail

    me = lax.axis_index("dp")
    counts = valid_count

    block = width // dp
    row = jnp.arange(width, dtype=jnp.int32)
    index = row // block
    mirrored = jnp.zeros_like(index)
    for bit in range(bits):
        mirrored = mirrored | (((index >> (bits - 1 - bit)) & 1) << bit)
    source = (mirrored ^ me) * block + row % block
    order = (source[:, None] == row[None, :]).astype(BF16)

    w_qkv = jnp.transpose(w_qkv, (0, 2, 1, 3))
    qkv = (w_qkv, swap(w_qkv))
    qv = (qv_bias, swap(qv_bias))

    images_2d = images.reshape(tokens, width)
    cotangent_2d = cotangent.reshape(tokens, width)
    smem = pl.BlockSpec(memory_space=pltpu.SMEM)
    wide = (tokens, width)
    flops_wide = 2 * width * width * tokens

    normed, normed_t, cotangent_t, wide_cotangent = call(
        prep_kernel,
        "prep",
        (),
        [images_2d, cotangent_2d, ln_gain, ln_bias, order],
        [whole()] * 5,
        [out(wide, BF16), out((width, tokens), BF16), out((width, tokens), BF16), out(wide, F32)],
        [whole()] * 4,
        flops=2 * flops_wide,
    )

    wout, wup, wdown = [
        (weight, swap(lax.optimization_barrier((weight, normed, qkv[1], qv[1]))[0]))
        for weight in (w_out, w_up, w_down)
    ]

    def attend(layer, normed, counts):
        lse_shape = (local_rows * heads, 1, slots)
        joint_out = out((3, tokens, half), BF16)
        att_out = out((tokens, half), BF16)
        lse_out = out(lse_shape, F32)
        results = call(
            functools.partial(attend_kernel, slots),
            "attend",
            (),
            [jnp.full((1,), layer, jnp.int32), counts, normed, in_hbm(qkv[0]), in_hbm(qkv[1]), qv[0], qv[1]],
            [smem, smem, whole(), hbm(), hbm(), whole(), whole()],
            [joint_out, joint_out, att_out, att_out, lse_out, lse_out],
            [whole()] * 6,
            [pltpu.VMEM((2, 3, width, half), BF16), pltpu.SemaphoreType.DMA((2, 3))],
            flops=12 * tokens * width * half + 8 * tokens * slots * half,
            limit=26,
        )
        return results[0::2], results[1::2]

    stream = images_2d
    saved = []
    got_cotangent_t = swap(cotangent_t)
    pooled = None
    for layer in range(LAYERS):
        last = layer == LAYERS - 1
        own, far = attend(layer, normed, counts)
        if layer == 0:
            upb = (up_bias, swap(up_bias))
        gain_in = ln_gain
        if layer > 0:
            before = saved[layer - 1]
            names = ("got_normed_t", "got_att", "got_mid_normed_t", "got_hid")
            gain_in, got_cotangent_t, *got = lax.optimization_barrier(
                (ln_gain, got_cotangent_t, *[before[name] for name in names])
            )
            before.update(zip(names, got))
        ff = pltpu.HBM((tokens, ff_half), BF16)
        extra = (
            [out((local_rows, width), F32)]
            if last
            else [out(wide, BF16), out((width, tokens), BF16)]
        )
        results = call(
            functools.partial(feed_kernel, layer, slots, last),
            "feed",
            (),
            [
                counts,
                stream,
                own[1],
                far[1],
                in_hbm(wout[0]),
                in_hbm(wout[1]),
                out_bias,
                gain_in,
                ln_bias,
                order,
                in_hbm(wup[0]),
                in_hbm(wup[1]),
                upb[0],
                upb[1],
                in_hbm(wdown[0]),
                in_hbm(wdown[1]),
            ],
            [smem]
            + [whole()] * 3
            + [hbm()] * 2
            + [whole()] * 4
            + [hbm()] * 2
            + [whole()] * 2
            + [hbm()] * 2,
            [out(wide, F32), out((width, tokens), BF16), ff, ff, ff, ff, out(wide, F32)] + extra,
            [whole()] * 2 + [hbm()] * 4 + [whole()] * (1 + len(extra)),
            [
                pltpu.VMEM(wide, BF16),
                pltpu.VMEM(wide, F32),
                pltpu.VMEM((2, tokens, tile), F32),
                pltpu.VMEM((2 * half, width), BF16),
                pltpu.VMEM((2 * steps, width, tile), BF16),
                pltpu.VMEM((2 * steps, tile, width), BF16),
                pltpu.VMEM((2 * steps, tokens, tile), BF16),
                pltpu.VMEM((2 * steps, tokens, tile), BF16),
                pltpu.SemaphoreType.DMA((2 + 4 * steps,)),
                pltpu.SemaphoreType.DMA((4 * steps,)),
            ],
            flops=8 * tokens * width * ff_half + 2 * flops_wide,
            limit=32,
        )
        mid, mid_normed_t, hid_own, hid_far, slope_own, slope_far, stream_next = results[:7]
        saved.append(
            dict(
                stream=stream,
                own=own,
                far=far,
                mid=mid,
                slope=(slope_own, slope_far),
                hid=hid_own,
                attended=own[1],
                normed_t=normed_t,
                mid_normed_t=mid_normed_t,
                got_hid=swap(hid_far),
                got_att=swap(far[1]),
                got_normed_t=swap(normed_t),
                got_mid_normed_t=swap(mid_normed_t),
            )
        )
        stream = stream_next
        if last:
            pooled = results[7]
        else:
            normed, normed_t = results[7:9]

    def feed_back(layer, grad, gain_in):
        kept = saved[layer]
        ff = pltpu.HBM((tokens, ff_half), BF16)
        bias_shape = out((steps, tile), F32)
        att_shape = out((tokens, half), BF16)
        return call(
            feed_back_kernel,
            "feed_back",
            (),
            [
                jnp.full((1,), layer, jnp.int32),
                grad,
                kept["mid"],
                gain_in,
                order,
                in_hbm(wdown[0]),
                in_hbm(wdown[1]),
                in_hbm(wup[0]),
                in_hbm(wup[1]),
                kept["slope"][0],
                kept["slope"][1],
                in_hbm(wout[0]),
                in_hbm(wout[1]),
            ],
            [smem] + [whole()] * 4 + [hbm()] * 8,
            [
                ff,
                ff,
                bias_shape,
                bias_shape,
                out(wide, F32),
                out((width, tokens), BF16),
                att_shape,
                att_shape,
                out((4, width), F32),
            ],
            [hbm()] * 2 + [whole()] * 7,
            [
                pltpu.VMEM(wide, BF16),
                pltpu.VMEM(wide, F32),
                pltpu.VMEM((2, tokens, tile), F32),
                pltpu.VMEM((4, 8, width), F32),
                pltpu.VMEM((2 * steps, tile, width), BF16),
                pltpu.VMEM((2 * steps, width, tile), BF16),
                pltpu.VMEM((2 * steps, tokens, tile), BF16),
                pltpu.VMEM((2 * steps, tokens, tile), BF16),
                pltpu.VMEM((2, half, width), BF16),
                pltpu.SemaphoreType.DMA((4, 2 * steps)),
                pltpu.SemaphoreType.DMA((2 * steps,)),
            ],
            flops=8 * tokens * width * ff_half + 2 * flops_wide,
            limit=32,
        )

    def attend_back(forward, grad_att, counts_in):
        joint, _, lse = forward
        return call(
            functools.partial(attend_back_kernel, slots),
            "attend_back",
            (),
            [counts_in, joint, lse, grad_att],
            [smem, whole(), whole(), whole()],
            [out(joint.shape, BF16), out((1, 2 * half), F32)],
            [whole()] * 2,
            flops=10 * tokens * slots * half,
        )

    def entry_back(layer, joint_own, joint_far, grad_mid, gain_in):
        with_low = layer > 0
        return call(
            functools.partial(entry_back_kernel, layer, with_low),
            "entry_back",
            (3,),
            [
                joint_own,
                joint_far,
                in_hbm(qkv[0]),
                in_hbm(qkv[1]),
                saved[layer]["stream"],
                gain_in,
                grad_mid,
                order,
            ],
            [whole()] * 2
            + [pl.BlockSpec((1, 1, width, half), lambda c: (layer, c, 0, 0))] * 2
            + [whole()] * 4,
            [out(wide, F32), out((2, width), F32)]
            + ([out((width, tokens), BF16)] if with_low else []),
            [whole()] * (3 if with_low else 2),
            [pltpu.VMEM(wide, F32), pltpu.VMEM((2, 8, width), F32)]
            + ([pltpu.VMEM(wide, BF16)] if with_low else []),
            flops=12 * tokens * width * half,
        )

    def down_halves(layer, order_of, grad_t, got_grad_t):
        kept = saved[layer]
        return weight_grad(
            "down_grad", order_of, (grad_t, got_grad_t), (in_hbm(kept["hid"]) if layer else kept["hid"], kept["got_hid"])
        )

    def up_halves(layer, order_of, pre_own, got_pre, tiles=None, first=0):
        kept = saved[layer]
        return weight_grad(
            "up_grad",
            order_of,
            (kept["mid_normed_t"], kept["got_mid_normed_t"]),
            (pre_own, got_pre),
            tiles=tiles,
            first=first,
        )

    def lefts(layer):
        return saved[layer]["normed_t"], saved[layer]["got_normed_t"]

    def extras(layer, mid_t, got_mid_t):
        return mid_t, got_mid_t, saved[layer]["attended"], saved[layer]["got_att"]

    small = [None] * LAYERS
    down_1 = DpSum(order_a, down_halves(1, order_a, cotangent_t, got_cotangent_t))
    gain_in = gate(ln_gain, [down_1])
    pre_own, pre_far, upb_own, upb_far, grad_mid, mid_t, att_own, att_far, sums_mid = feed_back(
        1, wide_cotangent, gain_in
    )
    got_pre, got_mid_t = swap(pre_far), swap(mid_t)
    joint_far, qv_far = attend_back(saved[1]["far"], att_far, counts)
    got_joint = swap(joint_far)
    pre_own = gate(pre_own, [], [], [qv_far], [down_1])
    pre_own = gate(pre_own, [down_1])
    up_1 = DpSum(order_a, up_halves(1, order_a, pre_own, got_pre))
    counts_in = gate(counts, [up_1])
    joint_own, qv_own = attend_back(saved[1]["own"], att_own, counts_in)
    gain_in = gate(gain_in, after=[qv_own])
    grad, sums_in, grad_t = entry_back(1, joint_own, joint_far, grad_mid, gain_in)
    got_grad_t = swap(grad_t)
    small[1] = (sums_mid, sums_in, qv_own, qv_far, upb_own, upb_far)
    joint_own = gate(joint_own, [], [down_1], [sums_in])
    rest_1 = DpSum(
        order_e,
        weight_grad(
            "qkv_out_grad",
            order_e,
            lefts(1),
            (joint_own, got_joint),
            extras(1, mid_t, got_mid_t),
            tiles=3,
        ),
    )
    grad_t = gate(grad_t, [rest_1])
    down_0 = DpSum(order_a, down_halves(0, order_a, grad_t, got_grad_t))

    gain_in = gate(gain_in, [down_0], [up_1], holds=[down_1])
    pre_own, pre_far, upb_own, upb_far, grad_mid, mid_t, att_own, att_far, sums_mid = feed_back(
        0, grad, gain_in
    )
    got_pre, got_mid_t = swap(pre_far), swap(mid_t)
    counts_in = gate(counts_in, [], [up_1], [sums_mid], [rest_1])
    joint_far, qv_far = attend_back(saved[0]["far"], att_far, counts_in)
    got_joint = swap(joint_far)
    pre_own = gate(pre_own, [], [], [qv_far], [down_0, up_1])
    late_1 = DpSum.joined([up_1, down_1])
    pre_own = gate(pre_own, [down_0, late_1])
    up_0 = DpSum(order_d, up_halves(0, order_d, pre_own, got_pre))
    counts_in = gate(counts_in, [up_0], [], [got_mid_t, got_joint])
    joint_own, qv_own = attend_back(saved[0]["own"], att_own, counts_in)
    rest_0 = DpSum(
        order_b,
        weight_grad(
            "qkv_out_grad",
            order_b,
            lefts(0),
            (joint_own, got_joint),
            extras(0, mid_t, got_mid_t),
            tiles=3,
        ),
    )
    gain_in = gate(gain_in, [rest_0], [down_0, late_1], [qv_own])
    grad, sums_in = entry_back(0, joint_own, joint_far, grad_mid, gain_in)
    last = gate(sums_in, [rest_1], [up_0])
    small[0] = (sums_mid, last, qv_own, qv_far, upb_own, upb_far)
    ins = [array for arrays in small for array in arrays]
    vector_shape = out(((7 + steps) * LAYERS, width), F32)
    mine, far = call(
        functools.partial(pack_kernel, LAYERS),
        "pack_small",
        (),
        ins,
        [whole()] * len(ins),
        [vector_shape] * 2,
        [whole()] * 2,
    )
    vector = Everywhere(mine, far, [(0, 1), (2,), (3,), *[(bit,) for bit in tail]])
    last = gate(last, holds=[down_0])
    last = gate(last, [], [rest_0, up_0, vector], [down_0.outgoing], [rest_1])
    last = gate(last, holds=[rest_0, up_0])
    last = gate(last, [rest_0, up_0, down_0, rest_1], [vector])
    last = gate(last, holds=[rest_0, rest_1])
    late_0 = DpSum.joined([rest_0, rest_1])
    last = gate(last, [late_0], [up_0, down_0, vector])
    last = gate(last, [], [late_0])
    last = gate(last, [], [vector])
    while vector.flying():
        vector.turn()
    running = [late_1, late_0, down_0, up_0]
    while any(unit.incoming is not None for unit in running):
        last = gate(last, [], [unit for unit in running if unit.incoming is not None][:4])

    def finish(first, second, shapes):
        ins = [*first, *second]
        return call(
            functools.partial(finish_kernel, len(first)),
            "finish",
            (),
            ins,
            [whole()] * len(ins),
            [out((LAYERS,) + shape, F32) for shape in shapes],
            [whole()] * len(shapes),
        )

    (down_grad,) = finish(down_0.members[0], late_1.members[1], [(1, block, ff_half)])
    (up_grad,) = finish(up_0.members[0], late_1.members[0], [(1, block, ff_half)])
    qkv_grad, out_grad = finish(late_0.members[0], late_0.members[1], [(3, block, half), (1, block, half)])
    total, qkv_grad = lax.optimization_barrier((vector.mine, qkv_grad))
    gain_grads, shift_grads, outb_grads, qv_grads, upb_grads = call(
        functools.partial(unpack_kernel, LAYERS),
        "unpack_small",
        (),
        [total],
        [whole()],
        [
            out(ln_gain.shape, F32),
            out(ln_bias.shape, F32),
            out(out_bias.shape, F32),
            out(qv_bias.shape, F32),
            out(up_bias.shape, F32),
        ],
        [whole()] * 5,
    )
    return (
        stream.reshape(images.shape),
        pooled,
        grad.reshape(images.shape),
        gain_grads,
        shift_grads,
        jnp.transpose(qkv_grad, (0, 2, 1, 3)),
        qv_grads,
        jnp.transpose(out_grad[:, 0], (0, 2, 1)),
        outb_grads,
        up_grad[:, 0],
        upb_grads,
        jnp.transpose(down_grad[:, 0], (0, 2, 1)),
    )


def solution(mesh):
    placed = (
        P(("dp", "tensor"), None, None),
        P("dp"),
        P(),
        P(),
        P(None, None, None, "tensor"),
        P(None, None, "tensor"),
        P(None, "tensor", None),
        P(),
        P(None, None, "tensor"),
        P(None, "tensor"),
        P(None, "tensor", None),
        P(("dp", "tensor"), None, None),
    )
    return jax.shard_map(
        shards,
        mesh=mesh,
        in_specs=placed,
        out_specs=(
            P(("dp", "tensor"), None, None),
            P(("dp", "tensor"), None),
            P(("dp", "tensor"), None, None),
            P(),
            P(),
            P(None, "dp", None, "tensor"),
            P(None, None, "tensor"),
            P(None, "tensor", "dp"),
            P(),
            P(None, "dp", "tensor"),
            P(None, "tensor"),
            P(None, "tensor", "dp"),
        ),
        check_vma=False,
    )
```
